32 devices in a mesh: dp: 2 (over x), ctx: 4 (over z), tp: 4 (over y, core).
Axes of the slice: x: 2, y: 2, z: 4, core: 2. Of those that a mesh axis runs over, the one named last changes fastest.
Arguments:
- prompt_x: bfloat16 [4, 2048, 768], P('dp', 'ctx'), may hold values from -6 to 6
- cont_x: bfloat16 [16, 256, 768], P(('dp', 'ctx')), may hold values from -6 to 6
- prompt_hist: bfloat16 [4, 4, 2048, 768], P(None, 'dp', 'ctx'), may hold values from -6 to 6
- cont_hist: bfloat16 [4, 16, 256, 768], P(None, ('dp', 'ctx')), may hold values from -6 to 6
- teacher: bfloat16 [16, 256, 768], P(('dp', 'ctx')), may hold values from -6 to 6
- valid_mask: int32 [16, 256], P(('dp', 'ctx')), may hold values 0 or 1
- cont_group: int32 [16], P(('dp', 'ctx')), may hold values from 0 to 1
- layer_ids: int32 [4], replicated, may hold values from 0 to 3, each once
- dwa_weights: float32 [5], replicated, may hold values from 0.3 to 1
- qkv_weight: bfloat16 [768, 3, 768], P('dp', None, 'tp'), may hold values from -0.21875 to 0.21875
- out_weight: bfloat16 [768, 768], P('tp', 'dp'), may hold values from -1.75 to 1.75
- up_weight: bfloat16 [768, 3072], P('dp', 'tp'), may hold values from -0.21875 to 0.21875
- down_weight: bfloat16 [3072, 768], P('tp', 'dp'), may hold values from -0.109375 to 0.109375
- ln1_gain: bfloat16 [768], P('dp'), may hold values from 0.5 to 1.5
- ln1_bias: bfloat16 [768], P('dp'), may hold values from -1.5 to 1.5
- ln2_gain: bfloat16 [768], P('dp'), may hold values from 0.5 to 1.5
- ln2_bias: bfloat16 [768], P('dp'), may hold values from -1.5 to 1.5
Outputs:
- prompt_out: bfloat16 [4, 2048, 768], P('dp', 'ctx')
- cont_out: bfloat16 [16, 256, 768], P(('dp', 'ctx'))
- loss: float32 [], replicated
- prompt_grad: bfloat16 [4, 2048, 768], P('dp', 'ctx')
- cont_grad: bfloat16 [16, 256, 768], P(('dp', 'ctx'))
- qkv_grad: float32 [768, 3, 768], P('dp', None, 'tp')
- out_grad: float32 [768, 768], P('tp', 'dp')
- up_grad: float32 [768, 3072], P('dp', 'tp')
- down_grad: float32 [3072, 768], P('tp', 'dp')
- ln1_gain_grad: float32 [768], P('dp')
- ln1_bias_grad: float32 [768], P('dp')
- ln2_gain_grad: float32 [768], P('dp')
- ln2_bias_grad: float32 [768], P('dp')
- dwa_grad: float32 [5], replicated
The draws below stay inside these ranges and needn't reach their ends.
Inputs may be any that keep to these rules, and one draw needn't show every extreme that they name: `cont_group`: each continuation names one of the 2 prompts held at its own dp index. `layer_ids`: each depth 0 to 3 is stored exactly once.
All inputs are finite; a program needn't handle non-finite values. No bound on the sum of `valid_mask` on one device may be relied on, other than what follows from the above.
Results may differ from the reference program's by a relative error of at most 0.015.
Values may be sent and summed in bfloat16 or wider, within the bound.
A program may use at most 512 MiB of HBM per device.

```python
import math
import jax
import jax.numpy as jnp
from jax import lax

D = 768
HEADS = 12
HEAD_DIM = 64
FF = 3072
PROMPT = 2048
CLEN = 256
GRP_DEV = 2
CONT_DEV = 2
PROMPTS = 4
CONT_ALL = 16
N_DP = 2
N_CTX = 4


def touch_ends(values, stream_key, least, high):
    extent = values.shape
    spot = [jax.random.randint(jax.random.fold_in(stream_key, axis), (), 0, extent[axis]) for axis in range(len(extent))]
    values = values.at[tuple(spot)].set(least)
    longest = extent.index(max(extent))
    spot[longest] = (spot[longest] + 1) % extent[longest]
    return values.at[tuple(spot)].set(high)


def level_of(stream_key, dims, pieces, smallest, top_value):
    def one(position, blocks):
        draws = jax.random.uniform(jax.random.fold_in(jax.random.fold_in(stream_key, 6), position), (blocks,), jnp.float32, smallest / len(pieces), top_value / len(pieces))
        return jnp.repeat(jnp.exp(draws), dims[position] // blocks).reshape((-1,) + (1,) * (len(dims) - position - 1))

    gain = one(*pieces[0])
    for cut in pieces[1:]:
        gain = gain * one(*cut)
    return gain


def gaussian(own_key, dims, width, bound, split=(), kind=jnp.bfloat16):
    array = width * jax.random.normal(own_key, dims, jnp.float32)
    if split:
        array = array * level_of(own_key, dims, split, -0.22, 0.18)
    return jnp.clip(array, -bound, bound).astype(kind)


def setup_inputs(seed: int = 0) -> dict:
    streams_of = jax.random.split(jax.random.key(seed), 18)
    return {
        "prompt_x": gaussian(streams_of[0], (PROMPTS, PROMPT, D), 1.0, 6.0, ((0, 2), (1, 4))),
        "cont_x": gaussian(streams_of[1], (CONT_ALL, CLEN, D), 1.0, 6.0, ((0, 8),)),
        "prompt_hist": gaussian(streams_of[2], (4, PROMPTS, PROMPT, D), 1.0, 6.0, ((1, 2), (2, 4))),
        "cont_hist": gaussian(streams_of[3], (4, CONT_ALL, CLEN, D), 1.0, 6.0, ((1, 8),)),
        "teacher": gaussian(streams_of[4], (CONT_ALL, CLEN, D), 1.0, 6.0, ((0, 8),)),
        "valid_mask": touch_ends((jax.random.randint(streams_of[5], (CONT_ALL, CLEN), 0, 4) < 3).astype(jnp.int32), jax.random.fold_in(streams_of[5], 1), 0, 1),
        "cont_group": touch_ends(jax.random.randint(streams_of[6], (CONT_ALL,), 0, GRP_DEV), jax.random.fold_in(streams_of[6], 1), 0, GRP_DEV - 1).astype(jnp.int32),
        "layer_ids": jax.random.permutation(streams_of[7], 4).astype(jnp.int32),
        "dwa_weights": jnp.clip(jax.random.uniform(streams_of[8], (5,), jnp.float32, 0.3, 1.0), 0.3, 1.0),
        "qkv_weight": gaussian(streams_of[9], (D, 3, D), D ** -0.5, 0.21875, ((0, 2), (2, 4))),
        "out_weight": gaussian(streams_of[10], (D, D), (D // 64) ** -0.5, 1.75, ((0, 4), (1, 2))),
        "up_weight": gaussian(streams_of[11], (D, FF), D ** -0.5, 0.21875, ((0, 2), (1, 4))),
        "down_weight": gaussian(streams_of[12], (FF, D), FF ** -0.5, 0.109375, ((0, 4), (1, 2))),
        "ln1_gain": jnp.clip(1.0 + 0.1 * jax.random.normal(streams_of[13], (D,), jnp.float32), 0.5, 1.5).astype(jnp.bfloat16),
        "ln1_bias": gaussian(streams_of[14], (D,), 0.3, 1.5, ((0, 2),)),
        "ln2_gain": jnp.clip(1.0 + 0.1 * jax.random.normal(streams_of[15], (D,), jnp.float32), 0.5, 1.5).astype(jnp.bfloat16),
        "ln2_bias": gaussian(streams_of[16], (D,), 0.3, 1.5, ((0, 2),)),
    }


EPS = 1e-05
NEG = -1e+30
HIGH = lax.Precision.HIGHEST

@jax.custom_vjp
def low(v):
    return lax.optimization_barrier(v.astype(jnp.bfloat16)).astype(jnp.float32)

@jax.custom_vjp
def low_back(v):
    return v

def low_keep(v):
    return (low(v), None)

def low_pass(kept, grad):
    return (grad,)

def back_keep(v):
    return (v, None)

def back_low(kept, grad):
    return (low(grad),)
low.defvjp(low_keep, low_pass)
low_back.defvjp(back_keep, back_low)

def matmul(left, right):
    return jnp.dot(left, right, precision=HIGH)

def layer_norm(x, norm_gain, norm_bias):
    row_mean = lax.optimization_barrier(jnp.mean(x, -1, keepdims=True))
    centered_input = x - row_mean
    var = lax.optimization_barrier(jnp.mean(centered_input * centered_input, -1, keepdims=True))
    return centered_input * lax.rsqrt(var + EPS) * norm_gain + norm_bias

def rope_tables(positions):
    half = HEAD_DIM // 2
    freq = jnp.exp(jnp.arange(half, dtype=jnp.float32) * (-2.0 * math.log(10000.0) / HEAD_DIM))
    angle = positions.astype(jnp.float32)[:, None] * freq[None, :]
    cosine = jnp.cos(angle)
    sine = jnp.sin(angle)
    return (jnp.concatenate([cosine, cosine], -1), jnp.concatenate([sine, sine], -1))

def rotate(x, cosine, sine):
    half = x.shape[-1] // 2
    turned = jnp.concatenate([-x[..., half:], x[..., :half]], -1)
    return x * cosine[:, None, :] + turned * sine[:, None, :]

def projections(rows, weights, positions):
    qkv_w, out_w, up_w, down_w, first_gain, first_bias, second_gain, second_bias = weights
    normed = low(layer_norm(rows, first_gain, first_bias))
    proj = matmul(normed, qkv_w.reshape(D, 3 * D)).reshape(-1, 3, HEADS, HEAD_DIM)
    cosine, sine = rope_tables(positions)
    query = low(rotate(low_back(proj[:, 0]), cosine, sine))
    key = low(rotate(low_back(proj[:, 1]), cosine, sine))
    value = low(low_back(proj[:, 2]))
    return (query, key, value)

def branch_tail(rows, attended, weights):
    qkv_w, out_w, up_w, down_w, first_gain, first_bias, second_gain, second_bias = weights
    attn = low_back(matmul(attended, out_w))
    hidden_in = rows + attn
    normed = low(layer_norm(hidden_in, second_gain, second_bias))
    upper = low_back(matmul(normed, up_w))
    hidden = low(jax.nn.gelu(upper, approximate=True))
    return hidden_in + low_back(matmul(hidden, down_w))

def prompt_step(weights, rows):
    positions = jnp.arange(PROMPT, dtype=jnp.int32)
    query, key, value = projections(rows, weights, positions)
    scale = 1.0 / math.sqrt(HEAD_DIM)
    scores = low_back(jnp.einsum('qhd,khd->hqk', query, key, precision=HIGH) * scale)
    allowed = positions[None, :] <= positions[:, None]
    probs = low(jax.nn.softmax(jnp.where(allowed[None], scores, NEG), -1))
    attended = low(low_back(jnp.einsum('hqk,khd->qhd', probs, value, precision=HIGH))).reshape(PROMPT, D)
    return (branch_tail(rows, attended, weights), key, value)

def cont_step(weights, block, keys, values, prompt_groups, mask):
    count_block = block.shape[0]
    rows = block.reshape(-1, D)
    positions = jnp.tile(PROMPT + jnp.arange(CLEN, dtype=jnp.int32), count_block)
    query, key, value = projections(rows, weights, positions)
    query = query.reshape(count_block, CLEN, HEADS, HEAD_DIM)
    key = key.reshape(count_block, CLEN, HEADS, HEAD_DIM)
    value = value.reshape(count_block, CLEN, HEADS, HEAD_DIM)
    all_keys = jnp.concatenate([jnp.take(keys, prompt_groups, axis=0), key], 1)
    all_values = jnp.concatenate([jnp.take(values, prompt_groups, axis=0), value], 1)
    scale = 1.0 / math.sqrt(HEAD_DIM)
    scores = low_back(jnp.einsum('cqhd,ckhd->chqk', query, all_keys, precision=HIGH) * scale)
    steps_idx = jnp.arange(CLEN, dtype=jnp.int32)
    causal = steps_idx[None, :] <= steps_idx[:, None]
    self_ok = causal[None] & (mask[:, None, :] == 1)
    allowed = jnp.concatenate([jnp.ones((count_block, CLEN, PROMPT), dtype=jnp.bool_), self_ok], -1)
    probs = low(jax.nn.softmax(jnp.where(allowed[:, None], scores, NEG), -1))
    attended = low(low_back(jnp.einsum('chqk,ckhd->cqhd', probs, all_values, precision=HIGH))).reshape(-1, D)
    return branch_tail(rows, attended, weights).reshape(count_block, CLEN, D)

def reference(prompt_x, cont_x, prompt_hist, cont_hist, teacher, valid_mask, cont_group, layer_ids, dwa_weights, qkv_weight, out_weight, up_weight, down_weight, ln1_gain, ln1_bias, ln2_gain, ln2_bias):
    f32 = jnp.float32
    slot_pick = (layer_ids[:, None] == jnp.arange(4, dtype=jnp.int32)[None, :]).astype(f32)
    maskf = valid_mask.astype(f32)
    count = jnp.maximum(jnp.sum(maskf), 1.0)
    block_conts = CONT_DEV * N_CTX
    prompt_fn = jax.checkpoint(prompt_step)
    cont_fn = jax.checkpoint(cont_step)

    def loss_fn(prompt_in, cont_in, dwa, qkv_w, out_w, up_w, down_w, first_gain, first_bias, second_gain, second_bias):
        weights = (qkv_w, out_w, up_w, down_w, first_gain, first_bias, second_gain, second_bias)

        def prompt_scan(carry, rows):
            return (carry, prompt_fn(weights, rows))
        _, (y_prompt, keys, values) = lax.scan(prompt_scan, jnp.zeros((), f32), prompt_in)
        keys = keys.reshape(N_DP, GRP_DEV, PROMPT, HEADS, HEAD_DIM)
        values = values.reshape(N_DP, GRP_DEV, PROMPT, HEADS, HEAD_DIM)
        inputs = (cont_in.reshape(N_DP, block_conts, CLEN, D), keys, values, cont_group.reshape(N_DP, block_conts), valid_mask.reshape(N_DP, block_conts, CLEN))

        def cont_scan(carry, items):
            return (carry, cont_fn(weights, items[0], items[1], items[2], items[3], items[4]))
        _, y_cont = lax.scan(cont_scan, jnp.zeros((), f32), inputs)
        y_cont = y_cont.reshape(CONT_ALL, CLEN, D)
        slot_w = jnp.dot(slot_pick, dwa[:4], precision=HIGH)
        mixed_p = dwa[4] * y_prompt
        mixed_c = dwa[4] * y_cont
        for slot in range(4):
            mixed_p = mixed_p + slot_w[slot] * prompt_hist[slot].astype(f32)
            mixed_c = mixed_c + slot_w[slot] * cont_hist[slot].astype(f32)
        diff = mixed_c - teacher.astype(f32)
        loss = jnp.sum(maskf[..., None] * diff * diff) / (count * D)
        return (loss, (mixed_p, mixed_c))
    primals = (prompt_x.astype(f32), cont_x.astype(f32), dwa_weights, qkv_weight.astype(f32), out_weight.astype(f32), up_weight.astype(f32), down_weight.astype(f32), ln1_gain.astype(f32), ln1_bias.astype(f32), ln2_gain.astype(f32), ln2_bias.astype(f32))
    loss, back, outputs = jax.vjp(loss_fn, *primals, has_aux=True)
    grads = back(jnp.ones((), f32))
    return (outputs[0].astype(jnp.bfloat16), outputs[1].astype(jnp.bfloat16), loss, grads[0].astype(jnp.bfloat16), grads[1].astype(jnp.bfloat16), grads[3], grads[4], grads[5], grads[6], grads[7], grads[8], grads[9], grads[10], grads[2])
```

```python
import functools
import math

import jax
import jax.numpy as jnp
from jax import lax
from jax.experimental import pallas as pl
from jax.experimental.pallas import tpu as pltpu
from jax.sharding import PartitionSpec as P

HEAD_DIM = 64
EPS = 1e-05
NEG = -1e30
MESH = pl.DeviceIdType.MESH
f32 = jnp.float32
bf16 = jnp.bfloat16
VMEM_SPEC = pl.BlockSpec(memory_space=pltpu.VMEM)
SMEM_SPEC = pl.BlockSpec(memory_space=pltpu.SMEM)
HBM_SPEC = pl.BlockSpec(memory_space=pl.ANY)
DMA = pltpu.SemaphoreType.DMA
LIMIT = 56 << 20
NT = (((1,), (1,)), ((), ()))
TN = (((0,), (0,)), ((), ()))
CH = 128
BIG = 256


def dot(a, b):
    return jnp.dot(a, b, preferred_element_type=f32)


def dot_nt(a, b):
    return lax.dot_general(a, b, NT, preferred_element_type=f32)


def dot_tn(a, b):
    return lax.dot_general(a, b, TN, preferred_element_type=f32)


def rows(start, size):
    return pl.ds(pl.multiple_of(start, size), size)


def loop(count, body):
    def step(i, carry):
        body(i)
        return carry

    lax.fori_loop(0, count, step, 0)


def kernel_call(body, outs, scratch, cid, specs, args, flops=0, name=None):
    return pl.pallas_call(
        body,
        out_shape=[jax.ShapeDtypeStruct(s, d) for s, d in outs],
        in_specs=specs,
        out_specs=[VMEM_SPEC] * len(outs),
        scratch_shapes=scratch,
        compiler_params=pltpu.CompilerParams(
            collective_id=cid, has_side_effects=True, vmem_limit_bytes=LIMIT
        ),
        cost_estimate=pl.CostEstimate(flops=flops, bytes_accessed=30 << 20, transcendentals=0),
        name=name,
    )(*args)


def greet(partners):
    barrier = pltpu.get_barrier_semaphore()
    for device in partners:
        pl.semaphore_signal(barrier, inc=1, device_id=device, device_id_type=MESH)
    pl.semaphore_wait(barrier, len(partners))


def remote(src, dst, send, recv, device):
    return pltpu.make_async_remote_copy(
        src_ref=src,
        dst_ref=dst,
        send_sem=send,
        recv_sem=recv,
        device_id=device,
        device_id_type=MESH,
    )


def axis_peers(axis, count):
    me = lax.axis_index(axis)
    return [{axis: lax.rem(me + d, count)} for d in range(1, count)]


def tp_place():
    tp = lax.axis_index("tp")
    core = lax.rem(tp, 2)
    mate = {"tp": tp + 1 - 2 * core}
    across = {"tp": lax.rem(tp + 2, 4)}
    return core, mate, across


def norm_rows(x):
    mean = jnp.mean(x, -1, keepdims=True)
    centered = x - mean
    var = jnp.mean(centered * centered, -1, keepdims=True)
    inverse = lax.rsqrt(var + EPS)
    return centered * inverse, inverse


def norm_back(gradient, whitened, inverse, gain):
    e = gradient * gain
    return inverse * (
        e - jnp.mean(e, -1, keepdims=True) - whitened * jnp.mean(e * whitened, -1, keepdims=True)
    )


def lanes_below(shape, bound):
    return lax.broadcasted_iota(jnp.int32, shape, len(shape) - 1) < bound


def turn(y, tab, sign, half):
    cos, low, high = tab[:, :128], tab[:, 128:256], tab[:, 256:384]
    turned = sign * (pltpu.roll(y, 96, 1) * low + pltpu.roll(y, 32, 1) * high)
    if not half:
        return y * cos + turned
    return jnp.where(lanes_below(y.shape, 64), y * cos + turned, y)


COLS = ((0, 256), (256, 512), (512, 640))


def project_body(
    n_dp, n_ctx, plen, clen,
    px, cx, w, g1, b1, g2, b2, valid,
    q, kv, xn, gains, tab, cnt_out, w_full,
    gb, gbs, cnt, cnts, send, recv,
):
    me = lax.axis_index("dp")
    depth = w.shape[0]
    width = px.shape[1]
    peers = axis_peers("dp", n_dp)
    for i, vector in enumerate((g1, b1, g2, b2)):
        gb[i:i + 1] = vector[...].astype(f32)
    gb[4:8] = jnp.zeros((4, depth), f32)
    cnt[...] = jnp.zeros(cnt.shape, f32) + jnp.sum(valid[...].astype(f32))
    greet(peers)
    here = rows(me * depth, depth)
    copies = []
    for d, device in enumerate(peers):
        pairs = [(gb, gbs.at[me]), (cnt, cnts.at[me])]
        pairs += [(w.at[:, a:b], w_full.at[here, a:b]) for a, b in COLS]
        copies.append(
            [remote(s, t, send.at[d, i], recv.at[d, i], device) for i, (s, t) in enumerate(pairs)]
        )
    for i in range(5):
        for group in copies:
            group[i].start()
    gbs[me] = gb[...]
    cnts[me] = cnt[...]
    w_full[here] = w[...]

    first = lax.axis_index("ctx") * plen

    def table(count, base, start):
        def body(i):
            shape = (CH, 128)
            lane = lax.broadcasted_iota(jnp.int32, shape, 1)
            row = lax.broadcasted_iota(jnp.int32, shape, 0)
            turns = lax.rem(lane, 32).astype(f32) * (-2.0 * math.log(10000.0) / HEAD_DIM)
            angle = (row + (start + i * CH)).astype(f32) * jnp.exp(turns)
            sin = jnp.sin(angle)
            left = lax.rem(lane, 64) < 32
            at = rows(base + i * CH, CH)
            tab[at, 0:128] = jnp.cos(angle)
            tab[at, 128:256] = jnp.where(left, -sin, 0.0)
            tab[at, 256:384] = jnp.where(left, 0.0, sin)

        loop(count // CH, body)

    table(plen, 0, first)
    table(clen, plen, n_ctx * plen)
    for group in copies:
        group[0].wait_recv()
        group[1].wait_recv()
    total = jnp.zeros(gains.shape, f32)
    count = jnp.zeros(cnt.shape, f32)
    for d in range(n_dp):
        row = lax.broadcasted_iota(jnp.int32, (depth, width), 0) + d * depth
        col = lax.broadcasted_iota(jnp.int32, (depth, width), 1)
        total += dot(gbs[d].astype(bf16), (row == col).astype(f32).astype(bf16))
        count += cnts[d]
    gains[...] = total
    cnt_out[...] = count
    n_prompt = px.shape[0]

    def norm_part(x, base):
        def body(i):
            whitened, _ = norm_rows(x[rows(i * CH, CH)].astype(f32))
            xn[rows(base + i * CH, CH)] = (whitened * gains[0:1] + gains[1:2]).astype(bf16)

        loop(x.shape[0] // CH, body)

    norm_part(px, 0)
    norm_part(cx, n_prompt)

    def project_part(store, lo, hi):
        def part(count, base, tab_base, period):
            def body(i):
                at = rows(base + i * BIG, BIG)
                t = tab[rows(tab_base + lax.rem(i * BIG, period), BIG)]
                store(at, t, dot(xn[at], w_full[:, lo:hi]))

            loop(count // BIG, body)

        part(n_prompt, 0, 0, plen)
        part(cx.shape[0], n_prompt, plen, clen)

    def store_q(at, t, y):
        q[at, 0:128] = (turn(y[:, 0:128], t, 1.0, False) * 0.125).astype(bf16)
        q[at, 128:256] = (turn(y[:, 128:256], t, 1.0, True) * 0.125).astype(bf16)

    def store_pair(at, t, y):
        kv[at, 0:128] = turn(y[:, 0:128], t, 1.0, False).astype(bf16)
        kv[at, 128:256] = y[:, 128:256].astype(bf16)

    def store_third(at, t, y):
        kv[at, 256:384] = turn(y, t, 1.0, True).astype(bf16)

    for i, store in enumerate((store_q, store_pair, store_third)):
        for group in copies:
            group[2 + i].wait_recv()
        project_part(store, *COLS[i])
    for group in copies:
        for copy in group:
            copy.wait_send()


def attend_body(
    n_ctx, n_dp, share, plen, clen, groups, conts,
    sel, q, kv, bias, cnt, *refs,
):
    if share:
        wo, wu, wd = refs[:3]
        refs = refs[3:]
        o, lse, msgs, wo_full, wu_full, wd_full = refs[:6]
        refs = refs[6:]
        kvs, cnts, m_s, l_s, acc_s, s_kv, r_kv, s_c, r_c, s_w, r_w = refs
    else:
        o, lse, msgs = refs[:3]
        kvs, cnts, m_s, l_s, acc_s, s_kv, r_kv, s_c, r_c = refs[3:]
    me = lax.axis_index("ctx")
    last = n_ctx - 1
    n_prompt = groups * plen
    tile = clen
    peers = axis_peers("ctx", n_ctx)
    greet(peers + (axis_peers("dp", n_dp) if share else []))

    def hop(slot, step, side):
        there = kvs.at[slot]
        return remote(there, there, s_kv.at[side, slot], r_kv.at[slot], {"ctx": me + step})

    kvs[me] = kv[0:n_prompt]

    @pl.when(me < last)
    def _():
        hop(me, 1, 0).start()

    @pl.when(me > 0)
    def _():
        hop(me, -1, 1).start()

    note = cnts.at[me]
    cnts[me] = cnt[...]
    for i in range(conts):
        cnts[me, 1 + i:2 + i] = jnp.zeros((1, 128), f32) + sel[i].astype(f32)
    counts = [remote(note, note, s_c.at[d], r_c.at[d], device) for d, device in enumerate(peers)]
    for copy in counts:
        copy.start()
    weights = []
    if share:
        mine = lax.axis_index("dp")
        depth = wu.shape[0]
        cols = pl.ds(pl.multiple_of(mine * depth, 128), depth)
        here = rows(mine * depth, depth)
        top = 2 * HEAD_DIM
        gap = top + HEAD_DIM
        for d, device in enumerate(axis_peers("dp", n_dp)):
            for i, (s, t) in enumerate((
                (wo.at[0:top], wo_full.at[0:top, cols]),
                (wo.at[top:gap], wo_full.at[gap:gap + HEAD_DIM, cols]),
                (wu, wu_full.at[here]),
                (wd, wd_full.at[:, cols]),
            )):
                weights.append(remote(s, t, s_w.at[d, i], r_w.at[d, i], device))
        for copy in weights:
            copy.start()
        wo_full[top:gap] = jnp.zeros((HEAD_DIM, wo_full.shape[1]), bf16)
        wo_full[0:top, cols] = wo[0:top]
        wo_full[gap:gap + HEAD_DIM, cols] = wo[top:gap]
        wu_full[here] = wu[...]
        wd_full[:, cols] = wd[...]

    def update(at, q_rows, k, v, mask, first):
        s = dot_nt(q_rows, k)
        if mask is not None:
            s = mask(s)
        top = jnp.max(s, -1, keepdims=True)
        if first:
            m_new = jnp.broadcast_to(top, (s.shape[0], 128))
        else:
            m_old = m_s[at]
            m_new = jnp.maximum(m_old, top)
        total = None
        parts = []
        for j in range(s.shape[1] // 128):
            p = jnp.exp(s[:, 128 * j:128 * j + 128] - m_new)
            total = p if total is None else total + p
            parts.append(p.astype(bf16))
        pv = dot(jnp.concatenate(parts, 1), v)
        m_s[at] = m_new
        if first:
            l_s[at] = total
            acc_s[at] = pv
        else:
            fade = jnp.exp(m_old - m_new)
            l_s[at] = l_s[at] * fade + total
            acc_s[at] = acc_s[at] * fade + pv

    low = lanes_below((tile, 128), 64)

    def heads(q_at, state, k_b, k_c, k_d, mask, first):
        a = q[q_at, 0:128]
        zero = jnp.zeros_like(a)
        update(state, jnp.where(low, a, zero), k_b, k_c, mask, first)
        update(state + 1, jnp.where(low, zero, a), k_b, k_c, mask, first)
        update(state + 2, q[q_at, 128:256], k_d, k_d, mask, first)

    tiles = plen // tile

    def prompt_part(slot, diagonal):
        def body(i):
            group = i // tiles
            t = lax.rem(i, tiles)
            at = rows(group * plen, plen)
            b = kvs[slot, at, 0:128]
            c = kvs[slot, at, 128:256]
            d = kvs[slot, at, 256:384]
            mask = None
            if diagonal:
                def mask(s):
                    row = lax.broadcasted_iota(jnp.int32, s.shape, 0) + t * tile
                    col = lax.broadcasted_iota(jnp.int32, s.shape, 1)
                    return jnp.where(col <= row, s, NEG)
            heads(rows(i * tile, tile), 3 * i, b, c, d, mask, diagonal)

        loop(groups * tiles, body)

    def cont_part(slot, first):
        def body(i):
            k = kvs[slot, 0:plen]
            for g in range(1, groups):
                k = jnp.where(sel[i] == g, kvs[slot, g * plen:(g + 1) * plen], k)
            heads(
                rows(n_prompt + i * tile, tile),
                3 * (groups * tiles + i),
                k[:, 0:128], k[:, 128:256], k[:, 256:384],
                None, first,
            )

        loop(conts, body)

    def self_part():
        def body(i):
            at = rows(n_prompt + i * tile, tile)

            def mask(s):
                row = lax.broadcasted_iota(jnp.int32, s.shape, 0)
                col = lax.broadcasted_iota(jnp.int32, s.shape, 1)
                return jnp.where(col <= row, s + bias[pl.ds(i, 1)], NEG)

            heads(
                at, 3 * (groups * tiles + i),
                kv[at, 0:128], kv[at, 128:256], kv[at, 256:384],
                mask, False,
            )

        loop(conts, body)

    cont_part(me, True)
    prompt_part(me, True)
    self_part()

    def ring(e):
        d = e + 1

        @pl.when(me - d >= 0)
        def _():
            hop(me - d, 1, 0).wait_recv()

            @pl.when(me < last)
            def _():
                hop(me - d, 1, 0).start()

        @pl.when(me + d <= last)
        def _():
            hop(me + d, -1, 1).wait_recv()

            @pl.when(me > 0)
            def _():
                hop(me + d, -1, 1).start()

        @pl.when(me - d >= 0)
        def _():
            prompt_part(me - d, False)
            cont_part(me - d, False)

        @pl.when(me + d <= last)
        def _():
            cont_part(me + d, False)

    loop(last, ring)

    for copy in counts:
        copy.wait()
    for d in range(n_ctx):
        msgs[8 * d:8 * d + 8] = cnts[d]

    def finish(at, state):
        l0 = jnp.sum(l_s[state], -1, keepdims=True)
        l1 = jnp.sum(l_s[state + 1], -1, keepdims=True)
        l2 = jnp.sum(l_s[state + 2], -1, keepdims=True)
        o[at, 0:128] = jnp.where(low, acc_s[state] / l0, acc_s[state + 1] / l1).astype(bf16)
        o[at, 128:256] = jnp.where(low, 0.0, acc_s[state + 2] / l2).astype(bf16)
        return (l0, l1, l2)

    def finish_prompt(i):
        finish(rows(i * tile, tile), 3 * i)

    loop(groups * tiles, finish_prompt)
    for i in range(conts):
        state = 3 * (groups * tiles + i)
        sums = finish(rows(n_prompt + i * tile, tile), state)
        lse[8 * i:8 * i + 8] = jnp.zeros((8, tile), f32)
        for h in range(3):
            value = m_s[state + h] + jnp.log(sums[h])
            lse[8 * i + h:8 * i + h + 1] = jnp.transpose(value)[0:1]

    for slot in range(n_ctx):
        @pl.when((slot <= me) & (me < last))
        def _():
            hop(slot, 1, 0).wait_send()

        @pl.when((slot >= me) & (me > 0))
        def _():
            hop(slot, -1, 1).wait_send()

    for copy in weights:
        copy.wait()


def full_at(a, core, split, c_split):
    b = a // split
    return a + core * split * (1 - b) + b * (split + core * c_split)


class TpSum:
    @staticmethod
    def scratch(half, width):
        n = half // CH
        return [
            pltpu.VMEM((half, width), bf16), pltpu.VMEM((half, width), bf16),
            pltpu.VMEM((half, width), bf16), pltpu.VMEM((half, width), bf16),
            pltpu.VMEM((half, width), f32), DMA((2, n)), DMA((2, n)),
        ]

    def __init__(self, half, start, place, scratch, compute):
        self.half, self.start, self.place, self.compute = half, start, place, compute
        self.snd1, self.rcv1, self.snd2, self.rcv2, self.own, self.send, self.recv = scratch
        self.core, self.mate, self.across = tp_place()
        self.n = half // CH

    def row(self, i):
        return lax.rem(self.start + i * CH, self.half)

    def pair(self, i):
        at = rows(self.row(i), CH)
        return remote(
            self.snd1.at[at], self.rcv1.at[at], self.send.at[0, i], self.recv.at[0, i], self.mate
        )

    def link(self, i):
        at = rows(self.row(i), CH)
        return remote(
            self.snd2.at[at], self.rcv2.at[at], self.send.at[1, i], self.recv.at[1, i], self.across
        )

    def second(self, i):
        at = rows(self.row(i), CH)
        self.pair(i).wait_recv()
        self.snd2[at] = (self.own[at] + self.rcv1[at].astype(f32)).astype(bf16)
        self.link(i).start()

    def begin(self):
        per = BIG // CH

        def block(b):
            a = self.row(b * per)
            at = rows(a, BIG)
            self.snd1[at] = self.compute(self.place(a, 1 - self.core)).astype(bf16)
            for s in range(per):
                self.pair(b * per + s).start()
            self.own[at] = self.compute(self.place(a, self.core))

            @pl.when(b > 0)
            def _():
                for s in range(per):
                    self.second((b - 1) * per + s)

        loop(self.n // per, block)
        for s in range(per):
            self.second(self.n - per + s)

    def take(self, i):
        at = rows(self.row(i), CH)
        self.link(i).wait_recv()
        return self.snd2[at].astype(f32) + self.rcv2[at].astype(f32)

    def close(self):
        def body(i):
            self.pair(i).wait_send()
            self.link(i).wait_send()

        loop(self.n, body)


class Share:
    def __init__(self, ref, place, sems):
        self.ref, self.place = ref, place
        self.send, self.recv = sems
        _, self.mate, _ = tp_place()

    def copy(self, i, a):
        at = rows(self.place(a), CH)
        return remote(self.ref.at[at], self.ref.at[at], self.send.at[i], self.recv.at[i], self.mate)


def share_scratch(half):
    return [DMA((half // CH,)), DMA((half // CH,))]


GELU = 0.7978845608028654


def gelu_tanh(u):
    return jnp.tanh(GELU * (u + 0.044715 * (u * u * u)))


def mixed_states(sc, hist, at, y):
    mixed = sc[4] * y
    for j in range(4):
        mixed += sc[j] * hist[j, at].astype(f32)
    return mixed


def middle_body(
    n_ctx, n_prompt, clen,
    sc, o, q, msgs, wo, wu, wd, cx, gains, mask, hist, teach,
    out, dm, hid, xn, du, da, do, dh1, stat, qs,
    hc, tc, slope, h1, dy, hsem, s_q, r_q, *scratch,
):
    core, mate, across = tp_place()
    ctx = lax.axis_index("ctx")
    half = clen
    n_cont = 2 * half
    mine = rows(core * half, half)
    loads = [
        pltpu.make_async_copy(hist.at[:, mine], hc, hsem.at[0]),
        pltpu.make_async_copy(teach.at[mine], tc, hsem.at[1]),
    ]
    for copy in loads:
        copy.start()
    low = lanes_below((clen, 128), 64)
    e0 = q[n_prompt:n_prompt + clen, 128:256].astype(f32)
    e1 = q[n_prompt + clen:n_prompt + n_cont, 128:256].astype(f32)
    qs[ctx, 0:n_cont] = q[n_prompt:n_prompt + n_cont, 0:128]
    qs[ctx, n_cont:n_cont + clen] = jnp.where(low, e0, pltpu.roll(e1, 64, 1)).astype(bf16)
    stat[...] = jnp.zeros(stat.shape, f32)
    others = axis_peers("ctx", n_ctx)
    greet([mate, across] + others)
    s1, s2, s3 = scratch[0:7], scratch[7:14], scratch[14:21]
    shares = scratch[21:]

    def place(a, c):
        return a + c * half

    def home(a):
        return a + core * half

    def each(body):
        loop(half // CH, body)

    def attn(at):
        return dot(o[rows(n_prompt + at, BIG)], wo[...])

    first = TpSum(half, 0, place, s1, attn)
    first.begin()
    moves = [
        remote(qs.at[ctx], qs.at[ctx], s_q.at[d], r_q.at[d], device)
        for d, device in enumerate(others)
    ]
    for copy in moves:
        copy.start()
    give_xn = Share(xn, home, shares[0:2])

    def normed(i):
        a = first.row(i)
        h = cx[rows(home(a), CH)].astype(f32) + first.take(i)
        h1[rows(a, CH)] = h
        whitened, _ = norm_rows(h)
        xn[rows(home(a), CH)] = (whitened * gains[2:3] + gains[3:4]).astype(bf16)
        give_xn.copy(i, a).start()

    each(normed)
    each(lambda i: give_xn.copy(i, first.row(i)).wait())

    def hidden(at):
        here = rows(at, BIG)
        u = dot(xn[here], wu[...])
        t = gelu_tanh(u)
        g = (0.5 * u * (1.0 + t)).astype(bf16)
        hid[here] = g
        slope[here] = 0.5 * (1.0 + t) + (0.5 * GELU) * u * (1.0 - t * t) * (
            1.0 + (3.0 * 0.044715) * (u * u)
        )
        return dot(g, wd[...])

    second = TpSum(half, 0, place, s2, hidden)
    second.begin()
    for copy in loads:
        copy.wait()
    give_dm = Share(dm, home, shares[2:4])
    give_out = Share(out, home, shares[4:6])
    count = msgs[0:1]
    for j in range(1, n_ctx):
        count += msgs[8 * j:8 * j + 1]
    coef = (2.0 * sc[4]) / (jnp.maximum(count, 1.0) * (1.0 * cx.shape[1]))

    def add(row, value):
        stat[row:row + 1] += jnp.sum(value, 0, keepdims=True)

    def lossy(i):
        a = second.row(i)
        here, there = rows(a, CH), rows(home(a), CH)
        y = h1[here] + second.take(i)
        mixed = mixed_states(sc, hc, here, y)
        diff = mixed - tc[here].astype(f32)
        weighted = diff * mask[there][:, 0:1]
        grad = weighted * coef[:, 0:1]
        dy[here] = grad
        dm[there] = grad.astype(bf16)
        give_dm.copy(i, a).start()
        out[there] = mixed.astype(bf16)
        give_out.copy(i, a).start()
        add(4, weighted * diff)
        for j in range(4):
            add(5 + j, weighted * hc[j, here].astype(f32))
        add(9, weighted * y)

    each(lossy)
    each(lambda i: give_dm.copy(i, second.row(i)).wait())

    def back(at):
        here = rows(at, BIG)
        d = (dot_nt(dm[here], wd[...]) * slope[here]).astype(bf16)
        du[here] = d
        return dot_nt(d, wu[...])

    third = TpSum(half, 0, place, s3, back)
    third.begin()
    give_da = Share(da, home, shares[6:8])

    def grads(i):
        a = third.row(i)
        here = rows(a, CH)
        total = third.take(i)
        whitened, inverse = norm_rows(h1[here])
        grad = dy[here] + norm_back(total, whitened, inverse, gains[2:3])
        dh1[here] = grad
        da[rows(home(a), CH)] = grad.astype(bf16)
        give_da.copy(i, a).start()
        add(2, total * whitened)
        add(3, total)

    each(grads)
    each(lambda i: give_da.copy(i, third.row(i)).wait())

    def last(i):
        at = rows(i * BIG, BIG)
        do[at] = dot_nt(da[at], wo[...]).astype(bf16)

    loop(n_cont // BIG, last)
    each(lambda i: give_out.copy(i, second.row(i)).wait())
    for part in (first, second, third):
        part.close()
    for copy in moves:
        copy.wait()


def weight_grads(hid, dm, xn, du, o, da, cols, store):
    ff = hid.shape[1]
    size = cols.size
    for j in range(ff // 256):
        store(j * 256, dot_tn(hid[:, 256 * j:256 * j + 256], dm[:, cols]))
    for j in range(ff // size):
        store(ff + j * size, dot_tn(xn[:, cols], du[:, size * j:size * j + size]))
    g = dot_tn(o[...], da[:, cols])
    store(ff + ff, g[0:128])
    store(ff + ff + 128, g[192:256])


def attend_back_body(
    n_ctx, n_dp, share, plen, clen, groups, conts, depth,
    sc, msgs, qs, do, o, lse, kv, valid, tab, gains, hid_h, dm_h, xn2_h, du_h, da_h,
    wo_h, wu_h, wd_h, px_h, hist_h, *refs,
):
    if share:
        dcat, out, gsh = refs[:3]
        refs = refs[3:]
    else:
        dcat, out, g_down, g_up, g_out = refs[:5]
        refs = refs[5:]
    (
        hid, dm, xn2, du, da, wo, wu, wd, px, hist, lsem,
        dos, sts, dqs, kd, acc_k, acc_v, acc_kd, acc_vd, dq_f, send, recv,
        xp, h1,
    ) = refs[:24]
    s1, s2 = refs[24:31], refs[31:38]
    shares = refs[38:42]
    core, mate, across = tp_place()
    me = lax.axis_index("ctx")
    dp = lax.axis_index("dp")
    peers = axis_peers("ctx", n_ctx)
    dp_peers = axis_peers("dp", n_dp) if share else []
    n_prompt = groups * plen
    n_cont = conts * clen
    half = plen
    own_rows = rows(core * half, half)
    pairs = [
        (wo_h, wo), (px_h.at[own_rows], px), (hid_h, hid), (dm_h, dm), (xn2_h, xn2), (du_h, du),
        (da_h, da), (wu_h, wu), (wd_h, wd), (hist_h.at[:, own_rows], hist),
    ]
    loads = [
        pltpu.make_async_copy(s, t, lsem.at[i]) for i, (s, t) in enumerate(pairs)
    ]
    for copy in loads:
        copy.start()
    low = lanes_below((clen, 128), 64)
    zero = jnp.zeros((clen, 128), bf16)

    g0 = do[0:clen, 128:256].astype(f32)
    g1 = do[clen:2 * clen, 128:256].astype(f32)
    dos[me, 0:n_cont] = do[:, 0:128]
    dos[me, n_cont:n_cont + clen] = jnp.where(low, pltpu.roll(g0, 64, 1), g1).astype(bf16)
    for c in range(conts):
        at = slice(c * clen, (c + 1) * clen)
        full = slice(n_prompt + c * clen, n_prompt + (c + 1) * clen)
        pa = do[at, 0:128].astype(f32) * o[full, 0:128].astype(f32)
        pe = do[at, 128:256].astype(f32) * o[full, 128:256].astype(f32)
        ta = jnp.transpose(pa)
        te = jnp.transpose(pe)
        st = 16 * c
        sts[me, st:st + 8] = lse[8 * c:8 * c + 8]
        sts[me, st + 8:st + 9] = jnp.sum(ta[0:64], 0, keepdims=True)
        sts[me, st + 9:st + 10] = jnp.sum(ta[64:128], 0, keepdims=True)
        sts[me, st + 10:st + 11] = jnp.sum(te[64:128], 0, keepdims=True)
        sts[me, st + 11:st + 16] = jnp.zeros((5, clen), f32)
    greet(peers + [mate, across] + dp_peers)
    sends = []
    for d, device in enumerate(peers):
        for i, ref in enumerate((sts, dos)):
            sends.append(remote(ref.at[me], ref.at[me], send.at[d, i], recv.at[d, i], device))
    for copy in sends:
        copy.start()

    def place(a, c):
        return a + c * half

    def home(a):
        return a + core * half

    loads[0].wait()
    loads[1].wait()

    def attn(at):
        return dot(o[rows(at, BIG)], wo[...])

    first = TpSum(half, 0, place, s1, attn)
    first.begin()

    for copy in loads[2:7]:
        copy.wait()
    gives = []
    if share:
        gsnd, grcv, gown, s_g, r_g = refs[42:47]
        for d in range(n_dp - 1):
            other = lax.rem(dp + d + 1, n_dp)

            def keep(at, value, d=d):
                gsnd[d, at:at + value.shape[0]] = value.astype(bf16)

            cols = pl.ds(pl.multiple_of(other * depth, 128), depth)
            weight_grads(hid, dm, xn2, du, o.at[n_prompt:n_prompt + n_cont], da, cols, keep)
            copy = remote(
                gsnd.at[d], grcv.at[d], s_g.at[d], r_g.at[d], {"dp": other}
            )
            copy.start()
            gives.append(copy)
    else:
        width = dm.shape[1]
        for j in range(width // 256):
            cols = pl.ds(256 * j, 256)

            def keep(at, value, j=j):
                ff = hid.shape[1]
                span = slice(256 * j, 256 * j + 256)
                if at < ff:
                    g_down[at:at + 256, span] = value.astype(bf16)
                elif at < 2 * ff:
                    g_up[span, at - ff:at - ff + 256] = value.astype(bf16)
                else:
                    g_out[at - 2 * ff:at - 2 * ff + value.shape[0], span] = value.astype(bf16)

            weight_grads(hid, dm, xn2, du, o.at[n_prompt:n_prompt + n_cont], da, cols, keep)

    kd[...] = pltpu.roll(kv[0:n_prompt, 256:384].astype(f32), 64, 1).astype(bf16)
    for acc in (acc_k, acc_v, acc_kd, acc_vd):
        acc[...] = jnp.zeros(acc.shape, f32)

    def one_head(q_rows, do_rows, k, v, lse_row, delta_row, mask):
        s = dot_nt(k, q_rows)
        p = jnp.exp(s - lse_row)
        if mask is not None:
            p = mask(p)
        dp_ = dot_nt(v, do_rows)
        ds = (p * (dp_ - delta_row)).astype(bf16)
        return p.astype(bf16), ds

    def halves(a):
        return jnp.where(low, a, zero), jnp.where(low, zero, a)

    def continuation(src, c, k_b, k_c, k_d, k_s, mask):
        base = c * clen
        a0, a1 = halves(qs[src, base:base + clen])
        d0, d1 = halves(dos[src, base:base + clen])
        e = halves(qs[src, n_cont:n_cont + clen])[c]
        g = halves(dos[src, n_cont:n_cont + clen])[c]
        st = 16 * c
        row = lambda i: sts[src, st + i:st + i + 1]
        p0, s0 = one_head(a0, d0, k_b, k_c, row(0), row(8), mask)
        dv = dot(p0, d0)
        dk = dot(s0, a0)
        dq0 = dot_tn(s0, k_b)
        p1, s1_ = one_head(a1, d1, k_b, k_c, row(1), row(9), mask)
        dv += dot(p1, d1)
        dk += dot(s1_, a1)
        dq1 = dot_tn(s1_, k_b)
        keys, values = (k_d, k_s) if c == 0 else (k_s, k_d)
        p2, s2_ = one_head(e, g, keys, values, row(2), row(10), mask)
        dvd = dot(p2, g)
        dkd = dot(s2_, e)
        dq2 = dot_tn(s2_, keys)
        return dk, dv, dkd, dvd, jnp.where(low, dq0, dq1), dq2

    def source(src, own):
        pair = []
        for c in range(conts):
            pick = msgs[pl.ds(src * 8 + 1 + c, 1)]

            def choose(one, two):
                return jnp.where(pick == 0.0, one.astype(f32), two.astype(f32)).astype(bf16)

            k_b = choose(kv[0:plen, 0:128], kv[plen:2 * plen, 0:128])
            k_c = choose(kv[0:plen, 128:256], kv[plen:2 * plen, 128:256])
            k_d = choose(kv[0:plen, 256:384], kv[plen:2 * plen, 256:384])
            k_s = choose(kd[0:plen], kd[plen:2 * plen])
            dk, dv, dkd, dvd, dqa, dqd = continuation(src, c, k_b, k_c, k_d, k_s, None)
            for g in range(groups):
                keep = (pick == 1.0 * g).astype(f32)
                at = slice(g * plen, (g + 1) * plen)
                acc_k[at] += keep * dk
                acc_v[at] += keep * dv
                acc_kd[at] += keep * dkd
                acc_vd[at] += keep * dvd
            pair.append(dqd)
            if own:
                dq_f[c * clen:(c + 1) * clen] = dqa
            else:
                dqs[n_ctx + src, c * clen:(c + 1) * clen] = dqa.astype(bf16)
        third = jnp.where(low, pair[0], pair[1])
        if own:
            dq_f[n_cont:n_cont + clen] = third
        else:
            dqs[n_ctx + src, n_cont:n_cont + clen] = third.astype(bf16)

    def other_of(d):
        return lax.rem(me + 2 * n_ctx - (d + 1), n_ctx)

    def back_copy(d):
        other = other_of(d)
        return remote(
            dqs.at[n_ctx + other], dqs.at[me], send.at[d, 2], recv.at[d, 2], {"ctx": other}
        )

    def visit(d):
        other = other_of(d)
        for i, ref in enumerate((sts, dos)):
            remote(ref.at[other], ref.at[other], send.at[d, i], recv.at[d, i], {"ctx": other}).wait_recv()
        source(other, False)
        back_copy(d).start()

    source(me, True)
    loop(n_ctx - 1, visit)

    give_xn = Share(xp, home, shares[0:2])

    def normed(i):
        a = first.row(i)
        h = px[rows(a, CH)].astype(f32) + first.take(i)
        h1[rows(a, CH)] = h
        whitened, _ = norm_rows(h)
        xp[rows(home(a), CH)] = (whitened * gains[2:3] + gains[3:4]).astype(bf16)
        give_xn.copy(i, a).start()

    loop(half // CH, normed)
    loop(half // CH, lambda i: give_xn.copy(i, first.row(i)).wait())
    for copy in loads[7:9]:
        copy.wait()

    def hidden(at):
        u = dot(xp[rows(at, BIG)], wu[...])
        return dot((0.5 * u * (1.0 + gelu_tanh(u))).astype(bf16), wd[...])

    second = TpSum(half, 0, place, s2, hidden)
    second.begin()

    for c in range(conts):
        at = slice(n_prompt + c * clen, n_prompt + (c + 1) * clen)
        k_d = kv[at, 256:384]
        k_s = pltpu.roll(k_d.astype(f32), 64, 1).astype(bf16)

        def mask(p):
            key = lax.broadcasted_iota(jnp.int32, p.shape, 0)
            query = lax.broadcasted_iota(jnp.int32, p.shape, 1)
            return jnp.where(
                key <= query, p * valid[c * clen:(c + 1) * clen, 0:1], 0.0
            )

        dk, dv, dkd, dvd, dqa, dqd = continuation(
            me, c, kv[at, 0:128], kv[at, 128:256], k_d, k_s, mask
        )
        dq_f[c * clen:(c + 1) * clen] += dqa
        keep = low if c == 0 else jnp.logical_not(low)
        dq_f[n_cont:n_cont + clen] += jnp.where(keep, dqd, 0.0)
        t = tab[plen:plen + clen]
        dcat[at, 256:384] = turn(dk, t, -1.0, False).astype(bf16)
        dcat[at, 384:512] = dv.astype(bf16)
        if c == 0:
            joined = jnp.where(low, dkd, pltpu.roll(dvd, 64, 1))
        else:
            joined = jnp.where(low, pltpu.roll(dkd, 64, 1), dvd)
        dcat[at, 512:640] = turn(joined, t, -1.0, True).astype(bf16)

    zq = jnp.zeros((plen, 256), bf16)
    wide = lanes_below((plen, 128), 64)
    for g in range(groups):
        at = slice(g * plen, (g + 1) * plen)
        t = tab[0:plen]
        dcat[at, 0:256] = zq
        dcat[at, 256:384] = turn(acc_k[at], t, -1.0, False).astype(bf16)
        dcat[at, 384:512] = acc_v[at].astype(bf16)
        k2 = acc_kd[at] + pltpu.roll(acc_kd[at], 64, 1)
        v2 = acc_vd[at] + pltpu.roll(acc_vd[at], 64, 1)
        dcat[at, 512:640] = turn(jnp.where(wide, k2, v2), t, -1.0, True).astype(bf16)

    if share:
        def stay(at, value):
            gown[at:at + value.shape[0]] = value

        cols = pl.ds(pl.multiple_of(dp * depth, 128), depth)
        weight_grads(hid, dm, xn2, du, o.at[n_prompt:n_prompt + n_cont], da, cols, stay)
        for copy in gives:
            copy.wait()

        def settle(i):
            at = rows(i * 64, 64)
            total = gown[at]
            for d in range(n_dp - 1):
                total += grcv[d, at].astype(f32)
            gsh[at] = total.astype(bf16)

        loop(gsh.shape[0] // 64, settle)

    for d in range(n_ctx - 1):
        back_copy(d).wait_send()
        other = lax.rem(me + d + 1, n_ctx)
        remote(
            dqs.at[n_ctx + other], dqs.at[other], send.at[d, 2], recv.at[d, 2], {"ctx": other}
        ).wait_recv()
        dq_f[...] += dqs[other].astype(f32)
    for c in range(conts):
        at = slice(n_prompt + c * clen, n_prompt + (c + 1) * clen)
        t = tab[plen:plen + clen]
        pair = dq_f[c * clen:(c + 1) * clen] * 0.125
        dcat[at, 0:128] = turn(pair, t, -1.0, False).astype(bf16)
        third = dq_f[n_cont:n_cont + clen] * 0.125
        if c == 1:
            third = pltpu.roll(third, 64, 1)
        third = jnp.where(low, third, 0.0)
        dcat[at, 128:256] = turn(third, t, -1.0, True).astype(bf16)

    loads[9].wait()
    give_out = Share(out, home, shares[2:4])

    def mixed(i):
        a = second.row(i)
        here = rows(a, CH)
        y = h1[here] + second.take(i)
        out[rows(home(a), CH)] = mixed_states(sc, hist, here, y).astype(bf16)
        give_out.copy(i, a).start()

    loop(half // CH, mixed)
    loop(half // CH, lambda i: give_out.copy(i, second.row(i)).wait())
    first.close()
    second.close()
    for copy in sends:
        copy.wait_send()


class LineSum:
    @staticmethod
    def scratch(count, size, width):
        return [
            pltpu.VMEM((count, size, width), bf16), pltpu.VMEM((count, size, width), bf16),
            pltpu.VMEM((count, size, width), bf16), DMA((2, count)), DMA((2, count)),
        ]

    def __init__(self, me, src, dst, scratch, count, size):
        self.src, self.dst, self.count, self.size = src, dst, count, size
        self.got, self.pair, self.far, self.send, self.recv = scratch
        side = me // 2
        self.outer = (me == 0) | (me == 3)
        self.inner = (me == 1) | (me == 2)
        self.near = {"ctx": 1 + side}
        self.back = {"ctx": 3 * side}
        self.twin = {"ctx": 2 - side}

    def at(self, k):
        return rows(k * self.size, self.size)

    def up(self, k):
        return remote(
            self.src.at[self.at(k)], self.got.at[k], self.send.at[0, k], self.recv.at[0, k], self.near
        )

    def cross(self, k):
        return remote(
            self.pair.at[k], self.far.at[k], self.send.at[1, k], self.recv.at[1, k], self.twin
        )

    def down(self, k):
        return remote(
            self.pair.at[k], self.got.at[k], self.send.at[0, k], self.recv.at[0, k], self.back
        )

    def launch(self, k):
        @pl.when(self.outer)
        def _():
            self.up(k).start()

    def meet(self, k):
        @pl.when(self.inner)
        def _():
            self.up(k).wait_recv()
            self.pair[k] = (
                self.src[self.at(k)].astype(f32) + self.got[k].astype(f32)
            ).astype(bf16)
            self.cross(k).start()

    def turn(self, k):
        @pl.when(self.inner)
        def _():
            self.cross(k).wait()
            total = (self.pair[k].astype(f32) + self.far[k].astype(f32)).astype(bf16)
            self.pair[k] = total
            self.down(k).start()
            self.dst[self.at(k)] = total.astype(f32)

    def land(self, k):
        @pl.when(self.outer)
        def _():
            self.up(k).wait_send()
            self.down(k).wait_recv()
            self.dst[self.at(k)] = self.got[k].astype(f32)

        @pl.when(self.inner)
        def _():
            self.down(k).wait_send()


def input_grad_body(
    n_dp, n_ctx, share, split, c_split, depth,
    dcat, w, px, cx, gains, dh1, stat_in, xn_h, *refs,
):
    if share:
        gsh, grad_p, grad_c, fin, r_rest, r_qkv = refs[:6]
        refs = refs[6:]
    else:
        grad_p, grad_c, fin, g_qkv = refs[:4]
        refs = refs[4:]
    xn, lsem, grad, stat, stats_m, stats_c, stats_d, s_s, r_s = refs[:9]
    s1 = refs[9:16]
    shares = refs[16:18]
    refs = refs[18:]
    core, mate, across = tp_place()
    me = lax.axis_index("ctx")
    dp = lax.axis_index("dp")
    ctx_peers = axis_peers("ctx", n_ctx)
    dp_peers = axis_peers("dp", n_dp)
    half = split + c_split
    n_prompt = 2 * split
    load = pltpu.make_async_copy(xn_h, xn, lsem.at[0])
    load.start()
    stat[...] = stat_in[...]
    greet([mate, across] + ctx_peers + dp_peers)
    if share:
        gsnd, gown, grcv, s_g, r_g, qsh = refs[:6]
        rest = LineSum(me, gsh, r_rest, refs[6:11], REST, gsh.shape[0] // REST)
        tail = LineSum(me, qsh, r_qkv, refs[11:16], TAIL, depth // TAIL)
        loop(REST, rest.launch)

    def place(a, c):
        return full_at(a, c, split, c_split)

    def home(a):
        return full_at(a, core, split, c_split)

    def compute(at):
        return dot_nt(dcat[rows(at, BIG)], w[...])

    total = TpSum(half, split, place, s1, compute)
    total.begin()
    load.wait()
    gives = []
    if share:
        for d in range(n_dp - 1):
            other = lax.rem(dp + d + 1, n_dp)
            cols = pl.ds(pl.multiple_of(other * depth, 128), depth)
            for j in range(depth // 128):
                part = pl.ds(pl.multiple_of(other * depth + 128 * j, 128), 128)
                gsnd[d, 128 * j:128 * j + 128] = dot_tn(xn[:, part], dcat[...]).astype(bf16)
            del cols
            copy = remote(gsnd.at[d], grcv.at[d], s_g.at[d], r_g.at[d], {"dp": other})
            copy.start()
            gives.append(copy)
        for j in range(depth // 128):
            part = pl.ds(pl.multiple_of(dp * depth + 128 * j, 128), 128)
            gown[128 * j:128 * j + 128] = dot_tn(xn[:, part], dcat[...])
    else:
        for j in range(xn.shape[1] // 128):
            part = slice(128 * j, 128 * j + 128)
            g_qkv[part] = dot_tn(xn[:, part], dcat[...]).astype(bf16)
    give = Share(grad, home, shares)

    def finish(i):
        a = total.row(i)
        b = a // split
        value = total.take(i)
        p = px[rows((core * split + a) * (1 - b), CH)].astype(f32)
        c = cx[rows((core * c_split + a - split) * b, CH)].astype(f32)
        whitened, inverse = norm_rows(jnp.where(b == 0, p, c))
        back = norm_back(value, whitened, inverse, gains[0:1])
        extra = dh1[rows((a - split) * b, CH)]
        grad[rows(home(a), CH)] = jnp.where(b == 0, back, back + extra).astype(bf16)
        give.copy(i, a).start()
        stat[0:1] += jnp.sum(value * whitened, 0, keepdims=True)
        stat[1:2] += jnp.sum(value, 0, keepdims=True)
        if share:
            rest.meet(i)

            @pl.when(i > 0)
            def _():
                rest.turn(i - 1)

    loop(total.n, finish)

    def small(src, dst, s, r, device):
        return remote(src, dst, s_s.at[s], r_s.at[r], device)

    stats_m[0] = stat[...]
    to_mate = small(stats_m.at[0], stats_m.at[1], 0, 0, mate)
    to_mate.start()
    if share:
        rest.turn(REST - 1)
        for copy in gives:
            copy.wait()

        def settle(i):
            at = rows(i * 64, 64)
            value = gown[at]
            for d in range(n_dp - 1):
                value += grcv[d, at].astype(f32)
            qsh[at] = value.astype(bf16)

        loop(depth // 64, settle)
        loop(TAIL, tail.launch)
    to_mate.wait()
    stats_c[me] = stats_m[0] + stats_m[1]
    to_ctx = [
        small(stats_c.at[me], stats_c.at[me], 1 + d, 1 + d, device)
        for d, device in enumerate(ctx_peers)
    ]
    for copy in to_ctx:
        copy.start()
    if share:
        loop(TAIL, tail.meet)
    for copy in to_ctx:
        copy.wait()
    value = stats_c[0]
    for d in range(1, n_ctx):
        value += stats_c[d]
    stats_d[dp] = value
    to_dp = [
        small(stats_d.at[dp], stats_d.at[dp], n_ctx + d, n_ctx + d, device)
        for d, device in enumerate(dp_peers)
    ]
    for copy in to_dp:
        copy.start()
    if share:
        loop(TAIL, tail.turn)
        loop(REST, rest.land)
    loop(total.n, lambda i: give.copy(i, total.row(i)).wait())
    grad_p[...] = grad[0:n_prompt]
    grad_c[...] = grad[n_prompt:n_prompt + 2 * c_split]
    for copy in to_dp:
        copy.wait()
    value = stats_d[0]
    for d in range(1, n_dp):
        value += stats_d[d]
    fin[...] = value
    total.close()
    if share:
        loop(TAIL, tail.land)


REST = 6
TAIL = 4


def per_device(
    n_dp, n_ctx,
    prompt_x, cont_x, prompt_hist, cont_hist, teacher, valid_mask, cont_group, layer_ids,
    dwa_weights, qkv_weight, out_weight, up_weight, down_weight,
    ln1_gain, ln1_bias, ln2_gain, ln2_bias,
):
    groups, plen, width = prompt_x.shape
    conts, clen, _ = cont_x.shape
    depth = qkv_weight.shape[0]
    n_prompt, n_cont = groups * plen, conts * clen
    n_rows = n_prompt + n_cont
    split, c_split = n_prompt // 2, n_cont // 2
    half = split + c_split
    ff = up_weight.shape[1]
    share = depth % 128 == 0

    w_q, w_k, w_v = qkv_weight[:, 0], qkv_weight[:, 1], qkv_weight[:, 2]
    w_loc = jnp.concatenate(
        [
            w_q, jnp.zeros((depth, 64), bf16), w_k[:, :128], w_v[:, :128],
            w_k[:, 128:], w_v[:, 128:],
        ],
        1,
    )
    px = prompt_x.reshape(n_prompt, width)
    cx = cont_x.reshape(n_cont, width)
    vectors = [v.reshape(1, depth) for v in (ln1_gain, ln1_bias, ln2_gain, ln2_bias)]
    tab_rows = plen + clen
    q, kv, xn1, gains, tab, cnt_dp, w_full = kernel_call(
        functools.partial(project_body, n_dp, n_ctx, plen, clen),
        [
            ((n_rows, 256), bf16), ((n_rows, 384), bf16), ((n_rows, width), bf16),
            ((8, width), f32), ((tab_rows, 384), f32), ((8, 128), f32), ((width, 640), bf16),
        ],
        [
            pltpu.VMEM((8, depth), f32), pltpu.VMEM((n_dp, 8, depth), f32),
            pltpu.VMEM((8, 128), f32), pltpu.VMEM((n_dp, 8, 128), f32),
            DMA((n_dp - 1, 5)), DMA((n_dp - 1, 5)),
        ],
        0, [VMEM_SPEC] * 8, (px, cx, w_loc, *vectors, valid_mask), name="project",
    )

    maskf = valid_mask.astype(f32)
    bias = jnp.where(valid_mask == 1, 0.0, NEG).astype(f32)
    bias = jnp.concatenate([bias, jnp.zeros((8 - conts, clen), f32)], 0)
    mask_rows = jnp.broadcast_to(maskf.reshape(n_cont, 1), (n_cont, 128))
    slot_pick = (layer_ids[:, None] == jnp.arange(4, dtype=jnp.int32)[None, :]).astype(f32)
    slot_w = jnp.sum(slot_pick * dwa_weights[None, :4], 1)
    sc = jnp.concatenate([slot_w, dwa_weights[4:5]])
    states = 3 * (n_prompt // clen + conts)
    outs = [((n_rows, 256), bf16), ((8 * conts, clen), f32), ((8 * n_ctx, 128), f32)]
    args = (cont_group, q, kv, bias, cnt_dp)
    specs = [SMEM_SPEC] + [VMEM_SPEC] * 4
    scratch = [
        pltpu.VMEM((n_ctx, n_prompt, 384), bf16), pltpu.VMEM((n_ctx, 8, 128), f32),
        pltpu.VMEM((states, clen, 128), f32), pltpu.VMEM((states, clen, 128), f32),
        pltpu.VMEM((states, clen, 128), f32),
        DMA((2, n_ctx)), DMA((n_ctx,)), DMA((n_ctx - 1,)), DMA((n_ctx - 1,)),
    ]
    if share:
        args += (out_weight, up_weight, down_weight)
        specs += [VMEM_SPEC] * 3
        outs += [((256, width), bf16), ((width, ff), bf16), ((ff, width), bf16)]
        scratch += [DMA((n_dp - 1, 4)), DMA((n_dp - 1, 4))]
    got = kernel_call(
        functools.partial(attend_body, n_ctx, n_dp, share, plen, clen, groups, conts),
        outs, scratch, 1, specs, args, name="attend",
    )
    o, lse, msgs = got[:3]
    if share:
        wo, wu, wd = got[3:]
    else:
        out_w = lax.all_gather(out_weight, "dp", axis=1, tiled=True)
        wu = lax.all_gather(up_weight, "dp", axis=0, tiled=True)
        wd = lax.all_gather(down_weight, "dp", axis=1, tiled=True)
        wo = jnp.concatenate([out_w[:128], jnp.zeros((64, width), bf16), out_w[128:]], 0)

    packed = n_cont + clen
    cont_out, dm, hid, xn2, du, da, do, dh1, stat, qs = kernel_call(
        functools.partial(middle_body, n_ctx, n_prompt, clen),
        [
            ((n_cont, width), bf16), ((n_cont, width), bf16), ((n_cont, ff), bf16),
            ((n_cont, width), bf16), ((n_cont, ff), bf16), ((n_cont, width), bf16),
            ((n_cont, 256), bf16), ((c_split, width), f32), ((16, width), f32),
            ((n_ctx, packed, 128), bf16),
        ],
        [
            pltpu.VMEM((4, c_split, width), bf16), pltpu.VMEM((c_split, width), bf16),
            pltpu.VMEM((n_cont, ff), f32), pltpu.VMEM((c_split, width), f32),
            pltpu.VMEM((c_split, width), f32), DMA((2,)), DMA((n_ctx - 1,)), DMA((n_ctx - 1,)),
        ]
        + TpSum.scratch(c_split, width) * 3
        + share_scratch(c_split) * 4,
        2,
        [SMEM_SPEC] + [VMEM_SPEC] * 9 + [HBM_SPEC] * 2,
        (
            sc, o, q, msgs, wo, wu, wd, cx, gains, mask_rows,
            cont_hist.reshape(4, n_cont, width), teacher.reshape(n_cont, width),
        ),
        name="middle",
    )

    grad_rows = 2 * ff + 3 * HEAD_DIM
    outs = [((n_rows, 640), bf16), ((n_prompt, width), bf16)]
    extra = []
    if share:
        outs += [((grad_rows, depth), bf16)]
        extra = [
            pltpu.VMEM((n_dp - 1, grad_rows, depth), bf16),
            pltpu.VMEM((n_dp - 1, grad_rows, depth), bf16),
            pltpu.VMEM((grad_rows, depth), f32), DMA((n_dp - 1,)), DMA((n_dp - 1,)),
        ]
    else:
        outs += [((ff, width), bf16), ((width, ff), bf16), ((3 * HEAD_DIM, width), bf16)]
    acc = pltpu.VMEM((n_prompt, 128), f32)
    got = kernel_call(
        functools.partial(
            attend_back_body, n_ctx, n_dp, share, plen, clen, groups, conts, depth
        ),
        outs,
        [
            pltpu.VMEM((n_cont, ff), bf16), pltpu.VMEM((n_cont, width), bf16),
            pltpu.VMEM((n_cont, width), bf16), pltpu.VMEM((n_cont, ff), bf16),
            pltpu.VMEM((n_cont, width), bf16), pltpu.VMEM((256, width), bf16),
            pltpu.VMEM((width, ff), bf16), pltpu.VMEM((ff, width), bf16),
            pltpu.VMEM((split, width), bf16), pltpu.VMEM((4, split, width), bf16), DMA((10,)),
            pltpu.VMEM((n_ctx, packed, 128), bf16), pltpu.VMEM((n_ctx, 16 * conts, clen), f32),
            pltpu.VMEM((2 * n_ctx, packed, 128), bf16), pltpu.VMEM((n_prompt, 128), bf16),
            acc, acc, acc, acc, pltpu.VMEM((packed, 128), f32),
            DMA((n_ctx - 1, 3)), DMA((n_ctx - 1, 3)),
            pltpu.VMEM((n_prompt, width), bf16), pltpu.VMEM((split, width), f32),
        ]
        + TpSum.scratch(split, width) * 2
        + share_scratch(split) * 2
        + extra,
        3,
        [SMEM_SPEC] + [VMEM_SPEC] * 9 + [HBM_SPEC] * 10,
        (
            sc, msgs, qs, do, o, lse, kv, mask_rows, tab, gains, hid, dm, xn2, du, da,
            wo, wu, wd, px, prompt_hist.reshape(4, n_prompt, width),
        ),
        name="attend_back",
    )
    dcat, prompt_out = got[:2]

    stat_rows = pltpu.VMEM((16, width), f32)
    outs = [((n_prompt, width), bf16), ((n_cont, width), bf16), ((16, width), f32)]
    args = (dcat, w_full, px, cx, gains, dh1, stat, xn1)
    specs = [VMEM_SPEC] * 7 + [HBM_SPEC]
    extra = []
    if share:
        args += (got[2],)
        specs += [VMEM_SPEC]
        outs += [((grad_rows, depth), f32), ((depth, 640), f32)]
        extra = [
            pltpu.VMEM((n_dp - 1, depth, 640), bf16), pltpu.VMEM((depth, 640), f32),
            pltpu.VMEM((n_dp - 1, depth, 640), bf16), DMA((n_dp - 1,)), DMA((n_dp - 1,)),
            pltpu.VMEM((depth, 640), bf16),
        ]
        extra += LineSum.scratch(REST, grad_rows // REST, depth)
        extra += LineSum.scratch(TAIL, depth // TAIL, 640)
    else:
        outs += [((width, 640), bf16)]
    last = kernel_call(
        functools.partial(input_grad_body, n_dp, n_ctx, share, split, c_split, depth),
        outs,
        [
            pltpu.VMEM((n_rows, width), bf16), DMA((1,)), pltpu.VMEM((n_rows, width), bf16),
            stat_rows, pltpu.VMEM((2, 16, width), f32), pltpu.VMEM((n_ctx, 16, width), f32),
            pltpu.VMEM((n_dp, 16, width), f32), DMA((n_ctx + n_dp,)), DMA((n_ctx + n_dp,)),
        ]
        + TpSum.scratch(half, width)
        + share_scratch(half)
        + extra,
        4, specs, args, name="input_grad",
    )
    grad_p, grad_c, fin = last[:3]

    def three(g):
        return jnp.stack(
            [
                g[:, 0:192],
                jnp.concatenate([g[:, 256:384], g[:, 512:576]], 1),
                jnp.concatenate([g[:, 384:512], g[:, 576:640]], 1),
            ],
            1,
        )

    if share:
        rest, qkv = last[3:]
        r_down = rest[:ff]
        r_up = jnp.concatenate(
            [rest[ff + j * depth:ff + (j + 1) * depth] for j in range(ff // depth)], 1
        )
        r_out = rest[2 * ff:]
        r_qkv = three(qkv)
    else:
        def scattered(g, dim):
            part = lax.psum_scatter(g, "dp", scatter_dimension=dim, tiled=True)
            return lax.psum(part, "ctx").astype(f32)

        g_down, g_up, g_out = got[2:]
        r_down = scattered(g_down, 1)
        r_up = scattered(g_up, 0)
        r_out = scattered(g_out, 1)
        r_qkv = scattered(three(last[3]), 0)
    norms = lax.dynamic_slice_in_dim(fin[:4], lax.axis_index("dp") * depth, depth, 1)
    sums = jnp.sum(fin[4:10], 1)
    count = msgs[0, 0]
    for j in range(1, n_ctx):
        count = count + msgs[8 * j, 0]
    denom = jnp.maximum(count, 1.0) * width
    raw = jnp.concatenate([jnp.sum(slot_pick * sums[1:5, None], 0), sums[5:6]])
    return (
        prompt_out.reshape(groups, plen, width),
        cont_out.reshape(conts, clen, width),
        sums[0] / denom,
        grad_p.reshape(groups, plen, width),
        grad_c.reshape(conts, clen, width),
        r_qkv, r_out, r_up, r_down,
        norms[0], norms[1], norms[2], norms[3],
        raw * (2.0 / denom),
    )


def solution(mesh):
    n_dp, n_ctx = mesh.shape["dp"], mesh.shape["ctx"]
    in_specs = (
        P("dp", "ctx", None), P(("dp", "ctx"), None, None), P(None, "dp", "ctx", None),
        P(None, ("dp", "ctx"), None, None), P(("dp", "ctx"), None, None), P(("dp", "ctx"), None),
        P(("dp", "ctx")), P(), P(), P("dp", None, "tp"), P("tp", "dp"), P("dp", "tp"),
        P("tp", "dp"), P("dp"), P("dp"), P("dp"), P("dp"),
    )
    out_specs = (
        P("dp", "ctx", None), P(("dp", "ctx"), None, None), P(), P("dp", "ctx", None),
        P(("dp", "ctx"), None, None), P("dp", None, "tp"), P("tp", "dp"), P("dp", "tp"),
        P("tp", "dp"), P("dp"), P("dp"), P("dp"), P("dp"), P(),
    )
    return jax.shard_map(
        functools.partial(per_device, n_dp, n_ctx),
        mesh=mesh, in_specs=in_specs, out_specs=out_specs, check_vma=False,
    )
```

```python
import functools
import math

import jax
import jax.numpy as jnp
from jax import lax
from jax.experimental import pallas as pl
from jax.experimental.pallas import tpu as pltpu
from jax.sharding import PartitionSpec as P

HEAD_DIM = 64
EPS = 1e-05
NEG = -1e30
MESH = pl.DeviceIdType.MESH
f32 = jnp.float32
bf16 = jnp.bfloat16
VMEM_SPEC = pl.BlockSpec(memory_space=pltpu.VMEM)
SMEM_SPEC = pl.BlockSpec(memory_space=pltpu.SMEM)
HBM_SPEC = pl.BlockSpec(memory_space=pl.ANY)
DMA = pltpu.SemaphoreType.DMA
LIMIT = 56 << 20
NT = (((1,), (1,)), ((), ()))
TN = (((0,), (0,)), ((), ()))
CH = 128
BIG = 256
REST = 7
LINE_STEP = 2


def dot(a, b):
    return jnp.dot(a, b, preferred_element_type=f32)


def dot_nt(a, b):
    return lax.dot_general(a, b, NT, preferred_element_type=f32)


def dot_tn(a, b):
    return lax.dot_general(a, b, TN, preferred_element_type=f32)


def rows(start, size):
    return pl.ds(pl.multiple_of(start, size), size)


def loop(count, body):
    def step(i, carry):
        body(i)
        return carry

    lax.fori_loop(0, count, step, 0)


def kernel_call(body, outs, scratch, cid, specs, args, name, out_specs=None):
    return pl.pallas_call(
        body,
        out_shape=[jax.ShapeDtypeStruct(s, d) for s, d in outs],
        in_specs=specs,
        out_specs=out_specs or [VMEM_SPEC] * len(outs),
        scratch_shapes=scratch,
        compiler_params=pltpu.CompilerParams(
            collective_id=cid, has_side_effects=True, vmem_limit_bytes=LIMIT
        ),
        cost_estimate=pl.CostEstimate(flops=0, bytes_accessed=30 << 20, transcendentals=0),
        name=name,
    )(*args)


def greet(partners):
    barrier = pltpu.get_barrier_semaphore()
    for device in partners:
        pl.semaphore_signal(barrier, inc=1, device_id=device, device_id_type=MESH)
    pl.semaphore_wait(barrier, len(partners))


def remote(src, dst, send, recv, device):
    return pltpu.make_async_remote_copy(
        src_ref=src,
        dst_ref=dst,
        send_sem=send,
        recv_sem=recv,
        device_id=device,
        device_id_type=MESH,
    )


def axis_peers(axis, count):
    me = lax.axis_index(axis)
    return [{axis: lax.rem(me + d, count)} for d in range(1, count)]


def tp_place():
    tp = lax.axis_index("tp")
    core = lax.rem(tp, 2)
    mate = {"tp": tp + 1 - 2 * core}
    across = {"tp": lax.rem(tp + 2, 4)}
    return core, mate, across


def norm_rows(x):
    mean = jnp.mean(x, -1, keepdims=True)
    centered = x - mean
    var = jnp.mean(centered * centered, -1, keepdims=True)
    inverse = lax.rsqrt(var + EPS)
    return centered * inverse, inverse


def norm_back(gradient, whitened, inverse, gain):
    e = gradient * gain
    return inverse * (
        e - jnp.mean(e, -1, keepdims=True) - whitened * jnp.mean(e * whitened, -1, keepdims=True)
    )


def lanes_below(shape, bound):
    return lax.broadcasted_iota(jnp.int32, shape, len(shape) - 1) < bound


def turn(y, tab, sign, half):
    cos, low, high = tab[:, :128], tab[:, 128:256], tab[:, 256:384]
    turned = sign * (pltpu.roll(y, 96, 1) * low + pltpu.roll(y, 32, 1) * high)
    if not half:
        return y * cos + turned
    return jnp.where(lanes_below(y.shape, 64), y * cos + turned, y)


W_PARTS = ((1, 0, 128, 256), (2, 0, 128, 384), (1, 128, 64, 512), (2, 128, 64, 576), (0, 0, 192, 0))


def front_body(
    n_ctx, n_dp, share, plen, clen, groups, conts,
    sel, px, cx, w, g1, b1, g2, b2, valid, wo, wu, wd,
    xn_o, kv_o, tab_o, w_o, wu_o, wd_o, wo_o, o, lse, msgs, gains, qpack,
    xn, q, kvs, kvc, tab, w_full, gb, gbs, cnt, cnts, notes, m_s, l_s, acc_s,
    wgs, s_x, r_x, s_kv, r_kv, s_c, r_c, s_w, r_w, osem,
):
    me = lax.axis_index("ctx")
    mine = lax.axis_index("dp")
    depth = w.shape[2]
    width = px.shape[1]
    last = n_ctx - 1
    n_prompt = groups * plen
    n_cont = conts * clen
    tile = clen
    dp_peers = axis_peers("dp", n_dp)
    peers = axis_peers("ctx", n_ctx)
    for i, vector in enumerate((g1, b1, g2, b2)):
        gb[i:i + 1] = vector[...].astype(f32).reshape(1, depth)
    gb[4:8] = jnp.zeros((4, depth), f32)
    cnt[...] = jnp.zeros(cnt.shape, f32) + jnp.sum(valid[...].astype(f32))
    greet(dp_peers + peers)

    copies = []
    weights = []
    if share:
        cols = pl.ds(pl.multiple_of(mine * depth, 128), depth)
        here = rows(mine * depth, depth)
    for d, device in enumerate(dp_peers):
        pairs = [(gb, gbs.at[mine]), (cnt, cnts.at[mine])]
        if share:
            pairs += [
                (w.at[p, a:a + n], w_full.at[t:t + n, cols]) for p, a, n, t in W_PARTS
            ]
        else:
            pairs += [(w, wgs.at[mine])]
        copies.append(
            [remote(s, t, s_x.at[d, i], r_x.at[d, i], device) for i, (s, t) in enumerate(pairs)]
        )
    for i in range(len(copies[0])):
        for group in copies:
            group[i].start()
    local = []
    if share:
        pairs = [
            (wo.at[0:128], wo_o.at[0:128, cols]), (wo.at[128:192], wo_o.at[192:256, cols]),
            (wu, wu_o.at[here]), (wd, wd_o.at[:, cols]),
        ]
        for d, device in enumerate(dp_peers):
            for i, (s, t) in enumerate(pairs):
                weights.append(remote(s, t, s_w.at[d, i], r_w.at[d, i], device))
        for copy in weights:
            copy.start()
        local += [pltpu.make_async_copy(s, t, osem.at[i]) for i, (s, t) in enumerate(pairs)]
        for copy in local:
            copy.start()
        for p, a, n, t in W_PARTS:
            w_full[t:t + n, cols] = w[p, a:a + n]
    else:
        wgs[mine] = w[...]
    wo_o[128:192] = jnp.zeros((64, width), bf16)
    w_full[192:256] = jnp.zeros((64, width), bf16)
    gbs[mine] = gb[...]
    cnts[mine] = cnt[...]

    def table(count, base, start):
        def body(i):
            shape = (CH, 128)
            lane = lax.broadcasted_iota(jnp.int32, shape, 1)
            row = lax.broadcasted_iota(jnp.int32, shape, 0)
            turns = lax.rem(lane, 32).astype(f32) * (-2.0 * math.log(10000.0) / HEAD_DIM)
            angle = (row + (start + i * CH)).astype(f32) * jnp.exp(turns)
            sin = jnp.sin(angle)
            left = lax.rem(lane, 64) < 32
            at = rows(base + i * CH, CH)
            tab[at, 0:128] = jnp.cos(angle)
            tab[at, 128:256] = jnp.where(left, -sin, 0.0)
            tab[at, 256:384] = jnp.where(left, 0.0, sin)

        loop(count // CH, body)

    table(plen, 0, me * plen)
    table(clen, plen, n_ctx * plen)

    def save(src, dst, i):
        copy = pltpu.make_async_copy(src, dst, osem.at[i])
        copy.start()
        local.append(copy)

    save(tab, tab_o, 4)
    for group in copies:
        group[0].wait_recv()
        group[1].wait_recv()

    def one_hot(d):
        row = lax.broadcasted_iota(jnp.int32, (depth, width), 0) + d * depth
        col = lax.broadcasted_iota(jnp.int32, (depth, width), 1)
        return (row == col).astype(f32).astype(bf16)

    total = jnp.zeros(gains.shape, f32)
    count = jnp.zeros(cnt.shape, f32)
    for d in range(n_dp):
        total += dot(gbs[d].astype(bf16), one_hot(d))
        count += cnts[d]
    gains[...] = total
    note = notes.at[me]
    notes[me] = count
    for i in range(conts):
        notes[me, 1 + i:2 + i] = jnp.zeros((1, 128), f32) + sel[i].astype(f32)
    counts = [remote(note, note, s_c.at[d], r_c.at[d], device) for d, device in enumerate(peers)]
    for copy in counts:
        copy.start()

    def norm_part(x, base):
        def body(i):
            whitened, _ = norm_rows(x[rows(i * CH, CH)].astype(f32))
            xn[rows(base + i * CH, CH)] = (whitened * gains[0:1] + gains[1:2]).astype(bf16)

        loop(x.shape[0] // CH, body)

    norm_part(px, 0)
    norm_part(cx, n_prompt)
    save(xn, xn_o, 5)

    def arrive(i):
        if share:
            for group in copies:
                group[2 + i].wait_recv()
        elif i == 0:
            for group in copies:
                group[2].wait_recv()
            for p, a, n, t in W_PARTS:
                part = jnp.zeros((n, width), f32)
                for d in range(n_dp):
                    part += dot(wgs[d, p, a:a + n], one_hot(d))
                w_full[t:t + n] = part.astype(bf16)

    def hop(slot, step, side):
        there = kvs.at[slot]
        return remote(there, there, s_kv.at[side, slot], r_kv.at[slot], {"ctx": me + step})

    def kv_rows(count, base, tab_base, period, dst):
        def body(i):
            at = rows(i * BIG, BIG)
            t = tab[rows(tab_base + lax.rem(i * BIG, period), BIG)]
            x = xn[rows(base + i * BIG, BIG)]
            y = dot_nt(x, w_full[256:512])
            dst[at, 0:128] = turn(y[:, 0:128], t, 1.0, False).astype(bf16)
            dst[at, 128:256] = y[:, 128:256].astype(bf16)
            dst[at, 256:384] = turn(dot_nt(x, w_full[512:640]), t, 1.0, True).astype(bf16)

        loop(count // BIG, body)

    def q_rows_of(count, base, tab_base, period):
        def body(i):
            at = rows(base + i * BIG, BIG)
            t = tab[rows(tab_base + lax.rem(i * BIG, period), BIG)]
            y = dot_nt(xn[at], w_full[0:256])
            q[at, 0:128] = (turn(y[:, 0:128], t, 1.0, False) * 0.125).astype(bf16)
            q[at, 128:256] = (turn(y[:, 128:256], t, 1.0, True) * 0.125).astype(bf16)

        loop(count // BIG, body)

    for i in range(4):
        arrive(i)
    kv_rows(n_prompt, 0, 0, plen, kvs.at[me])

    @pl.when(me < last)
    def _():
        hop(me, 1, 0).start()

    @pl.when(me > 0)
    def _():
        hop(me, -1, 1).start()

    save(kvs.at[me], kv_o.at[0:n_prompt], 6)
    kv_rows(n_cont, n_prompt, plen, clen, kvc)
    save(kvc, kv_o.at[n_prompt:n_prompt + n_cont], 7)
    arrive(4)
    save(w_full, w_o, 8)
    q_rows_of(n_cont, n_prompt, plen, clen)
    q_rows_of(n_prompt, 0, 0, plen)

    def update(at, q_rows, k, v, mask, first):
        s = dot_nt(q_rows, k)
        if mask is not None:
            s = mask(s)
        top = jnp.max(s, -1, keepdims=True)
        if first:
            m_new = jnp.broadcast_to(top, (s.shape[0], 128))
        else:
            m_old = m_s[at]
            m_new = jnp.maximum(m_old, top)
        total = None
        parts = []
        for j in range(s.shape[1] // 128):
            p = jnp.exp(s[:, 128 * j:128 * j + 128] - m_new)
            total = p if total is None else total + p
            parts.append(p.astype(bf16))
        pv = dot(jnp.concatenate(parts, 1), v)
        m_s[at] = m_new
        if first:
            l_s[at] = total
            acc_s[at] = pv
        else:
            fade = jnp.exp(m_old - m_new)
            l_s[at] = l_s[at] * fade + total
            acc_s[at] = acc_s[at] * fade + pv

    low = lanes_below((tile, 128), 64)

    def heads(q_at, state, k_b, k_c, k_d, mask, first):
        a = q[q_at, 0:128]
        zero = jnp.zeros_like(a)
        update(state, jnp.where(low, a, zero), k_b, k_c, mask, first)
        update(state + 1, jnp.where(low, zero, a), k_b, k_c, mask, first)
        update(state + 2, q[q_at, 128:256], k_d, k_d, mask, first)

    tiles = plen // tile

    def prompt_part(slot, diagonal):
        def body(i):
            group = i // tiles
            t = lax.rem(i, tiles)
            at = rows(group * plen, plen)
            mask = None
            if diagonal:
                def mask(s):
                    row = lax.broadcasted_iota(jnp.int32, s.shape, 0) + t * tile
                    col = lax.broadcasted_iota(jnp.int32, s.shape, 1)
                    return jnp.where(col <= row, s, NEG)
            heads(
                rows(i * tile, tile), 3 * i,
                kvs[slot, at, 0:128], kvs[slot, at, 128:256], kvs[slot, at, 256:384],
                mask, diagonal,
            )

        loop(groups * tiles, body)

    def cont_part(slot, first):
        def body(i):
            k = kvs[slot, 0:plen]
            for g in range(1, groups):
                k = jnp.where(sel[i] == g, kvs[slot, g * plen:(g + 1) * plen], k)
            heads(
                rows(n_prompt + i * tile, tile), 3 * (groups * tiles + i),
                k[:, 0:128], k[:, 128:256], k[:, 256:384], None, first,
            )

        loop(conts, body)

    def self_part():
        def body(i):
            at = rows(i * tile, tile)

            def mask(s):
                row = lax.broadcasted_iota(jnp.int32, s.shape, 0)
                col = lax.broadcasted_iota(jnp.int32, s.shape, 1)
                bias = (valid[pl.ds(i, 1)].astype(f32) - 1.0) * (-NEG)
                return jnp.where(col <= row, s + bias, NEG)

            heads(
                rows(n_prompt + i * tile, tile), 3 * (groups * tiles + i),
                kvc[at, 0:128], kvc[at, 128:256], kvc[at, 256:384], mask, False,
            )

        loop(conts, body)

    cont_part(me, True)
    prompt_part(me, True)
    self_part()
    e0 = q[n_prompt:n_prompt + clen, 128:256].astype(f32)
    e1 = q[n_prompt + clen:n_prompt + n_cont, 128:256].astype(f32)
    qpack[0:n_cont] = q[n_prompt:n_prompt + n_cont, 0:128]
    qpack[n_cont:n_cont + clen] = jnp.where(low, e0, pltpu.roll(e1, 64, 1)).astype(bf16)

    def ring(e):
        d = e + 1

        @pl.when(me - d >= 0)
        def _():
            hop(me - d, 1, 0).wait_recv()

            @pl.when(me < last)
            def _():
                hop(me - d, 1, 0).start()

        @pl.when(me + d <= last)
        def _():
            hop(me + d, -1, 1).wait_recv()

            @pl.when(me > 0)
            def _():
                hop(me + d, -1, 1).start()

        @pl.when(me - d >= 0)
        def _():
            cont_part(me - d, False)
            prompt_part(me - d, False)

        @pl.when(me + d <= last)
        def _():
            cont_part(me + d, False)

    loop(last, ring)

    for copy in counts:
        copy.wait()
    for d in range(n_ctx):
        msgs[8 * d:8 * d + 8] = notes[d]

    def finish(at, state):
        l0 = jnp.sum(l_s[state], -1, keepdims=True)
        l1 = jnp.sum(l_s[state + 1], -1, keepdims=True)
        l2 = jnp.sum(l_s[state + 2], -1, keepdims=True)
        o[at, 0:128] = jnp.where(low, acc_s[state] / l0, acc_s[state + 1] / l1).astype(bf16)
        o[at, 128:256] = jnp.where(low, 0.0, acc_s[state + 2] / l2).astype(bf16)
        return (l0, l1, l2)

    def finish_prompt(i):
        finish(rows(i * tile, tile), 3 * i)

    loop(groups * tiles, finish_prompt)
    for i in range(conts):
        state = 3 * (groups * tiles + i)
        sums = finish(rows(n_prompt + i * tile, tile), state)
        lse[8 * i:8 * i + 8] = jnp.zeros((8, tile), f32)
        for h in range(3):
            value = m_s[state + h] + jnp.log(sums[h])
            lse[8 * i + h:8 * i + h + 1] = jnp.transpose(value)[0:1]

    for slot in range(n_ctx):
        @pl.when((slot <= me) & (me < last))
        def _():
            hop(slot, 1, 0).wait_send()

        @pl.when((slot >= me) & (me > 0))
        def _():
            hop(slot, -1, 1).wait_send()

    for group in copies:
        for copy in group:
            copy.wait_send()
    for copy in weights:
        copy.wait()
    for copy in local:
        copy.wait()


def full_at(a, core, split, c_split):
    b = a // split
    return a + core * split * (1 - b) + b * (split + core * c_split)


class TpSum:
    @staticmethod
    def scratch(half, width):
        n = half // CH
        return [
            pltpu.VMEM((half, width), bf16), pltpu.VMEM((half, width), bf16),
            pltpu.VMEM((half, width), bf16), pltpu.VMEM((half, width), bf16),
            pltpu.VMEM((half, width), f32), DMA((2, n)), DMA((2, n)),
        ]

    def __init__(self, half, start, place, scratch, compute):
        self.half, self.start, self.place, self.compute = half, start, place, compute
        self.snd1, self.rcv1, self.snd2, self.rcv2, self.own, self.send, self.recv = scratch
        self.core, self.mate, self.across = tp_place()
        self.n = half // CH

    def row(self, i):
        return lax.rem(self.start + i * CH, self.half)

    def pair(self, i):
        at = rows(self.row(i), CH)
        return remote(
            self.snd1.at[at], self.rcv1.at[at], self.send.at[0, i], self.recv.at[0, i], self.mate
        )

    def link(self, i):
        at = rows(self.row(i), CH)
        return remote(
            self.snd2.at[at], self.rcv2.at[at], self.send.at[1, i], self.recv.at[1, i], self.across
        )

    def second(self, i):
        at = rows(self.row(i), CH)
        self.pair(i).wait_recv()
        self.snd2[at] = (self.own[at] + self.rcv1[at].astype(f32)).astype(bf16)
        self.link(i).start()

    def launch(self, i):
        a = self.row(i)
        at = rows(a, CH)
        self.snd1[at] = self.compute(self.place(a, 1 - self.core), CH).astype(bf16)
        self.pair(i).start()
        self.own[at] = self.compute(self.place(a, self.core), CH)

    def begin(self):
        def body(i):
            self.launch(i)

            @pl.when(i > 0)
            def _():
                self.second(i - 1)

        loop(self.n, body)
        self.second(self.n - 1)

    def take(self, i):
        at = rows(self.row(i), CH)
        self.link(i).wait_recv()
        return self.snd2[at].astype(f32) + self.rcv2[at].astype(f32)

    def close(self):
        def body(i):
            self.pair(i).wait_send()
            self.link(i).wait_send()

        loop(self.n, body)


class Share:
    def __init__(self, ref, place, sems):
        self.ref, self.place = ref, place
        self.send, self.recv = sems
        _, self.mate, _ = tp_place()

    def copy(self, i, a):
        at = rows(self.place(a), CH)
        return remote(self.ref.at[at], self.ref.at[at], self.send.at[i], self.recv.at[i], self.mate)


def share_scratch(half):
    return [DMA((half // CH,)), DMA((half // CH,))]


GELU = 0.7978845608028654


def gelu_tanh(u):
    return jnp.tanh(GELU * (u + 0.044715 * (u * u * u)))


def mixed_states(ids, dwa, hist, at, y):
    mixed = dwa[4] * y
    for j in range(4):
        mixed += dwa[ids[j]] * hist[j, at].astype(f32)
    return mixed


def column(row):
    return jnp.transpose(jnp.broadcast_to(row, (128, row.shape[1])))


def middle_body(
    n_ctx, n_prompt, clen,
    ids, dwa, o, qpack, msgs, wo, wu, wd, cx, gains, valid, hist, teach,
    out, dm, hid, xn, du, da, do, dh1, stat, qs,
    hc, tc, slope, h1, dy, mask, hsem, s_q, r_q, *scratch,
):
    core, mate, across = tp_place()
    ctx = lax.axis_index("ctx")
    half = clen
    n_cont = 2 * half
    mine = rows(core * half, half)
    loads = [
        pltpu.make_async_copy(hist.at[:, mine], hc, hsem.at[0]),
        pltpu.make_async_copy(teach.at[mine], tc, hsem.at[1]),
    ]
    for copy in loads:
        copy.start()
    qs[ctx] = qpack[...]
    mask[...] = column(valid[pl.ds(core, 1)].astype(f32))
    stat[...] = jnp.zeros(stat.shape, f32)
    others = axis_peers("ctx", n_ctx)
    greet([mate, across] + others)
    s1, s2, s3 = scratch[0:7], scratch[7:14], scratch[14:21]
    shares = scratch[21:]

    def place(a, c):
        return a + c * half

    def home(a):
        return a + core * half

    def each(body):
        loop(half // CH, body)

    def attn(at, size):
        return dot(o[rows(n_prompt + at, size)], wo[...])

    first = TpSum(half, 0, place, s1, attn)
    each(first.launch)
    each(first.second)
    moves = [
        remote(qs.at[ctx], qs.at[ctx], s_q.at[d], r_q.at[d], device)
        for d, device in enumerate(others)
    ]
    for copy in moves:
        copy.start()
    give_xn = Share(xn, home, shares[0:2])

    def normed(i):
        a = first.row(i)
        h = cx[rows(home(a), CH)].astype(f32) + first.take(i)
        h1[rows(a, CH)] = h
        whitened, _ = norm_rows(h)
        xn[rows(home(a), CH)] = (whitened * gains[2:3] + gains[3:4]).astype(bf16)
        give_xn.copy(i, a).start()

    def hidden(at, size):
        here = rows(at, size)
        u = dot(xn[here], wu[...])
        t = gelu_tanh(u)
        g = (0.5 * u * (1.0 + t)).astype(bf16)
        hid[here] = g
        slope[here] = 0.5 * (1.0 + t) + (0.5 * GELU) * u * (1.0 - t * t) * (
            1.0 + (3.0 * 0.044715) * (u * u)
        )
        return dot(g, wd[...])

    second = TpSum(half, 0, place, s2, hidden)

    def onward(before, share, after):
        def body(i):
            before(i)

            @pl.when(i > 0)
            def _():
                after.second(i - 1)

            share.copy(i, after.row(i)).wait()
            after.launch(i)

        each(body)
        after.second(after.n - 1)

    onward(normed, give_xn, second)
    for copy in loads:
        copy.wait()
    give_dm = Share(dm, home, shares[2:4])
    give_out = Share(out, home, shares[4:6])
    count = msgs[0:1]
    for j in range(1, n_ctx):
        count += msgs[8 * j:8 * j + 1]
    coef = (2.0 * dwa[4]) / (jnp.maximum(count, 1.0) * (1.0 * cx.shape[1]))

    def add(row, value):
        stat[row:row + 1] += jnp.sum(value, 0, keepdims=True)

    def lossy(i):
        a = second.row(i)
        here, there = rows(a, CH), rows(home(a), CH)
        y = h1[here] + second.take(i)
        mixed = mixed_states(ids, dwa, hc, here, y)
        diff = mixed - tc[here].astype(f32)
        weighted = diff * mask[here][:, 0:1]
        grad = weighted * coef[:, 0:1]
        dy[here] = grad
        dm[there] = grad.astype(bf16)
        give_dm.copy(i, a).start()
        out[there] = mixed.astype(bf16)
        give_out.copy(i, a).start()
        add(4, weighted * diff)
        for j in range(4):
            add(5 + j, weighted * hc[j, here].astype(f32))
        add(9, weighted * y)

    def back(at, size):
        here = rows(at, size)
        d = (dot_nt(dm[here], wd[...]) * slope[here]).astype(bf16)
        du[here] = d
        return dot_nt(d, wu[...])

    third = TpSum(half, 0, place, s3, back)
    onward(lossy, give_dm, third)
    give_da = Share(da, home, shares[6:8])

    def grads(i):
        a = third.row(i)
        here = rows(a, CH)
        total = third.take(i)
        whitened, inverse = norm_rows(h1[here])
        grad = dy[here] + norm_back(total, whitened, inverse, gains[2:3])
        dh1[here] = grad
        da[rows(home(a), CH)] = grad.astype(bf16)
        give_da.copy(i, a).start()
        add(2, total * whitened)
        add(3, total)

    each(grads)
    each(lambda i: give_da.copy(i, third.row(i)).wait())

    def last(i):
        at = rows(i * BIG, BIG)
        do[at] = dot_nt(da[at], wo[...]).astype(bf16)

    loop(n_cont // BIG, last)
    each(lambda i: give_out.copy(i, second.row(i)).wait())
    for part in (first, second, third):
        part.close()
    for copy in moves:
        copy.wait()


class LineSum:
    @staticmethod
    def scratch(count, size, width):
        return [
            pltpu.VMEM((count, size, width), bf16), pltpu.VMEM((count, size, width), bf16),
            pltpu.VMEM((count, size, width), bf16), DMA((2, count)), DMA((2, count)),
        ]

    def __init__(self, me, src, dst, scratch, count, size):
        self.src, self.dst, self.count, self.size = src, dst, count, size
        self.got, self.pair, self.far, self.send, self.recv = scratch
        side = me // 2
        self.outer = (me == 0) | (me == 3)
        self.inner = (me == 1) | (me == 2)
        self.near = {"ctx": 1 + side}
        self.back = {"ctx": 3 * side}
        self.twin = {"ctx": 2 - side}

    def at(self, k):
        return rows(k * self.size, self.size)

    def up(self, k):
        return remote(
            self.src.at[self.at(k)], self.got.at[k], self.send.at[0, k], self.recv.at[0, k], self.near
        )

    def cross(self, k):
        return remote(
            self.pair.at[k], self.far.at[k], self.send.at[1, k], self.recv.at[1, k], self.twin
        )

    def down(self, k):
        return remote(
            self.pair.at[k], self.got.at[k], self.send.at[0, k], self.recv.at[0, k], self.back
        )

    def launch(self, k):
        @pl.when(self.outer)
        def _():
            self.up(k).start()

    def meet(self, k):
        @pl.when(self.inner)
        def _():
            self.up(k).wait_recv()
            self.pair[k] = (
                self.src[self.at(k)].astype(f32) + self.got[k].astype(f32)
            ).astype(bf16)
            self.cross(k).start()

    def turn(self, k):
        @pl.when(self.inner)
        def _():
            self.cross(k).wait()
            total = (self.pair[k].astype(f32) + self.far[k].astype(f32)).astype(bf16)
            self.pair[k] = total
            self.down(k).start()
            self.dst[self.at(k)] = total

    def land(self, k):
        @pl.when(self.outer)
        def _():
            self.up(k).wait_send()
            self.down(k).wait_recv()
            self.dst[self.at(k)] = self.got[k]

        @pl.when(self.inner)
        def _():
            self.down(k).wait_send()


def down_grads(hid, dm, cols, store):
    for j in range(hid.shape[1] // 256):
        store(j * 256, dot_tn(hid[:, 256 * j:256 * j + 256], dm[:, cols]))


def other_grads(ff, xn, du, o, da, cols, store):
    size = cols.size
    for j in range(ff // size):
        store(ff + j * size, dot_tn(xn[:, cols], du[:, size * j:size * j + size]))
    g = dot_tn(o[...], da[:, cols])
    store(ff + ff, g[0:128])
    store(ff + ff + 128, g[192:256])


def attend_back_body(
    n_ctx, n_dp, share, plen, clen, groups, conts, depth,
    ids, dwa, msgs, qs, do, o, lse, kv, valid, tab, gains, hid_h, dm_h, xn2_h, du_h, da_h,
    wo_h, wu_h, wd_h, px_h, hist_h, xn1_h, *refs,
):
    if share:
        dcat, out, g_sum, g_part = refs[:4]
        refs = refs[4:]
    else:
        dcat, out, g_down, g_up, g_out, g_kv = refs[:6]
        refs = refs[6:]
    (
        hid, dm, xn2, du, da, wo, wu, wd, px, hist, lsem,
        dos, sts, dqs, kd, acc_k, acc_v, acc_kd, acc_vd, dq_f, send, recv,
        xp, h1, xn1, flags,
    ) = refs[:26]
    s1, s2 = refs[26:33], refs[33:40]
    shares = refs[40:44]
    refs = refs[44:]
    core, mate, across = tp_place()
    me = lax.axis_index("ctx")
    dp = lax.axis_index("dp")
    peers = axis_peers("ctx", n_ctx)
    dp_peers = axis_peers("dp", n_dp) if share else []
    n_prompt = groups * plen
    n_cont = conts * clen
    half = plen
    own_rows = rows(core * half, half)
    pairs = [
        (wo_h, wo), (px_h.at[own_rows], px), (hid_h, hid), (dm_h, dm), (xn2_h, xn2), (du_h, du),
        (da_h, da), (wu_h, wu), (wd_h, wd), (hist_h.at[:, own_rows], hist), (xn1_h, xn1),
    ]
    loads = [
        pltpu.make_async_copy(s, t, lsem.at[i]) for i, (s, t) in enumerate(pairs)
    ]
    for copy in loads:
        copy.start()
    low = lanes_below((clen, 128), 64)
    zero = jnp.zeros((clen, 128), bf16)
    for c in range(conts):
        flags[c * clen:(c + 1) * clen] = column(valid[c:c + 1].astype(f32))

    g0 = do[0:clen, 128:256].astype(f32)
    g1 = do[clen:2 * clen, 128:256].astype(f32)
    dos[me, 0:n_cont] = do[:, 0:128]
    dos[me, n_cont:n_cont + clen] = jnp.where(low, pltpu.roll(g0, 64, 1), g1).astype(bf16)
    for c in range(conts):
        at = slice(c * clen, (c + 1) * clen)
        full = slice(n_prompt + c * clen, n_prompt + (c + 1) * clen)
        pa = do[at, 0:128].astype(f32) * o[full, 0:128].astype(f32)
        pe = do[at, 128:256].astype(f32) * o[full, 128:256].astype(f32)
        ta = jnp.transpose(pa)
        te = jnp.transpose(pe)
        st = 8 * c
        sts[me, st:st + 8] = lse[8 * c:8 * c + 8]
        sts[me, st + 3:st + 4] = jnp.sum(ta[0:64], 0, keepdims=True)
        sts[me, st + 4:st + 5] = jnp.sum(ta[64:128], 0, keepdims=True)
        sts[me, st + 5:st + 6] = jnp.sum(te[64:128], 0, keepdims=True)
    greet(peers + [mate, across] + dp_peers)
    sends = []
    for d, device in enumerate(peers):
        for i, ref in enumerate((sts, dos)):
            sends.append(remote(ref.at[me], ref.at[me], send.at[d, i], recv.at[d, i], device))
    for copy in sends:
        copy.start()

    def place(a, c):
        return a + c * half

    def home(a):
        return a + core * half

    loads[0].wait()
    loads[1].wait()

    def attn(at, size):
        return dot(o[rows(at, size)], wo[...])

    first = TpSum(half, 0, place, s1, attn)
    first.begin()

    for copy in loads[2:7]:
        copy.wait()
    ff = hid.shape[1]
    o_c = o.at[n_prompt:n_prompt + n_cont]
    bounds = (0, ff, 2 * ff + 192, 2 * ff + 576)
    if share:
        gsnd, grcv, gown, gdn, s_g, r_g = refs[:6]
        line = LineSum(me, gdn, g_sum, refs[6:11], 4, ff // 4)

    def cols_of(d):
        return pl.ds(pl.multiple_of(lax.rem(dp + d, n_dp) * depth, 128), depth)

    def give(d, i):
        span = slice(bounds[i], bounds[i + 1])
        return remote(
            gsnd.at[d - 1, span], grcv.at[d - 1, span], s_g.at[d - 1, i], r_g.at[d - 1, i],
            {"dp": lax.rem(dp + d, n_dp)},
        )

    def keeper(d):
        if d == 0:
            def store(at, value):
                gown[at:at + value.shape[0]] = value
        else:
            def store(at, value):
                gsnd[d - 1, at:at + value.shape[0]] = value.astype(bf16)
        return store

    def kv_grads(cols, store):
        for lo, hi in ((256, 384), (384, 512), (512, 640)):
            store(2 * ff + 192 + lo - 256, dot_tn(dcat[:, lo:hi], xn1[:, cols]))

    def settle(dst, i):
        for d in range(1, n_dp):
            give(d, i).wait()

        def body(j):
            at = rows(bounds[i] + j * 64, 64)
            total = gown[at]
            for d in range(n_dp - 1):
                total += grcv[d, at].astype(f32)
            dst(at, j, total.astype(bf16))

        loop((bounds[i + 1] - bounds[i]) // 64, body)

    if share:
        for d in range(1, n_dp):
            down_grads(hid, dm, cols_of(d), keeper(d))
            give(d, 0).start()
        for d in range(1, n_dp):
            other_grads(ff, xn2, du, o_c, da, cols_of(d), keeper(d))
            give(d, 1).start()
    else:
        width = dm.shape[1]
        for j in range(width // 256):
            cols = pl.ds(256 * j, 256)
            span = slice(256 * j, 256 * j + 256)

            def lay(at, value, span=span):
                if at < ff:
                    g_down[at:at + 256, span] = value.astype(bf16)
                elif at < 2 * ff:
                    g_up[span, at - ff:at - ff + 256] = value.astype(bf16)
                else:
                    g_out[at - 2 * ff:at - 2 * ff + value.shape[0], span] = value.astype(bf16)

            down_grads(hid, dm, cols, lay)
            other_grads(ff, xn2, du, o_c, da, cols, lay)

    kd[...] = pltpu.roll(kv[0:n_prompt, 256:384].astype(f32), 64, 1).astype(bf16)
    for acc in (acc_k, acc_v, acc_kd, acc_vd):
        acc[...] = jnp.zeros(acc.shape, f32)

    def one_head(q_rows, do_rows, k, v, lse_row, delta_row, mask):
        s = dot_nt(k, q_rows)
        p = jnp.exp(s - lse_row)
        if mask is not None:
            p = mask(p)
        dp_ = dot_nt(v, do_rows)
        ds = (p * (dp_ - delta_row)).astype(bf16)
        return p.astype(bf16), ds

    def halves(a):
        return jnp.where(low, a, zero), jnp.where(low, zero, a)

    def continuation(src, c, k_b, k_c, k_d, k_s, mask):
        base = c * clen
        a0, a1 = halves(qs[src, base:base + clen])
        d0, d1 = halves(dos[src, base:base + clen])
        e = halves(qs[src, n_cont:n_cont + clen])[c]
        g = halves(dos[src, n_cont:n_cont + clen])[c]
        st = 8 * c
        row = lambda i: sts[src, st + i:st + i + 1]
        p0, s0 = one_head(a0, d0, k_b, k_c, row(0), row(3), mask)
        dv = dot(p0, d0)
        dk = dot(s0, a0)
        dq0 = dot_tn(s0, k_b)
        p1, s1_ = one_head(a1, d1, k_b, k_c, row(1), row(4), mask)
        dv += dot(p1, d1)
        dk += dot(s1_, a1)
        dq1 = dot_tn(s1_, k_b)
        keys, values = (k_d, k_s) if c == 0 else (k_s, k_d)
        p2, s2_ = one_head(e, g, keys, values, row(2), row(5), mask)
        dvd = dot(p2, g)
        dkd = dot(s2_, e)
        dq2 = dot_tn(s2_, keys)
        return dk, dv, dkd, dvd, jnp.where(low, dq0, dq1), dq2

    def source(src, own):
        pair = []
        for c in range(conts):
            pick = msgs[pl.ds(src * 8 + 1 + c, 1)]

            def choose(one, two):
                return jnp.where(pick == 0.0, one.astype(f32), two.astype(f32)).astype(bf16)

            k_b = choose(kv[0:plen, 0:128], kv[plen:2 * plen, 0:128])
            k_c = choose(kv[0:plen, 128:256], kv[plen:2 * plen, 128:256])
            k_d = choose(kv[0:plen, 256:384], kv[plen:2 * plen, 256:384])
            k_s = choose(kd[0:plen], kd[plen:2 * plen])
            dk, dv, dkd, dvd, dqa, dqd = continuation(src, c, k_b, k_c, k_d, k_s, None)
            for g in range(groups):
                keep = (pick == 1.0 * g).astype(f32)
                at = slice(g * plen, (g + 1) * plen)
                acc_k[at] += keep * dk
                acc_v[at] += keep * dv
                acc_kd[at] += keep * dkd
                acc_vd[at] += keep * dvd
            pair.append(dqd)
            if own:
                dq_f[c * clen:(c + 1) * clen] = dqa
            else:
                dqs[n_ctx + src, c * clen:(c + 1) * clen] = dqa.astype(bf16)
        third = jnp.where(low, pair[0], pair[1])
        if own:
            dq_f[n_cont:n_cont + clen] = third
        else:
            dqs[n_ctx + src, n_cont:n_cont + clen] = third.astype(bf16)

    def other_of(d):
        return lax.rem(me + 2 * n_ctx - (d + 1), n_ctx)

    def back_copy(d):
        other = other_of(d)
        return remote(
            dqs.at[n_ctx + other], dqs.at[me], send.at[d, 2], recv.at[d, 2], {"ctx": other}
        )

    def visit(d):
        other = other_of(d)
        for i, ref in enumerate((sts, dos)):
            remote(ref.at[other], ref.at[other], send.at[d, i], recv.at[d, i], {"ctx": other}).wait_recv()
        source(other, False)
        back_copy(d).start()

    give_xn = Share(xp, home, shares[0:2])

    def normed(i):
        a = first.row(i)
        h = px[rows(a, CH)].astype(f32) + first.take(i)
        h1[rows(a, CH)] = h
        whitened, _ = norm_rows(h)
        xp[rows(home(a), CH)] = (whitened * gains[2:3] + gains[3:4]).astype(bf16)
        give_xn.copy(i, a).start()

    def hidden(at, size):
        u = dot(xp[rows(at, size)], wu[...])
        return dot((0.5 * u * (1.0 + gelu_tanh(u))).astype(bf16), wd[...])

    second = TpSum(half, 0, place, s2, hidden)
    def to_line(at, j, value):
        gdn[rows(j * 64, 64)] = value

    def to_part(at, j, value):
        g_part[rows(at.start - ff, 64)] = value

    source(me, True)
    for copy in loads[7:9]:
        copy.wait()

    def step(i):
        @pl.when(i < first.n)
        def _():
            normed(i)
            give_xn.copy(i, first.row(i)).wait()
            second.launch(i)

        @pl.when((i > 0) & (i < n_ctx))
        def _():
            visit(i - 1)

        @pl.when(i < first.n)
        def _():
            second.second(i)

        if share:
            @pl.when(i == LINE_STEP)
            def _():
                down_grads(hid, dm, cols_of(0), keeper(0))
                settle(to_line, 0)
                loop(4, line.launch)

    loop(max(half // CH, n_ctx), step)

    for c in range(conts):
        at = slice(n_prompt + c * clen, n_prompt + (c + 1) * clen)
        k_d = kv[at, 256:384]
        k_s = pltpu.roll(k_d.astype(f32), 64, 1).astype(bf16)

        def mask(p):
            key = lax.broadcasted_iota(jnp.int32, p.shape, 0)
            query = lax.broadcasted_iota(jnp.int32, p.shape, 1)
            return jnp.where(
                key <= query, p * flags[c * clen:(c + 1) * clen, 0:1], 0.0
            )

        dk, dv, dkd, dvd, dqa, dqd = continuation(
            me, c, kv[at, 0:128], kv[at, 128:256], k_d, k_s, mask
        )
        dq_f[c * clen:(c + 1) * clen] += dqa
        keep = low if c == 0 else jnp.logical_not(low)
        dq_f[n_cont:n_cont + clen] += jnp.where(keep, dqd, 0.0)
        t = tab[plen:plen + clen]
        dcat[at, 256:384] = turn(dk, t, -1.0, False).astype(bf16)
        dcat[at, 384:512] = dv.astype(bf16)
        if c == 0:
            joined = jnp.where(low, dkd, pltpu.roll(dvd, 64, 1))
        else:
            joined = jnp.where(low, pltpu.roll(dkd, 64, 1), dvd)
        dcat[at, 512:640] = turn(joined, t, -1.0, True).astype(bf16)

    zq = jnp.zeros((plen, 256), bf16)
    wide = lanes_below((plen, 128), 64)
    for g in range(groups):
        at = slice(g * plen, (g + 1) * plen)
        t = tab[0:plen]
        dcat[at, 0:256] = zq
        dcat[at, 256:384] = turn(acc_k[at], t, -1.0, False).astype(bf16)
        dcat[at, 384:512] = acc_v[at].astype(bf16)
        k2 = acc_kd[at] + pltpu.roll(acc_kd[at], 64, 1)
        v2 = acc_vd[at] + pltpu.roll(acc_vd[at], 64, 1)
        dcat[at, 512:640] = turn(jnp.where(wide, k2, v2), t, -1.0, True).astype(bf16)

    loads[10].wait()
    if share:
        for d in range(1, n_dp):
            kv_grads(cols_of(d), keeper(d))
            give(d, 2).start()
        other_grads(ff, xn2, du, o_c, da, cols_of(0), keeper(0))
        kv_grads(cols_of(0), keeper(0))
        loop(4, line.meet)
        settle(to_part, 1)
    else:
        for j in range(xn1.shape[1] // 256):
            span = slice(256 * j, 256 * j + 256)

            def lay_kv(at, value, span=span):
                at = at - 2 * ff - 192
                g_kv[at:at + 128, span] = value.astype(bf16)

            kv_grads(pl.ds(256 * j, 256), lay_kv)

    for d in range(n_ctx - 1):
        back_copy(d).wait_send()
        other = lax.rem(me + d + 1, n_ctx)
        remote(
            dqs.at[n_ctx + other], dqs.at[other], send.at[d, 2], recv.at[d, 2], {"ctx": other}
        ).wait_recv()
        dq_f[...] += dqs[other].astype(f32)
    for c in range(conts):
        at = slice(n_prompt + c * clen, n_prompt + (c + 1) * clen)
        t = tab[plen:plen + clen]
        pair = dq_f[c * clen:(c + 1) * clen] * 0.125
        dcat[at, 0:128] = turn(pair, t, -1.0, False).astype(bf16)
        third = dq_f[n_cont:n_cont + clen] * 0.125
        if c == 1:
            third = pltpu.roll(third, 64, 1)
        third = jnp.where(low, third, 0.0)
        dcat[at, 128:256] = turn(third, t, -1.0, True).astype(bf16)

    if share:
        loop(4, line.turn)

    loads[9].wait()
    give_out = Share(out, home, shares[2:4])

    def mixed(i):
        a = second.row(i)
        here = rows(a, CH)
        y = h1[here] + second.take(i)
        out[rows(home(a), CH)] = mixed_states(ids, dwa, hist, here, y).astype(bf16)
        give_out.copy(i, a).start()

    loop(half // CH, mixed)
    loop(half // CH, lambda i: give_out.copy(i, second.row(i)).wait())
    if share:
        settle(to_part, 2)
        loop(4, line.land)
    first.close()
    second.close()
    for copy in sends:
        copy.wait_send()


def input_grad_body(
    n_dp, n_ctx, share, split, c_split, depth,
    dcat, w, px, cx, gains, dh1, stat_in, xn_h, *refs,
):
    if share:
        g_part, grad_p, grad_c, fin, g_rest = refs[:5]
        refs = refs[5:]
    else:
        grad_p, grad_c, fin, g_q = refs[:4]
        refs = refs[4:]
    xn, lsem, grad, stat, stats_m, stats_y, stats_c, stats_d, s_s, r_s = refs[:10]
    s1 = refs[10:17]
    shares = refs[17:19]
    refs = refs[19:]
    core, mate, across = tp_place()
    me = lax.axis_index("ctx")
    dp = lax.axis_index("dp")
    ctx_peers = axis_peers("ctx", n_ctx)
    dp_peers = axis_peers("dp", n_dp)
    half = split + c_split
    n_prompt = 2 * split
    n_cont = 2 * c_split
    load = pltpu.make_async_copy(xn_h.at[n_prompt:n_prompt + n_cont], xn, lsem.at[0])
    load.start()
    stat[...] = 0.5 * stat_in[...]
    greet([mate, across] + ctx_peers + dp_peers)
    if share:
        gsnd, gown, grcv, s_g, r_g, qsh, qsum = refs[:7]
        n_rest = g_part.shape[0]
        rest = LineSum(me, g_part, g_rest.at[0:n_rest], refs[7:12], REST, n_rest // REST)
        tail = LineSum(me, qsh, qsum, refs[12:17], 1, 3 * HEAD_DIM)
        loop(REST, rest.launch)

    def place(a, c):
        return full_at(a, c, split, c_split)

    def home(a):
        return full_at(a, core, split, c_split)

    def compute(at, size):
        part = dot(dcat[rows(at, size)], w[...])
        b = at // n_prompt
        p = px[rows(at * (1 - b), size)].astype(f32)
        c = cx[rows((at - n_prompt) * b, size)].astype(f32)
        whitened, _ = norm_rows(jnp.where(b == 0, p, c))
        stat[0:1] += jnp.sum(part * whitened, 0, keepdims=True)
        stat[1:2] += jnp.sum(part, 0, keepdims=True)
        return part

    total = TpSum(half, split, place, s1, compute)
    total.begin()

    def small(src, dst, i, device):
        return remote(src, dst, s_s.at[i], r_s.at[i], device)

    stats_m[0] = stat[...]
    to_mate = small(stats_m.at[0], stats_m.at[1], 0, mate)
    to_mate.start()
    load.wait()

    def q_grads(cols):
        return dot_tn(dcat[n_prompt:n_prompt + n_cont, 0:256], xn[:, cols])[0:3 * HEAD_DIM]

    gives = []
    if share:
        for d in range(1, n_dp):
            other = lax.rem(dp + d, n_dp)
            cols = pl.ds(pl.multiple_of(other * depth, 128), depth)
            gsnd[d - 1] = q_grads(cols).astype(bf16)
            copy = remote(
                gsnd.at[d - 1], grcv.at[d - 1], s_g.at[d - 1], r_g.at[d - 1], {"dp": other}
            )
            copy.start()
            gives.append(copy)
        gown[...] = q_grads(pl.ds(pl.multiple_of(dp * depth, 128), depth))
    else:
        g_q[...] = q_grads(slice(None)).astype(bf16)
    to_mate.wait()
    stats_y[0] = stats_m[0] + stats_m[1]
    to_far = small(stats_y.at[0], stats_y.at[1], 1, across)
    to_far.start()
    give = Share(grad, home, shares)

    def finish(i):
        a = total.row(i)
        b = a // split
        value = total.take(i)
        p = px[rows((core * split + a) * (1 - b), CH)].astype(f32)
        c = cx[rows((core * c_split + a - split) * b, CH)].astype(f32)
        whitened, inverse = norm_rows(jnp.where(b == 0, p, c))
        back = norm_back(value, whitened, inverse, gains[0:1])
        extra = dh1[rows((a - split) * b, CH)]
        grad[rows(home(a), CH)] = jnp.where(b == 0, back, back + extra).astype(bf16)
        give.copy(i, a).start()
        if share:
            rest.meet(i + 1)

            @pl.when(i > 0)
            def _():
                rest.turn(i - 1)

    def part(lo, hi):
        loop(hi - lo, lambda i: finish(i + lo))

    if share:
        rest.meet(0)
    third = total.n // 3
    part(0, third)
    to_far.wait()
    stats_c[me] = stats_y[0] + stats_y[1]
    to_ctx = [
        small(stats_c.at[me], stats_c.at[me], 2 + d, device) for d, device in enumerate(ctx_peers)
    ]
    for copy in to_ctx:
        copy.start()
    if share:
        for copy in gives:
            copy.wait()
        value = gown[...]
        for d in range(n_dp - 1):
            value += grcv[d].astype(f32)
        qsh[...] = value.astype(bf16)
        tail.launch(0)
    part(third, 2 * third)
    for copy in to_ctx:
        copy.wait()
    value = stats_c[0]
    for d in range(1, n_ctx):
        value += stats_c[d]
    stats_d[dp] = value
    to_dp = [
        small(stats_d.at[dp], stats_d.at[dp], 1 + n_ctx + d, device)
        for d, device in enumerate(dp_peers)
    ]
    for copy in to_dp:
        copy.start()
    part(2 * third, total.n)
    if share:
        tail.meet(0)
        rest.turn(REST - 2)
        rest.turn(REST - 1)
        tail.turn(0)
    loop(total.n, lambda i: give.copy(i, total.row(i)).wait())
    grad_p[...] = grad[0:n_prompt]
    grad_c[...] = grad[n_prompt:n_prompt + n_cont]
    for copy in to_dp:
        copy.wait()
    value = stats_d[0]
    for d in range(1, n_dp):
        value += stats_d[d]
    fin[...] = value
    total.close()
    if share:
        loop(REST, rest.land)
        tail.land(0)
        g_rest[n_rest:n_rest + 3 * HEAD_DIM] = qsum[...]


def output_body(
    n_ctx, n_dp, share, ff,
    ids, msgs, fin, p_out, c_out, p_grad, c_grad, *refs,
):
    n = 2 if share else 0
    parts = refs[:n]
    p_out_o, c_out_o, p_grad_o, c_grad_o, loss, dwa_g, g1, b1, g2, b2 = refs[n:n + 10]
    refs = refs[n + 10:]
    if share:
        r_qkv, r_out, r_up, r_down = refs[:4]
        refs = refs[4:]
    held, sem = refs[:4], refs[4]
    moves = (
        (p_out, p_out_o), (c_out, c_out_o), (p_grad, p_grad_o), (c_grad, c_grad_o)
    )
    reads = [
        pltpu.make_async_copy(s, h, sem.at[0, i]) for i, ((s, _), h) in enumerate(zip(moves, held))
    ]
    copies = [
        pltpu.make_async_copy(h, t, sem.at[1, i]) for i, ((_, t), h) in enumerate(zip(moves, held))
    ]
    for copy in reads:
        copy.start()
    depth = g1.shape[0]
    width = fin.shape[1]
    count = msgs[0:1, 0:1]
    for j in range(1, n_ctx):
        count += msgs[8 * j:8 * j + 1, 0:1]
    factor = 1.0 / (jnp.maximum(count, 1.0) * (1.0 * width))
    sums = jnp.sum(fin[...], -1, keepdims=True) * factor
    row = lax.broadcasted_iota(jnp.int32, sums.shape, 0)

    def entry(i):
        return jnp.sum(jnp.where(row == i, sums, 0.0))

    loss[0] = entry(4)
    for k in range(4):
        value = 0.0
        for j in range(4):
            value += jnp.where(ids[j] == k, 2.0 * entry(5 + j), 0.0)
        dwa_g[k] = value
    dwa_g[4] = 2.0 * entry(9)
    for i, ref in enumerate((g1, b1, g2, b2)):
        if share:
            ref[...] = fin[i, pl.ds(pl.multiple_of(lax.axis_index("dp") * depth, 128), depth)]
        else:
            piece = jnp.zeros((1, depth), f32)
            for d in range(n_dp):
                here = fin[i:i + 1, d * depth:(d + 1) * depth]
                piece += jnp.where(lax.axis_index("dp") == d, here, 0.0)
            ref[...] = piece.reshape(depth)
    for read, copy in zip(reads, copies):
        read.wait()
        copy.start()
    if share:
        down, rest = parts
        r_down[...] = down[...].astype(f32)
        for j in range(ff // depth):
            r_up[:, j * depth:(j + 1) * depth] = rest[j * depth:(j + 1) * depth].astype(f32)
        r_out[...] = rest[ff:ff + 192].astype(f32)
        base = ff + 192
        r_qkv[1, 0:128] = rest[base:base + 128].astype(f32)
        r_qkv[2, 0:128] = rest[base + 128:base + 256].astype(f32)
        r_qkv[1, 128:192] = rest[base + 256:base + 320].astype(f32)
        r_qkv[2, 128:192] = rest[base + 320:base + 384].astype(f32)
        r_qkv[0] = rest[base + 384:base + 576].astype(f32)
    for copy in copies:
        copy.wait()


def per_device(
    n_dp, n_ctx,
    prompt_x, cont_x, prompt_hist, cont_hist, teacher, valid_mask, cont_group, layer_ids,
    dwa_weights, qkv_weight, out_weight, up_weight, down_weight,
    ln1_gain, ln1_bias, ln2_gain, ln2_bias,
):
    groups, plen, width = prompt_x.shape
    conts, clen, _ = cont_x.shape
    depth = qkv_weight.shape[0]
    n_prompt, n_cont = groups * plen, conts * clen
    n_rows = n_prompt + n_cont
    split, c_split = n_prompt // 2, n_cont // 2
    half = split + c_split
    ff = up_weight.shape[1]
    share = depth % 128 == 0
    packed = n_cont + clen
    tab_rows = plen + clen
    vmem = pltpu.VMEM

    w_t = qkv_weight.transpose(1, 2, 0)
    px = prompt_x.reshape(n_prompt, width)
    cx = cont_x.reshape(n_cont, width)
    vectors = (ln1_gain, ln1_bias, ln2_gain, ln2_bias)
    states = vmem((3 * (n_prompt // clen + conts), clen, 128), f32)
    xn1, kv, tab, w_full, wu, wd, wo, o, lse, msgs, gains, qpack = kernel_call(
        functools.partial(front_body, n_ctx, n_dp, share, plen, clen, groups, conts),
        [
            ((n_rows, width), bf16), ((n_rows, 384), bf16), ((tab_rows, 384), f32),
            ((640, width), bf16), ((width, ff), bf16), ((ff, width), bf16), ((256, width), bf16),
            ((n_rows, 256), bf16), ((8 * conts, clen), f32), ((8 * n_ctx, 128), f32),
            ((8, width), f32), ((packed, 128), bf16),
        ],
        [
            vmem((n_rows, width), bf16), vmem((n_rows, 256), bf16),
            vmem((n_ctx, n_prompt, 384), bf16), vmem((n_cont, 384), bf16),
            vmem((tab_rows, 384), f32), vmem((640, width), bf16),
            vmem((8, depth), f32), vmem((n_dp, 8, depth), f32),
            vmem((8, 128), f32), vmem((n_dp, 8, 128), f32), vmem((n_ctx, 8, 128), f32),
            states, states, states,
            vmem((1, 3, 192, depth) if share else (n_dp, 3, 192, depth), bf16),
            DMA((n_dp - 1, 7)), DMA((n_dp - 1, 7)),
            DMA((2, n_ctx)), DMA((n_ctx,)), DMA((n_ctx - 1,)), DMA((n_ctx - 1,)),
            DMA((n_dp - 1, 4)), DMA((n_dp - 1, 4)), DMA((9,)),
        ],
        0,
        [SMEM_SPEC] + [VMEM_SPEC] * 11,
        (cont_group, px, cx, w_t, *vectors, valid_mask, out_weight, up_weight, down_weight),
        "front",
        [HBM_SPEC] * 6 + [VMEM_SPEC] * 6,
    )
    if not share:
        out_w = lax.all_gather(out_weight, "dp", axis=1, tiled=True)
        wu = lax.all_gather(up_weight, "dp", axis=0, tiled=True)
        wd = lax.all_gather(down_weight, "dp", axis=1, tiled=True)
        wo = jnp.concatenate([out_w[:128], jnp.zeros((64, width), bf16), out_w[128:]], 0)

    cont_out, dm, hid, xn2, du, da, do, dh1, stat, qs = kernel_call(
        functools.partial(middle_body, n_ctx, n_prompt, clen),
        [
            ((n_cont, width), bf16), ((n_cont, width), bf16), ((n_cont, ff), bf16),
            ((n_cont, width), bf16), ((n_cont, ff), bf16), ((n_cont, width), bf16),
            ((n_cont, 256), bf16), ((c_split, width), f32), ((16, width), f32),
            ((n_ctx, packed, 128), bf16),
        ],
        [
            vmem((4, c_split, width), bf16), vmem((c_split, width), bf16),
            vmem((n_cont, ff), f32), vmem((c_split, width), f32),
            vmem((c_split, width), f32), vmem((clen, 128), f32),
            DMA((2,)), DMA((n_ctx - 1,)), DMA((n_ctx - 1,)),
        ]
        + TpSum.scratch(c_split, width) * 3
        + share_scratch(c_split) * 4,
        1,
        [SMEM_SPEC] * 2 + [VMEM_SPEC] * 9 + [HBM_SPEC] * 2,
        (
            layer_ids, dwa_weights, o, qpack, msgs, wo, wu, wd, cx, gains, valid_mask,
            cont_hist.reshape(4, n_cont, width), teacher.reshape(n_cont, width),
        ),
        "middle",
    )

    grad_rows = 2 * ff + 9 * HEAD_DIM
    outs = [((n_rows, 640), bf16), ((n_prompt, width), bf16)]
    if share:
        outs += [((ff, depth), bf16), ((grad_rows - ff, depth), bf16)]
        extra = [
            vmem((n_dp - 1, grad_rows, depth), bf16), vmem((n_dp - 1, grad_rows, depth), bf16),
            vmem((grad_rows, depth), f32), vmem((ff, depth), bf16),
            DMA((n_dp - 1, 3)), DMA((n_dp - 1, 3)),
        ] + LineSum.scratch(4, ff // 4, depth)
    else:
        outs += [
            ((ff, width), bf16), ((width, ff), bf16), ((3 * HEAD_DIM, width), bf16),
            ((384, width), bf16),
        ]
        extra = []
    acc = vmem((n_prompt, 128), f32)
    got = kernel_call(
        functools.partial(
            attend_back_body, n_ctx, n_dp, share, plen, clen, groups, conts, depth
        ),
        outs,
        [
            vmem((n_cont, ff), bf16), vmem((n_cont, width), bf16),
            vmem((n_cont, width), bf16), vmem((n_cont, ff), bf16),
            vmem((n_cont, width), bf16), vmem((256, width), bf16),
            vmem((width, ff), bf16), vmem((ff, width), bf16),
            vmem((split, width), bf16), vmem((4, split, width), bf16), DMA((11,)),
            vmem((n_ctx, packed, 128), bf16), vmem((n_ctx, 8 * conts, clen), f32),
            vmem((2 * n_ctx, packed, 128), bf16), vmem((n_prompt, 128), bf16),
            acc, acc, acc, acc, vmem((packed, 128), f32),
            DMA((n_ctx - 1, 3)), DMA((n_ctx - 1, 3)),
            vmem((n_prompt, width), bf16), vmem((split, width), f32),
            vmem((n_rows, width), bf16), vmem((n_cont, 128), f32),
        ]
        + TpSum.scratch(split, width) * 2
        + share_scratch(split) * 2
        + extra,
        2,
        [SMEM_SPEC] * 2 + [VMEM_SPEC] * 9 + [HBM_SPEC] * 11,
        (
            layer_ids, dwa_weights, msgs, qs, do, o, lse, kv, valid_mask, tab, gains,
            hid, dm, xn2, du, da, wo, wu, wd, px, prompt_hist.reshape(4, n_prompt, width), xn1,
        ),
        "attend_back",
    )
    dcat, prompt_out = got[:2]

    stat_rows = vmem((16, width), f32)
    outs = [((n_prompt, width), bf16), ((n_cont, width), bf16), ((16, width), f32)]
    args = (dcat, w_full, px, cx, gains, dh1, stat, xn1)
    specs = [VMEM_SPEC] * 7 + [HBM_SPEC]
    if share:
        args += (got[3],)
        specs += [VMEM_SPEC]
        outs += [((grad_rows - ff + 3 * HEAD_DIM, depth), bf16)]
        third = vmem((3 * HEAD_DIM, depth), bf16)
        extra = [
            vmem((n_dp - 1, 3 * HEAD_DIM, depth), bf16), vmem((3 * HEAD_DIM, depth), f32),
            vmem((n_dp - 1, 3 * HEAD_DIM, depth), bf16), DMA((n_dp - 1,)), DMA((n_dp - 1,)),
            third, third,
        ]
        extra += LineSum.scratch(REST, (grad_rows - ff) // REST, depth)
        extra += LineSum.scratch(1, 3 * HEAD_DIM, depth)
    else:
        outs += [((3 * HEAD_DIM, width), bf16)]
        extra = []
    last = kernel_call(
        functools.partial(input_grad_body, n_dp, n_ctx, share, split, c_split, depth),
        outs,
        [
            vmem((n_cont, width), bf16), DMA((1,)), vmem((n_rows, width), bf16),
            stat_rows, vmem((2, 16, width), f32), vmem((2, 16, width), f32),
            vmem((n_ctx, 16, width), f32), vmem((n_dp, 16, width), f32),
            DMA((1 + n_ctx + n_dp,)), DMA((1 + n_ctx + n_dp,)),
        ]
        + TpSum.scratch(half, width)
        + share_scratch(half)
        + extra,
        3, specs, args, "input_grad",
    )
    grad_p, grad_c, fin = last[:3]

    outs = [
        ((n_prompt, width), bf16), ((n_cont, width), bf16), ((n_prompt, width), bf16),
        ((n_cont, width), bf16), ((1,), f32), ((5,), f32),
    ] + [((depth,), f32)] * 4
    out_specs = [HBM_SPEC] * 4 + [SMEM_SPEC] * 2 + [VMEM_SPEC] * 4
    specs = [SMEM_SPEC] + [VMEM_SPEC] * 2 + [HBM_SPEC] * 4
    args = (layer_ids, msgs, fin, prompt_out, cont_out, grad_p, grad_c)
    if share:
        outs += [((3, 192, depth), f32), ((192, depth), f32), ((depth, ff), f32), ((ff, depth), f32)]
        out_specs += [VMEM_SPEC] * 4
        args += (got[2], last[3])
        specs += [VMEM_SPEC] * 2
    done = pl.pallas_call(
        functools.partial(output_body, n_ctx, n_dp, share, ff),
        out_shape=[jax.ShapeDtypeStruct(s, d) for s, d in outs],
        in_specs=specs,
        out_specs=out_specs,
        scratch_shapes=[
            vmem((n_prompt, width), bf16), vmem((n_cont, width), bf16),
            vmem((n_prompt, width), bf16), vmem((n_cont, width), bf16), DMA((2, 4)),
        ],
        compiler_params=pltpu.CompilerParams(vmem_limit_bytes=LIMIT),
        name="outputs",
    )(*args)
    if share:
        r_qkv, r_out, r_up, r_down = done[10:]
        r_qkv = r_qkv.transpose(2, 0, 1)
    else:
        def scattered(g, dim):
            part = lax.psum_scatter(g, "dp", scatter_dimension=dim, tiled=True)
            return lax.psum(part, "ctx").astype(f32)

        g_down, g_up, g_out, g_kv = got[2:]
        r_down = scattered(g_down, 1)
        r_up = scattered(g_up, 0)
        r_out = scattered(g_out, 1)
        g_k = jnp.concatenate([g_kv[0:128], g_kv[256:320]], 0)
        g_v = jnp.concatenate([g_kv[128:256], g_kv[320:384]], 0)
        r_qkv = scattered(jnp.stack([last[3], g_k, g_v]).transpose(2, 0, 1), 0)
    return (
        done[0].reshape(groups, plen, width),
        done[1].reshape(conts, clen, width),
        done[4].reshape(()),
        done[2].reshape(groups, plen, width),
        done[3].reshape(conts, clen, width),
        r_qkv, r_out, r_up, r_down,
        done[6], done[7], done[8], done[9],
        done[5],
    )


def solution(mesh):
    n_dp, n_ctx = mesh.shape["dp"], mesh.shape["ctx"]
    in_specs = (
        P("dp", "ctx", None), P(("dp", "ctx"), None, None), P(None, "dp", "ctx", None),
        P(None, ("dp", "ctx"), None, None), P(("dp", "ctx"), None, None), P(("dp", "ctx"), None),
        P(("dp", "ctx")), P(), P(), P("dp", None, "tp"), P("tp", "dp"), P("dp", "tp"),
        P("tp", "dp"), P("dp"), P("dp"), P("dp"), P("dp"),
    )
    out_specs = (
        P("dp", "ctx", None), P(("dp", "ctx"), None, None), P(), P("dp", "ctx", None),
        P(("dp", "ctx"), None, None), P("dp", None, "tp"), P("tp", "dp"), P("dp", "tp"),
        P("tp", "dp"), P("dp"), P("dp"), P("dp"), P("dp"), P(),
    )
    return jax.shard_map(
        functools.partial(per_device, n_dp, n_ctx),
        mesh=mesh, in_specs=in_specs, out_specs=out_specs, check_vma=False,
    )
```

```python
import functools
import math

import jax
import jax.numpy as jnp
from jax import lax
from jax.experimental import pallas as pl
from jax.experimental.pallas import tpu as pltpu
from jax.sharding import PartitionSpec as P

HEAD_DIM = 64
EPS = 1e-05
NEG = -1e30
MESH = pl.DeviceIdType.MESH
f32 = jnp.float32
bf16 = jnp.bfloat16
VMEM_SPEC = pl.BlockSpec(memory_space=pltpu.VMEM)
SMEM_SPEC = pl.BlockSpec(memory_space=pltpu.SMEM)
HBM_SPEC = pl.BlockSpec(memory_space=pl.ANY)
DMA = pltpu.SemaphoreType.DMA
LIMIT = 56 << 20
NT = (((1,), (1,)), ((), ()))
TN = (((0,), (0,)), ((), ()))
CH = 128
BIG = 256
LINE = 192


def dot(a, b):
    return jnp.dot(a, b, preferred_element_type=f32)


def dot_nt(a, b):
    return lax.dot_general(a, b, NT, preferred_element_type=f32)


def dot_tn(a, b):
    return lax.dot_general(a, b, TN, preferred_element_type=f32)


def rows(start, size):
    return pl.ds(pl.multiple_of(start, size), size)


def loop(count, body):
    def step(i, carry):
        body(i)
        return carry

    lax.fori_loop(0, count, step, 0)


def kernel_call(body, outs, scratch, cid, specs, args, name, out_specs=None):
    return pl.pallas_call(
        body,
        out_shape=[jax.ShapeDtypeStruct(s, d) for s, d in outs],
        in_specs=specs,
        out_specs=out_specs or [VMEM_SPEC] * len(outs),
        scratch_shapes=scratch,
        compiler_params=pltpu.CompilerParams(
            collective_id=cid, has_side_effects=True, vmem_limit_bytes=LIMIT
        ),
        cost_estimate=pl.CostEstimate(flops=0, bytes_accessed=30 << 20, transcendentals=0),
        name=name,
    )(*args)


def greet(partners):
    barrier = pltpu.get_barrier_semaphore()
    for device in partners:
        pl.semaphore_signal(barrier, inc=1, device_id=device, device_id_type=MESH)
    pl.semaphore_wait(barrier, len(partners))


def remote(src, dst, send, recv, device):
    return pltpu.make_async_remote_copy(
        src_ref=src,
        dst_ref=dst,
        send_sem=send,
        recv_sem=recv,
        device_id=device,
        device_id_type=MESH,
    )


def axis_peers(axis, count):
    me = lax.axis_index(axis)
    return [{axis: lax.rem(me + d, count)} for d in range(1, count)]


def tp_place():
    tp = lax.axis_index("tp")
    core = lax.rem(tp, 2)
    mate = {"tp": tp + 1 - 2 * core}
    across = {"tp": lax.rem(tp + 2, 4)}
    return core, mate, across


def norm_rows(x):
    mean = jnp.mean(x, -1, keepdims=True)
    centered = x - mean
    var = jnp.mean(centered * centered, -1, keepdims=True)
    inverse = lax.rsqrt(var + EPS)
    return centered * inverse, inverse


def norm_back(gradient, whitened, inverse, gain):
    e = gradient * gain
    return inverse * (
        e - jnp.mean(e, -1, keepdims=True) - whitened * jnp.mean(e * whitened, -1, keepdims=True)
    )


def lanes_below(shape, bound):
    return lax.broadcasted_iota(jnp.int32, shape, len(shape) - 1) < bound


def turn(y, tab, sign, half):
    cos, low, high = tab[:, :128], tab[:, 128:256], tab[:, 256:384]
    turned = sign * (pltpu.roll(y, 96, 1) * low + pltpu.roll(y, 32, 1) * high)
    if not half:
        return y * cos + turned
    return jnp.where(lanes_below(y.shape, 64), y * cos + turned, y)


W_PARTS = ((1, 0, 128, 256), (2, 0, 128, 384), (1, 128, 64, 512), (2, 128, 64, 576), (0, 0, 192, 0))


def front_body(
    n_ctx, n_dp, share, plen, clen, groups, conts,
    sel, px, cx, w, g1, b1, g2, b2, valid, wo, wu, wd,
    xn_o, kv_o, tab_o, w_o, wu_o, wd_o, wo_o, o, lse, msgs, gains, qpack,
    xn, q, kvs, kvc, tab, w_full, gb, gbs, cnt, cnts, notes, m_s, l_s, acc_s,
    wgs, s_x, r_x, s_kv, r_kv, s_c, r_c, s_w, r_w, osem,
):
    me = lax.axis_index("ctx")
    mine = lax.axis_index("dp")
    depth = w.shape[2]
    width = px.shape[1]
    last = n_ctx - 1
    n_prompt = groups * plen
    n_cont = conts * clen
    tile = clen
    dp_peers = axis_peers("dp", n_dp)
    peers = axis_peers("ctx", n_ctx)
    for i, vector in enumerate((g1, b1, g2, b2)):
        gb[i:i + 1] = vector[...].astype(f32).reshape(1, depth)
    gb[4:8] = jnp.zeros((4, depth), f32)
    cnt[...] = jnp.zeros(cnt.shape, f32) + jnp.sum(valid[...].astype(f32))
    greet(dp_peers + peers)

    copies = []
    weights = []
    if share:
        cols = pl.ds(pl.multiple_of(mine * depth, 128), depth)
        here = rows(mine * depth, depth)
    for d, device in enumerate(dp_peers):
        pairs = [(gb, gbs.at[mine]), (cnt, cnts.at[mine])]
        if share:
            pairs += [
                (w.at[p, a:a + n], w_full.at[t:t + n, cols]) for p, a, n, t in W_PARTS
            ]
        else:
            pairs += [(w, wgs.at[mine])]
        copies.append(
            [remote(s, t, s_x.at[d, i], r_x.at[d, i], device) for i, (s, t) in enumerate(pairs)]
        )
    for i in range(len(copies[0])):
        for group in copies:
            group[i].start()
    local = []
    if share:
        pairs = [
            (wo.at[0:128], wo_o.at[0:128, cols]), (wo.at[128:192], wo_o.at[192:256, cols]),
            (wu, wu_o.at[here]), (wd, wd_o.at[:, cols]),
        ]
        for d, device in enumerate(dp_peers):
            for i, (s, t) in enumerate(pairs):
                weights.append(remote(s, t, s_w.at[d, i], r_w.at[d, i], device))
        for copy in weights:
            copy.start()
        local += [pltpu.make_async_copy(s, t, osem.at[i]) for i, (s, t) in enumerate(pairs)]
        for copy in local:
            copy.start()
        for p, a, n, t in W_PARTS:
            w_full[t:t + n, cols] = w[p, a:a + n]
    else:
        wgs[mine] = w[...]
    wo_o[128:192] = jnp.zeros((64, width), bf16)
    w_full[192:256] = jnp.zeros((64, width), bf16)
    gbs[mine] = gb[...]
    cnts[mine] = cnt[...]

    def table(count, base, start):
        def body(i):
            shape = (CH, 128)
            lane = lax.broadcasted_iota(jnp.int32, shape, 1)
            row = lax.broadcasted_iota(jnp.int32, shape, 0)
            turns = lax.rem(lane, 32).astype(f32) * (-2.0 * math.log(10000.0) / HEAD_DIM)
            angle = (row + (start + i * CH)).astype(f32) * jnp.exp(turns)
            sin = jnp.sin(angle)
            left = lax.rem(lane, 64) < 32
            at = rows(base + i * CH, CH)
            tab[at, 0:128] = jnp.cos(angle)
            tab[at, 128:256] = jnp.where(left, -sin, 0.0)
            tab[at, 256:384] = jnp.where(left, 0.0, sin)

        loop(count // CH, body)

    table(plen, 0, me * plen)
    table(clen, plen, n_ctx * plen)

    def save(src, dst, i):
        copy = pltpu.make_async_copy(src, dst, osem.at[i])
        copy.start()
        local.append(copy)

    save(tab, tab_o, 4)
    for group in copies:
        group[0].wait_recv()
        group[1].wait_recv()

    def one_hot(d):
        row = lax.broadcasted_iota(jnp.int32, (depth, width), 0) + d * depth
        col = lax.broadcasted_iota(jnp.int32, (depth, width), 1)
        return (row == col).astype(f32).astype(bf16)

    total = jnp.zeros(gains.shape, f32)
    count = jnp.zeros(cnt.shape, f32)
    for d in range(n_dp):
        total += dot(gbs[d].astype(bf16), one_hot(d))
        count += cnts[d]
    gains[...] = total
    note = notes.at[me]
    notes[me] = count
    for i in range(conts):
        notes[me, 1 + i:2 + i] = jnp.zeros((1, 128), f32) + sel[i].astype(f32)
    counts = [remote(note, note, s_c.at[d], r_c.at[d], device) for d, device in enumerate(peers)]
    for copy in counts:
        copy.start()

    def norm_part(x, base):
        def body(i):
            whitened, _ = norm_rows(x[rows(i * CH, CH)].astype(f32))
            xn[rows(base + i * CH, CH)] = (whitened * gains[0:1] + gains[1:2]).astype(bf16)

        loop(x.shape[0] // CH, body)

    norm_part(px, 0)
    norm_part(cx, n_prompt)
    save(xn, xn_o, 5)

    def arrive(i):
        if share:
            for group in copies:
                group[2 + i].wait_recv()
        elif i == 0:
            for group in copies:
                group[2].wait_recv()
            for p, a, n, t in W_PARTS:
                part = jnp.zeros((n, width), f32)
                for d in range(n_dp):
                    part += dot(wgs[d, p, a:a + n], one_hot(d))
                w_full[t:t + n] = part.astype(bf16)

    def hop(slot, step, side):
        there = kvs.at[slot]
        return remote(there, there, s_kv.at[side, slot], r_kv.at[slot], {"ctx": me + step})

    def kv_rows(count, base, tab_base, period, dst):
        def body(i):
            at = rows(i * BIG, BIG)
            t = tab[rows(tab_base + lax.rem(i * BIG, period), BIG)]
            x = xn[rows(base + i * BIG, BIG)]
            y = dot_nt(x, w_full[256:512])
            dst[at, 0:128] = turn(y[:, 0:128], t, 1.0, False).astype(bf16)
            dst[at, 128:256] = y[:, 128:256].astype(bf16)
            dst[at, 256:384] = turn(dot_nt(x, w_full[512:640]), t, 1.0, True).astype(bf16)

        loop(count // BIG, body)

    def q_rows_of(count, base, tab_base, period):
        def body(i):
            at = rows(base + i * BIG, BIG)
            t = tab[rows(tab_base + lax.rem(i * BIG, period), BIG)]
            y = dot_nt(xn[at], w_full[0:256])
            q[at, 0:128] = (turn(y[:, 0:128], t, 1.0, False) * 0.125).astype(bf16)
            q[at, 128:256] = (turn(y[:, 128:256], t, 1.0, True) * 0.125).astype(bf16)

        loop(count // BIG, body)

    for i in range(4):
        arrive(i)
    kv_rows(n_prompt, 0, 0, plen, kvs.at[me])

    @pl.when(me < last)
    def _():
        hop(me, 1, 0).start()

    @pl.when(me > 0)
    def _():
        hop(me, -1, 1).start()

    save(kvs.at[me], kv_o.at[0:n_prompt], 6)
    kv_rows(n_cont, n_prompt, plen, clen, kvc)
    save(kvc, kv_o.at[n_prompt:n_prompt + n_cont], 7)
    arrive(4)
    save(w_full, w_o, 8)
    q_rows_of(n_cont, n_prompt, plen, clen)
    q_rows_of(n_prompt, 0, 0, plen)

    def update(at, q_rows, k, v, mask, first):
        s = dot_nt(q_rows, k)
        if mask is not None:
            s = mask(s)
        top = jnp.max(s, -1, keepdims=True)
        if first:
            m_new = jnp.broadcast_to(top, (s.shape[0], 128))
        else:
            m_old = m_s[at]
            m_new = jnp.maximum(m_old, top)
        total = None
        parts = []
        for j in range(s.shape[1] // 128):
            p = jnp.exp(s[:, 128 * j:128 * j + 128] - m_new)
            total = p if total is None else total + p
            parts.append(p.astype(bf16))
        pv = dot(jnp.concatenate(parts, 1), v)
        m_s[at] = m_new
        if first:
            l_s[at] = total
            acc_s[at] = pv
        else:
            fade = jnp.exp(m_old - m_new)
            l_s[at] = l_s[at] * fade + total
            acc_s[at] = acc_s[at] * fade + pv

    low = lanes_below((tile, 128), 64)

    def heads(q_at, state, k_b, k_c, k_d, mask, first):
        a = q[q_at, 0:128]
        zero = jnp.zeros_like(a)
        update(state, jnp.where(low, a, zero), k_b, k_c, mask, first)
        update(state + 1, jnp.where(low, zero, a), k_b, k_c, mask, first)
        update(state + 2, q[q_at, 128:256], k_d, k_d, mask, first)

    tiles = plen // tile

    def prompt_part(slot, diagonal):
        def body(i):
            group = i // tiles
            t = lax.rem(i, tiles)
            at = rows(group * plen, plen)
            mask = None
            if diagonal:
                def mask(s):
                    row = lax.broadcasted_iota(jnp.int32, s.shape, 0) + t * tile
                    col = lax.broadcasted_iota(jnp.int32, s.shape, 1)
                    return jnp.where(col <= row, s, NEG)
            heads(
                rows(i * tile, tile), 3 * i,
                kvs[slot, at, 0:128], kvs[slot, at, 128:256], kvs[slot, at, 256:384],
                mask, diagonal,
            )

        loop(groups * tiles, body)

    def cont_part(slot, first):
        def body(i):
            k = kvs[slot, 0:plen]
            for g in range(1, groups):
                k = jnp.where(sel[i] == g, kvs[slot, g * plen:(g + 1) * plen], k)
            heads(
                rows(n_prompt + i * tile, tile), 3 * (groups * tiles + i),
                k[:, 0:128], k[:, 128:256], k[:, 256:384], None, first,
            )

        loop(conts, body)

    def self_part():
        def body(i):
            at = rows(i * tile, tile)

            def mask(s):
                row = lax.broadcasted_iota(jnp.int32, s.shape, 0)
                col = lax.broadcasted_iota(jnp.int32, s.shape, 1)
                bias = (valid[pl.ds(i, 1)].astype(f32) - 1.0) * (-NEG)
                return jnp.where(col <= row, s + bias, NEG)

            heads(
                rows(n_prompt + i * tile, tile), 3 * (groups * tiles + i),
                kvc[at, 0:128], kvc[at, 128:256], kvc[at, 256:384], mask, False,
            )

        loop(conts, body)

    cont_part(me, True)
    prompt_part(me, True)
    self_part()
    e0 = q[n_prompt:n_prompt + clen, 128:256].astype(f32)
    e1 = q[n_prompt + clen:n_prompt + n_cont, 128:256].astype(f32)
    qpack[0:n_cont] = q[n_prompt:n_prompt + n_cont, 0:128]
    qpack[n_cont:n_cont + clen] = jnp.where(low, e0, pltpu.roll(e1, 64, 1)).astype(bf16)

    def ring(e):
        d = e + 1

        @pl.when(me - d >= 0)
        def _():
            hop(me - d, 1, 0).wait_recv()

            @pl.when(me < last)
            def _():
                hop(me - d, 1, 0).start()

        @pl.when(me + d <= last)
        def _():
            hop(me + d, -1, 1).wait_recv()

            @pl.when(me > 0)
            def _():
                hop(me + d, -1, 1).start()

        @pl.when(me - d >= 0)
        def _():
            cont_part(me - d, False)
            prompt_part(me - d, False)

        @pl.when(me + d <= last)
        def _():
            cont_part(me + d, False)

    loop(last, ring)

    for copy in counts:
        copy.wait()
    for d in range(n_ctx):
        msgs[8 * d:8 * d + 8] = notes[d]

    def finish(at, state):
        l0 = jnp.sum(l_s[state], -1, keepdims=True)
        l1 = jnp.sum(l_s[state + 1], -1, keepdims=True)
        l2 = jnp.sum(l_s[state + 2], -1, keepdims=True)
        o[at, 0:128] = jnp.where(low, acc_s[state] / l0, acc_s[state + 1] / l1).astype(bf16)
        o[at, 128:256] = jnp.where(low, 0.0, acc_s[state + 2] / l2).astype(bf16)
        return (l0, l1, l2)

    def finish_prompt(i):
        finish(rows(i * tile, tile), 3 * i)

    loop(groups * tiles, finish_prompt)
    for i in range(conts):
        state = 3 * (groups * tiles + i)
        sums = finish(rows(n_prompt + i * tile, tile), state)
        lse[8 * i:8 * i + 8] = jnp.zeros((8, tile), f32)
        for h in range(3):
            value = m_s[state + h] + jnp.log(sums[h])
            lse[8 * i + h:8 * i + h + 1] = jnp.transpose(value)[0:1]

    for slot in range(n_ctx):
        @pl.when((slot <= me) & (me < last))
        def _():
            hop(slot, 1, 0).wait_send()

        @pl.when((slot >= me) & (me > 0))
        def _():
            hop(slot, -1, 1).wait_send()

    for group in copies:
        for copy in group:
            copy.wait_send()
    for copy in weights:
        copy.wait()
    for copy in local:
        copy.wait()


def full_at(a, core, split, c_split):
    b = a // split
    return a + core * split * (1 - b) + b * (split + core * c_split)


class TpSum:
    @staticmethod
    def scratch(half, width):
        n = half // CH
        return [
            pltpu.VMEM((half, width), bf16), pltpu.VMEM((half, width), bf16),
            pltpu.VMEM((half, width), bf16), pltpu.VMEM((half, width), bf16),
            pltpu.VMEM((half, width), f32), DMA((2, n)), DMA((2, n)),
        ]

    def __init__(self, half, start, place, scratch, compute):
        self.half, self.start, self.place, self.compute = half, start, place, compute
        self.snd1, self.rcv1, self.snd2, self.rcv2, self.own, self.send, self.recv = scratch
        self.core, self.mate, self.across = tp_place()
        self.n = half // CH

    def row(self, i):
        return lax.rem(self.start + i * CH, self.half)

    def pair(self, i):
        at = rows(self.row(i), CH)
        return remote(
            self.snd1.at[at], self.rcv1.at[at], self.send.at[0, i], self.recv.at[0, i], self.mate
        )

    def link(self, i):
        at = rows(self.row(i), CH)
        return remote(
            self.snd2.at[at], self.rcv2.at[at], self.send.at[1, i], self.recv.at[1, i], self.across
        )

    def second(self, i):
        at = rows(self.row(i), CH)
        self.pair(i).wait_recv()
        self.snd2[at] = (self.own[at] + self.rcv1[at].astype(f32)).astype(bf16)
        self.link(i).start()

    def launch(self, i):
        a = self.row(i)
        at = rows(a, CH)
        self.snd1[at] = self.compute(self.place(a, 1 - self.core), CH).astype(bf16)
        self.pair(i).start()
        self.own[at] = self.compute(self.place(a, self.core), CH)

    def begin(self, held=0):
        def body(i):
            self.launch(i)

            @pl.when((i > 0) & (i <= self.n - held))
            def _():
                self.second(i - 1)

        loop(self.n, body)
        if not held:
            self.second(self.n - 1)

    def resume(self, held):
        for i in range(self.n - held, self.n):
            self.second(i)

    def take(self, i):
        at = rows(self.row(i), CH)
        self.link(i).wait_recv()
        return self.snd2[at].astype(f32) + self.rcv2[at].astype(f32)

    def close(self):
        def body(i):
            self.pair(i).wait_send()
            self.link(i).wait_send()

        loop(self.n, body)


class Share:
    def __init__(self, ref, place, sems):
        self.ref, self.place = ref, place
        self.send, self.recv = sems
        _, self.mate, _ = tp_place()

    def copy(self, i, a):
        at = rows(self.place(a), CH)
        return remote(self.ref.at[at], self.ref.at[at], self.send.at[i], self.recv.at[i], self.mate)


def share_scratch(half):
    return [DMA((half // CH,)), DMA((half // CH,))]


GELU = 0.7978845608028654


def gelu_tanh(u):
    return jnp.tanh(GELU * (u + 0.044715 * (u * u * u)))


def mixed_states(ids, dwa, hist, at, y):
    mixed = dwa[4] * y
    for j in range(4):
        mixed += dwa[ids[j]] * hist[j, at].astype(f32)
    return mixed


def column(row):
    return jnp.transpose(jnp.broadcast_to(row, (128, row.shape[1])))


def middle_body(
    n_ctx, n_prompt, clen,
    ids, dwa, o, qpack, msgs, wo, wu, wd, cx, gains, valid, hist, teach,
    out, dm, hid, xn, du, da, do, dh1, stat, qs,
    hc, tc, slope, h1, dy, mask, hsem, s_q, r_q, *scratch,
):
    core, mate, across = tp_place()
    ctx = lax.axis_index("ctx")
    half = clen
    n_cont = 2 * half
    mine = rows(core * half, half)
    loads = [
        pltpu.make_async_copy(hist.at[:, mine], hc, hsem.at[0]),
        pltpu.make_async_copy(teach.at[mine], tc, hsem.at[1]),
    ]
    for copy in loads:
        copy.start()
    qs[ctx] = qpack[...]
    mask[...] = column(valid[pl.ds(core, 1)].astype(f32))
    stat[...] = jnp.zeros(stat.shape, f32)
    others = axis_peers("ctx", n_ctx)
    greet([mate, across] + others)
    s1, s2, s3 = scratch[0:7], scratch[7:14], scratch[14:21]
    shares = scratch[21:]

    def place(a, c):
        return a + c * half

    def home(a):
        return a + core * half

    def each(body):
        loop(half // CH, body)

    def attn(at, size):
        return dot(o[rows(n_prompt + at, size)], wo[...])

    first = TpSum(half, 0, place, s1, attn)
    each(first.launch)
    each(first.second)
    moves = [
        remote(qs.at[ctx], qs.at[ctx], s_q.at[d], r_q.at[d], device)
        for d, device in enumerate(others)
    ]
    for copy in moves:
        copy.start()
    give_xn = Share(xn, home, shares[0:2])

    def normed(i):
        a = first.row(i)
        h = cx[rows(home(a), CH)].astype(f32) + first.take(i)
        h1[rows(a, CH)] = h
        whitened, _ = norm_rows(h)
        xn[rows(home(a), CH)] = (whitened * gains[2:3] + gains[3:4]).astype(bf16)
        give_xn.copy(i, a).start()

    def hidden(at, size):
        here = rows(at, size)
        u = dot(xn[here], wu[...])
        t = gelu_tanh(u)
        g = (0.5 * u * (1.0 + t)).astype(bf16)
        hid[here] = g
        slope[here] = 0.5 * (1.0 + t) + (0.5 * GELU) * u * (1.0 - t * t) * (
            1.0 + (3.0 * 0.044715) * (u * u)
        )
        return dot(g, wd[...])

    second = TpSum(half, 0, place, s2, hidden)

    def onward(before, share, after):
        def body(i):
            before(i)

            @pl.when(i > 0)
            def _():
                after.second(i - 1)

            share.copy(i, after.row(i)).wait()
            after.launch(i)

        each(body)
        after.second(after.n - 1)

    onward(normed, give_xn, second)
    for copy in loads:
        copy.wait()
    give_dm = Share(dm, home, shares[2:4])
    give_out = Share(out, home, shares[4:6])
    count = msgs[0:1]
    for j in range(1, n_ctx):
        count += msgs[8 * j:8 * j + 1]
    coef = (2.0 * dwa[4]) / (jnp.maximum(count, 1.0) * (1.0 * cx.shape[1]))

    def add(row, value):
        stat[row:row + 1] += jnp.sum(value, 0, keepdims=True)

    def lossy(i):
        a = second.row(i)
        here, there = rows(a, CH), rows(home(a), CH)
        y = h1[here] + second.take(i)
        mixed = mixed_states(ids, dwa, hc, here, y)
        diff = mixed - tc[here].astype(f32)
        weighted = diff * mask[here][:, 0:1]
        grad = weighted * coef[:, 0:1]
        dy[here] = grad
        dm[there] = grad.astype(bf16)
        give_dm.copy(i, a).start()
        out[there] = mixed.astype(bf16)
        give_out.copy(i, a).start()
        add(4, weighted * diff)
        for j in range(4):
            add(5 + j, weighted * hc[j, here].astype(f32))
        add(9, weighted * y)

    def back(at, size):
        here = rows(at, size)
        d = (dot_nt(dm[here], wd[...]) * slope[here]).astype(bf16)
        du[here] = d
        return dot_nt(d, wu[...])

    third = TpSum(half, 0, place, s3, back)
    onward(lossy, give_dm, third)
    give_da = Share(da, home, shares[6:8])

    def grads(i):
        a = third.row(i)
        here = rows(a, CH)
        total = third.take(i)
        whitened, inverse = norm_rows(h1[here])
        grad = dy[here] + norm_back(total, whitened, inverse, gains[2:3])
        dh1[here] = grad
        da[rows(home(a), CH)] = grad.astype(bf16)
        give_da.copy(i, a).start()
        add(2, total * whitened)
        add(3, total)

    each(grads)
    each(lambda i: give_da.copy(i, third.row(i)).wait())

    def last(i):
        at = rows(i * BIG, BIG)
        do[at] = dot_nt(da[at], wo[...]).astype(bf16)

    loop(n_cont // BIG, last)
    each(lambda i: give_out.copy(i, second.row(i)).wait())
    for part in (first, second, third):
        part.close()
    for copy in moves:
        copy.wait()


class LineSum:
    @staticmethod
    def scratch(count, width):
        buffer = pltpu.VMEM((count, LINE, width), bf16)
        return [buffer, buffer, buffer, DMA((2, count)), DMA((2, count))]

    def __init__(self, me, src, dst, scratch, ready):
        self.src, self.dst, self.ready = src, dst, ready
        self.got, self.pair, self.far, self.send, self.recv = scratch
        side = me // 2
        self.outer = (me == 0) | (me == 3)
        self.inner = (me == 1) | (me == 2)
        self.near = {"ctx": 1 + side}
        self.back = {"ctx": 3 * side}
        self.twin = {"ctx": 2 - side}

    def at(self, k):
        return rows(k * LINE, LINE)

    def up(self, k):
        return remote(
            self.src.at[self.at(k)], self.got.at[k], self.send.at[0, k], self.recv.at[0, k], self.near
        )

    def cross(self, k):
        return remote(
            self.pair.at[k], self.far.at[k], self.send.at[1, k], self.recv.at[1, k], self.twin
        )

    def down(self, k):
        return remote(
            self.pair.at[k], self.got.at[k], self.send.at[0, k], self.recv.at[0, k], self.back
        )

    def launch(self, k):
        @pl.when(self.outer)
        def _():
            self.up(k).start()

    def skip(self, k):
        @pl.when(self.inner)
        def _():
            self.pair[k] = self.src[self.at(k)]
            self.cross(k).start()

    def meet(self, k):
        @pl.when(self.inner)
        def _():
            self.up(k).wait_recv()
            self.pair[k] = (
                self.src[self.at(k)].astype(f32) + self.got[k].astype(f32)
            ).astype(bf16)
            self.cross(k).start()

    def turn(self, k):
        @pl.when(self.inner)
        def _():
            self.cross(k).wait()
            total = (self.pair[k].astype(f32) + self.far[k].astype(f32)).astype(bf16)
            self.pair[k] = total
            self.down(k).start()
            self.dst[self.at(k)] = total

    def land(self, k):
        @pl.when(self.outer & (k >= self.ready))
        def _():
            self.up(k).wait_send()

        @pl.when(self.outer)
        def _():
            self.down(k).wait_recv()
            self.dst[self.at(k)] = self.got[k]

        @pl.when(self.inner)
        def _():
            self.down(k).wait_send()


def down_grads(hid, dm, cols, store):
    for j in range(hid.shape[1] // 256):
        store(j * 256, dot_tn(hid[:, 256 * j:256 * j + 256], dm[:, cols]))


def other_grads(ff, xn, du, o, da, cols, store):
    size = cols.size
    for j in range(ff // size):
        store(ff + j * size, dot_tn(xn[:, cols], du[:, size * j:size * j + size]))
    g = dot_tn(o[...], da[:, cols])
    store(ff + ff, g[0:128])
    store(ff + ff + 128, g[192:256])


def attend_back_body(
    n_ctx, n_dp, share, plen, clen, groups, conts, depth,
    ids, dwa, msgs, qs, do, o, lse, kv, valid, tab, gains, hid_h, dm_h, xn2_h, du_h, da_h,
    wo_h, wu_h, wd_h, px_h, hist_h, xn1_h, *refs,
):
    if share:
        dcat, out, g_all = refs[:3]
        refs = refs[3:]
    else:
        dcat, out, g_down, g_up, g_out, g_kv = refs[:6]
        refs = refs[6:]
    (
        hid, dm, xn2, du, da, wo, wu, wd, px, hist, lsem,
        dos, sts, dqs, kd, acc_k, acc_v, acc_kd, acc_vd, dq_f, send, recv,
        xp, h1, xn1, flags,
    ) = refs[:26]
    s1, s2 = refs[26:33], refs[33:40]
    shares = refs[40:44]
    refs = refs[44:]
    core, mate, across = tp_place()
    me = lax.axis_index("ctx")
    dp = lax.axis_index("dp")
    peers = axis_peers("ctx", n_ctx)
    dp_peers = axis_peers("dp", n_dp) if share else []
    n_prompt = groups * plen
    n_cont = conts * clen
    half = plen
    own_rows = rows(core * half, half)
    pairs = [
        (wo_h, wo), (px_h.at[own_rows], px), (hid_h, hid), (dm_h, dm), (xn2_h, xn2), (du_h, du),
        (da_h, da), (wu_h, wu), (wd_h, wd), (hist_h.at[:, own_rows], hist), (xn1_h, xn1),
    ]
    loads = [
        pltpu.make_async_copy(s, t, lsem.at[i]) for i, (s, t) in enumerate(pairs)
    ]
    for copy in loads:
        copy.start()
    low = lanes_below((clen, 128), 64)
    zero = jnp.zeros((clen, 128), bf16)
    for c in range(conts):
        flags[c * clen:(c + 1) * clen] = column(valid[c:c + 1].astype(f32))

    g0 = do[0:clen, 128:256].astype(f32)
    g1 = do[clen:2 * clen, 128:256].astype(f32)
    dos[me, 0:n_cont] = do[:, 0:128]
    dos[me, n_cont:n_cont + clen] = jnp.where(low, pltpu.roll(g0, 64, 1), g1).astype(bf16)
    for c in range(conts):
        at = slice(c * clen, (c + 1) * clen)
        full = slice(n_prompt + c * clen, n_prompt + (c + 1) * clen)
        pa = do[at, 0:128].astype(f32) * o[full, 0:128].astype(f32)
        pe = do[at, 128:256].astype(f32) * o[full, 128:256].astype(f32)
        ta = jnp.transpose(pa)
        te = jnp.transpose(pe)
        st = 8 * c
        sts[me, st:st + 8] = lse[8 * c:8 * c + 8]
        sts[me, st + 3:st + 4] = jnp.sum(ta[0:64], 0, keepdims=True)
        sts[me, st + 4:st + 5] = jnp.sum(ta[64:128], 0, keepdims=True)
        sts[me, st + 5:st + 6] = jnp.sum(te[64:128], 0, keepdims=True)
    greet(peers + [mate, across] + dp_peers)
    sends = []
    for d, device in enumerate(peers):
        for i, ref in enumerate((sts, dos)):
            sends.append(remote(ref.at[me], ref.at[me], send.at[d, i], recv.at[d, i], device))
    for copy in sends:
        copy.start()

    def place(a, c):
        return a + c * half

    def home(a):
        return a + core * half

    loads[0].wait()
    loads[1].wait()

    def attn(at, size):
        return dot(o[rows(at, size)], wo[...])

    first = TpSum(half, 0, place, s1, attn)
    first.begin()

    for copy in loads[2:7]:
        copy.wait()
    ff = hid.shape[1]
    o_c = o.at[n_prompt:n_prompt + n_cont]
    bounds = (0, ff, 2 * ff + 192, 2 * ff + 576)
    if share:
        gsnd, grcv, gown, gdn, s_g, r_g = refs[:6]
        got, s_l, r_l = refs[6:9]
        outer = (me == 0) | (me == 3)
        inner = (me == 1) | (me == 2)

        def up(k):
            at = rows(k * LINE, LINE)
            return remote(gdn.at[at], got.at[at], s_l.at[k], r_l.at[k], {"ctx": 1 + me // 2})

    def cols_of(d):
        return pl.ds(pl.multiple_of(lax.rem(dp + d, n_dp) * depth, 128), depth)

    def give(d, i):
        span = slice(bounds[i], bounds[i + 1])
        return remote(
            gsnd.at[d - 1, span], grcv.at[d - 1, span], s_g.at[d - 1, i], r_g.at[d - 1, i],
            {"dp": lax.rem(dp + d, n_dp)},
        )

    def keeper(d):
        if d == 0:
            def store(at, value):
                gown[at:at + value.shape[0]] = value
        else:
            def store(at, value):
                gsnd[d - 1, at:at + value.shape[0]] = value.astype(bf16)
        return store

    def kv_grads(cols, store):
        for lo, hi in ((256, 384), (384, 512), (512, 640)):
            store(2 * ff + 192 + lo - 256, dot_tn(dcat[:, lo:hi], xn1[:, cols]))

    def settle(dst, i):
        for d in range(1, n_dp):
            give(d, i).wait()

        def body(j):
            at = rows(bounds[i] + j * 64, 64)
            total = gown[at]
            for d in range(n_dp - 1):
                total += grcv[d, at].astype(f32)
            dst(at, j, total.astype(bf16))

        loop((bounds[i + 1] - bounds[i]) // 64, body)

    if share:
        for d in range(1, n_dp):
            down_grads(hid, dm, cols_of(d), keeper(d))
            give(d, 0).start()
        for d in range(1, n_dp):
            other_grads(ff, xn2, du, o_c, da, cols_of(d), keeper(d))
            give(d, 1).start()
    else:
        width = dm.shape[1]
        for j in range(width // 256):
            cols = pl.ds(256 * j, 256)
            span = slice(256 * j, 256 * j + 256)

            def lay(at, value, span=span):
                if at < ff:
                    g_down[at:at + 256, span] = value.astype(bf16)
                elif at < 2 * ff:
                    g_up[span, at - ff:at - ff + 256] = value.astype(bf16)
                else:
                    g_out[at - 2 * ff:at - 2 * ff + value.shape[0], span] = value.astype(bf16)

            down_grads(hid, dm, cols, lay)
            other_grads(ff, xn2, du, o_c, da, cols, lay)

    kd[...] = pltpu.roll(kv[0:n_prompt, 256:384].astype(f32), 64, 1).astype(bf16)
    for acc in (acc_k, acc_v, acc_kd, acc_vd):
        acc[...] = jnp.zeros(acc.shape, f32)

    def one_head(q_rows, do_rows, k, v, lse_row, delta_row, mask):
        s = dot_nt(k, q_rows)
        p = jnp.exp(s - lse_row)
        if mask is not None:
            p = mask(p)
        dp_ = dot_nt(v, do_rows)
        ds = (p * (dp_ - delta_row)).astype(bf16)
        return p.astype(bf16), ds

    def halves(a):
        return jnp.where(low, a, zero), jnp.where(low, zero, a)

    def continuation(src, c, k_b, k_c, k_d, k_s, mask):
        base = c * clen
        a0, a1 = halves(qs[src, base:base + clen])
        d0, d1 = halves(dos[src, base:base + clen])
        e = halves(qs[src, n_cont:n_cont + clen])[c]
        g = halves(dos[src, n_cont:n_cont + clen])[c]
        st = 8 * c
        row = lambda i: sts[src, st + i:st + i + 1]
        p0, s0 = one_head(a0, d0, k_b, k_c, row(0), row(3), mask)
        dv = dot(p0, d0)
        dk = dot(s0, a0)
        dq0 = dot_tn(s0, k_b)
        p1, s1_ = one_head(a1, d1, k_b, k_c, row(1), row(4), mask)
        dv += dot(p1, d1)
        dk += dot(s1_, a1)
        dq1 = dot_tn(s1_, k_b)
        keys, values = (k_d, k_s) if c == 0 else (k_s, k_d)
        p2, s2_ = one_head(e, g, keys, values, row(2), row(5), mask)
        dvd = dot(p2, g)
        dkd = dot(s2_, e)
        dq2 = dot_tn(s2_, keys)
        return dk, dv, dkd, dvd, jnp.where(low, dq0, dq1), dq2

    def source(src, own):
        pair = []
        for c in range(conts):
            pick = msgs[pl.ds(src * 8 + 1 + c, 1)]

            def choose(one, two):
                return jnp.where(pick == 0.0, one.astype(f32), two.astype(f32)).astype(bf16)

            k_b = choose(kv[0:plen, 0:128], kv[plen:2 * plen, 0:128])
            k_c = choose(kv[0:plen, 128:256], kv[plen:2 * plen, 128:256])
            k_d = choose(kv[0:plen, 256:384], kv[plen:2 * plen, 256:384])
            k_s = choose(kd[0:plen], kd[plen:2 * plen])
            dk, dv, dkd, dvd, dqa, dqd = continuation(src, c, k_b, k_c, k_d, k_s, None)
            for g in range(groups):
                keep = (pick == 1.0 * g).astype(f32)
                at = slice(g * plen, (g + 1) * plen)
                acc_k[at] += keep * dk
                acc_v[at] += keep * dv
                acc_kd[at] += keep * dkd
                acc_vd[at] += keep * dvd
            pair.append(dqd)
            if own:
                dq_f[c * clen:(c + 1) * clen] = dqa
            else:
                dqs[n_ctx + src, c * clen:(c + 1) * clen] = dqa.astype(bf16)
        third = jnp.where(low, pair[0], pair[1])
        if own:
            dq_f[n_cont:n_cont + clen] = third
        else:
            dqs[n_ctx + src, n_cont:n_cont + clen] = third.astype(bf16)

    def other_of(d):
        return lax.rem(me + 2 * n_ctx - (d + 1), n_ctx)

    def back_copy(d):
        other = other_of(d)
        return remote(
            dqs.at[n_ctx + other], dqs.at[me], send.at[d, 2], recv.at[d, 2], {"ctx": other}
        )

    def visit(d):
        other = other_of(d)
        for i, ref in enumerate((sts, dos)):
            remote(ref.at[other], ref.at[other], send.at[d, i], recv.at[d, i], {"ctx": other}).wait_recv()
        source(other, False)
        back_copy(d).start()

    give_xn = Share(xp, home, shares[0:2])

    def normed(i):
        a = first.row(i)
        h = px[rows(a, CH)].astype(f32) + first.take(i)
        h1[rows(a, CH)] = h
        whitened, _ = norm_rows(h)
        xp[rows(home(a), CH)] = (whitened * gains[2:3] + gains[3:4]).astype(bf16)
        give_xn.copy(i, a).start()

    def hidden(at, size):
        u = dot(xp[rows(at, size)], wu[...])
        return dot((0.5 * u * (1.0 + gelu_tanh(u))).astype(bf16), wd[...])

    second = TpSum(half, 0, place, s2, hidden)
    def to_line(at, j, value):
        gdn[rows(j * 64, 64)] = value

    def to_part(at, j, value):
        g_all[at] = value

    source(me, True)
    for copy in loads[7:9]:
        copy.wait()

    def step(i):
        @pl.when(i < first.n)
        def _():
            normed(i)
            give_xn.copy(i, first.row(i)).wait()
            second.launch(i)

        @pl.when((i > 0) & (i < n_ctx))
        def _():
            visit(i - 1)

        @pl.when(i < first.n)
        def _():
            second.second(i)

    loop(max(half // CH, n_ctx), step)
    if share:
        down_grads(hid, dm, cols_of(0), keeper(0))
        settle(to_line, 0)

        @pl.when(outer)
        def _():
            loop(ff // LINE, lambda k: up(k).start())

    for c in range(conts):
        at = slice(n_prompt + c * clen, n_prompt + (c + 1) * clen)
        k_d = kv[at, 256:384]
        k_s = pltpu.roll(k_d.astype(f32), 64, 1).astype(bf16)

        def mask(p):
            key = lax.broadcasted_iota(jnp.int32, p.shape, 0)
            query = lax.broadcasted_iota(jnp.int32, p.shape, 1)
            return jnp.where(
                key <= query, p * flags[c * clen:(c + 1) * clen, 0:1], 0.0
            )

        dk, dv, dkd, dvd, dqa, dqd = continuation(
            me, c, kv[at, 0:128], kv[at, 128:256], k_d, k_s, mask
        )
        dq_f[c * clen:(c + 1) * clen] += dqa
        keep = low if c == 0 else jnp.logical_not(low)
        dq_f[n_cont:n_cont + clen] += jnp.where(keep, dqd, 0.0)
        t = tab[plen:plen + clen]
        dcat[at, 256:384] = turn(dk, t, -1.0, False).astype(bf16)
        dcat[at, 384:512] = dv.astype(bf16)
        if c == 0:
            joined = jnp.where(low, dkd, pltpu.roll(dvd, 64, 1))
        else:
            joined = jnp.where(low, pltpu.roll(dkd, 64, 1), dvd)
        dcat[at, 512:640] = turn(joined, t, -1.0, True).astype(bf16)

    zq = jnp.zeros((plen, 256), bf16)
    wide = lanes_below((plen, 128), 64)
    for g in range(groups):
        at = slice(g * plen, (g + 1) * plen)
        t = tab[0:plen]
        dcat[at, 0:256] = zq
        dcat[at, 256:384] = turn(acc_k[at], t, -1.0, False).astype(bf16)
        dcat[at, 384:512] = acc_v[at].astype(bf16)
        k2 = acc_kd[at] + pltpu.roll(acc_kd[at], 64, 1)
        v2 = acc_vd[at] + pltpu.roll(acc_vd[at], 64, 1)
        dcat[at, 512:640] = turn(jnp.where(wide, k2, v2), t, -1.0, True).astype(bf16)

    loads[10].wait()
    if share:
        for d in range(1, n_dp):
            kv_grads(cols_of(d), keeper(d))
            give(d, 2).start()
        other_grads(ff, xn2, du, o_c, da, cols_of(0), keeper(0))
        kv_grads(cols_of(0), keeper(0))
        settle(to_part, 1)
    else:
        for j in range(xn1.shape[1] // 256):
            span = slice(256 * j, 256 * j + 256)

            def lay_kv(at, value, span=span):
                at = at - 2 * ff - 192
                g_kv[at:at + 128, span] = value.astype(bf16)

            kv_grads(pl.ds(256 * j, 256), lay_kv)

    for d in range(n_ctx - 1):
        back_copy(d).wait_send()
        other = lax.rem(me + d + 1, n_ctx)
        remote(
            dqs.at[n_ctx + other], dqs.at[other], send.at[d, 2], recv.at[d, 2], {"ctx": other}
        ).wait_recv()
        dq_f[...] += dqs[other].astype(f32)
    for c in range(conts):
        at = slice(n_prompt + c * clen, n_prompt + (c + 1) * clen)
        t = tab[plen:plen + clen]
        pair = dq_f[c * clen:(c + 1) * clen] * 0.125
        dcat[at, 0:128] = turn(pair, t, -1.0, False).astype(bf16)
        third = dq_f[n_cont:n_cont + clen] * 0.125
        if c == 1:
            third = pltpu.roll(third, 64, 1)
        third = jnp.where(low, third, 0.0)
        dcat[at, 128:256] = turn(third, t, -1.0, True).astype(bf16)

    loads[9].wait()
    give_out = Share(out, home, shares[2:4])

    def mixed(i):
        a = second.row(i)
        here = rows(a, CH)
        y = h1[here] + second.take(i)
        out[rows(home(a), CH)] = mixed_states(ids, dwa, hist, here, y).astype(bf16)
        give_out.copy(i, a).start()

    loop(half // CH, mixed)
    loop(half // CH, lambda i: give_out.copy(i, second.row(i)).wait())
    if share:
        settle(to_part, 2)

        @pl.when(outer)
        def _():
            g_all[0:ff] = gdn[...]
            loop(ff // LINE, lambda k: up(k).wait_send())

        @pl.when(inner)
        def _():
            def meet(k):
                at = rows(k * LINE, LINE)
                up(k).wait_recv()
                g_all[at] = (gdn[at].astype(f32) + got[at].astype(f32)).astype(bf16)

            loop(ff // LINE, meet)
    first.close()
    second.close()
    for copy in sends:
        copy.wait_send()


def input_grad_body(
    n_dp, n_ctx, share, split, c_split, depth, ready,
    dcat, w, px, cx, gains, dh1, stat_in, xn_h, *refs,
):
    if share:
        g_part, grad_p, grad_c, fin, g_sum = refs[:5]
        refs = refs[5:]
    else:
        grad_p, grad_c, fin, g_q = refs[:4]
        refs = refs[4:]
    xn, lsem, grad, stat, stats_m, stats_y, stats_c, stats_d, s_s, r_s = refs[:10]
    s1 = refs[10:17]
    shares = refs[17:19]
    refs = refs[19:]
    core, mate, across = tp_place()
    me = lax.axis_index("ctx")
    dp = lax.axis_index("dp")
    ctx_peers = axis_peers("ctx", n_ctx)
    dp_peers = axis_peers("dp", n_dp)
    half = split + c_split
    n_prompt = 2 * split
    n_cont = 2 * c_split
    load = pltpu.make_async_copy(xn_h.at[n_prompt:n_prompt + n_cont], xn, lsem.at[0])
    load.start()
    stat[...] = 0.5 * stat_in[...]
    greet([mate, across] + ctx_peers + dp_peers)
    if share:
        gsnd, gown, grcv, s_g, r_g, gall = refs[:6]
        n_part = g_part.shape[0]
        n_line = n_part // LINE
        take_part = pltpu.make_async_copy(g_part, gall.at[0:n_part], lsem.at[1])
        take_part.start()
        line = LineSum(me, gall, g_sum, refs[6:11], ready)
        take_part.wait()
        loop(n_line - ready, lambda k: line.launch(k + ready))
        loop(ready, line.skip)

    def place(a, c):
        return full_at(a, c, split, c_split)

    def home(a):
        return full_at(a, core, split, c_split)

    def compute(at, size):
        part = dot(dcat[rows(at, size)], w[...])
        b = at // n_prompt
        p = px[rows(at * (1 - b), size)].astype(f32)
        c = cx[rows((at - n_prompt) * b, size)].astype(f32)
        whitened, _ = norm_rows(jnp.where(b == 0, p, c))
        stat[0:1] += jnp.sum(part * whitened, 0, keepdims=True)
        stat[1:2] += jnp.sum(part, 0, keepdims=True)
        return part

    total = TpSum(half, split, place, s1, compute)
    total.begin(2)

    def small(src, dst, i, device):
        return remote(src, dst, s_s.at[i], r_s.at[i], device)

    stats_m[0] = stat[...]
    to_mate = small(stats_m.at[0], stats_m.at[1], 0, mate)
    to_mate.start()
    load.wait()

    def q_grads(cols):
        return dot_tn(dcat[n_prompt:n_prompt + n_cont, 0:256], xn[:, cols])[0:3 * HEAD_DIM]

    gives = []
    if share:
        for d in range(1, n_dp):
            other = lax.rem(dp + d, n_dp)
            cols = pl.ds(pl.multiple_of(other * depth, 128), depth)
            gsnd[d - 1] = q_grads(cols).astype(bf16)
            copy = remote(
                gsnd.at[d - 1], grcv.at[d - 1], s_g.at[d - 1], r_g.at[d - 1], {"dp": other}
            )
            copy.start()
            gives.append(copy)
        gown[...] = q_grads(pl.ds(pl.multiple_of(dp * depth, 128), depth))
    else:
        g_q[...] = q_grads(slice(None)).astype(bf16)
    to_mate.wait()
    stats_y[0] = stats_m[0] + stats_m[1]
    to_far = small(stats_y.at[0], stats_y.at[1], 1, across)
    to_far.start()
    total.resume(2)
    give = Share(grad, home, shares)

    def finish(i):
        a = total.row(i)
        b = a // split
        value = total.take(i)
        p = px[rows((core * split + a) * (1 - b), CH)].astype(f32)
        c = cx[rows((core * c_split + a - split) * b, CH)].astype(f32)
        whitened, inverse = norm_rows(jnp.where(b == 0, p, c))
        back = norm_back(value, whitened, inverse, gains[0:1])
        extra = dh1[rows((a - split) * b, CH)]
        grad[rows(home(a), CH)] = jnp.where(b == 0, back, back + extra).astype(bf16)
        give.copy(i, a).start()
        if share:
            line.meet(ready + i + 1)
            line.turn(2 * i)
            line.turn(2 * i + 1)

    def part(lo, hi):
        loop(hi - lo, lambda i: finish(i + lo))

    if share:
        line.meet(ready)
    part(0, 2)
    if share:
        for copy in gives:
            copy.wait()
        value = gown[...]
        for d in range(n_dp - 1):
            value += grcv[d].astype(f32)
        gall[n_part:n_part + 3 * HEAD_DIM] = value.astype(bf16)
        line.launch(n_line)
    part(2, 4)
    to_far.wait()
    stats_c[me] = stats_y[0] + stats_y[1]
    to_ctx = [
        small(stats_c.at[me], stats_c.at[me], 2 + d, device) for d, device in enumerate(ctx_peers)
    ]
    for copy in to_ctx:
        copy.start()
    part(4, 5)
    if share:
        line.meet(n_line)
    part(5, 6)
    for copy in to_ctx:
        copy.wait()
    value = stats_c[0]
    for d in range(1, n_ctx):
        value += stats_c[d]
    stats_d[dp] = value
    to_dp = [
        small(stats_d.at[dp], stats_d.at[dp], 1 + n_ctx + d, device)
        for d, device in enumerate(dp_peers)
    ]
    for copy in to_dp:
        copy.start()
    loop(total.n, lambda i: give.copy(i, total.row(i)).wait())
    grad_p[...] = grad[0:n_prompt]
    grad_c[...] = grad[n_prompt:n_prompt + n_cont]
    for copy in to_dp:
        copy.wait()
    value = stats_d[0]
    for d in range(1, n_dp):
        value += stats_d[d]
    fin[...] = value
    total.close()
    if share:
        loop(n_line + 1, line.land)


def output_body(
    n_ctx, n_dp, share, ff,
    ids, msgs, fin, p_out, c_out, p_grad, c_grad, *refs,
):
    n = 1 if share else 0
    parts = refs[:n]
    p_out_o, c_out_o, p_grad_o, c_grad_o, loss, dwa_g, g1, b1, g2, b2 = refs[n:n + 10]
    refs = refs[n + 10:]
    if share:
        r_qkv, r_out, r_up, r_down = refs[:4]
        refs = refs[4:]
    held, sem = refs[:4], refs[4]
    moves = (
        (p_out, p_out_o), (c_out, c_out_o), (p_grad, p_grad_o), (c_grad, c_grad_o)
    )
    reads = [
        pltpu.make_async_copy(s, h, sem.at[0, i]) for i, ((s, _), h) in enumerate(zip(moves, held))
    ]
    copies = [
        pltpu.make_async_copy(h, t, sem.at[1, i]) for i, ((_, t), h) in enumerate(zip(moves, held))
    ]
    for copy in reads:
        copy.start()
    depth = g1.shape[0]
    width = fin.shape[1]
    count = msgs[0:1, 0:1]
    for j in range(1, n_ctx):
        count += msgs[8 * j:8 * j + 1, 0:1]
    factor = 1.0 / (jnp.maximum(count, 1.0) * (1.0 * width))
    sums = jnp.sum(fin[...], -1, keepdims=True) * factor
    row = lax.broadcasted_iota(jnp.int32, sums.shape, 0)

    def entry(i):
        return jnp.sum(jnp.where(row == i, sums, 0.0))

    loss[0] = entry(4)
    for k in range(4):
        value = 0.0
        for j in range(4):
            value += jnp.where(ids[j] == k, 2.0 * entry(5 + j), 0.0)
        dwa_g[k] = value
    dwa_g[4] = 2.0 * entry(9)
    for i, ref in enumerate((g1, b1, g2, b2)):
        if share:
            ref[...] = fin[i, pl.ds(pl.multiple_of(lax.axis_index("dp") * depth, 128), depth)]
        else:
            piece = jnp.zeros((1, depth), f32)
            for d in range(n_dp):
                here = fin[i:i + 1, d * depth:(d + 1) * depth]
                piece += jnp.where(lax.axis_index("dp") == d, here, 0.0)
            ref[...] = piece.reshape(depth)
    for read, copy in zip(reads, copies):
        read.wait()
        copy.start()
    if share:
        rest = parts[0].at[ff:]
        r_down[...] = parts[0][0:ff].astype(f32)
        for j in range(ff // depth):
            r_up[:, j * depth:(j + 1) * depth] = rest[j * depth:(j + 1) * depth].astype(f32)
        r_out[...] = rest[ff:ff + 192].astype(f32)
        base = ff + 192
        r_qkv[1, 0:128] = rest[base:base + 128].astype(f32)
        r_qkv[2, 0:128] = rest[base + 128:base + 256].astype(f32)
        r_qkv[1, 128:192] = rest[base + 256:base + 320].astype(f32)
        r_qkv[2, 128:192] = rest[base + 320:base + 384].astype(f32)
        r_qkv[0] = rest[base + 384:base + 576].astype(f32)
    for copy in copies:
        copy.wait()


def per_device(
    n_dp, n_ctx,
    prompt_x, cont_x, prompt_hist, cont_hist, teacher, valid_mask, cont_group, layer_ids,
    dwa_weights, qkv_weight, out_weight, up_weight, down_weight,
    ln1_gain, ln1_bias, ln2_gain, ln2_bias,
):
    groups, plen, width = prompt_x.shape
    conts, clen, _ = cont_x.shape
    depth = qkv_weight.shape[0]
    n_prompt, n_cont = groups * plen, conts * clen
    n_rows = n_prompt + n_cont
    split, c_split = n_prompt // 2, n_cont // 2
    half = split + c_split
    ff = up_weight.shape[1]
    share = depth % 128 == 0
    packed = n_cont + clen
    tab_rows = plen + clen
    vmem = pltpu.VMEM

    w_t = qkv_weight.transpose(1, 2, 0)
    px = prompt_x.reshape(n_prompt, width)
    cx = cont_x.reshape(n_cont, width)
    vectors = (ln1_gain, ln1_bias, ln2_gain, ln2_bias)
    states = vmem((3 * (n_prompt // clen + conts), clen, 128), f32)
    xn1, kv, tab, w_full, wu, wd, wo, o, lse, msgs, gains, qpack = kernel_call(
        functools.partial(front_body, n_ctx, n_dp, share, plen, clen, groups, conts),
        [
            ((n_rows, width), bf16), ((n_rows, 384), bf16), ((tab_rows, 384), f32),
            ((640, width), bf16), ((width, ff), bf16), ((ff, width), bf16), ((256, width), bf16),
            ((n_rows, 256), bf16), ((8 * conts, clen), f32), ((8 * n_ctx, 128), f32),
            ((8, width), f32), ((packed, 128), bf16),
        ],
        [
            vmem((n_rows, width), bf16), vmem((n_rows, 256), bf16),
            vmem((n_ctx, n_prompt, 384), bf16), vmem((n_cont, 384), bf16),
            vmem((tab_rows, 384), f32), vmem((640, width), bf16),
            vmem((8, depth), f32), vmem((n_dp, 8, depth), f32),
            vmem((8, 128), f32), vmem((n_dp, 8, 128), f32), vmem((n_ctx, 8, 128), f32),
            states, states, states,
            vmem((1, 3, 192, depth) if share else (n_dp, 3, 192, depth), bf16),
            DMA((n_dp - 1, 7)), DMA((n_dp - 1, 7)),
            DMA((2, n_ctx)), DMA((n_ctx,)), DMA((n_ctx - 1,)), DMA((n_ctx - 1,)),
            DMA((n_dp - 1, 4)), DMA((n_dp - 1, 4)), DMA((9,)),
        ],
        0,
        [SMEM_SPEC] + [VMEM_SPEC] * 11,
        (cont_group, px, cx, w_t, *vectors, valid_mask, out_weight, up_weight, down_weight),
        "front",
        [HBM_SPEC] * 6 + [VMEM_SPEC] * 6,
    )
    if not share:
        out_w = lax.all_gather(out_weight, "dp", axis=1, tiled=True)
        wu = lax.all_gather(up_weight, "dp", axis=0, tiled=True)
        wd = lax.all_gather(down_weight, "dp", axis=1, tiled=True)
        wo = jnp.concatenate([out_w[:128], jnp.zeros((64, width), bf16), out_w[128:]], 0)

    cont_out, dm, hid, xn2, du, da, do, dh1, stat, qs = kernel_call(
        functools.partial(middle_body, n_ctx, n_prompt, clen),
        [
            ((n_cont, width), bf16), ((n_cont, width), bf16), ((n_cont, ff), bf16),
            ((n_cont, width), bf16), ((n_cont, ff), bf16), ((n_cont, width), bf16),
            ((n_cont, 256), bf16), ((c_split, width), f32), ((16, width), f32),
            ((n_ctx, packed, 128), bf16),
        ],
        [
            vmem((4, c_split, width), bf16), vmem((c_split, width), bf16),
            vmem((n_cont, ff), f32), vmem((c_split, width), f32),
            vmem((c_split, width), f32), vmem((clen, 128), f32),
            DMA((2,)), DMA((n_ctx - 1,)), DMA((n_ctx - 1,)),
        ]
        + TpSum.scratch(c_split, width) * 3
        + share_scratch(c_split) * 4,
        1,
        [SMEM_SPEC] * 2 + [VMEM_SPEC] * 9 + [HBM_SPEC] * 2,
        (
            layer_ids, dwa_weights, o, qpack, msgs, wo, wu, wd, cx, gains, valid_mask,
            cont_hist.reshape(4, n_cont, width), teacher.reshape(n_cont, width),
        ),
        "middle",
    )

    grad_rows = 2 * ff + 9 * HEAD_DIM
    outs = [((n_rows, 640), bf16), ((n_prompt, width), bf16)]
    if share:
        outs += [((grad_rows, depth), bf16)]
        extra = [
            vmem((n_dp - 1, grad_rows, depth), bf16), vmem((n_dp - 1, grad_rows, depth), bf16),
            vmem((grad_rows, depth), f32), vmem((ff, depth), bf16),
            DMA((n_dp - 1, 3)), DMA((n_dp - 1, 3)),
            vmem((ff, depth), bf16), DMA((ff // LINE,)), DMA((ff // LINE,)),
        ]
    else:
        outs += [
            ((ff, width), bf16), ((width, ff), bf16), ((3 * HEAD_DIM, width), bf16),
            ((384, width), bf16),
        ]
        extra = []
    acc = vmem((n_prompt, 128), f32)
    got = kernel_call(
        functools.partial(
            attend_back_body, n_ctx, n_dp, share, plen, clen, groups, conts, depth
        ),
        outs,
        [
            vmem((n_cont, ff), bf16), vmem((n_cont, width), bf16),
            vmem((n_cont, width), bf16), vmem((n_cont, ff), bf16),
            vmem((n_cont, width), bf16), vmem((256, width), bf16),
            vmem((width, ff), bf16), vmem((ff, width), bf16),
            vmem((split, width), bf16), vmem((4, split, width), bf16), DMA((11,)),
            vmem((n_ctx, packed, 128), bf16), vmem((n_ctx, 8 * conts, clen), f32),
            vmem((2 * n_ctx, packed, 128), bf16), vmem((n_prompt, 128), bf16),
            acc, acc, acc, acc, vmem((packed, 128), f32),
            DMA((n_ctx - 1, 3)), DMA((n_ctx - 1, 3)),
            vmem((n_prompt, width), bf16), vmem((split, width), f32),
            vmem((n_rows, width), bf16), vmem((n_cont, 128), f32),
        ]
        + TpSum.scratch(split, width) * 2
        + share_scratch(split) * 2
        + extra,
        2,
        [SMEM_SPEC] * 2 + [VMEM_SPEC] * 9 + [HBM_SPEC] * 11,
        (
            layer_ids, dwa_weights, msgs, qs, do, o, lse, kv, valid_mask, tab, gains,
            hid, dm, xn2, du, da, wo, wu, wd, px, prompt_hist.reshape(4, n_prompt, width), xn1,
        ),
        "attend_back",
    )
    dcat, prompt_out = got[:2]

    stat_rows = vmem((16, width), f32)
    outs = [((n_prompt, width), bf16), ((n_cont, width), bf16), ((16, width), f32)]
    args = (dcat, w_full, px, cx, gains, dh1, stat, xn1)
    specs = [VMEM_SPEC] * 7 + [HBM_SPEC]
    if share:
        args += (got[2],)
        specs += [HBM_SPEC]
        outs += [((grad_rows + LINE, depth), bf16)]
        extra = [
            vmem((n_dp - 1, 3 * HEAD_DIM, depth), bf16), vmem((3 * HEAD_DIM, depth), f32),
            vmem((n_dp - 1, 3 * HEAD_DIM, depth), bf16), DMA((n_dp - 1,)), DMA((n_dp - 1,)),
            vmem((grad_rows + LINE, depth), bf16),
        ] + LineSum.scratch(grad_rows // LINE + 1, depth)
    else:
        outs += [((3 * HEAD_DIM, width), bf16)]
        extra = []
    last = kernel_call(
        functools.partial(
            input_grad_body, n_dp, n_ctx, share, split, c_split, depth, ff // LINE
        ),
        outs,
        [
            vmem((n_cont, width), bf16), DMA((2,)), vmem((n_rows, width), bf16),
            stat_rows, vmem((2, 16, width), f32), vmem((2, 16, width), f32),
            vmem((n_ctx, 16, width), f32), vmem((n_dp, 16, width), f32),
            DMA((1 + n_ctx + n_dp,)), DMA((1 + n_ctx + n_dp,)),
        ]
        + TpSum.scratch(half, width)
        + share_scratch(half)
        + extra,
        3, specs, args, "input_grad",
    )
    grad_p, grad_c, fin = last[:3]

    outs = [
        ((n_prompt, width), bf16), ((n_cont, width), bf16), ((n_prompt, width), bf16),
        ((n_cont, width), bf16), ((1,), f32), ((5,), f32),
    ] + [((depth,), f32)] * 4
    out_specs = [HBM_SPEC] * 4 + [SMEM_SPEC] * 2 + [VMEM_SPEC] * 4
    specs = [SMEM_SPEC] + [VMEM_SPEC] * 2 + [HBM_SPEC] * 4
    args = (layer_ids, msgs, fin, prompt_out, cont_out, grad_p, grad_c)
    if share:
        outs += [((3, 192, depth), f32), ((192, depth), f32), ((depth, ff), f32), ((ff, depth), f32)]
        out_specs += [VMEM_SPEC] * 4
        args += (last[3],)
        specs += [VMEM_SPEC]
    done = pl.pallas_call(
        functools.partial(output_body, n_ctx, n_dp, share, ff),
        out_shape=[jax.ShapeDtypeStruct(s, d) for s, d in outs],
        in_specs=specs,
        out_specs=out_specs,
        scratch_shapes=[
            vmem((n_prompt, width), bf16), vmem((n_cont, width), bf16),
            vmem((n_prompt, width), bf16), vmem((n_cont, width), bf16), DMA((2, 4)),
        ],
        compiler_params=pltpu.CompilerParams(vmem_limit_bytes=LIMIT),
        name="outputs",
    )(*args)
    if share:
        r_qkv, r_out, r_up, r_down = done[10:]
        r_qkv = r_qkv.transpose(2, 0, 1)
    else:
        def scattered(g, dim):
            part = lax.psum_scatter(g, "dp", scatter_dimension=dim, tiled=True)
            return lax.psum(part, "ctx").astype(f32)

        g_down, g_up, g_out, g_kv = got[2:]
        r_down = scattered(g_down, 1)
        r_up = scattered(g_up, 0)
        r_out = scattered(g_out, 1)
        g_k = jnp.concatenate([g_kv[0:128], g_kv[256:320]], 0)
        g_v = jnp.concatenate([g_kv[128:256], g_kv[320:384]], 0)
        r_qkv = scattered(jnp.stack([last[3], g_k, g_v]).transpose(2, 0, 1), 0)
    return (
        done[0].reshape(groups, plen, width),
        done[1].reshape(conts, clen, width),
        done[4].reshape(()),
        done[2].reshape(groups, plen, width),
        done[3].reshape(conts, clen, width),
        r_qkv, r_out, r_up, r_down,
        done[6], done[7], done[8], done[9],
        done[5],
    )


def solution(mesh):
    n_dp, n_ctx = mesh.shape["dp"], mesh.shape["ctx"]
    in_specs = (
        P("dp", "ctx", None), P(("dp", "ctx"), None, None), P(None, "dp", "ctx", None),
        P(None, ("dp", "ctx"), None, None), P(("dp", "ctx"), None, None), P(("dp", "ctx"), None),
        P(("dp", "ctx")), P(), P(), P("dp", None, "tp"), P("tp", "dp"), P("dp", "tp"),
        P("tp", "dp"), P("dp"), P("dp"), P("dp"), P("dp"),
    )
    out_specs = (
        P("dp", "ctx", None), P(("dp", "ctx"), None, None), P(), P("dp", "ctx", None),
        P(("dp", "ctx"), None, None), P("dp", None, "tp"), P("tp", "dp"), P("dp", "tp"),
        P("tp", "dp"), P("dp"), P("dp"), P("dp"), P("dp"), P(),
    )
    return jax.shard_map(
        functools.partial(per_device, n_dp, n_ctx),
        mesh=mesh, in_specs=in_specs, out_specs=out_specs, check_vma=False,
    )
```

```python
import functools
import math

import jax
import jax.numpy as jnp
from jax import lax
from jax.experimental import pallas as pl
from jax.experimental.pallas import tpu as pltpu
from jax.sharding import PartitionSpec as P

HEAD_DIM = 64
EPS = 1e-05
NEG = -1e30
MESH = pl.DeviceIdType.MESH
f32 = jnp.float32
bf16 = jnp.bfloat16
VMEM_SPEC = pl.BlockSpec(memory_space=pltpu.VMEM)
SMEM_SPEC = pl.BlockSpec(memory_space=pltpu.SMEM)
HBM_SPEC = pl.BlockSpec(memory_space=pl.ANY)
DMA = pltpu.SemaphoreType.DMA
LIMIT = 62 << 20
NT = (((1,), (1,)), ((), ()))
TN = (((0,), (0,)), ((), ()))
CH = 128
BIG = 256
LINE = 192
EARLY = 2 * LINE


def dot(a, b):
    return jnp.dot(a, b, preferred_element_type=f32)


def dot_nt(a, b):
    return lax.dot_general(a, b, NT, preferred_element_type=f32)


def dot_tn(a, b):
    return lax.dot_general(a, b, TN, preferred_element_type=f32)


def rows(start, size):
    return pl.ds(pl.multiple_of(start, size), size)


def loop(count, body):
    def step(i, carry):
        body(i)
        return carry

    lax.fori_loop(0, count, step, 0)


def kernel_call(body, outs, scratch, cid, specs, args, name, out_specs=None):
    return pl.pallas_call(
        body,
        out_shape=[jax.ShapeDtypeStruct(s, d) for s, d in outs],
        in_specs=specs,
        out_specs=out_specs or [VMEM_SPEC] * len(outs),
        scratch_shapes=scratch,
        compiler_params=pltpu.CompilerParams(
            collective_id=cid, has_side_effects=True, vmem_limit_bytes=LIMIT
        ),
        cost_estimate=pl.CostEstimate(flops=0, bytes_accessed=30 << 20, transcendentals=0),
        name=name,
    )(*args)


def greet(partners):
    barrier = pltpu.get_barrier_semaphore()
    for device in partners:
        pl.semaphore_signal(barrier, inc=1, device_id=device, device_id_type=MESH)
    pl.semaphore_wait(barrier, len(partners))


def remote(src, dst, send, recv, device):
    return pltpu.make_async_remote_copy(
        src_ref=src,
        dst_ref=dst,
        send_sem=send,
        recv_sem=recv,
        device_id=device,
        device_id_type=MESH,
    )


def fetch(pairs, sems):
    copies = [pltpu.make_async_copy(s, d, sems.at[i]) for i, (s, d) in enumerate(pairs)]
    for copy in copies:
        copy.start()
    return copies


def like(*arrays):
    return [pltpu.VMEM(a.shape, a.dtype) for a in arrays]


def axis_peers(axis, count):
    me = lax.axis_index(axis)
    return [{axis: lax.rem(me + d, count)} for d in range(1, count)]


def me_of(axis):
    return lax.axis_index(axis)


def tp_place():
    tp = lax.axis_index("tp")
    core = lax.rem(tp, 2)
    mate = {"tp": tp + 1 - 2 * core}
    across = {"tp": lax.rem(tp + 2, 4)}
    return core, mate, across


def norm_rows(x):
    mean = jnp.mean(x, -1, keepdims=True)
    centered = x - mean
    var = jnp.mean(centered * centered, -1, keepdims=True)
    inverse = lax.rsqrt(var + EPS)
    return centered * inverse, inverse


def norm_back(gradient, whitened, inverse, gain):
    e = gradient * gain
    return inverse * (
        e - jnp.mean(e, -1, keepdims=True) - whitened * jnp.mean(e * whitened, -1, keepdims=True)
    )


def lanes_below(shape, bound):
    return lax.broadcasted_iota(jnp.int32, shape, len(shape) - 1) < bound


def turn(y, tab, sign, half):
    cos, low, high = tab[:, :128], tab[:, 128:256], tab[:, 256:384]
    turned = sign * (pltpu.roll(y, 96, 1) * low + pltpu.roll(y, 32, 1) * high)
    if not half:
        return y * cos + turned
    return jnp.where(lanes_below(y.shape, 64), y * cos + turned, y)


W_PARTS = ((1, 0, 128, 256), (2, 0, 128, 384), (1, 128, 64, 512), (2, 128, 64, 576), (0, 0, 192, 0))


def front_body(
    n_ctx, n_dp, share, plen, clen, groups, conts,
    sel, px_h, cx_h, w_h, g1, b1, g2, b2, valid, wo_h, wu_h, wd_h,
    xn_o, kv_o, tab_o, w_o, wu_o, wd_o, wo_o, o, lse, msgs, gains, qpack,
    xn, q, kvs, kvc, tab, w_full, gb, gbs, cnt, cnts, notes, m_s, l_s, acc_s,
    wgs, s_x, r_x, s_kv, r_kv, s_c, r_c, s_w, r_w, osem,
    w, px, cx, wo, wu, wd, lsem,
):
    loads = fetch(
        ((w_h, w), (px_h, px), (cx_h, cx), (wo_h, wo), (wu_h, wu), (wd_h, wd)), lsem
    )
    me = lax.axis_index("ctx")
    mine = lax.axis_index("dp")
    depth = w.shape[2]
    width = px.shape[1]
    last = n_ctx - 1
    n_prompt = groups * plen
    n_cont = conts * clen
    tile = clen
    dp_peers = axis_peers("dp", n_dp)
    peers = axis_peers("ctx", n_ctx)
    for i, vector in enumerate((g1, b1, g2, b2)):
        gb[i:i + 1] = vector[...].astype(f32).reshape(1, depth)
    gb[4:8] = jnp.zeros((4, depth), f32)
    cnt[...] = jnp.zeros(cnt.shape, f32) + jnp.sum(valid[...].astype(f32))
    greet(dp_peers + peers)
    loads[0].wait()

    copies = []
    weights = []
    if share:
        cols = pl.ds(pl.multiple_of(mine * depth, 128), depth)
        here = rows(mine * depth, depth)
    for d, device in enumerate(dp_peers):
        pairs = [(gb, gbs.at[mine]), (cnt, cnts.at[mine])]
        if share:
            pairs += [
                (w.at[p, a:a + n], w_full.at[t:t + n, cols]) for p, a, n, t in W_PARTS
            ]
        else:
            pairs += [(w, wgs.at[mine])]
        copies.append(
            [remote(s, t, s_x.at[d, i], r_x.at[d, i], device) for i, (s, t) in enumerate(pairs)]
        )
    for i in range(len(copies[0])):
        for group in copies:
            group[i].start()
    local = []
    if share:
        for p, a, n, t in W_PARTS:
            w_full[t:t + n, cols] = w[p, a:a + n]
    else:
        wgs[mine] = w[...]
    for copy in loads[1:]:
        copy.wait()
    if share:
        pairs = [
            (wo.at[0:128], wo_o.at[0:128, cols]), (wo.at[128:192], wo_o.at[192:256, cols]),
            (wu, wu_o.at[here]), (wd, wd_o.at[:, cols]),
        ]
        for d, device in enumerate(dp_peers):
            for i, (s, t) in enumerate(pairs):
                weights.append(remote(s, t, s_w.at[d, i], r_w.at[d, i], device))
        for copy in weights:
            copy.start()
        local += fetch(pairs, osem)
    wo_o[128:192] = jnp.zeros((64, width), bf16)
    w_full[192:256] = jnp.zeros((64, width), bf16)
    gbs[mine] = gb[...]
    cnts[mine] = cnt[...]

    def table(count, base, start):
        def body(i):
            shape = (CH, 128)
            lane = lax.broadcasted_iota(jnp.int32, shape, 1)
            row = lax.broadcasted_iota(jnp.int32, shape, 0)
            turns = lax.rem(lane, 32).astype(f32) * (-2.0 * math.log(10000.0) / HEAD_DIM)
            angle = (row + (start + i * CH)).astype(f32) * jnp.exp(turns)
            sin = jnp.sin(angle)
            left = lax.rem(lane, 64) < 32
            at = rows(base + i * CH, CH)
            tab[at, 0:128] = jnp.cos(angle)
            tab[at, 128:256] = jnp.where(left, -sin, 0.0)
            tab[at, 256:384] = jnp.where(left, 0.0, sin)

        loop(count // CH, body)

    table(plen, 0, me * plen)
    table(clen, plen, n_ctx * plen)

    def save(src, dst, i):
        copy = pltpu.make_async_copy(src, dst, osem.at[i])
        copy.start()
        local.append(copy)

    save(tab, tab_o, 4)
    for group in copies:
        group[0].wait_recv()
        group[1].wait_recv()

    def one_hot(d):
        row = lax.broadcasted_iota(jnp.int32, (depth, width), 0) + d * depth
        col = lax.broadcasted_iota(jnp.int32, (depth, width), 1)
        return (row == col).astype(f32).astype(bf16)

    total = jnp.zeros(gains.shape, f32)
    count = jnp.zeros(cnt.shape, f32)
    for d in range(n_dp):
        total += dot(gbs[d].astype(bf16), one_hot(d))
        count += cnts[d]
    gains[...] = total
    note = notes.at[me]
    notes[me] = count
    for i in range(conts):
        notes[me, 1 + i:2 + i] = jnp.zeros((1, 128), f32) + sel[i].astype(f32)
    counts = [remote(note, note, s_c.at[d], r_c.at[d], device) for d, device in enumerate(peers)]
    for copy in counts:
        copy.start()

    def norm_part(x, base):
        def body(i):
            whitened, _ = norm_rows(x[rows(i * CH, CH)].astype(f32))
            xn[rows(base + i * CH, CH)] = (whitened * gains[0:1] + gains[1:2]).astype(bf16)

        loop(x.shape[0] // CH, body)

    norm_part(px, 0)
    norm_part(cx, n_prompt)
    save(xn, xn_o, 5)

    def arrive(i):
        if share:
            for group in copies:
                group[2 + i].wait_recv()
        elif i == 0:
            for group in copies:
                group[2].wait_recv()
            for p, a, n, t in W_PARTS:
                part = jnp.zeros((n, width), f32)
                for d in range(n_dp):
                    part += dot(wgs[d, p, a:a + n], one_hot(d))
                w_full[t:t + n] = part.astype(bf16)

    def hop(slot, g, step, side):
        there = kvs.at[slot, rows(g * plen, plen)]
        return remote(there, there, s_kv.at[side, slot, g], r_kv.at[slot, g], {"ctx": me + step})

    def kv_rows(count, base, tab_base, period, dst, first):
        def body(i):
            at = rows(first + i * BIG, BIG)
            t = tab[rows(tab_base + lax.rem(i * BIG, period), BIG)]
            x = xn[rows(base + i * BIG, BIG)]
            y = dot_nt(x, w_full[256:512])
            dst[at, 0:128] = turn(y[:, 0:128], t, 1.0, False).astype(bf16)
            dst[at, 128:256] = y[:, 128:256].astype(bf16)
            dst[at, 256:384] = turn(dot_nt(x, w_full[512:640]), t, 1.0, True).astype(bf16)

        loop(count // BIG, body)

    def q_rows_of(count, base, tab_base, period):
        def body(i):
            at = rows(base + i * BIG, BIG)
            t = tab[rows(tab_base + lax.rem(i * BIG, period), BIG)]
            y = dot_nt(xn[at], w_full[0:256])
            q[at, 0:128] = (turn(y[:, 0:128], t, 1.0, False) * 0.125).astype(bf16)
            q[at, 128:256] = (turn(y[:, 128:256], t, 1.0, True) * 0.125).astype(bf16)

        loop(count // BIG, body)

    for i in range(4):
        arrive(i)

    def send_own(g):
        kv_rows(plen, g * plen, 0, plen, kvs.at[me], g * plen)

        @pl.when(me < last)
        def _():
            hop(me, g, 1, 0).start()

        @pl.when(me > 0)
        def _():
            hop(me, g, -1, 1).start()

    loop(groups, send_own)
    save(kvs.at[me], kv_o.at[0:n_prompt], 6)
    kv_rows(n_cont, n_prompt, plen, clen, kvc, 0)
    save(kvc, kv_o.at[n_prompt:n_prompt + n_cont], 7)
    arrive(4)
    save(w_full, w_o, 8)
    q_rows_of(n_cont, n_prompt, plen, clen)
    q_rows_of(n_prompt, 0, 0, plen)

    def update(at, q_rows, k, v, mask, first):
        s = dot_nt(q_rows, k)
        if mask is not None:
            s = mask(s)
        top = jnp.max(s, -1, keepdims=True)
        if first:
            m_new = jnp.broadcast_to(top, (s.shape[0], 128))
        else:
            m_old = m_s[at]
            m_new = jnp.maximum(m_old, top)
        total = None
        parts = []
        for j in range(s.shape[1] // 128):
            p = jnp.exp(s[:, 128 * j:128 * j + 128] - m_new)
            total = p if total is None else total + p
            parts.append(p.astype(bf16))
        pv = dot(jnp.concatenate(parts, 1), v)
        m_s[at] = m_new
        if first:
            l_s[at] = total
            acc_s[at] = pv
        else:
            fade = jnp.exp(m_old - m_new)
            l_s[at] = l_s[at] * fade + total
            acc_s[at] = acc_s[at] * fade + pv

    low = lanes_below((tile, 128), 64)

    def heads(q_at, state, k_b, k_c, k_d, mask, first):
        a = q[q_at, 0:128]
        zero = jnp.zeros_like(a)
        update(state, jnp.where(low, a, zero), k_b, k_c, mask, first)
        update(state + 1, jnp.where(low, zero, a), k_b, k_c, mask, first)
        update(state + 2, q[q_at, 128:256], k_d, k_d, mask, first)

    tiles = plen // tile

    def prompt_part(slot, group, diagonal):
        def body(t):
            i = group * tiles + t
            at = rows(group * plen, plen)
            mask = None
            if diagonal:
                def mask(s):
                    row = lax.broadcasted_iota(jnp.int32, s.shape, 0) + t * tile
                    col = lax.broadcasted_iota(jnp.int32, s.shape, 1)
                    return jnp.where(col <= row, s, NEG)
            heads(
                rows(i * tile, tile), 3 * i,
                kvs[slot, at, 0:128], kvs[slot, at, 128:256], kvs[slot, at, 256:384],
                mask, diagonal,
            )

        loop(tiles, body)

    def cont_part(slot, first):
        def body(i):
            k = kvs[slot, 0:plen]
            for g in range(1, groups):
                k = jnp.where(sel[i] == g, kvs[slot, g * plen:(g + 1) * plen], k)
            heads(
                rows(n_prompt + i * tile, tile), 3 * (groups * tiles + i),
                k[:, 0:128], k[:, 128:256], k[:, 256:384], None, first,
            )

        loop(conts, body)

    def self_part():
        def body(i):
            at = rows(i * tile, tile)

            def mask(s):
                row = lax.broadcasted_iota(jnp.int32, s.shape, 0)
                col = lax.broadcasted_iota(jnp.int32, s.shape, 1)
                bias = (valid[pl.ds(i, 1)].astype(f32) - 1.0) * (-NEG)
                return jnp.where(col <= row, s + bias, NEG)

            heads(
                rows(n_prompt + i * tile, tile), 3 * (groups * tiles + i),
                kvc[at, 0:128], kvc[at, 128:256], kvc[at, 256:384], mask, False,
            )

        loop(conts, body)

    cont_part(me, True)
    loop(groups, lambda g: prompt_part(me, g, True))
    self_part()
    e0 = q[n_prompt:n_prompt + clen, 128:256].astype(f32)
    e1 = q[n_prompt + clen:n_prompt + n_cont, 128:256].astype(f32)
    qpack[0:n_cont] = q[n_prompt:n_prompt + n_cont, 0:128]
    qpack[n_cont:n_cont + clen] = jnp.where(low, e0, pltpu.roll(e1, 64, 1)).astype(bf16)

    def ring(e):
        d = e + 1

        def group(g):
            @pl.when(me - d >= 0)
            def _():
                hop(me - d, g, 1, 0).wait_recv()

                @pl.when(me < last)
                def _():
                    hop(me - d, g, 1, 0).start()

            @pl.when(me + d <= last)
            def _():
                hop(me + d, g, -1, 1).wait_recv()

                @pl.when(me > 0)
                def _():
                    hop(me + d, g, -1, 1).start()

            @pl.when(me - d >= 0)
            def _():
                prompt_part(me - d, g, False)

        loop(groups, group)

        @pl.when(me - d >= 0)
        def _():
            cont_part(me - d, False)

        @pl.when(me + d <= last)
        def _():
            cont_part(me + d, False)

    loop(last, ring)

    for copy in counts:
        copy.wait()
    for d in range(n_ctx):
        msgs[8 * d:8 * d + 8] = notes[d]

    def finish(at, state):
        l0 = jnp.sum(l_s[state], -1, keepdims=True)
        l1 = jnp.sum(l_s[state + 1], -1, keepdims=True)
        l2 = jnp.sum(l_s[state + 2], -1, keepdims=True)
        o[at, 0:128] = jnp.where(low, acc_s[state] / l0, acc_s[state + 1] / l1).astype(bf16)
        o[at, 128:256] = jnp.where(low, 0.0, acc_s[state + 2] / l2).astype(bf16)
        return (l0, l1, l2)

    def finish_prompt(i):
        finish(rows(i * tile, tile), 3 * i)

    loop(groups * tiles, finish_prompt)
    for i in range(conts):
        state = 3 * (groups * tiles + i)
        sums = finish(rows(n_prompt + i * tile, tile), state)
        lse[8 * i:8 * i + 8] = jnp.zeros((8, tile), f32)
        for h in range(3):
            value = m_s[state + h] + jnp.log(sums[h])
            lse[8 * i + h:8 * i + h + 1] = jnp.transpose(value)[0:1]

    for slot in range(n_ctx):
        for g in range(groups):
            @pl.when((slot <= me) & (me < last))
            def _():
                hop(slot, g, 1, 0).wait_send()

            @pl.when((slot >= me) & (me > 0))
            def _():
                hop(slot, g, -1, 1).wait_send()

    for group in copies:
        for copy in group:
            copy.wait_send()
    for copy in weights:
        copy.wait()
    for copy in local:
        copy.wait()


def full_at(a, core, split, c_split):
    b = a // split
    return a + core * split * (1 - b) + b * (split + core * c_split)


class TpSum:
    @staticmethod
    def scratch(half, width):
        n = half // CH
        return [
            pltpu.VMEM((half, width), bf16), pltpu.VMEM((half, width), bf16),
            pltpu.VMEM((half, width), bf16), pltpu.VMEM((half, width), bf16),
            pltpu.VMEM((half, width), f32), DMA((2, n)), DMA((2, n)),
        ]

    def __init__(self, half, start, place, scratch, compute):
        self.half, self.start, self.place, self.compute = half, start, place, compute
        self.snd1, self.rcv1, self.snd2, self.rcv2, self.own, self.send, self.recv = scratch
        self.core, self.mate, self.across = tp_place()
        self.n = half // CH

    def row(self, i):
        return lax.rem(self.start + i * CH, self.half)

    def pair(self, i):
        at = rows(self.row(i), CH)
        return remote(
            self.snd1.at[at], self.rcv1.at[at], self.send.at[0, i], self.recv.at[0, i], self.mate
        )

    def link(self, i):
        at = rows(self.row(i), CH)
        return remote(
            self.snd2.at[at], self.rcv2.at[at], self.send.at[1, i], self.recv.at[1, i], self.across
        )

    def second(self, i):
        at = rows(self.row(i), CH)
        self.pair(i).wait()
        self.snd2[at] = (self.own[at] + self.rcv1[at].astype(f32)).astype(bf16)
        self.link(i).start()

    def launch(self, i):
        a = self.row(i)
        at = rows(a, CH)
        self.snd1[at] = self.compute(self.place(a, 1 - self.core), CH).astype(bf16)
        self.pair(i).start()
        self.own[at] = self.compute(self.place(a, self.core), CH)

    def begin(self, held=0):
        def body(i):
            self.launch(i)

            @pl.when((i > 0) & (i <= self.n - held))
            def _():
                self.second(i - 1)

        loop(self.n, body)
        if not held:
            self.second(self.n - 1)

    def resume(self, held):
        for i in range(self.n - held, self.n):
            self.second(i)

    def take(self, i):
        at = rows(self.row(i), CH)
        self.link(i).wait()
        return self.snd2[at].astype(f32) + self.rcv2[at].astype(f32)

class Share:
    def __init__(self, ref, place, sems):
        self.ref, self.place = ref, place
        self.send, self.recv = sems
        _, self.mate, _ = tp_place()

    def copy(self, i, a):
        at = rows(self.place(a), CH)
        return remote(self.ref.at[at], self.ref.at[at], self.send.at[i], self.recv.at[i], self.mate)


def share_scratch(half):
    return [DMA((half // CH,)), DMA((half // CH,))]


GELU = 0.7978845608028654


def gelu_tanh(u):
    return jnp.tanh(GELU * (u + 0.044715 * (u * u * u)))


def mixed_states(ids, dwa, hist, at, y):
    mixed = dwa[4] * y
    for j in range(4):
        mixed += dwa[ids[j]] * hist[j, at].astype(f32)
    return mixed


def column(row):
    return jnp.transpose(jnp.broadcast_to(row, (128, row.shape[1])))


def down_grads(hid, dm, cols, lo, hi, store):
    for j in range(lo, hi, 128):
        store(j, dot_tn(hid[:, j:j + 128], dm[:, cols]))


def other_grads(ff, xn, du, o, da, cols, store):
    size = cols.size
    for j in range(ff // size):
        store(j * size, dot_tn(xn[:, cols], du[:, size * j:size * j + size]))
    g = dot_tn(o[...], da[:, cols])
    store(ff, g[0:128])
    store(ff + 128, g[192:256])


def middle_body(
    n_ctx, n_dp, share, n_prompt, clen, depth,
    ids, dwa, o_h, qpack, msgs, wo_h, wu_h, wd_h, cx_h, gains, valid, hist, teach, *refs,
):
    if share:
        gdn = refs[0]
        refs = refs[1:]
    out, dm, hid, xn, du, da, do, dh1, stat, qs = refs[:10]
    hc, tc, slope, h1, dy, mask, hsem, s_q, r_q, o, wo, cx, wu, wd = refs[10:24]
    scratch = refs[24:]
    core, mate, across = tp_place()
    ctx = lax.axis_index("ctx")
    dp = lax.axis_index("dp")
    half = clen
    n_cont = 2 * half
    mine = rows(core * half, half)
    loads = fetch(
        (
            (o_h.at[n_prompt:n_prompt + n_cont], o), (wo_h, wo), (cx_h.at[mine], cx),
            (wu_h, wu), (wd_h, wd), (hist.at[:, mine], hc), (teach.at[mine], tc),
        ),
        hsem,
    )
    qs[ctx] = qpack[...]
    mask[...] = column(valid[pl.ds(core, 1)].astype(f32))
    stat[...] = jnp.zeros(stat.shape, f32)
    others = axis_peers("ctx", n_ctx)
    greet([mate, across] + others + (axis_peers("dp", n_dp) if share else []))
    for copy in loads[:3]:
        copy.wait()
    s1, s2, s3 = scratch[0:7], scratch[7:14], scratch[14:21]
    shares = scratch[21:29]

    def place(a, c):
        return a + c * half

    def home(a):
        return a + core * half

    def each(body):
        loop(half // CH, body)

    def attn(at, size):
        return dot(o[rows(at, size)], wo[...])

    first = TpSum(half, 0, place, s1, attn)
    each(first.launch)
    each(first.second)
    moves = [
        remote(qs.at[ctx], qs.at[ctx], s_q.at[d], r_q.at[d], device)
        for d, device in enumerate(others)
    ]
    for copy in moves:
        copy.start()
    give_xn = Share(xn, home, shares[0:2])

    def normed(i):
        a = first.row(i)
        h = cx[rows(a, CH)].astype(f32) + first.take(i)
        h1[rows(a, CH)] = h
        whitened, _ = norm_rows(h)
        xn[rows(home(a), CH)] = (whitened * gains[2:3] + gains[3:4]).astype(bf16)
        give_xn.copy(i, a).start()

    def hidden(at, size):
        here = rows(at, size)
        u = dot(xn[here], wu[...])
        t = gelu_tanh(u)
        g = (0.5 * u * (1.0 + t)).astype(bf16)
        hid[here] = g
        slope[here] = 0.5 * (1.0 + t) + (0.5 * GELU) * u * (1.0 - t * t) * (
            1.0 + (3.0 * 0.044715) * (u * u)
        )
        return dot(g, wd[...])

    second = TpSum(half, 0, place, s2, hidden)

    def onward(before, share, after):
        def body(i):
            before(i)

            @pl.when(i > 0)
            def _():
                after.second(i - 1)

            share.copy(i, after.row(i)).wait()
            after.launch(i)

        each(body)
        after.second(after.n - 1)

    for copy in loads[3:]:
        copy.wait()
    onward(normed, give_xn, second)
    give_dm = Share(dm, home, shares[2:4])
    give_out = Share(out, home, shares[4:6])
    count = msgs[0:1]
    for j in range(1, n_ctx):
        count += msgs[8 * j:8 * j + 1]
    coef = (2.0 * dwa[4]) / (jnp.maximum(count, 1.0) * (1.0 * xn.shape[1]))

    def add(row, value):
        stat[row:row + 1] += jnp.sum(value, 0, keepdims=True)

    def lossy(i):
        a = second.row(i)
        here, there = rows(a, CH), rows(home(a), CH)
        y = h1[here] + second.take(i)
        mixed = mixed_states(ids, dwa, hc, here, y)
        diff = mixed - tc[here].astype(f32)
        weighted = diff * mask[here][:, 0:1]
        grad = weighted * coef[:, 0:1]
        dy[here] = grad
        dm[there] = grad.astype(bf16)
        give_dm.copy(i, a).start()
        out[there] = mixed.astype(bf16)
        give_out.copy(i, a).start()
        add(4, weighted * diff)
        for j in range(4):
            add(5 + j, weighted * hc[j, here].astype(f32))
        add(9, weighted * y)

    def back(at, size):
        here = rows(at, size)
        d = (dot_nt(dm[here], wd[...]) * slope[here]).astype(bf16)
        du[here] = d
        return dot_nt(d, wu[...])

    third = TpSum(half, 0, place, s3, back)
    onward(lossy, give_dm, third)
    if share:
        gsnd, grcv, gown, s_g, r_g = scratch[29:34]
        gives = []
        for d in range(1, n_dp):
            def lay(at, value, d=d):
                gsnd[d - 1, at:at + value.shape[0]] = value.astype(bf16)

            other = lax.rem(dp + d, n_dp)
            down_grads(hid, dm, pl.ds(pl.multiple_of(other * depth, 128), depth), 0, EARLY, lay)
            copy = remote(
                gsnd.at[d - 1], grcv.at[d - 1], s_g.at[d - 1], r_g.at[d - 1], {"dp": other}
            )
            copy.start()
            gives.append(copy)

        def stay(at, value):
            gown[at:at + value.shape[0]] = value

        down_grads(hid, dm, pl.ds(pl.multiple_of(dp * depth, 128), depth), 0, EARLY, stay)
    give_da = Share(da, home, shares[6:8])

    def grads(i):
        a = third.row(i)
        here = rows(a, CH)
        total = third.take(i)
        whitened, inverse = norm_rows(h1[here])
        grad = dy[here] + norm_back(total, whitened, inverse, gains[2:3])
        dh1[here] = grad
        da[rows(home(a), CH)] = grad.astype(bf16)
        give_da.copy(i, a).start()
        add(2, total * whitened)
        add(3, total)

    each(grads)
    each(lambda i: give_da.copy(i, third.row(i)).wait())

    def last(i):
        at = rows(i * BIG, BIG)
        do[at] = dot_nt(da[at], wo[...]).astype(bf16)

    loop(n_cont // BIG, last)
    each(lambda i: give_out.copy(i, second.row(i)).wait())
    for copy in moves:
        copy.wait()
    if share:
        for copy in gives:
            copy.wait()

        def settle(i):
            at = rows(i * 64, 64)
            total = gown[at]
            for d in range(n_dp - 1):
                total += grcv[d, at].astype(f32)
            gdn[at] = total.astype(bf16)

        loop(gdn.shape[0] // 64, settle)


class LineSum:
    @staticmethod
    def scratch(count, width):
        buffer = pltpu.VMEM((count, LINE, width), bf16)
        return [buffer, buffer, buffer, DMA((2, count)), DMA((2, count))]

    def __init__(self, me, src, dst, scratch):
        self.src, self.dst = src, dst
        self.got, self.pair, self.far, self.send, self.recv = scratch
        side = me // 2
        self.outer = (me == 0) | (me == 3)
        self.inner = (me == 1) | (me == 2)
        self.near = {"ctx": 1 + side}
        self.back = {"ctx": 3 * side}
        self.twin = {"ctx": 2 - side}

    def at(self, k):
        return rows(k * LINE, LINE)

    def up(self, k):
        return remote(
            self.src.at[self.at(k)], self.got.at[k], self.send.at[0, k], self.recv.at[0, k], self.near
        )

    def cross(self, k):
        return remote(
            self.pair.at[k], self.far.at[k], self.send.at[1, k], self.recv.at[1, k], self.twin
        )

    def down(self, k):
        return remote(
            self.pair.at[k], self.got.at[k], self.send.at[0, k], self.recv.at[0, k], self.back
        )

    def launch(self, k):
        @pl.when(self.outer)
        def _():
            self.up(k).start()

    def meet(self, k):
        @pl.when(self.inner)
        def _():
            self.up(k).wait_recv()
            self.pair[k] = (
                self.src[self.at(k)].astype(f32) + self.got[k].astype(f32)
            ).astype(bf16)
            self.cross(k).start()

    def turn(self, k):
        @pl.when(self.inner)
        def _():
            self.cross(k).wait()
            total = (self.pair[k].astype(f32) + self.far[k].astype(f32)).astype(bf16)
            self.pair[k] = total
            self.down(k).start()
            self.dst[self.at(k)] = total

    def land(self, k):
        @pl.when(self.outer)
        def _():
            self.up(k).wait_send()
            self.down(k).wait_recv()
            self.dst[self.at(k)] = self.got[k]

        @pl.when(self.inner)
        def _():
            self.down(k).wait_send()


def input_grad_tail(
    n_dp, n_ctx, share, split, c_split, depth,
    dcat, w, px, cx, gains, dh1, stat_in, xn1, grad_p, grad_c, fin,
    smalls, sums, shares, prompts_out, *q_state,
):
    grad, stat, stats_m, stats_y, stats_c, stats_d, s_s, r_s, osem = smalls
    core, mate, across = tp_place()
    me = lax.axis_index("ctx")
    dp = lax.axis_index("dp")
    ctx_peers = axis_peers("ctx", n_ctx)
    dp_peers = axis_peers("dp", n_dp)
    half = split + c_split
    n_prompt = 2 * split
    n_cont = 2 * c_split
    if share:
        qsnd, qrcv, s_q, r_q, gall, line, settle_kv, n_late = q_state
        n_line = gall.shape[0] // LINE - 1
    else:
        (g_q,) = q_state

    def q_grads(cols):
        part = dot_tn(dcat[n_prompt:n_prompt + n_cont, 0:256], xn1[n_prompt:n_prompt + n_cont, cols])
        return part[0:3 * HEAD_DIM]

    gives = []
    if share:
        for d in range(1, n_dp):
            other = lax.rem(dp + d, n_dp)
            cols = pl.ds(pl.multiple_of(other * depth, 128), depth)
            qsnd[d - 1] = q_grads(cols).astype(bf16)
            copy = remote(
                qsnd.at[d - 1], qrcv.at[d - 1], s_q.at[d - 1], r_q.at[d - 1], {"dp": other}
            )
            copy.start()
            gives.append(copy)

    stat[...] = 0.5 * stat_in[...]

    def place(a, c):
        return full_at(a, c, split, c_split)

    def home(a):
        return full_at(a, core, split, c_split)

    def compute(at, size):
        part = dot(dcat[rows(at, size)], w[...])
        b = at // n_prompt
        p = px[rows(at * (1 - b), size)].astype(f32)
        c = cx[rows((at - n_prompt) * b, size)].astype(f32)
        whitened, _ = norm_rows(jnp.where(b == 0, p, c))
        stat[0:1] += jnp.sum(part * whitened, 0, keepdims=True)
        stat[1:2] += jnp.sum(part, 0, keepdims=True)
        return part

    total = TpSum(half, split, place, sums, compute)
    total.begin(2)

    def small(src, dst, i, device):
        return remote(src, dst, s_s.at[i], r_s.at[i], device)

    stats_m[0] = stat[...]
    to_mate = small(stats_m.at[0], stats_m.at[1], 0, mate)
    to_mate.start()
    if share:
        settle_kv()
        loop(n_line - n_late, lambda k: line.launch(k + n_late))
    else:
        g_q[...] = q_grads(slice(None)).astype(bf16)
    to_mate.wait()
    stats_y[0] = stats_m[0] + stats_m[1]
    to_far = small(stats_y.at[0], stats_y.at[1], 1, across)
    to_far.start()
    total.resume(2)
    if share:
        for k in range(2, 5):
            line.meet(k)
        for copy in gives:
            copy.wait()
        value = q_grads(pl.ds(pl.multiple_of(dp * depth, 128), depth))
        for d in range(n_dp - 1):
            value += qrcv[d].astype(f32)
        gall[n_line * LINE:n_line * LINE + 3 * HEAD_DIM] = value.astype(bf16)
        line.launch(n_line)
    prompts_out()
    give = Share(grad, home, shares)

    def finish(i):
        a = total.row(i)
        b = a // split
        value = total.take(i)
        p = px[rows((core * split + a) * (1 - b), CH)].astype(f32)
        c = cx[rows((core * c_split + a - split) * b, CH)].astype(f32)
        whitened, inverse = norm_rows(jnp.where(b == 0, p, c))
        back = norm_back(value, whitened, inverse, gains[0:1])
        extra = dh1[rows((a - split) * b, CH)]
        grad[rows(home(a), CH)] = jnp.where(b == 0, back, back + extra).astype(bf16)
        give.copy(i, a).start()
        if share:
            k = i + i // 3
            line.turn(k)
            line.meet(5 + i)

            @pl.when(lax.rem(i, 3) == 2)
            def _():
                line.turn(k + 1)

    def part(lo, hi):
        loop(hi - lo, lambda i: finish(i + lo))

    part(0, 4)
    to_far.wait()
    stats_c[me] = stats_y[0] + stats_y[1]
    to_ctx = [
        small(stats_c.at[me], stats_c.at[me], 2 + d, device) for d, device in enumerate(ctx_peers)
    ]
    for copy in to_ctx:
        copy.start()
    part(4, 6)
    if share:
        line.meet(n_line)
        line.turn(8)
    for copy in to_ctx:
        copy.wait()
    value = stats_c[0]
    for d in range(1, n_ctx):
        value += stats_c[d]
    stats_d[dp] = value
    to_dp = [
        small(stats_d.at[dp], stats_d.at[dp], 1 + n_ctx + d, device)
        for d, device in enumerate(dp_peers)
    ]
    for copy in to_dp:
        copy.start()
    if share:
        for k in range(9, n_line + 1):
            line.turn(k)
    loop(total.n, lambda i: give.copy(i, total.row(i)).wait())
    saves = fetch(
        ((grad.at[0:n_prompt], grad_p), (grad.at[n_prompt:n_prompt + n_cont], grad_c)), osem
    )
    for copy in to_dp:
        copy.wait()
    value = stats_d[0]
    for d in range(1, n_dp):
        value += stats_d[d]
    fin[...] = value
    if share:
        loop(n_line + 1, line.land)
    for copy in saves:
        copy.wait()


def attend_back_body(
    n_ctx, n_dp, share, plen, clen, groups, conts, depth,
    ids, dwa, msgs, do_h, o_h, lse, valid, gains, kv_h, tab_h, qs_h, hid_h, dm_h, xn2_h, du_h, da_h,
    wo_h, wu_h, wd_h, px_h, hist_h, xn1_h, w_h, cx_h, dh1_h, stat_in, *refs,
):
    if share:
        g_first, out, grad_p, grad_c, fin, g_sum = refs[:6]
        refs = refs[6:]
    else:
        out, grad_p, grad_c, fin, g_down, g_up, g_out, g_kv, g_q = refs[:9]
        refs = refs[9:]
    (
        hid, dm, xn2, du, da, wo, wu, wd, px, hist, lsem,
        dos, sts, dqs, kd, acc_k, acc_v, acc_kd, acc_vd, dq_f, send, recv,
        xp, h1, xn1, flags, do, o, kv, tab, qs, w, cx, dh1, dcat,
    ) = refs[:35]
    snd1, own = refs[35:37]
    s1 = (snd1, refs[37], refs[39], refs[38], own, *refs[40:42])
    s2 = (snd1, refs[42], refs[39], refs[43], own, *refs[44:46])
    s3 = (snd1, refs[46], refs[47], refs[48], own, *refs[49:51])
    shares = refs[51:57]
    smalls = refs[57:66]
    refs = refs[66:]
    if share:
        gsnd, grcv, s_g, r_g, qsnd, qrcv, s_q, r_q, gall = refs[:9]
        line = LineSum(me_of("ctx"), gall, g_sum, refs[9:14])
    core, mate, across = tp_place()
    me = lax.axis_index("ctx")
    dp = lax.axis_index("dp")
    peers = axis_peers("ctx", n_ctx)
    dp_peers = axis_peers("dp", n_dp) if share else []
    n_prompt = groups * plen
    n_cont = conts * clen
    half = plen
    own_rows = rows(core * half, half)
    loads = fetch(
        (
            (do_h, do), (o_h, o), (wo_h, wo), (px_h, px), (kv_h, kv), (qs_h, qs),
            (hid_h, hid), (dm_h, dm), (xn2_h, xn2), (du_h, du), (da_h, da), (wu_h, wu), (wd_h, wd),
            (tab_h, tab), (xn1_h, xn1), (hist_h.at[:, own_rows], hist),
            (w_h, w), (cx_h, cx), (dh1_h, dh1),
        )
        + (((g_first, gall.at[0:EARLY]),) if share else ()),
        lsem,
    )
    low = lanes_below((clen, 128), 64)
    zero = jnp.zeros((clen, 128), bf16)
    for c in range(conts):
        flags[c * clen:(c + 1) * clen] = column(valid[c:c + 1].astype(f32))

    loads[0].wait()
    loads[1].wait()
    g0 = do[0:clen, 128:256].astype(f32)
    g1 = do[clen:2 * clen, 128:256].astype(f32)
    dos[me, 0:n_cont] = do[:, 0:128]
    dos[me, n_cont:n_cont + clen] = jnp.where(low, pltpu.roll(g0, 64, 1), g1).astype(bf16)
    for c in range(conts):
        at = slice(c * clen, (c + 1) * clen)
        full = slice(n_prompt + c * clen, n_prompt + (c + 1) * clen)
        pa = do[at, 0:128].astype(f32) * o[full, 0:128].astype(f32)
        pe = do[at, 128:256].astype(f32) * o[full, 128:256].astype(f32)
        ta = jnp.transpose(pa)
        te = jnp.transpose(pe)
        st = 8 * c
        sts[me, st:st + 8] = lse[8 * c:8 * c + 8]
        sts[me, st + 3:st + 4] = jnp.sum(ta[0:64], 0, keepdims=True)
        sts[me, st + 4:st + 5] = jnp.sum(ta[64:128], 0, keepdims=True)
        sts[me, st + 5:st + 6] = jnp.sum(te[64:128], 0, keepdims=True)
    greet(peers + [mate, across] + dp_peers)
    sends = []
    for d, device in enumerate(peers):
        for i, ref in enumerate((sts, dos)):
            sends.append(remote(ref.at[me], ref.at[me], send.at[d, i], recv.at[d, i], device))
    for copy in sends:
        copy.start()
    if share:
        loads[19].wait()
        loop(EARLY // LINE, line.launch)

    def place(a, c):
        return a + c * half

    def home(a):
        return a + core * half

    loads[2].wait()
    loads[3].wait()

    def attn(at, size):
        return dot(o[rows(at, size)], wo[...])

    first = TpSum(half, 0, place, s1, attn)
    first.begin()

    for copy in loads[4:11]:
        copy.wait()
    ff = hid.shape[1]
    o_c = o.at[n_prompt:n_prompt + n_cont]
    late = ff - EARLY
    bounds = (0, late + ff + 192, late + ff + 576)
    def cols_of(d):
        return pl.ds(pl.multiple_of(lax.rem(dp + d, n_dp) * depth, 128), depth)

    def give(d, i):
        span = slice(bounds[i], bounds[i + 1])
        return remote(
            gsnd.at[d - 1, span], grcv.at[d - 1, span], s_g.at[d - 1, i], r_g.at[d - 1, i],
            {"dp": lax.rem(dp + d, n_dp)},
        )

    def keeper(d):
        def store(at, value):
            here = slice(at, at + value.shape[0])
            if d > 0:
                gsnd[d - 1, here] = value.astype(bf16)
            else:
                for k in range(n_dp - 1):
                    value = value + grcv[k, here].astype(f32)
                gall[EARLY + at:EARLY + at + value.shape[0]] = value.astype(bf16)

        return store

    def late_grads(cols, store):
        down_grads(hid, dm, cols, EARLY, ff, lambda at, value: store(at - EARLY, value))
        other_grads(ff, xn2, du, o_c, da, cols, lambda at, value: store(at + late, value))

    def kv_grads(cols, store):
        for lo, hi in ((256, 384), (384, 512), (512, 640)):
            store(late + ff + 192 + lo - 256, dot_tn(dcat[:, lo:hi], xn1[:, cols]))

    def settle(i):
        for d in range(1, n_dp):
            give(d, i).wait()
        (late_grads, kv_grads)[i](cols_of(0), keeper(0))

    if share:
        for d in range(1, n_dp):
            late_grads(cols_of(d), keeper(d))
            give(d, 0).start()
    else:
        width = dm.shape[1]
        for j in range(width // 256):
            cols = pl.ds(256 * j, 256)
            span = slice(256 * j, 256 * j + 256)

            def lay_down(at, value, span=span):
                g_down[at:at + 128, span] = value.astype(bf16)

            def lay(at, value, span=span):
                if at < ff:
                    g_up[span, at:at + 256] = value.astype(bf16)
                else:
                    g_out[at - ff:at - ff + value.shape[0], span] = value.astype(bf16)

            down_grads(hid, dm, cols, 0, ff, lay_down)
            other_grads(ff, xn2, du, o_c, da, cols, lay)

    kd[...] = pltpu.roll(kv[0:n_prompt, 256:384].astype(f32), 64, 1).astype(bf16)
    for acc in (acc_k, acc_v, acc_kd, acc_vd):
        acc[...] = jnp.zeros(acc.shape, f32)

    def one_head(q_rows, do_rows, k, v, lse_row, delta_row, mask):
        s = dot_nt(k, q_rows)
        p = jnp.exp(s - lse_row)
        if mask is not None:
            p = mask(p)
        dp_ = dot_nt(v, do_rows)
        ds = (p * (dp_ - delta_row)).astype(bf16)
        return p.astype(bf16), ds

    def halves(a):
        return jnp.where(low, a, zero), jnp.where(low, zero, a)

    def continuation(src, c, k_b, k_c, k_d, k_s, mask):
        base = c * clen
        a0, a1 = halves(qs[src, base:base + clen])
        d0, d1 = halves(dos[src, base:base + clen])
        e = halves(qs[src, n_cont:n_cont + clen])[c]
        g = halves(dos[src, n_cont:n_cont + clen])[c]
        st = 8 * c
        row = lambda i: sts[src, st + i:st + i + 1]
        p0, s0 = one_head(a0, d0, k_b, k_c, row(0), row(3), mask)
        dv = dot(p0, d0)
        dk = dot(s0, a0)
        dq0 = dot_tn(s0, k_b)
        p1, s1_ = one_head(a1, d1, k_b, k_c, row(1), row(4), mask)
        dv += dot(p1, d1)
        dk += dot(s1_, a1)
        dq1 = dot_tn(s1_, k_b)
        keys, values = (k_d, k_s) if c == 0 else (k_s, k_d)
        p2, s2_ = one_head(e, g, keys, values, row(2), row(5), mask)
        dvd = dot(p2, g)
        dkd = dot(s2_, e)
        dq2 = dot_tn(s2_, keys)
        return dk, dv, dkd, dvd, jnp.where(low, dq0, dq1), dq2

    def source(src, own):
        pair = []
        for c in range(conts):
            pick = msgs[pl.ds(src * 8 + 1 + c, 1)]

            def choose(one, two):
                return jnp.where(pick == 0.0, one.astype(f32), two.astype(f32)).astype(bf16)

            k_b = choose(kv[0:plen, 0:128], kv[plen:2 * plen, 0:128])
            k_c = choose(kv[0:plen, 128:256], kv[plen:2 * plen, 128:256])
            k_d = choose(kv[0:plen, 256:384], kv[plen:2 * plen, 256:384])
            k_s = choose(kd[0:plen], kd[plen:2 * plen])
            dk, dv, dkd, dvd, dqa, dqd = continuation(src, c, k_b, k_c, k_d, k_s, None)
            for g in range(groups):
                keep = (pick == 1.0 * g).astype(f32)
                at = slice(g * plen, (g + 1) * plen)
                acc_k[at] += keep * dk
                acc_v[at] += keep * dv
                acc_kd[at] += keep * dkd
                acc_vd[at] += keep * dvd
            pair.append(dqd)
            if own:
                dq_f[c * clen:(c + 1) * clen] = dqa
            else:
                dqs[n_ctx + src, c * clen:(c + 1) * clen] = dqa.astype(bf16)
        third = jnp.where(low, pair[0], pair[1])
        if own:
            dq_f[n_cont:n_cont + clen] = third
        else:
            dqs[n_ctx + src, n_cont:n_cont + clen] = third.astype(bf16)

    def other_of(d):
        return lax.rem(me + 2 * n_ctx - (d + 1), n_ctx)

    def back_copy(d):
        other = other_of(d)
        return remote(
            dqs.at[n_ctx + other], dqs.at[me], send.at[d, 2], recv.at[d, 2], {"ctx": other}
        )

    def visit(d):
        other = other_of(d)
        for i, ref in enumerate((sts, dos)):
            remote(ref.at[other], ref.at[other], send.at[d, i], recv.at[d, i], {"ctx": other}).wait_recv()
        source(other, False)
        back_copy(d).start()

    give_xn = Share(xp, home, shares[0:2])

    def normed(i):
        a = first.row(i)
        h = px[rows(home(a), CH)].astype(f32) + first.take(i)
        h1[rows(a, CH)] = h
        whitened, _ = norm_rows(h)
        xp[rows(home(a), CH)] = (whitened * gains[2:3] + gains[3:4]).astype(bf16)
        give_xn.copy(i, a).start()

    def hidden(at, size):
        u = dot(xp[rows(at, size)], wu[...])
        return dot((0.5 * u * (1.0 + gelu_tanh(u))).astype(bf16), wd[...])

    second = TpSum(half, 0, place, s2, hidden)
    source(me, True)
    for copy in loads[11:13]:
        copy.wait()

    def step(i):
        @pl.when(i < first.n)
        def _():
            normed(i)
            give_xn.copy(i, first.row(i)).wait()
            second.launch(i)

        @pl.when((i > 0) & (i < n_ctx))
        def _():
            visit(i - 1)

        @pl.when(i < first.n)
        def _():
            second.second(i)

    loop(max(half // CH, n_ctx), step)
    if share:
        loop(EARLY // LINE, line.meet)
    loads[13].wait()

    for c in range(conts):
        at = slice(n_prompt + c * clen, n_prompt + (c + 1) * clen)
        k_d = kv[at, 256:384]
        k_s = pltpu.roll(k_d.astype(f32), 64, 1).astype(bf16)

        def mask(p):
            key = lax.broadcasted_iota(jnp.int32, p.shape, 0)
            query = lax.broadcasted_iota(jnp.int32, p.shape, 1)
            return jnp.where(
                key <= query, p * flags[c * clen:(c + 1) * clen, 0:1], 0.0
            )

        dk, dv, dkd, dvd, dqa, dqd = continuation(
            me, c, kv[at, 0:128], kv[at, 128:256], k_d, k_s, mask
        )
        dq_f[c * clen:(c + 1) * clen] += dqa
        keep = low if c == 0 else jnp.logical_not(low)
        dq_f[n_cont:n_cont + clen] += jnp.where(keep, dqd, 0.0)
        t = tab[plen:plen + clen]
        dcat[at, 256:384] = turn(dk, t, -1.0, False).astype(bf16)
        dcat[at, 384:512] = dv.astype(bf16)
        if c == 0:
            joined = jnp.where(low, dkd, pltpu.roll(dvd, 64, 1))
        else:
            joined = jnp.where(low, pltpu.roll(dkd, 64, 1), dvd)
        dcat[at, 512:640] = turn(joined, t, -1.0, True).astype(bf16)

    zq = jnp.zeros((plen, 256), bf16)
    wide = lanes_below((plen, 128), 64)
    for g in range(groups):
        at = slice(g * plen, (g + 1) * plen)
        t = tab[0:plen]
        dcat[at, 0:256] = zq
        dcat[at, 256:384] = turn(acc_k[at], t, -1.0, False).astype(bf16)
        dcat[at, 384:512] = acc_v[at].astype(bf16)
        k2 = acc_kd[at] + pltpu.roll(acc_kd[at], 64, 1)
        v2 = acc_vd[at] + pltpu.roll(acc_vd[at], 64, 1)
        dcat[at, 512:640] = turn(jnp.where(wide, k2, v2), t, -1.0, True).astype(bf16)

    loads[14].wait()
    if share:
        for d in range(1, n_dp):
            kv_grads(cols_of(d), keeper(d))
            give(d, 1).start()
        settle(0)
        n_late = (EARLY + bounds[1]) // LINE
        loop(n_late - EARLY // LINE, lambda k: line.launch(k + EARLY // LINE))
    else:
        for j in range(xn1.shape[1] // 256):
            span = slice(256 * j, 256 * j + 256)

            def lay_kv(at, value, span=span):
                at = at - late - ff - 192
                g_kv[at:at + 128, span] = value.astype(bf16)

            kv_grads(pl.ds(256 * j, 256), lay_kv)

    for d in range(n_ctx - 1):
        back_copy(d).wait_send()
        other = lax.rem(me + d + 1, n_ctx)
        remote(
            dqs.at[n_ctx + other], dqs.at[other], send.at[d, 2], recv.at[d, 2], {"ctx": other}
        ).wait_recv()
        dq_f[...] += dqs[other].astype(f32)
    for c in range(conts):
        at = slice(n_prompt + c * clen, n_prompt + (c + 1) * clen)
        t = tab[plen:plen + clen]
        pair = dq_f[c * clen:(c + 1) * clen] * 0.125
        dcat[at, 0:128] = turn(pair, t, -1.0, False).astype(bf16)
        third = dq_f[n_cont:n_cont + clen] * 0.125
        if c == 1:
            third = pltpu.roll(third, 64, 1)
        third = jnp.where(low, third, 0.0)
        dcat[at, 128:256] = turn(third, t, -1.0, True).astype(bf16)

    give_out = Share(out, home, shares[2:4])

    def mixed(i):
        a = second.row(i)
        here = rows(a, CH)
        y = h1[here] + second.take(i)
        out[rows(home(a), CH)] = mixed_states(ids, dwa, hist, here, y).astype(bf16)
        give_out.copy(i, a).start()

    def prompts_out():
        loads[15].wait()
        loop(half // CH, mixed)

    for copy in loads[16:19]:
        copy.wait()
    if share:
        q_state = (qsnd, qrcv, s_q, r_q, gall, line, lambda: settle(1), n_late)
    else:
        q_state = (g_q,)
    input_grad_tail(
        n_dp, n_ctx, share, plen, clen, depth,
        dcat, w, px, cx, gains, dh1, stat_in, xn1, grad_p, grad_c, fin,
        smalls, s3, shares[4:6], prompts_out, *q_state,
    )
    loop(half // CH, lambda i: give_out.copy(i, second.row(i)).wait())
    for copy in sends:
        copy.wait_send()


def output_body(
    n_ctx, n_dp, share, ff,
    ids, msgs, fin, p_out, c_out, p_grad, c_grad, *refs,
):
    n = 1 if share else 0
    parts = refs[:n]
    p_out_o, c_out_o, p_grad_o, c_grad_o, loss, dwa_g, g1, b1, g2, b2 = refs[n:n + 10]
    refs = refs[n + 10:]
    if share:
        r_qkv, r_out, r_up, r_down = refs[:4]
        refs = refs[4:]
    held, sem = refs[:4], refs[4]
    moves = (
        (p_out, p_out_o), (c_out, c_out_o), (p_grad, p_grad_o), (c_grad, c_grad_o)
    )
    reads = [
        pltpu.make_async_copy(s, h, sem.at[0, i]) for i, ((s, _), h) in enumerate(zip(moves, held))
    ]
    copies = [
        pltpu.make_async_copy(h, t, sem.at[1, i]) for i, ((_, t), h) in enumerate(zip(moves, held))
    ]
    for copy in reads:
        copy.start()
    depth = g1.shape[0]
    width = fin.shape[1]
    count = msgs[0:1, 0:1]
    for j in range(1, n_ctx):
        count += msgs[8 * j:8 * j + 1, 0:1]
    factor = 1.0 / (jnp.maximum(count, 1.0) * (1.0 * width))
    sums = jnp.sum(fin[...], -1, keepdims=True) * factor
    row = lax.broadcasted_iota(jnp.int32, sums.shape, 0)

    def entry(i):
        return jnp.sum(jnp.where(row == i, sums, 0.0))

    loss[0] = entry(4)
    for k in range(4):
        value = 0.0
        for j in range(4):
            value += jnp.where(ids[j] == k, 2.0 * entry(5 + j), 0.0)
        dwa_g[k] = value
    dwa_g[4] = 2.0 * entry(9)
    for i, ref in enumerate((g1, b1, g2, b2)):
        if share:
            ref[...] = fin[i, pl.ds(pl.multiple_of(lax.axis_index("dp") * depth, 128), depth)]
        else:
            piece = jnp.zeros((1, depth), f32)
            for d in range(n_dp):
                here = fin[i:i + 1, d * depth:(d + 1) * depth]
                piece += jnp.where(lax.axis_index("dp") == d, here, 0.0)
            ref[...] = piece.reshape(depth)
    for read, copy in zip(reads, copies):
        read.wait()
        copy.start()
    if share:
        rest = parts[0].at[ff:]
        r_down[...] = parts[0][0:ff].astype(f32)
        for j in range(ff // depth):
            r_up[:, j * depth:(j + 1) * depth] = rest[j * depth:(j + 1) * depth].astype(f32)
        r_out[...] = rest[ff:ff + 192].astype(f32)
        base = ff + 192
        r_qkv[1, 0:128] = rest[base:base + 128].astype(f32)
        r_qkv[2, 0:128] = rest[base + 128:base + 256].astype(f32)
        r_qkv[1, 128:192] = rest[base + 256:base + 320].astype(f32)
        r_qkv[2, 128:192] = rest[base + 320:base + 384].astype(f32)
        r_qkv[0] = rest[base + 384:base + 576].astype(f32)
    for copy in copies:
        copy.wait()


def per_device(
    n_dp, n_ctx,
    prompt_x, cont_x, prompt_hist, cont_hist, teacher, valid_mask, cont_group, layer_ids,
    dwa_weights, qkv_weight, out_weight, up_weight, down_weight,
    ln1_gain, ln1_bias, ln2_gain, ln2_bias,
):
    groups, plen, width = prompt_x.shape
    conts, clen, _ = cont_x.shape
    depth = qkv_weight.shape[0]
    n_prompt, n_cont = groups * plen, conts * clen
    n_rows = n_prompt + n_cont
    split, c_split = n_prompt // 2, n_cont // 2
    half = split + c_split
    ff = up_weight.shape[1]
    share = depth % 128 == 0
    packed = n_cont + clen
    tab_rows = plen + clen
    vmem = pltpu.VMEM

    w_t = qkv_weight.transpose(1, 2, 0)
    px = prompt_x.reshape(n_prompt, width)
    cx = cont_x.reshape(n_cont, width)
    vectors = (ln1_gain, ln1_bias, ln2_gain, ln2_bias)
    states = vmem((3 * (n_prompt // clen + conts), clen, 128), f32)
    xn1, kv, tab, w_full, wu, wd, wo, o, lse, msgs, gains, qpack = kernel_call(
        functools.partial(front_body, n_ctx, n_dp, share, plen, clen, groups, conts),
        [
            ((n_rows, width), bf16), ((n_rows, 384), bf16), ((tab_rows, 384), f32),
            ((640, width), bf16), ((width, ff), bf16), ((ff, width), bf16), ((256, width), bf16),
            ((n_rows, 256), bf16), ((8 * conts, clen), f32), ((8 * n_ctx, 128), f32),
            ((8, width), f32), ((packed, 128), bf16),
        ],
        [
            vmem((n_rows, width), bf16), vmem((n_rows, 256), bf16),
            vmem((n_ctx, n_prompt, 384), bf16), vmem((n_cont, 384), bf16),
            vmem((tab_rows, 384), f32), vmem((640, width), bf16),
            vmem((8, depth), f32), vmem((n_dp, 8, depth), f32),
            vmem((8, 128), f32), vmem((n_dp, 8, 128), f32), vmem((n_ctx, 8, 128), f32),
            states, states, states,
            vmem((1, 3, 192, depth) if share else (n_dp, 3, 192, depth), bf16),
            DMA((n_dp - 1, 7)), DMA((n_dp - 1, 7)),
            DMA((2, n_ctx, groups)), DMA((n_ctx, groups)), DMA((n_ctx - 1,)), DMA((n_ctx - 1,)),
            DMA((n_dp - 1, 4)), DMA((n_dp - 1, 4)), DMA((9,)),
        ]
        + like(w_t, px, cx, out_weight, up_weight, down_weight)
        + [DMA((6,))],
        0,
        [SMEM_SPEC] + [HBM_SPEC] * 3 + [VMEM_SPEC] * 5 + [HBM_SPEC] * 3,
        (cont_group, px, cx, w_t, *vectors, valid_mask, out_weight, up_weight, down_weight),
        "front",
        [HBM_SPEC] * 6 + [VMEM_SPEC] * 6,
    )
    if not share:
        out_w = lax.all_gather(out_weight, "dp", axis=1, tiled=True)
        wu = lax.all_gather(up_weight, "dp", axis=0, tiled=True)
        wd = lax.all_gather(down_weight, "dp", axis=1, tiled=True)
        wo = jnp.concatenate([out_w[:128], jnp.zeros((64, width), bf16), out_w[128:]], 0)

    outs = [((EARLY, depth), bf16)] if share else []
    extra = []
    if share:
        extra = [
            vmem((n_dp - 1, EARLY, depth), bf16), vmem((n_dp - 1, EARLY, depth), bf16),
            vmem((EARLY, depth), f32), DMA((n_dp - 1,)), DMA((n_dp - 1,)),
        ]
    got = kernel_call(
        functools.partial(middle_body, n_ctx, n_dp, share, n_prompt, clen, depth),
        outs
        + [
            ((n_cont, width), bf16), ((n_cont, width), bf16), ((n_cont, ff), bf16),
            ((n_cont, width), bf16), ((n_cont, ff), bf16), ((n_cont, width), bf16),
            ((n_cont, 256), bf16), ((c_split, width), f32), ((16, width), f32),
            ((n_ctx, packed, 128), bf16),
        ],
        [
            vmem((4, c_split, width), bf16), vmem((c_split, width), bf16),
            vmem((n_cont, ff), f32), vmem((c_split, width), f32),
            vmem((c_split, width), f32), vmem((clen, 128), f32),
            DMA((7,)), DMA((n_ctx - 1,)), DMA((n_ctx - 1,)),
            vmem((n_cont, 256), bf16), vmem((256, width), bf16), vmem((c_split, width), bf16),
            vmem((width, ff), bf16), vmem((ff, width), bf16),
        ]
        + TpSum.scratch(c_split, width) * 3
        + share_scratch(c_split) * 4
        + extra,
        1,
        [SMEM_SPEC] * 2
        + [HBM_SPEC] + [VMEM_SPEC] * 2 + [HBM_SPEC] * 4 + [VMEM_SPEC] * 2 + [HBM_SPEC] * 2,
        (
            layer_ids, dwa_weights, o, qpack, msgs, wo, wu, wd, cx, gains, valid_mask,
            cont_hist.reshape(4, n_cont, width), teacher.reshape(n_cont, width),
        ),
        "middle",
    )
    cont_out, dm, hid, xn2, du, da, do, dh1, stat, qs = got[-10:]
    g_first = list(got[:-10])

    grad_rows = 2 * ff + 12 * HEAD_DIM
    outs = [
        ((n_prompt, width), bf16), ((n_prompt, width), bf16), ((n_cont, width), bf16),
        ((16, width), f32),
    ]
    out_specs = [VMEM_SPEC] + [HBM_SPEC] * 2 + [VMEM_SPEC]
    if share:
        outs += [((grad_rows, depth), bf16)]
        out_specs += [VMEM_SPEC]
        late = grad_rows - EARLY - 3 * HEAD_DIM
        third = (n_dp - 1, 3 * HEAD_DIM, depth)
        extra = [
            vmem((n_dp - 1, late, depth), bf16), vmem((n_dp - 1, late, depth), bf16),
            DMA((n_dp - 1, 2)), DMA((n_dp - 1, 2)),
            vmem(third, bf16), vmem(third, bf16),
            DMA((n_dp - 1,)), DMA((n_dp - 1,)), vmem((grad_rows, depth), bf16),
        ] + LineSum.scratch(grad_rows // LINE, depth)
    else:
        outs += [
            ((ff, width), bf16), ((width, ff), bf16), ((3 * HEAD_DIM, width), bf16),
            ((384, width), bf16), ((3 * HEAD_DIM, width), bf16),
        ]
        out_specs += [VMEM_SPEC] * 5
        extra = []
    acc = vmem((n_prompt, 128), f32)
    wide = vmem((split, width), bf16)
    tall = vmem((half, width), bf16)
    n_p, n_h = split // CH, half // CH
    back = kernel_call(
        functools.partial(
            attend_back_body, n_ctx, n_dp, share, plen, clen, groups, conts, depth
        ),
        outs,
        [
            vmem((n_cont, ff), bf16), vmem((n_cont, width), bf16),
            vmem((n_cont, width), bf16), vmem((n_cont, ff), bf16),
            vmem((n_cont, width), bf16), vmem((256, width), bf16),
            vmem((width, ff), bf16), vmem((ff, width), bf16),
            vmem((n_prompt, width), bf16), vmem((4, split, width), bf16), DMA((20,)),
            vmem((n_ctx, packed, 128), bf16), vmem((n_ctx, 8 * conts, clen), f32),
            vmem((2 * n_ctx, packed, 128), bf16), vmem((n_prompt, 128), bf16),
            acc, acc, acc, acc, vmem((packed, 128), f32),
            DMA((n_ctx - 1, 3)), DMA((n_ctx - 1, 3)),
            vmem((n_prompt, width), bf16), vmem((split, width), f32),
            vmem((n_rows, width), bf16), vmem((n_cont, 128), f32),
        ]
        + like(do, o, kv, tab, qs, w_full, cx, dh1)
        + [
            vmem((n_rows, 640), bf16), tall, vmem((half, width), f32),
            wide, wide, wide, DMA((2, n_p)), DMA((2, n_p)),
            wide, wide, DMA((2, n_p)), DMA((2, n_p)),
            tall, tall, tall, DMA((2, n_h)), DMA((2, n_h)),
        ]
        + share_scratch(split) * 2
        + share_scratch(half)
        + [
            vmem((n_rows, width), bf16), vmem((16, width), f32), vmem((2, 16, width), f32),
            vmem((2, 16, width), f32), vmem((n_ctx, 16, width), f32),
            vmem((n_dp, 16, width), f32),
            DMA((1 + n_ctx + n_dp,)), DMA((1 + n_ctx + n_dp,)), DMA((2,)),
        ]
        + extra,
        2,
        [SMEM_SPEC] * 2
        + [VMEM_SPEC] + [HBM_SPEC] * 2 + [VMEM_SPEC] * 3 + [HBM_SPEC] * 17 + [VMEM_SPEC]
        + [HBM_SPEC] * len(g_first),
        (
            layer_ids, dwa_weights, msgs, do, o, lse, valid_mask, gains, kv, tab, qs,
            hid, dm, xn2, du, da, wo, wu, wd, px, prompt_hist.reshape(4, n_prompt, width), xn1,
            w_full, cx, dh1, stat, *g_first,
        ),
        "back",
        out_specs,
    )
    prompt_out, grad_p, grad_c, fin = back[:4]

    outs = [
        ((n_prompt, width), bf16), ((n_cont, width), bf16), ((n_prompt, width), bf16),
        ((n_cont, width), bf16), ((1,), f32), ((5,), f32),
    ] + [((depth,), f32)] * 4
    out_specs = [HBM_SPEC] * 4 + [SMEM_SPEC] * 2 + [VMEM_SPEC] * 4
    specs = [SMEM_SPEC] + [VMEM_SPEC] * 2 + [HBM_SPEC] * 4
    args = (layer_ids, msgs, fin, prompt_out, cont_out, grad_p, grad_c)
    if share:
        outs += [((3, 192, depth), f32), ((192, depth), f32), ((depth, ff), f32), ((ff, depth), f32)]
        out_specs += [VMEM_SPEC] * 4
        args += (back[4],)
        specs += [VMEM_SPEC]
    done = pl.pallas_call(
        functools.partial(output_body, n_ctx, n_dp, share, ff),
        out_shape=[jax.ShapeDtypeStruct(s, d) for s, d in outs],
        in_specs=specs,
        out_specs=out_specs,
        scratch_shapes=[
            vmem((n_prompt, width), bf16), vmem((n_cont, width), bf16),
            vmem((n_prompt, width), bf16), vmem((n_cont, width), bf16), DMA((2, 4)),
        ],
        compiler_params=pltpu.CompilerParams(vmem_limit_bytes=LIMIT),
        name="outputs",
    )(*args)
    if share:
        r_qkv, r_out, r_up, r_down = done[10:]
        r_qkv = r_qkv.transpose(2, 0, 1)
    else:
        def scattered(g, dim):
            part = lax.psum_scatter(g, "dp", scatter_dimension=dim, tiled=True)
            return lax.psum(part, "ctx").astype(f32)

        g_down, g_up, g_out, g_kv, g_q = back[4:]
        r_down = scattered(g_down, 1)
        r_up = scattered(g_up, 0)
        r_out = scattered(g_out, 1)
        g_k = jnp.concatenate([g_kv[0:128], g_kv[256:320]], 0)
        g_v = jnp.concatenate([g_kv[128:256], g_kv[320:384]], 0)
        r_qkv = scattered(jnp.stack([g_q, g_k, g_v]).transpose(2, 0, 1), 0)
    return (
        done[0].reshape(groups, plen, width),
        done[1].reshape(conts, clen, width),
        done[4].reshape(()),
        done[2].reshape(groups, plen, width),
        done[3].reshape(conts, clen, width),
        r_qkv, r_out, r_up, r_down,
        done[6], done[7], done[8], done[9],
        done[5],
    )


def solution(mesh):
    n_dp, n_ctx = mesh.shape["dp"], mesh.shape["ctx"]
    in_specs = (
        P("dp", "ctx", None), P(("dp", "ctx"), None, None), P(None, "dp", "ctx", None),
        P(None, ("dp", "ctx"), None, None), P(("dp", "ctx"), None, None), P(("dp", "ctx"), None),
        P(("dp", "ctx")), P(), P(), P("dp", None, "tp"), P("tp", "dp"), P("dp", "tp"),
        P("tp", "dp"), P("dp"), P("dp"), P("dp"), P("dp"),
    )
    out_specs = (
        P("dp", "ctx", None), P(("dp", "ctx"), None, None), P(), P("dp", "ctx", None),
        P(("dp", "ctx"), None, None), P("dp", None, "tp"), P("tp", "dp"), P("dp", "tp"),
        P("tp", "dp"), P("dp"), P("dp"), P("dp"), P("dp"), P(),
    )
    return jax.shard_map(
        functools.partial(per_device, n_dp, n_ctx),
        mesh=mesh, in_specs=in_specs, out_specs=out_specs, check_vma=False,
    )
```

```python
import functools
import math

import jax
import jax.numpy as jnp
from jax import lax
from jax.experimental import pallas as pl
from jax.experimental.pallas import tpu as pltpu
from jax.sharding import PartitionSpec as P

HEAD_DIM = 64
EPS = 1e-05
NEG = -1e30
MESH = pl.DeviceIdType.MESH
f32 = jnp.float32
bf16 = jnp.bfloat16
VMEM_SPEC = pl.BlockSpec(memory_space=pltpu.VMEM)
SMEM_SPEC = pl.BlockSpec(memory_space=pltpu.SMEM)
HBM_SPEC = pl.BlockSpec(memory_space=pl.ANY)
DMA = pltpu.SemaphoreType.DMA
LIMIT = 62 << 20
NT = (((1,), (1,)), ((), ()))
TN = (((0,), (0,)), ((), ()))
CH = 128
BIG = 256
LINE = 192
EARLY = 2 * LINE


def dot(a, b):
    return jnp.dot(a, b, preferred_element_type=f32)


def dot_nt(a, b):
    return lax.dot_general(a, b, NT, preferred_element_type=f32)


def dot_tn(a, b):
    return lax.dot_general(a, b, TN, preferred_element_type=f32)


def rows(start, size):
    return pl.ds(pl.multiple_of(start, size), size)


def loop(count, body):
    def step(i, carry):
        body(i)
        return carry

    lax.fori_loop(0, count, step, 0)


def kernel_call(body, outs, scratch, cid, specs, args, name, out_specs=None):
    return pl.pallas_call(
        body,
        out_shape=[jax.ShapeDtypeStruct(s, d) for s, d in outs],
        in_specs=specs,
        out_specs=out_specs or [VMEM_SPEC] * len(outs),
        scratch_shapes=scratch,
        compiler_params=pltpu.CompilerParams(
            collective_id=cid, has_side_effects=True, vmem_limit_bytes=LIMIT
        ),
        cost_estimate=pl.CostEstimate(flops=0, bytes_accessed=30 << 20, transcendentals=0),
        name=name,
    )(*args)


def greet(partners):
    barrier = pltpu.get_barrier_semaphore()
    for device in partners:
        pl.semaphore_signal(barrier, inc=1, device_id=device, device_id_type=MESH)
    pl.semaphore_wait(barrier, len(partners))


def remote(src, dst, send, recv, device):
    return pltpu.make_async_remote_copy(
        src_ref=src,
        dst_ref=dst,
        send_sem=send,
        recv_sem=recv,
        device_id=device,
        device_id_type=MESH,
    )


def fetch(pairs, sems):
    copies = [pltpu.make_async_copy(s, d, sems.at[i]) for i, (s, d) in enumerate(pairs)]
    for copy in copies:
        copy.start()
    return copies


def like(*arrays):
    return [pltpu.VMEM(a.shape, a.dtype) for a in arrays]


def axis_peers(axis, count):
    me = lax.axis_index(axis)
    return [{axis: lax.rem(me + d, count)} for d in range(1, count)]


def me_of(axis):
    return lax.axis_index(axis)


def tp_place():
    tp = lax.axis_index("tp")
    core = lax.rem(tp, 2)
    mate = {"tp": tp + 1 - 2 * core}
    across = {"tp": lax.rem(tp + 2, 4)}
    return core, mate, across


def norm_rows(x):
    mean = jnp.mean(x, -1, keepdims=True)
    centered = x - mean
    var = jnp.mean(centered * centered, -1, keepdims=True)
    inverse = lax.rsqrt(var + EPS)
    return centered * inverse, inverse


def norm_back(gradient, whitened, inverse, gain):
    e = gradient * gain
    return inverse * (
        e - jnp.mean(e, -1, keepdims=True) - whitened * jnp.mean(e * whitened, -1, keepdims=True)
    )


def lanes_below(shape, bound):
    return lax.broadcasted_iota(jnp.int32, shape, len(shape) - 1) < bound


def turn(y, tab, sign, half):
    cos, low, high = tab[:, :128], tab[:, 128:256], tab[:, 256:384]
    turned = sign * (pltpu.roll(y, 96, 1) * low + pltpu.roll(y, 32, 1) * high)
    if not half:
        return y * cos + turned
    return jnp.where(lanes_below(y.shape, 64), y * cos + turned, y)


W_PARTS = ((1, 0, 128, 256), (2, 0, 128, 384), (1, 128, 64, 512), (2, 128, 64, 576), (0, 0, 192, 0))


def front_body(
    n_ctx, n_dp, share, plen, clen, groups, conts,
    sel, ids, dwa, px_h, cx_h, w_h, g1, b1, g2, b2, valid, wo_h, wu_h, wd_h, hist, teach, *refs,
):
    xn_o, kv_o, tab_o, w_o, o, lse, msgs, gains = refs[:8]
    middle_outs = refs[8:18]
    refs = refs[18:]
    if share:
        gdn, wu_o, wd_o, wo_o = refs[:4]
        refs = refs[4:]
    (
        qpack, xn, q, kvs, kvc, tab, w_full, gb, gbs, cnt, cnts, notes, m_s, l_s, acc_s,
        wgs, s_x, r_x, s_kv, r_kv, s_c, r_c, s_w, r_w, osem, w, px, cx, lsem, wu_f, wd_f,
    ) = refs[:31]
    refs = refs[31:]
    if share:
        wo, wu, wd = refs[:3]
        refs = refs[3:]
        weight_pairs = ((wo_h, wo), (wu_h, wu), (wd_h, wd))
    else:
        wo_o = refs[0]
        gdn = None
        refs = refs[1:]
        weight_pairs = ((wo_h, wo_o), (wu_h, wu_f), (wd_h, wd_f))
    core, mate, across = tp_place()
    loads = fetch(((w_h, w), (px_h, px), (cx_h, cx)) + weight_pairs, lsem)
    me = lax.axis_index("ctx")
    mine = lax.axis_index("dp")
    depth = w.shape[2]
    width = px.shape[1]
    last = n_ctx - 1
    n_prompt = groups * plen
    n_cont = conts * clen
    tile = clen
    dp_peers = axis_peers("dp", n_dp)
    peers = axis_peers("ctx", n_ctx)
    for i, vector in enumerate((g1, b1, g2, b2)):
        gb[i:i + 1] = vector[...].astype(f32).reshape(1, depth)
    gb[4:8] = jnp.zeros((4, depth), f32)
    cnt[...] = jnp.zeros(cnt.shape, f32) + jnp.sum(valid[...].astype(f32))
    greet(dp_peers + peers + [mate, across])
    loads[0].wait()

    copies = []
    weights = []
    if share:
        cols = pl.ds(pl.multiple_of(mine * depth, 128), depth)
        here = rows(mine * depth, depth)
    for d, device in enumerate(dp_peers):
        pairs = [(gb, gbs.at[mine]), (cnt, cnts.at[mine])]
        if share:
            pairs += [
                (w.at[p, a:a + n], w_full.at[t:t + n, cols]) for p, a, n, t in W_PARTS
            ]
        else:
            pairs += [(w, wgs.at[mine])]
        copies.append(
            [remote(s, t, s_x.at[d, i], r_x.at[d, i], device) for i, (s, t) in enumerate(pairs)]
        )
    for i in range(len(copies[0])):
        for group in copies:
            group[i].start()
    local = []
    if share:
        for p, a, n, t in W_PARTS:
            w_full[t:t + n, cols] = w[p, a:a + n]
    else:
        wgs[mine] = w[...]
    for copy in loads[1:]:
        copy.wait()
    if share:
        pairs = [
            (wo.at[0:128], wo_o.at[0:128, cols]), (wo.at[128:192], wo_o.at[192:256, cols]),
            (wu, wu_f.at[here]), (wd, wd_f.at[:, cols]),
        ]
        for d, device in enumerate(dp_peers):
            for i, (s, t) in enumerate(pairs):
                weights.append(remote(s, t, s_w.at[d, i], r_w.at[d, i], device))
        for copy in weights:
            copy.start()
        local += fetch(pairs, osem)
    if share:
        wo_o[128:192] = jnp.zeros((64, width), bf16)
    w_full[192:256] = jnp.zeros((64, width), bf16)
    gbs[mine] = gb[...]
    cnts[mine] = cnt[...]

    def table(count, base, start):
        def body(i):
            shape = (CH, 128)
            lane = lax.broadcasted_iota(jnp.int32, shape, 1)
            row = lax.broadcasted_iota(jnp.int32, shape, 0)
            turns = lax.rem(lane, 32).astype(f32) * (-2.0 * math.log(10000.0) / HEAD_DIM)
            angle = (row + (start + i * CH)).astype(f32) * jnp.exp(turns)
            sin = jnp.sin(angle)
            left = lax.rem(lane, 64) < 32
            at = rows(base + i * CH, CH)
            tab[at, 0:128] = jnp.cos(angle)
            tab[at, 128:256] = jnp.where(left, -sin, 0.0)
            tab[at, 256:384] = jnp.where(left, 0.0, sin)

        loop(count // CH, body)

    table(plen, 0, me * plen)
    table(clen, plen, n_ctx * plen)

    def save(src, dst, i):
        copy = pltpu.make_async_copy(src, dst, osem.at[i])
        copy.start()
        local.append(copy)

    save(tab, tab_o, 4)
    for group in copies:
        group[0].wait_recv()
        group[1].wait_recv()

    def one_hot(d):
        row = lax.broadcasted_iota(jnp.int32, (depth, width), 0) + d * depth
        col = lax.broadcasted_iota(jnp.int32, (depth, width), 1)
        return (row == col).astype(f32).astype(bf16)

    total = jnp.zeros(gains.shape, f32)
    count = jnp.zeros(cnt.shape, f32)
    for d in range(n_dp):
        total += dot(gbs[d].astype(bf16), one_hot(d))
        count += cnts[d]
    gains[...] = total
    note = notes.at[me]
    notes[me] = count
    for i in range(conts):
        notes[me, 1 + i:2 + i] = jnp.zeros((1, 128), f32) + sel[i].astype(f32)
    counts = [remote(note, note, s_c.at[d], r_c.at[d], device) for d, device in enumerate(peers)]
    for copy in counts:
        copy.start()

    def norm_part(x, base):
        def body(i):
            whitened, _ = norm_rows(x[rows(i * CH, CH)].astype(f32))
            xn[rows(base + i * CH, CH)] = (whitened * gains[0:1] + gains[1:2]).astype(bf16)

        loop(x.shape[0] // CH, body)

    norm_part(px, 0)
    norm_part(cx, n_prompt)
    save(xn, xn_o, 5)

    def arrive(i):
        if share:
            for group in copies:
                group[2 + i].wait_recv()
        elif i == 0:
            for group in copies:
                group[2].wait_recv()
            for p, a, n, t in W_PARTS:
                part = jnp.zeros((n, width), f32)
                for d in range(n_dp):
                    part += dot(wgs[d, p, a:a + n], one_hot(d))
                w_full[t:t + n] = part.astype(bf16)

    def hop(slot, g, step, side):
        there = kvs.at[slot, rows(g * plen, plen)]
        return remote(there, there, s_kv.at[side, slot, g], r_kv.at[slot, g], {"ctx": me + step})

    def kv_rows(count, base, tab_base, period, dst, first):
        def body(i):
            at = rows(first + i * BIG, BIG)
            t = tab[rows(tab_base + lax.rem(i * BIG, period), BIG)]
            x = xn[rows(base + i * BIG, BIG)]
            y = dot_nt(x, w_full[256:512])
            dst[at, 0:128] = turn(y[:, 0:128], t, 1.0, False).astype(bf16)
            dst[at, 128:256] = y[:, 128:256].astype(bf16)
            dst[at, 256:384] = turn(dot_nt(x, w_full[512:640]), t, 1.0, True).astype(bf16)

        loop(count // BIG, body)

    def q_rows_of(count, base, tab_base, period):
        def body(i):
            at = rows(base + i * BIG, BIG)
            t = tab[rows(tab_base + lax.rem(i * BIG, period), BIG)]
            y = dot_nt(xn[at], w_full[0:256])
            q[at, 0:128] = (turn(y[:, 0:128], t, 1.0, False) * 0.125).astype(bf16)
            q[at, 128:256] = (turn(y[:, 128:256], t, 1.0, True) * 0.125).astype(bf16)

        loop(count // BIG, body)

    for i in range(4):
        arrive(i)

    def send_own(g):
        kv_rows(plen, g * plen, 0, plen, kvs.at[me], g * plen)

        @pl.when(me < last)
        def _():
            hop(me, g, 1, 0).start()

        @pl.when(me > 0)
        def _():
            hop(me, g, -1, 1).start()

    loop(groups, send_own)
    save(kvs.at[me], kv_o.at[0:n_prompt], 6)
    kv_rows(n_cont, n_prompt, plen, clen, kvc, 0)
    save(kvc, kv_o.at[n_prompt:n_prompt + n_cont], 7)
    arrive(4)
    save(w_full, w_o, 8)
    q_rows_of(n_cont, n_prompt, plen, clen)
    q_rows_of(n_prompt, 0, 0, plen)

    def update(at, q_rows, k, v, mask, first):
        s = dot_nt(q_rows, k)
        if mask is not None:
            s = mask(s)
        top = jnp.max(s, -1, keepdims=True)
        if first:
            m_new = jnp.broadcast_to(top, (s.shape[0], 128))
        else:
            m_old = m_s[at]
            m_new = jnp.maximum(m_old, top)
        total = None
        parts = []
        for j in range(s.shape[1] // 128):
            p = jnp.exp(s[:, 128 * j:128 * j + 128] - m_new)
            total = p if total is None else total + p
            parts.append(p.astype(bf16))
        pv = dot(jnp.concatenate(parts, 1), v)
        m_s[at] = m_new
        if first:
            l_s[at] = total
            acc_s[at] = pv
        else:
            fade = jnp.exp(m_old - m_new)
            l_s[at] = l_s[at] * fade + total
            acc_s[at] = acc_s[at] * fade + pv

    low = lanes_below((tile, 128), 64)

    def heads(q_at, state, k_b, k_c, k_d, mask, first):
        a = q[q_at, 0:128]
        zero = jnp.zeros_like(a)
        update(state, jnp.where(low, a, zero), k_b, k_c, mask, first)
        update(state + 1, jnp.where(low, zero, a), k_b, k_c, mask, first)
        update(state + 2, q[q_at, 128:256], k_d, k_d, mask, first)

    tiles = plen // tile

    def prompt_part(slot, group, diagonal):
        def body(t):
            i = group * tiles + t
            at = rows(group * plen, plen)
            mask = None
            if diagonal:
                def mask(s):
                    row = lax.broadcasted_iota(jnp.int32, s.shape, 0) + t * tile
                    col = lax.broadcasted_iota(jnp.int32, s.shape, 1)
                    return jnp.where(col <= row, s, NEG)
            heads(
                rows(i * tile, tile), 3 * i,
                kvs[slot, at, 0:128], kvs[slot, at, 128:256], kvs[slot, at, 256:384],
                mask, diagonal,
            )

        loop(tiles, body)

    def cont_part(slot, first):
        def body(i):
            k = kvs[slot, 0:plen]
            for g in range(1, groups):
                k = jnp.where(sel[i] == g, kvs[slot, g * plen:(g + 1) * plen], k)
            heads(
                rows(n_prompt + i * tile, tile), 3 * (groups * tiles + i),
                k[:, 0:128], k[:, 128:256], k[:, 256:384], None, first,
            )

        loop(conts, body)

    def self_part():
        def body(i):
            at = rows(i * tile, tile)

            def mask(s):
                row = lax.broadcasted_iota(jnp.int32, s.shape, 0)
                col = lax.broadcasted_iota(jnp.int32, s.shape, 1)
                bias = (valid[pl.ds(i, 1)].astype(f32) - 1.0) * (-NEG)
                return jnp.where(col <= row, s + bias, NEG)

            heads(
                rows(n_prompt + i * tile, tile), 3 * (groups * tiles + i),
                kvc[at, 0:128], kvc[at, 128:256], kvc[at, 256:384], mask, False,
            )

        loop(conts, body)

    cont_part(me, True)
    loop(groups, lambda g: prompt_part(me, g, True))
    self_part()
    e0 = q[n_prompt:n_prompt + clen, 128:256].astype(f32)
    e1 = q[n_prompt + clen:n_prompt + n_cont, 128:256].astype(f32)
    qpack[0:n_cont] = q[n_prompt:n_prompt + n_cont, 0:128]
    qpack[n_cont:n_cont + clen] = jnp.where(low, e0, pltpu.roll(e1, 64, 1)).astype(bf16)

    def ring(e):
        d = e + 1

        def group(g):
            @pl.when(me - d >= 0)
            def _():
                hop(me - d, g, 1, 0).wait_recv()

                @pl.when(me < last)
                def _():
                    hop(me - d, g, 1, 0).start()

            @pl.when(me + d <= last)
            def _():
                hop(me + d, g, -1, 1).wait_recv()

                @pl.when(me > 0)
                def _():
                    hop(me + d, g, -1, 1).start()

            @pl.when((me - d > 0) | ((me == d) & (g < groups - 1)))
            def _():
                prompt_part(me - d, g, False)

        loop(groups, group)

        @pl.when(me - d >= 0)
        def _():
            cont_part(me - d, False)

        @pl.when(me + d <= last)
        def _():
            cont_part(me + d, False)

    loop(last, ring)

    for copy in counts:
        copy.wait()
    for d in range(n_ctx):
        msgs[8 * d:8 * d + 8] = notes[d]

    def finish(at, state):
        l0 = jnp.sum(l_s[state], -1, keepdims=True)
        l1 = jnp.sum(l_s[state + 1], -1, keepdims=True)
        l2 = jnp.sum(l_s[state + 2], -1, keepdims=True)
        o[at, 0:128] = jnp.where(low, acc_s[state] / l0, acc_s[state + 1] / l1).astype(bf16)
        o[at, 128:256] = jnp.where(low, 0.0, acc_s[state + 2] / l2).astype(bf16)
        return (l0, l1, l2)

    def rest_of_prompts():
        @pl.when(me > 0)
        def _():
            prompt_part(0, groups - 1, False)

        loop(groups * tiles, lambda i: finish(rows(i * tile, tile), 3 * i))

    for i in range(conts):
        state = 3 * (groups * tiles + i)
        sums = finish(rows(n_prompt + i * tile, tile), state)
        lse[8 * i:8 * i + 8] = jnp.zeros((8, tile), f32)
        for h in range(3):
            value = m_s[state + h] + jnp.log(sums[h])
            lse[8 * i + h:8 * i + h + 1] = jnp.transpose(value)[0:1]

    for copy in weights:
        copy.wait()
    for copy in local:
        copy.wait()
    if share:
        local = fetch(((wu_f, wu_o), (wd_f, wd_o)), osem)
    else:
        local = []
    middle_part(
        n_ctx, n_dp, share, n_prompt, clen, depth, rest_of_prompts,
        ids, dwa, o, qpack, msgs, wo_o, wu_f, wd_f, cx, gains, valid, hist, teach,
        gdn, middle_outs, refs,
    )
    for slot in range(n_ctx):
        for g in range(groups):
            @pl.when((slot <= me) & (me < last))
            def _():
                hop(slot, g, 1, 0).wait_send()

            @pl.when((slot >= me) & (me > 0))
            def _():
                hop(slot, g, -1, 1).wait_send()

    for group in copies:
        for copy in group:
            copy.wait_send()
    for copy in local:
        copy.wait()


def full_at(a, core, split, c_split):
    b = a // split
    return a + core * split * (1 - b) + b * (split + core * c_split)


class TpSum:
    @staticmethod
    def scratch(half, width):
        n = half // CH
        return [
            pltpu.VMEM((half, width), bf16), pltpu.VMEM((half, width), bf16),
            pltpu.VMEM((half, width), bf16), pltpu.VMEM((half, width), bf16),
            pltpu.VMEM((half, width), f32), DMA((2, n)), DMA((2, n)),
        ]

    def __init__(self, half, start, place, scratch, compute):
        self.half, self.start, self.place, self.compute = half, start, place, compute
        self.snd1, self.rcv1, self.snd2, self.rcv2, self.own, self.send, self.recv = scratch
        self.core, self.mate, self.across = tp_place()
        self.n = half // CH

    def row(self, i):
        return lax.rem(self.start + i * CH, self.half)

    def pair(self, i):
        at = rows(self.row(i), CH)
        return remote(
            self.snd1.at[at], self.rcv1.at[at], self.send.at[0, i], self.recv.at[0, i], self.mate
        )

    def link(self, i):
        at = rows(self.row(i), CH)
        return remote(
            self.snd2.at[at], self.rcv2.at[at], self.send.at[1, i], self.recv.at[1, i], self.across
        )

    def second(self, i):
        at = rows(self.row(i), CH)
        self.pair(i).wait()
        self.snd2[at] = (self.own[at] + self.rcv1[at].astype(f32)).astype(bf16)
        self.link(i).start()

    def launch(self, i):
        a = self.row(i)
        at = rows(a, CH)
        self.snd1[at] = self.compute(self.place(a, 1 - self.core), CH).astype(bf16)
        self.pair(i).start()
        self.own[at] = self.compute(self.place(a, self.core), CH)

    def begin(self, held=0, after=None):
        def body(i):
            self.launch(i)

            @pl.when((i > 0) & (i <= self.n - held))
            def _():
                self.second(i - 1)

            if after is not None:
                after(i)

        loop(self.n, body)
        if not held:
            self.second(self.n - 1)

    def resume(self, held):
        for i in range(self.n - held, self.n):
            self.second(i)

    def take(self, i):
        at = rows(self.row(i), CH)
        self.link(i).wait()
        return self.snd2[at].astype(f32) + self.rcv2[at].astype(f32)

class Share:
    def __init__(self, ref, place, sems):
        self.ref, self.place = ref, place
        self.send, self.recv = sems
        _, self.mate, _ = tp_place()

    def copy(self, i, a):
        at = rows(self.place(a), CH)
        return remote(self.ref.at[at], self.ref.at[at], self.send.at[i], self.recv.at[i], self.mate)


def share_scratch(half):
    return [DMA((half // CH,)), DMA((half // CH,))]


GELU = 0.7978845608028654


def gelu_tanh(u):
    return jnp.tanh(GELU * (u + 0.044715 * (u * u * u)))


def mixed_states(ids, dwa, hist, at, y):
    mixed = dwa[4] * y
    for j in range(4):
        mixed += dwa[ids[j]] * hist[j, at].astype(f32)
    return mixed


def column(row):
    return jnp.transpose(jnp.broadcast_to(row, (128, row.shape[1])))


def down_grads(hid, dm, cols, lo, hi, store):
    for j in range(lo, hi, 128):
        store(j, dot_tn(hid[:, j:j + 128], dm[:, cols]))


def other_grads(ff, xn, du, o, da, cols, store):
    size = cols.size
    for j in range(ff // size):
        store(j * size, dot_tn(xn[:, cols], du[:, size * j:size * j + size]))
    g = dot_tn(o[...], da[:, cols])
    store(ff, g[0:128])
    store(ff + 128, g[192:256])


def middle_part(
    n_ctx, n_dp, share, n_prompt, clen, depth, between,
    ids, dwa, o, qpack, msgs, wo, wu, wd, cx, gains, valid, hist, teach, gdn, outs, refs,
):
    out, dm, hid, xn, du, da, do, dh1, stat, qs = outs
    hc, tc, slope, h1, dy, mask, hsem, s_q, r_q = refs[:9]
    scratch = refs[9:]
    core, mate, across = tp_place()
    ctx = lax.axis_index("ctx")
    dp = lax.axis_index("dp")
    half = clen
    n_cont = 2 * half
    mine = rows(core * half, half)
    loads = fetch(((hist.at[:, mine], hc), (teach.at[mine], tc)), hsem)
    qs[ctx] = qpack[...]
    mask[...] = column(valid[pl.ds(core, 1)].astype(f32))
    stat[...] = jnp.zeros(stat.shape, f32)
    others = axis_peers("ctx", n_ctx)
    s1, s2, s3 = scratch[0:7], scratch[7:14], scratch[14:21]
    shares = scratch[21:29]

    def place(a, c):
        return a + c * half

    def home(a):
        return a + core * half

    def each(body):
        loop(half // CH, body)

    def attn(at, size):
        return dot(o[rows(n_prompt + at, size)], wo[...])

    first = TpSum(half, 0, place, s1, attn)
    each(first.launch)
    each(first.second)
    moves = [
        remote(qs.at[ctx], qs.at[ctx], s_q.at[d], r_q.at[d], device)
        for d, device in enumerate(others)
    ]
    between()
    give_xn = Share(xn, home, shares[0:2])

    def normed(i):
        a = first.row(i)
        h = cx[rows(home(a), CH)].astype(f32) + first.take(i)
        h1[rows(a, CH)] = h
        whitened, _ = norm_rows(h)
        xn[rows(home(a), CH)] = (whitened * gains[2:3] + gains[3:4]).astype(bf16)
        give_xn.copy(i, a).start()

    def hidden(at, size):
        here = rows(at, size)
        u = dot(xn[here], wu[...])
        t = gelu_tanh(u)
        g = (0.5 * u * (1.0 + t)).astype(bf16)
        hid[here] = g
        slope[here] = 0.5 * (1.0 + t) + (0.5 * GELU) * u * (1.0 - t * t) * (
            1.0 + (3.0 * 0.044715) * (u * u)
        )
        return dot(g, wd[...])

    second = TpSum(half, 0, place, s2, hidden)

    def onward(before, share, after):
        def body(i):
            before(i)

            @pl.when(i > 0)
            def _():
                after.second(i - 1)

            share.copy(i, after.row(i)).wait()
            after.launch(i)

        each(body)
        after.second(after.n - 1)

    for copy in loads:
        copy.wait()
    onward(normed, give_xn, second)
    for copy in moves:
        copy.start()
    give_dm = Share(dm, home, shares[2:4])
    give_out = Share(out, home, shares[4:6])
    count = msgs[0:1]
    for j in range(1, n_ctx):
        count += msgs[8 * j:8 * j + 1]
    coef = (2.0 * dwa[4]) / (jnp.maximum(count, 1.0) * (1.0 * xn.shape[1]))

    def add(row, value):
        stat[row:row + 1] += jnp.sum(value, 0, keepdims=True)

    def lossy(i):
        a = second.row(i)
        here, there = rows(a, CH), rows(home(a), CH)
        y = h1[here] + second.take(i)
        mixed = mixed_states(ids, dwa, hc, here, y)
        diff = mixed - tc[here].astype(f32)
        weighted = diff * mask[here][:, 0:1]
        grad = weighted * coef[:, 0:1]
        dy[here] = grad
        dm[there] = grad.astype(bf16)
        give_dm.copy(i, a).start()
        out[there] = mixed.astype(bf16)
        give_out.copy(i, a).start()
        add(4, weighted * diff)
        for j in range(4):
            add(5 + j, weighted * hc[j, here].astype(f32))
        add(9, weighted * y)

    def back(at, size):
        here = rows(at, size)
        d = (dot_nt(dm[here], wd[...]) * slope[here]).astype(bf16)
        du[here] = d
        return dot_nt(d, wu[...])

    third = TpSum(half, 0, place, s3, back)
    onward(lossy, give_dm, third)
    if share:
        gsnd, grcv, gown, s_g, r_g = scratch[29:34]
        gives = []
        for d in range(1, n_dp):
            def lay(at, value, d=d):
                gsnd[d - 1, at:at + value.shape[0]] = value.astype(bf16)

            other = lax.rem(dp + d, n_dp)
            down_grads(hid, dm, pl.ds(pl.multiple_of(other * depth, 128), depth), 0, EARLY, lay)
            copy = remote(
                gsnd.at[d - 1], grcv.at[d - 1], s_g.at[d - 1], r_g.at[d - 1], {"dp": other}
            )
            copy.start()
            gives.append(copy)

        def stay(at, value):
            gown[at:at + value.shape[0]] = value

        down_grads(hid, dm, pl.ds(pl.multiple_of(dp * depth, 128), depth), 0, EARLY, stay)
    give_da = Share(da, home, shares[6:8])

    def grads(i):
        a = third.row(i)
        here = rows(a, CH)
        total = third.take(i)
        whitened, inverse = norm_rows(h1[here])
        grad = dy[here] + norm_back(total, whitened, inverse, gains[2:3])
        dh1[here] = grad
        da[rows(home(a), CH)] = grad.astype(bf16)
        give_da.copy(i, a).start()
        add(2, total * whitened)
        add(3, total)

    each(grads)
    each(lambda i: give_da.copy(i, third.row(i)).wait())

    def last(i):
        at = rows(i * BIG, BIG)
        do[at] = dot_nt(da[at], wo[...]).astype(bf16)

    loop(n_cont // BIG, last)
    each(lambda i: give_out.copy(i, second.row(i)).wait())
    for copy in moves:
        copy.wait()
    if share:
        for copy in gives:
            copy.wait()

        def settle(i):
            at = rows(i * 64, 64)
            total = gown[at]
            for d in range(n_dp - 1):
                total += grcv[d, at].astype(f32)
            gdn[at] = total.astype(bf16)

        loop(gdn.shape[0] // 64, settle)


class LineSum:
    @staticmethod
    def scratch(count, width):
        buffer = pltpu.VMEM((count, LINE, width), bf16)
        return [buffer, buffer, buffer, DMA((2, count)), DMA((2, count))]

    def __init__(self, me, src, dst, scratch):
        self.src, self.dst = src, dst
        self.got, self.pair, self.far, self.send, self.recv = scratch
        side = me // 2
        self.outer = (me == 0) | (me == 3)
        self.inner = (me == 1) | (me == 2)
        self.near = {"ctx": 1 + side}
        self.back = {"ctx": 3 * side}
        self.twin = {"ctx": 2 - side}

    def at(self, k):
        return rows(k * LINE, LINE)

    def up(self, k):
        return remote(
            self.src.at[self.at(k)], self.got.at[k], self.send.at[0, k], self.recv.at[0, k], self.near
        )

    def cross(self, k):
        return remote(
            self.pair.at[k], self.far.at[k], self.send.at[1, k], self.recv.at[1, k], self.twin
        )

    def down(self, k):
        return remote(
            self.pair.at[k], self.got.at[k], self.send.at[0, k], self.recv.at[0, k], self.back
        )

    def launch(self, k):
        @pl.when(self.outer)
        def _():
            self.up(k).start()

    def meet(self, k):
        @pl.when(self.inner)
        def _():
            self.up(k).wait_recv()
            self.pair[k] = (
                self.src[self.at(k)].astype(f32) + self.got[k].astype(f32)
            ).astype(bf16)
            self.cross(k).start()

    def turn(self, k):
        @pl.when(self.inner)
        def _():
            self.cross(k).wait()
            total = (self.pair[k].astype(f32) + self.far[k].astype(f32)).astype(bf16)
            self.pair[k] = total
            self.down(k).start()
            self.dst[self.at(k)] = total

    def land(self, k):
        @pl.when(self.outer)
        def _():
            self.up(k).wait_send()
            self.down(k).wait_recv()
            self.dst[self.at(k)] = self.got[k]

        @pl.when(self.inner)
        def _():
            self.down(k).wait_send()


def input_grad_tail(
    n_dp, n_ctx, share, split, c_split, depth,
    dcat, w, px, cx, gains, dh1, stat_in, xn1, grad_p, grad_c, fin,
    smalls, sums, shares, prompts_out, *q_state,
):
    grad, stat, stats_m, stats_y, stats_c, stats_d, s_s, r_s, osem = smalls
    core, mate, across = tp_place()
    me = lax.axis_index("ctx")
    dp = lax.axis_index("dp")
    ctx_peers = axis_peers("ctx", n_ctx)
    dp_peers = axis_peers("dp", n_dp)
    half = split + c_split
    n_prompt = 2 * split
    n_cont = 2 * c_split
    if share:
        qsnd, qrcv, s_q, r_q, gall, line, settle_kv, n_late = q_state
        n_line = gall.shape[0] // LINE - 1
    else:
        (g_q,) = q_state

    def q_grads(cols):
        part = dot_tn(dcat[n_prompt:n_prompt + n_cont, 0:256], xn1[n_prompt:n_prompt + n_cont, cols])
        return part[0:3 * HEAD_DIM]

    gives = []
    if share:
        for d in range(1, n_dp):
            other = lax.rem(dp + d, n_dp)
            cols = pl.ds(pl.multiple_of(other * depth, 128), depth)
            qsnd[d - 1] = q_grads(cols).astype(bf16)
            copy = remote(
                qsnd.at[d - 1], qrcv.at[d - 1], s_q.at[d - 1], r_q.at[d - 1], {"dp": other}
            )
            copy.start()
            gives.append(copy)

    stat[...] = 0.5 * stat_in[...]

    def place(a, c):
        return full_at(a, c, split, c_split)

    def home(a):
        return full_at(a, core, split, c_split)

    def compute(at, size):
        part = dot(dcat[rows(at, size)], w[...])
        b = at // n_prompt
        p = px[rows(at * (1 - b), size)].astype(f32)
        c = cx[rows((at - n_prompt) * b, size)].astype(f32)
        whitened, _ = norm_rows(jnp.where(b == 0, p, c))
        stat[0:1] += jnp.sum(part * whitened, 0, keepdims=True)
        stat[1:2] += jnp.sum(part, 0, keepdims=True)
        return part

    total = TpSum(half, split, place, sums, compute)

    def also(i):
        if share:
            @pl.when(lax.rem(i, 2) == 0)
            def _():
                line.meet(2 + i // 2)

    total.begin(2, also)

    def small(src, dst, i, device):
        return remote(src, dst, s_s.at[i], r_s.at[i], device)

    stats_m[0] = stat[...]
    to_mate = small(stats_m.at[0], stats_m.at[1], 0, mate)
    to_mate.start()
    if share:
        settle_kv()
        loop(n_line - n_late, lambda k: line.launch(k + n_late))
    else:
        g_q[...] = q_grads(slice(None)).astype(bf16)
    to_mate.wait()
    stats_y[0] = stats_m[0] + stats_m[1]
    to_far = small(stats_y.at[0], stats_y.at[1], 1, across)
    to_far.start()
    total.resume(2)
    if share:
        line.meet(5)
        for copy in gives:
            copy.wait()
        value = q_grads(pl.ds(pl.multiple_of(dp * depth, 128), depth))
        for d in range(n_dp - 1):
            value += qrcv[d].astype(f32)
        gall[n_line * LINE:n_line * LINE + 3 * HEAD_DIM] = value.astype(bf16)
        line.launch(n_line)
    prompts_out()
    if share:
        line.turn(0)
        line.meet(6)
    give = Share(grad, home, shares)

    def finish(i):
        a = total.row(i)
        b = a // split
        value = total.take(i)
        p = px[rows((core * split + a) * (1 - b), CH)].astype(f32)
        c = cx[rows((core * c_split + a - split) * b, CH)].astype(f32)
        whitened, inverse = norm_rows(jnp.where(b == 0, p, c))
        back = norm_back(value, whitened, inverse, gains[0:1])
        extra = dh1[rows((a - split) * b, CH)]
        grad[rows(home(a), CH)] = jnp.where(b == 0, back, back + extra).astype(bf16)
        give.copy(i, a).start()
        if share:
            k = 1 + i + i // 3
            line.turn(k)

            @pl.when(i < 5)
            def _():
                line.meet(7 + i)

            @pl.when(lax.rem(i, 3) == 2)
            def _():
                line.turn(k + 1)

    def part(lo, hi):
        loop(hi - lo, lambda i: finish(i + lo))

    part(0, 4)
    to_far.wait()
    stats_c[me] = stats_y[0] + stats_y[1]
    to_ctx = [
        small(stats_c.at[me], stats_c.at[me], 2 + d, device) for d, device in enumerate(ctx_peers)
    ]
    for copy in to_ctx:
        copy.start()
    part(4, 6)
    if share:
        line.turn(9)
    for copy in to_ctx:
        copy.wait()
    value = stats_c[0]
    for d in range(1, n_ctx):
        value += stats_c[d]
    stats_d[dp] = value
    to_dp = [
        small(stats_d.at[dp], stats_d.at[dp], 1 + n_ctx + d, device)
        for d, device in enumerate(dp_peers)
    ]
    for copy in to_dp:
        copy.start()
    if share:
        for k in range(10, n_line + 1):
            line.turn(k)
    loop(total.n, lambda i: give.copy(i, total.row(i)).wait())
    saves = fetch(
        ((grad.at[0:n_prompt], grad_p), (grad.at[n_prompt:n_prompt + n_cont], grad_c)), osem
    )
    for copy in to_dp:
        copy.wait()
    value = stats_d[0]
    for d in range(1, n_dp):
        value += stats_d[d]
    fin[...] = value
    if share:
        loop(n_line + 1, line.land)
    for copy in saves:
        copy.wait()


def attend_back_body(
    n_ctx, n_dp, share, plen, clen, groups, conts, depth,
    ids, dwa, msgs, do_h, o_h, lse, valid, gains, kv_h, tab_h, qs_h, hid_h, dm_h, xn2_h, du_h, da_h,
    wo_h, wu_h, wd_h, px_h, hist_h, xn1_h, w_h, cx_h, dh1_h, stat_in, *refs,
):
    if share:
        g_first, out, grad_p, grad_c, fin, g_sum = refs[:6]
        refs = refs[6:]
    else:
        out, grad_p, grad_c, fin, g_down, g_up, g_out, g_kv, g_q = refs[:9]
        refs = refs[9:]
    (
        hid, dm, xn2, du, da, wo, wu, wd, px, hist, lsem,
        dos, sts, dqs, kd, acc_k, acc_v, acc_kd, acc_vd, dq_f, send, recv,
        xp, h1, xn1, flags, do, o, kv, tab, qs, w, cx, dh1, dcat,
    ) = refs[:35]
    snd1, own = refs[35:37]
    s1 = (snd1, refs[37], refs[39], refs[38], own, *refs[40:42])
    s2 = (snd1, refs[42], refs[39], refs[43], own, *refs[44:46])
    s3 = (snd1, refs[46], refs[47], refs[48], own, *refs[49:51])
    shares = refs[51:57]
    smalls = refs[57:66]
    refs = refs[66:]
    if share:
        gsnd, grcv, s_g, r_g, qsnd, qrcv, s_q, r_q, gall = refs[:9]
        line = LineSum(me_of("ctx"), gall, g_sum, refs[9:14])
    core, mate, across = tp_place()
    me = lax.axis_index("ctx")
    dp = lax.axis_index("dp")
    peers = axis_peers("ctx", n_ctx)
    dp_peers = axis_peers("dp", n_dp) if share else []
    n_prompt = groups * plen
    n_cont = conts * clen
    half = plen
    own_rows = rows(core * half, half)
    loads = fetch(
        (
            (do_h, do), (o_h, o), (wo_h, wo), (px_h, px), (kv_h, kv), (qs_h, qs),
            (hid_h, hid), (dm_h, dm), (xn2_h, xn2), (du_h, du), (da_h, da), (wu_h, wu), (wd_h, wd),
            (tab_h, tab), (xn1_h, xn1), (hist_h.at[:, own_rows], hist),
            (w_h, w), (cx_h, cx), (dh1_h, dh1),
        )
        + (((g_first, gall.at[0:EARLY]),) if share else ()),
        lsem,
    )
    low = lanes_below((clen, 128), 64)
    zero = jnp.zeros((clen, 128), bf16)
    for c in range(conts):
        flags[c * clen:(c + 1) * clen] = column(valid[c:c + 1].astype(f32))

    loads[0].wait()
    loads[1].wait()
    g0 = do[0:clen, 128:256].astype(f32)
    g1 = do[clen:2 * clen, 128:256].astype(f32)
    dos[me, 0:n_cont] = do[:, 0:128]
    dos[me, n_cont:n_cont + clen] = jnp.where(low, pltpu.roll(g0, 64, 1), g1).astype(bf16)
    for c in range(conts):
        at = slice(c * clen, (c + 1) * clen)
        full = slice(n_prompt + c * clen, n_prompt + (c + 1) * clen)
        pa = do[at, 0:128].astype(f32) * o[full, 0:128].astype(f32)
        pe = do[at, 128:256].astype(f32) * o[full, 128:256].astype(f32)
        ta = jnp.transpose(pa)
        te = jnp.transpose(pe)
        st = 8 * c
        sts[me, st:st + 8] = lse[8 * c:8 * c + 8]
        sts[me, st + 3:st + 4] = jnp.sum(ta[0:64], 0, keepdims=True)
        sts[me, st + 4:st + 5] = jnp.sum(ta[64:128], 0, keepdims=True)
        sts[me, st + 5:st + 6] = jnp.sum(te[64:128], 0, keepdims=True)
    greet(peers + [mate, across] + dp_peers)
    sends = []
    for d, device in enumerate(peers):
        for i, ref in enumerate((sts, dos)):
            sends.append(remote(ref.at[me], ref.at[me], send.at[d, i], recv.at[d, i], device))
    for copy in sends:
        copy.start()
    if share:
        loads[19].wait()
        loop(EARLY // LINE, line.launch)

    def place(a, c):
        return a + c * half

    def home(a):
        return a + core * half

    loads[2].wait()
    loads[3].wait()

    def attn(at, size):
        return dot(o[rows(at, size)], wo[...])

    first = TpSum(half, 0, place, s1, attn)
    first.begin()

    for copy in loads[4:11]:
        copy.wait()
    ff = hid.shape[1]
    o_c = o.at[n_prompt:n_prompt + n_cont]
    late = ff - EARLY
    bounds = (0, late + ff + 192, late + ff + 576)
    def cols_of(d):
        return pl.ds(pl.multiple_of(lax.rem(dp + d, n_dp) * depth, 128), depth)

    def give(d, i):
        span = slice(bounds[i], bounds[i + 1])
        return remote(
            gsnd.at[d - 1, span], grcv.at[d - 1, span], s_g.at[d - 1, i], r_g.at[d - 1, i],
            {"dp": lax.rem(dp + d, n_dp)},
        )

    def keeper(d):
        def store(at, value):
            here = slice(at, at + value.shape[0])
            if d > 0:
                gsnd[d - 1, here] = value.astype(bf16)
            else:
                for k in range(n_dp - 1):
                    value = value + grcv[k, here].astype(f32)
                gall[EARLY + at:EARLY + at + value.shape[0]] = value.astype(bf16)

        return store

    def late_grads(cols, store):
        down_grads(hid, dm, cols, EARLY, ff, lambda at, value: store(at - EARLY, value))
        other_grads(ff, xn2, du, o_c, da, cols, lambda at, value: store(at + late, value))

    def kv_grads(cols, store):
        for lo, hi in ((256, 384), (384, 512), (512, 640)):
            store(late + ff + 192 + lo - 256, dot_tn(dcat[:, lo:hi], xn1[:, cols]))

    def settle(i):
        for d in range(1, n_dp):
            give(d, i).wait()
        (late_grads, kv_grads)[i](cols_of(0), keeper(0))

    if share:
        for d in range(1, n_dp):
            late_grads(cols_of(d), keeper(d))
            give(d, 0).start()
    else:
        width = dm.shape[1]
        for j in range(width // 256):
            cols = pl.ds(256 * j, 256)
            span = slice(256 * j, 256 * j + 256)

            def lay_down(at, value, span=span):
                g_down[at:at + 128, span] = value.astype(bf16)

            def lay(at, value, span=span):
                if at < ff:
                    g_up[span, at:at + 256] = value.astype(bf16)
                else:
                    g_out[at - ff:at - ff + value.shape[0], span] = value.astype(bf16)

            down_grads(hid, dm, cols, 0, ff, lay_down)
            other_grads(ff, xn2, du, o_c, da, cols, lay)

    kd[...] = pltpu.roll(kv[0:n_prompt, 256:384].astype(f32), 64, 1).astype(bf16)
    for acc in (acc_k, acc_v, acc_kd, acc_vd):
        acc[...] = jnp.zeros(acc.shape, f32)

    def one_head(q_rows, do_rows, k, v, lse_row, delta_row, mask):
        s = dot_nt(k, q_rows)
        p = jnp.exp(s - lse_row)
        if mask is not None:
            p = mask(p)
        dp_ = dot_nt(v, do_rows)
        ds = (p * (dp_ - delta_row)).astype(bf16)
        return p.astype(bf16), ds

    def halves(a):
        return jnp.where(low, a, zero), jnp.where(low, zero, a)

    def beside(a, keeps):
        return a if keeps is None else jnp.concatenate([a * keep for keep in keeps], 1)

    def continuation(src, c, k_b, k_c, k_d, k_s, mask, keeps):
        base = c * clen
        a0, a1 = halves(qs[src, base:base + clen])
        d0, d1 = halves(dos[src, base:base + clen])
        e = halves(qs[src, n_cont:n_cont + clen])[c]
        g = halves(dos[src, n_cont:n_cont + clen])[c]
        st = 8 * c
        row = lambda i: sts[src, st + i:st + i + 1]
        p0, s0 = one_head(a0, d0, k_b, k_c, row(0), row(3), mask)
        p1, s1_ = one_head(a1, d1, k_b, k_c, row(1), row(4), mask)
        dv = dot(jnp.concatenate([p0, p1], 1), beside(jnp.concatenate([d0, d1], 0), keeps))
        dk = dot(jnp.concatenate([s0, s1_], 1), beside(jnp.concatenate([a0, a1], 0), keeps))
        dq = jnp.where(low, dot_tn(s0, k_b), dot_tn(s1_, k_b))
        keys, values = (k_d, k_s) if c == 0 else (k_s, k_d)
        p2, s2_ = one_head(e, g, keys, values, row(2), row(5), mask)
        dvd = dot(p2, beside(g, keeps))
        dkd = dot(s2_, beside(e, keeps))
        return dk, dv, dkd, dvd, dq, dot_tn(s2_, keys)

    def source(src, own):
        pair = []
        for c in range(conts):
            pick = msgs[pl.ds(src * 8 + 1 + c, 1)]
            keeps = [(pick == 1.0 * g).astype(f32).astype(bf16) for g in range(groups)]

            def choose(ref, lo, hi):
                return sum(
                    ref[g * plen:(g + 1) * plen, lo:hi] * keep for g, keep in enumerate(keeps)
                )

            dk, dv, dkd, dvd, dqa, dqd = continuation(
                src, c, choose(kv, 0, 128), choose(kv, 128, 256), choose(kv, 256, 384),
                choose(kd, 0, 128), None, keeps,
            )
            acc_k[...] += dk
            acc_v[...] += dv
            acc_kd[...] += dkd
            acc_vd[...] += dvd
            pair.append(dqd)
            if own:
                dq_f[c * clen:(c + 1) * clen] = dqa
            else:
                dqs[n_ctx + src, c * clen:(c + 1) * clen] = dqa.astype(bf16)
        third = jnp.where(low, pair[0], pair[1])
        if own:
            dq_f[n_cont:n_cont + clen] = third
        else:
            dqs[n_ctx + src, n_cont:n_cont + clen] = third.astype(bf16)

    def other_of(d):
        return lax.rem(me + 2 * n_ctx - (d + 1), n_ctx)

    def back_copy(d):
        other = other_of(d)
        return remote(
            dqs.at[n_ctx + other], dqs.at[me], send.at[d, 2], recv.at[d, 2], {"ctx": other}
        )

    def visit(d):
        other = other_of(d)
        for i, ref in enumerate((sts, dos)):
            remote(ref.at[other], ref.at[other], send.at[d, i], recv.at[d, i], {"ctx": other}).wait_recv()
        source(other, False)
        back_copy(d).start()

    give_xn = Share(xp, home, shares[0:2])

    def normed(i):
        a = first.row(i)
        h = px[rows(home(a), CH)].astype(f32) + first.take(i)
        h1[rows(a, CH)] = h
        whitened, _ = norm_rows(h)
        xp[rows(home(a), CH)] = (whitened * gains[2:3] + gains[3:4]).astype(bf16)
        give_xn.copy(i, a).start()

    def hidden(at, size):
        u = dot(xp[rows(at, size)], wu[...])
        return dot((0.5 * u * (1.0 + gelu_tanh(u))).astype(bf16), wd[...])

    second = TpSum(half, 0, place, s2, hidden)
    source(me, True)
    for copy in loads[11:13]:
        copy.wait()

    def step(i):
        @pl.when(i < first.n)
        def _():
            normed(i)

        @pl.when((i > 0) & (i <= first.n))
        def _():
            second.second(i - 1)

        @pl.when((i > 0) & (i < n_ctx))
        def _():
            visit(i - 1)

        @pl.when(i < first.n)
        def _():
            give_xn.copy(i, first.row(i)).wait()
            second.launch(i)

    loop(max(half // CH + 1, n_ctx), step)
    if share:
        settle(0)
        n_late = (EARLY + bounds[1]) // LINE
        loop(n_late - EARLY // LINE, lambda k: line.launch(k + EARLY // LINE))
        loop(EARLY // LINE, line.meet)
    loads[13].wait()

    for c in range(conts):
        at = slice(n_prompt + c * clen, n_prompt + (c + 1) * clen)
        k_d = kv[at, 256:384]
        k_s = pltpu.roll(k_d.astype(f32), 64, 1).astype(bf16)

        def mask(p):
            key = lax.broadcasted_iota(jnp.int32, p.shape, 0)
            query = lax.broadcasted_iota(jnp.int32, p.shape, 1)
            return jnp.where(
                key <= query, p * flags[c * clen:(c + 1) * clen, 0:1], 0.0
            )

        dk, dv, dkd, dvd, dqa, dqd = continuation(
            me, c, kv[at, 0:128], kv[at, 128:256], k_d, k_s, mask, None
        )
        dq_f[c * clen:(c + 1) * clen] += dqa
        keep = low if c == 0 else jnp.logical_not(low)
        dq_f[n_cont:n_cont + clen] += jnp.where(keep, dqd, 0.0)
        t = tab[plen:plen + clen]
        dcat[at, 256:384] = turn(dk, t, -1.0, False).astype(bf16)
        dcat[at, 384:512] = dv.astype(bf16)
        if c == 0:
            joined = jnp.where(low, dkd, pltpu.roll(dvd, 64, 1))
        else:
            joined = jnp.where(low, pltpu.roll(dkd, 64, 1), dvd)
        dcat[at, 512:640] = turn(joined, t, -1.0, True).astype(bf16)

    zq = jnp.zeros((plen, 256), bf16)
    wide = lanes_below((plen, 128), 64)
    for g in range(groups):
        at = slice(g * plen, (g + 1) * plen)
        t = tab[0:plen]
        dcat[at, 0:256] = zq
        part = slice(128 * g, 128 * g + 128)
        dcat[at, 256:384] = turn(acc_k[:, part], t, -1.0, False).astype(bf16)
        dcat[at, 384:512] = acc_v[:, part].astype(bf16)
        k2 = acc_kd[:, part] + pltpu.roll(acc_kd[:, part], 64, 1)
        v2 = acc_vd[:, part] + pltpu.roll(acc_vd[:, part], 64, 1)
        dcat[at, 512:640] = turn(jnp.where(wide, k2, v2), t, -1.0, True).astype(bf16)

    loads[14].wait()
    if share:
        for d in range(1, n_dp):
            kv_grads(cols_of(d), keeper(d))
            give(d, 1).start()
    else:
        for j in range(xn1.shape[1] // 256):
            span = slice(256 * j, 256 * j + 256)

            def lay_kv(at, value, span=span):
                at = at - late - ff - 192
                g_kv[at:at + 128, span] = value.astype(bf16)

            kv_grads(pl.ds(256 * j, 256), lay_kv)

    for d in range(n_ctx - 1):
        back_copy(d).wait_send()
        other = lax.rem(me + d + 1, n_ctx)
        remote(
            dqs.at[n_ctx + other], dqs.at[other], send.at[d, 2], recv.at[d, 2], {"ctx": other}
        ).wait_recv()
        dq_f[...] += dqs[other].astype(f32)
    for c in range(conts):
        at = slice(n_prompt + c * clen, n_prompt + (c + 1) * clen)
        t = tab[plen:plen + clen]
        pair = dq_f[c * clen:(c + 1) * clen] * 0.125
        dcat[at, 0:128] = turn(pair, t, -1.0, False).astype(bf16)
        third = dq_f[n_cont:n_cont + clen] * 0.125
        if c == 1:
            third = pltpu.roll(third, 64, 1)
        third = jnp.where(low, third, 0.0)
        dcat[at, 128:256] = turn(third, t, -1.0, True).astype(bf16)

    give_out = Share(out, home, shares[2:4])

    def mixed(i):
        a = second.row(i)
        here = rows(a, CH)
        y = h1[here] + second.take(i)
        out[rows(home(a), CH)] = mixed_states(ids, dwa, hist, here, y).astype(bf16)
        give_out.copy(i, a).start()

    def prompts_out():
        loads[15].wait()
        loop(half // CH, mixed)

    for copy in loads[16:19]:
        copy.wait()
    if share:
        q_state = (qsnd, qrcv, s_q, r_q, gall, line, lambda: settle(1), n_late)
    else:
        q_state = (g_q,)
    input_grad_tail(
        n_dp, n_ctx, share, plen, clen, depth,
        dcat, w, px, cx, gains, dh1, stat_in, xn1, grad_p, grad_c, fin,
        smalls, s3, shares[4:6], prompts_out, *q_state,
    )
    loop(half // CH, lambda i: give_out.copy(i, second.row(i)).wait())
    for copy in sends:
        copy.wait_send()


def output_body(
    n_ctx, n_dp, share, ff,
    ids, msgs, fin, p_out, c_out, p_grad, c_grad, *refs,
):
    n = 1 if share else 0
    parts = refs[:n]
    p_out_o, c_out_o, p_grad_o, c_grad_o, loss, dwa_g, g1, b1, g2, b2 = refs[n:n + 10]
    refs = refs[n + 10:]
    if share:
        r_qkv, r_out, r_up, r_down = refs[:4]
        refs = refs[4:]
    held, sem = refs[:4], refs[4]
    moves = (
        (p_out, p_out_o), (c_out, c_out_o), (p_grad, p_grad_o), (c_grad, c_grad_o)
    )
    reads = [
        pltpu.make_async_copy(s, h, sem.at[0, i]) for i, ((s, _), h) in enumerate(zip(moves, held))
    ]
    copies = [
        pltpu.make_async_copy(h, t, sem.at[1, i]) for i, ((_, t), h) in enumerate(zip(moves, held))
    ]
    for copy in reads:
        copy.start()
    depth = g1.shape[0]
    width = fin.shape[1]
    count = msgs[0:1, 0:1]
    for j in range(1, n_ctx):
        count += msgs[8 * j:8 * j + 1, 0:1]
    factor = 1.0 / (jnp.maximum(count, 1.0) * (1.0 * width))
    sums = jnp.sum(fin[...], -1, keepdims=True) * factor
    row = lax.broadcasted_iota(jnp.int32, sums.shape, 0)

    def entry(i):
        return jnp.sum(jnp.where(row == i, sums, 0.0))

    loss[0] = entry(4)
    for k in range(4):
        value = 0.0
        for j in range(4):
            value += jnp.where(ids[j] == k, 2.0 * entry(5 + j), 0.0)
        dwa_g[k] = value
    dwa_g[4] = 2.0 * entry(9)
    for i, ref in enumerate((g1, b1, g2, b2)):
        if share:
            ref[...] = fin[i, pl.ds(pl.multiple_of(lax.axis_index("dp") * depth, 128), depth)]
        else:
            piece = jnp.zeros((1, depth), f32)
            for d in range(n_dp):
                here = fin[i:i + 1, d * depth:(d + 1) * depth]
                piece += jnp.where(lax.axis_index("dp") == d, here, 0.0)
            ref[...] = piece.reshape(depth)
    for read, copy in zip(reads, copies):
        read.wait()
        copy.start()
    if share:
        rest = parts[0].at[ff:]
        r_down[...] = parts[0][0:ff].astype(f32)
        for j in range(ff // depth):
            r_up[:, j * depth:(j + 1) * depth] = rest[j * depth:(j + 1) * depth].astype(f32)
        r_out[...] = rest[ff:ff + 192].astype(f32)
        base = ff + 192
        r_qkv[1, 0:128] = rest[base:base + 128].astype(f32)
        r_qkv[2, 0:128] = rest[base + 128:base + 256].astype(f32)
        r_qkv[1, 128:192] = rest[base + 256:base + 320].astype(f32)
        r_qkv[2, 128:192] = rest[base + 320:base + 384].astype(f32)
        r_qkv[0] = rest[base + 384:base + 576].astype(f32)
    for copy in copies:
        copy.wait()


def per_device(
    n_dp, n_ctx,
    prompt_x, cont_x, prompt_hist, cont_hist, teacher, valid_mask, cont_group, layer_ids,
    dwa_weights, qkv_weight, out_weight, up_weight, down_weight,
    ln1_gain, ln1_bias, ln2_gain, ln2_bias,
):
    groups, plen, width = prompt_x.shape
    conts, clen, _ = cont_x.shape
    depth = qkv_weight.shape[0]
    n_prompt, n_cont = groups * plen, conts * clen
    n_rows = n_prompt + n_cont
    split, c_split = n_prompt // 2, n_cont // 2
    half = split + c_split
    ff = up_weight.shape[1]
    share = depth % 128 == 0
    packed = n_cont + clen
    tab_rows = plen + clen
    vmem = pltpu.VMEM

    w_t = qkv_weight.transpose(1, 2, 0)
    px = prompt_x.reshape(n_prompt, width)
    cx = cont_x.reshape(n_cont, width)
    vectors = (ln1_gain, ln1_bias, ln2_gain, ln2_bias)
    states = vmem((3 * (n_prompt // clen + conts), clen, 128), f32)
    if share:
        given = (out_weight, up_weight, down_weight)
    else:
        out_w = lax.all_gather(out_weight, "dp", axis=1, tiled=True)
        given = (
            jnp.concatenate([out_w[:128], jnp.zeros((64, width), bf16), out_w[128:]], 0),
            lax.all_gather(up_weight, "dp", axis=0, tiled=True),
            lax.all_gather(down_weight, "dp", axis=1, tiled=True),
        )
    outs = [
        ((n_rows, width), bf16), ((n_rows, 384), bf16), ((tab_rows, 384), f32),
        ((640, width), bf16),
        ((n_rows, 256), bf16), ((8 * conts, clen), f32), ((8 * n_ctx, 128), f32),
        ((8, width), f32),
        ((n_cont, width), bf16), ((n_cont, width), bf16), ((n_cont, ff), bf16),
        ((n_cont, width), bf16), ((n_cont, ff), bf16), ((n_cont, width), bf16),
        ((n_cont, 256), bf16), ((c_split, width), f32), ((16, width), f32),
        ((n_ctx, packed, 128), bf16),
    ]
    out_specs = [HBM_SPEC] * 4 + [VMEM_SPEC] * 14
    whole_out = vmem((256, width), bf16)
    extra = []
    held = [whole_out]
    if share:
        outs += [
            ((EARLY, depth), bf16), ((width, ff), bf16), ((ff, width), bf16), ((256, width), bf16),
        ]
        out_specs += [VMEM_SPEC] + [HBM_SPEC] * 2 + [VMEM_SPEC]
        held = like(*given)
        extra = [
            vmem((n_dp - 1, EARLY, depth), bf16), vmem((n_dp - 1, EARLY, depth), bf16),
            vmem((EARLY, depth), f32), DMA((n_dp - 1,)), DMA((n_dp - 1,)),
        ]
    got = kernel_call(
        functools.partial(front_body, n_ctx, n_dp, share, plen, clen, groups, conts),
        outs,
        [
            vmem((packed, 128), bf16),
            vmem((n_rows, width), bf16), vmem((n_rows, 256), bf16),
            vmem((n_ctx, n_prompt, 384), bf16), vmem((n_cont, 384), bf16),
            vmem((tab_rows, 384), f32), vmem((640, width), bf16),
            vmem((8, depth), f32), vmem((n_dp, 8, depth), f32),
            vmem((8, 128), f32), vmem((n_dp, 8, 128), f32), vmem((n_ctx, 8, 128), f32),
            states, states, states,
            vmem((1, 3, 192, depth) if share else (n_dp, 3, 192, depth), bf16),
            DMA((n_dp - 1, 7)), DMA((n_dp - 1, 7)),
            DMA((2, n_ctx, groups)), DMA((n_ctx, groups)), DMA((n_ctx - 1,)), DMA((n_ctx - 1,)),
            DMA((n_dp - 1, 4)), DMA((n_dp - 1, 4)), DMA((9,)),
        ]
        + like(w_t, px, cx)
        + [DMA((6,)), vmem((width, ff), bf16), vmem((ff, width), bf16)]
        + held
        + [
            vmem((4, c_split, width), bf16), vmem((c_split, width), bf16),
            vmem((n_cont, ff), f32), vmem((c_split, width), f32),
            vmem((c_split, width), f32), vmem((clen, 128), f32),
            DMA((2,)), DMA((n_ctx - 1,)), DMA((n_ctx - 1,)),
        ]
        + TpSum.scratch(c_split, width) * 3
        + share_scratch(c_split) * 4
        + extra,
        0,
        [SMEM_SPEC] * 3 + [HBM_SPEC] * 3 + [VMEM_SPEC] * 5 + [HBM_SPEC] * 5,
        (
            cont_group, layer_ids, dwa_weights, px, cx, w_t, *vectors, valid_mask, *given,
            cont_hist.reshape(4, n_cont, width), teacher.reshape(n_cont, width),
        ),
        "front",
        out_specs,
    )
    xn1, kv, tab, w_full, o, lse, msgs, gains = got[:8]
    cont_out, dm, hid, xn2, du, da, do, dh1, stat, qs = got[8:18]
    if share:
        g_first = [got[18]]
        wu, wd, wo = got[19:22]
    else:
        g_first = []
        wo, wu, wd = given

    grad_rows = 2 * ff + 12 * HEAD_DIM
    outs = [
        ((n_prompt, width), bf16), ((n_prompt, width), bf16), ((n_cont, width), bf16),
        ((16, width), f32),
    ]
    out_specs = [VMEM_SPEC] + [HBM_SPEC] * 2 + [VMEM_SPEC]
    if share:
        outs += [((grad_rows, depth), bf16)]
        out_specs += [VMEM_SPEC]
        late = grad_rows - EARLY - 3 * HEAD_DIM
        third = (n_dp - 1, 3 * HEAD_DIM, depth)
        extra = [
            vmem((n_dp - 1, late, depth), bf16), vmem((n_dp - 1, late, depth), bf16),
            DMA((n_dp - 1, 2)), DMA((n_dp - 1, 2)),
            vmem(third, bf16), vmem(third, bf16),
            DMA((n_dp - 1,)), DMA((n_dp - 1,)), vmem((grad_rows, depth), bf16),
        ] + LineSum.scratch(grad_rows // LINE, depth)
    else:
        outs += [
            ((ff, width), bf16), ((width, ff), bf16), ((3 * HEAD_DIM, width), bf16),
            ((384, width), bf16), ((3 * HEAD_DIM, width), bf16),
        ]
        out_specs += [VMEM_SPEC] * 5
        extra = []
    acc = vmem((plen, 128 * groups), f32)
    wide = vmem((split, width), bf16)
    tall = vmem((half, width), bf16)
    n_p, n_h = split // CH, half // CH
    back = kernel_call(
        functools.partial(
            attend_back_body, n_ctx, n_dp, share, plen, clen, groups, conts, depth
        ),
        outs,
        [
            vmem((n_cont, ff), bf16), vmem((n_cont, width), bf16),
            vmem((n_cont, width), bf16), vmem((n_cont, ff), bf16),
            vmem((n_cont, width), bf16), vmem((256, width), bf16),
            vmem((width, ff), bf16), vmem((ff, width), bf16),
            vmem((n_prompt, width), bf16), vmem((4, split, width), bf16), DMA((20,)),
            vmem((n_ctx, packed, 128), bf16), vmem((n_ctx, 8 * conts, clen), f32),
            vmem((2 * n_ctx, packed, 128), bf16), vmem((n_prompt, 128), bf16),
            acc, acc, acc, acc, vmem((packed, 128), f32),
            DMA((n_ctx - 1, 3)), DMA((n_ctx - 1, 3)),
            vmem((n_prompt, width), bf16), vmem((split, width), f32),
            vmem((n_rows, width), bf16), vmem((n_cont, 128), f32),
        ]
        + like(do, o, kv, tab, qs, w_full, cx, dh1)
        + [
            vmem((n_rows, 640), bf16), tall, vmem((half, width), f32),
            wide, wide, wide, DMA((2, n_p)), DMA((2, n_p)),
            wide, wide, DMA((2, n_p)), DMA((2, n_p)),
            tall, tall, tall, DMA((2, n_h)), DMA((2, n_h)),
        ]
        + share_scratch(split) * 2
        + share_scratch(half)
        + [
            vmem((n_rows, width), bf16), vmem((16, width), f32), vmem((2, 16, width), f32),
            vmem((2, 16, width), f32), vmem((n_ctx, 16, width), f32),
            vmem((n_dp, 16, width), f32),
            DMA((1 + n_ctx + n_dp,)), DMA((1 + n_ctx + n_dp,)), DMA((2,)),
        ]
        + extra,
        2,
        [SMEM_SPEC] * 2
        + [VMEM_SPEC] + [HBM_SPEC] * 2 + [VMEM_SPEC] * 3 + [HBM_SPEC] * 17 + [VMEM_SPEC]
        + [HBM_SPEC] * len(g_first),
        (
            layer_ids, dwa_weights, msgs, do, o, lse, valid_mask, gains, kv, tab, qs,
            hid, dm, xn2, du, da, wo, wu, wd, px, prompt_hist.reshape(4, n_prompt, width), xn1,
            w_full, cx, dh1, stat, *g_first,
        ),
        "back",
        out_specs,
    )
    prompt_out, grad_p, grad_c, fin = back[:4]

    outs = [
        ((n_prompt, width), bf16), ((n_cont, width), bf16), ((n_prompt, width), bf16),
        ((n_cont, width), bf16), ((1,), f32), ((5,), f32),
    ] + [((depth,), f32)] * 4
    out_specs = [HBM_SPEC] * 4 + [SMEM_SPEC] * 2 + [VMEM_SPEC] * 4
    specs = [SMEM_SPEC] + [VMEM_SPEC] * 2 + [HBM_SPEC] * 4
    args = (layer_ids, msgs, fin, prompt_out, cont_out, grad_p, grad_c)
    if share:
        outs += [((3, 192, depth), f32), ((192, depth), f32), ((depth, ff), f32), ((ff, depth), f32)]
        out_specs += [VMEM_SPEC] * 4
        args += (back[4],)
        specs += [VMEM_SPEC]
    done = pl.pallas_call(
        functools.partial(output_body, n_ctx, n_dp, share, ff),
        out_shape=[jax.ShapeDtypeStruct(s, d) for s, d in outs],
        in_specs=specs,
        out_specs=out_specs,
        scratch_shapes=[
            vmem((n_prompt, width), bf16), vmem((n_cont, width), bf16),
            vmem((n_prompt, width), bf16), vmem((n_cont, width), bf16), DMA((2, 4)),
        ],
        compiler_params=pltpu.CompilerParams(vmem_limit_bytes=LIMIT),
        name="outputs",
    )(*args)
    if share:
        r_qkv, r_out, r_up, r_down = done[10:]
        r_qkv = r_qkv.transpose(2, 0, 1)
    else:
        def scattered(g, dim):
            part = lax.psum_scatter(g, "dp", scatter_dimension=dim, tiled=True)
            return lax.psum(part, "ctx").astype(f32)

        g_down, g_up, g_out, g_kv, g_q = back[4:]
        r_down = scattered(g_down, 1)
        r_up = scattered(g_up, 0)
        r_out = scattered(g_out, 1)
        g_k = jnp.concatenate([g_kv[0:128], g_kv[256:320]], 0)
        g_v = jnp.concatenate([g_kv[128:256], g_kv[320:384]], 0)
        r_qkv = scattered(jnp.stack([g_q, g_k, g_v]).transpose(2, 0, 1), 0)
    return (
        done[0].reshape(groups, plen, width),
        done[1].reshape(conts, clen, width),
        done[4].reshape(()),
        done[2].reshape(groups, plen, width),
        done[3].reshape(conts, clen, width),
        r_qkv, r_out, r_up, r_down,
        done[6], done[7], done[8], done[9],
        done[5],
    )


def solution(mesh):
    n_dp, n_ctx = mesh.shape["dp"], mesh.shape["ctx"]
    in_specs = (
        P("dp", "ctx", None), P(("dp", "ctx"), None, None), P(None, "dp", "ctx", None),
        P(None, ("dp", "ctx"), None, None), P(("dp", "ctx"), None, None), P(("dp", "ctx"), None),
        P(("dp", "ctx")), P(), P(), P("dp", None, "tp"), P("tp", "dp"), P("dp", "tp"),
        P("tp", "dp"), P("dp"), P("dp"), P("dp"), P("dp"),
    )
    out_specs = (
        P("dp", "ctx", None), P(("dp", "ctx"), None, None), P(), P("dp", "ctx", None),
        P(("dp", "ctx"), None, None), P("dp", None, "tp"), P("tp", "dp"), P("dp", "tp"),
        P("tp", "dp"), P("dp"), P("dp"), P("dp"), P("dp"), P(),
    )
    return jax.shard_map(
        functools.partial(per_device, n_dp, n_ctx),
        mesh=mesh, in_specs=in_specs, out_specs=out_specs, check_vma=False,
    )
```

```python
import functools
import math

import jax
import jax.numpy as jnp
from jax import lax
from jax.experimental import pallas as pl
from jax.experimental.pallas import tpu as pltpu
from jax.sharding import PartitionSpec as P

HEAD_DIM = 64
EPS = 1e-05
NEG = -1e30
MESH = pl.DeviceIdType.MESH
f32 = jnp.float32
bf16 = jnp.bfloat16
VMEM_SPEC = pl.BlockSpec(memory_space=pltpu.VMEM)
SMEM_SPEC = pl.BlockSpec(memory_space=pltpu.SMEM)
HBM_SPEC = pl.BlockSpec(memory_space=pl.ANY)
DMA = pltpu.SemaphoreType.DMA
LIMIT = 62 << 20
NT = (((1,), (1,)), ((), ()))
TN = (((0,), (0,)), ((), ()))
CH = 128
BIG = 256
LINE = 192
SUB = 2
PIECE = LINE // SUB
EARLY = 2 * LINE


def dot(a, b):
    return jnp.dot(a, b, preferred_element_type=f32)


def dot_nt(a, b):
    return lax.dot_general(a, b, NT, preferred_element_type=f32)


def dot_tn(a, b):
    return lax.dot_general(a, b, TN, preferred_element_type=f32)


def rows(start, size):
    return pl.ds(pl.multiple_of(start, size), size)


def loop(count, body):
    def step(i, carry):
        body(i)
        return carry

    lax.fori_loop(0, count, step, 0)


def kernel_call(body, outs, scratch, cid, specs, args, name, out_specs=None):
    return pl.pallas_call(
        body,
        out_shape=[jax.ShapeDtypeStruct(s, d) for s, d in outs],
        in_specs=specs,
        out_specs=out_specs or [VMEM_SPEC] * len(outs),
        scratch_shapes=scratch,
        compiler_params=pltpu.CompilerParams(
            collective_id=cid, has_side_effects=True, vmem_limit_bytes=LIMIT
        ),
        cost_estimate=pl.CostEstimate(flops=0, bytes_accessed=30 << 20, transcendentals=0),
        name=name,
    )(*args)


def greet(partners):
    barrier = pltpu.get_barrier_semaphore()
    for device in partners:
        pl.semaphore_signal(barrier, inc=1, device_id=device, device_id_type=MESH)
    pl.semaphore_wait(barrier, len(partners))


def remote(src, dst, send, recv, device):
    return pltpu.make_async_remote_copy(
        src_ref=src,
        dst_ref=dst,
        send_sem=send,
        recv_sem=recv,
        device_id=device,
        device_id_type=MESH,
    )


def fetch(pairs, sems):
    copies = [pltpu.make_async_copy(s, d, sems.at[i]) for i, (s, d) in enumerate(pairs)]
    for copy in copies:
        copy.start()
    return copies


def like(*arrays):
    return [pltpu.VMEM(a.shape, a.dtype) for a in arrays]


def axis_peers(axis, count):
    me = lax.axis_index(axis)
    return [{axis: lax.rem(me + d, count)} for d in range(1, count)]


def me_of(axis):
    return lax.axis_index(axis)


def tp_place():
    tp = lax.axis_index("tp")
    core = lax.rem(tp, 2)
    mate = {"tp": tp + 1 - 2 * core}
    across = {"tp": lax.rem(tp + 2, 4)}
    return core, mate, across


def norm_rows(x):
    mean = jnp.mean(x, -1, keepdims=True)
    centered = x - mean
    var = jnp.mean(centered * centered, -1, keepdims=True)
    inverse = lax.rsqrt(var + EPS)
    return centered * inverse, inverse


def norm_back(gradient, whitened, inverse, gain):
    e = gradient * gain
    return inverse * (
        e - jnp.mean(e, -1, keepdims=True) - whitened * jnp.mean(e * whitened, -1, keepdims=True)
    )


def lanes_below(shape, bound):
    return lax.broadcasted_iota(jnp.int32, shape, len(shape) - 1) < bound


def turn(y, tab, sign, half):
    cos, low, high = tab[:, :128], tab[:, 128:256], tab[:, 256:384]
    turned = sign * (pltpu.roll(y, 96, 1) * low + pltpu.roll(y, 32, 1) * high)
    if not half:
        return y * cos + turned
    return jnp.where(lanes_below(y.shape, 64), y * cos + turned, y)


W_PARTS = ((1, 0, 128, 256), (2, 0, 128, 384), (1, 128, 64, 512), (2, 128, 64, 576), (0, 0, 192, 0))


def front_body(
    n_ctx, n_dp, share, plen, clen, groups, conts,
    sel, ids, dwa, px_h, cx_h, w_h, g1, b1, g2, b2, valid, wo_h, wu_h, wd_h, hist, teach, *refs,
):
    xn_o, kv_o, tab_o, w_o, o_o, lse, msgs, gains = refs[:8]
    out, *big, da, do, dh1, stat, qs = refs[8:18]
    o, *kept, ksem = refs[-6:]
    middle_outs = (out, *kept, da, do, dh1, stat, qs)
    leave = [
        pltpu.make_async_copy(s, d, ksem.at[i])
        for i, (s, d) in enumerate(zip((o, *kept), (o_o, *big)))
    ]
    refs = refs[18:-6]
    if share:
        gdn, wu_o, wd_o, wo_o = refs[:4]
        refs = refs[4:]
    (
        qpack, xn, q, kvs, kvc, tab, w_full, gb, gbs, cnt, cnts, notes, m_s, l_s, acc_s,
        wgs, s_x, r_x, s_kv, r_kv, s_c, r_c, s_w, r_w, osem, w, px, cx, lsem, wu_f, wd_f,
    ) = refs[:31]
    refs = refs[31:]
    if share:
        wo, wu, wd = refs[:3]
        refs = refs[3:]
        weight_pairs = ((wo_h, wo), (wu_h, wu), (wd_h, wd))
    else:
        wo_o = refs[0]
        gdn = None
        refs = refs[1:]
        weight_pairs = ((wo_h, wo_o), (wu_h, wu_f), (wd_h, wd_f))
    core, mate, across = tp_place()
    loads = fetch(((w_h, w), (px_h, px), (cx_h, cx)) + weight_pairs, lsem)
    me = lax.axis_index("ctx")
    mine = lax.axis_index("dp")
    depth = w.shape[2]
    width = px.shape[1]
    last = n_ctx - 1
    n_prompt = groups * plen
    n_cont = conts * clen
    tile = clen
    dp_peers = axis_peers("dp", n_dp)
    peers = axis_peers("ctx", n_ctx)
    for i, vector in enumerate((g1, b1, g2, b2)):
        gb[i:i + 1] = vector[...].astype(f32).reshape(1, depth)
    gb[4:8] = jnp.zeros((4, depth), f32)
    cnt[...] = jnp.zeros(cnt.shape, f32) + jnp.sum(valid[...].astype(f32))
    greet(dp_peers + peers + [mate, across])
    loads[0].wait()

    copies = []
    weights = []
    if share:
        cols = pl.ds(pl.multiple_of(mine * depth, 128), depth)
        here = rows(mine * depth, depth)
    for d, device in enumerate(dp_peers):
        pairs = [(gb, gbs.at[mine]), (cnt, cnts.at[mine])]
        if share:
            pairs += [
                (w.at[p, a:a + n], w_full.at[t:t + n, cols]) for p, a, n, t in W_PARTS
            ]
        else:
            pairs += [(w, wgs.at[mine])]
        copies.append(
            [remote(s, t, s_x.at[d, i], r_x.at[d, i], device) for i, (s, t) in enumerate(pairs)]
        )
    for i in range(len(copies[0])):
        for group in copies:
            group[i].start()
    local = []
    if share:
        for p, a, n, t in W_PARTS:
            w_full[t:t + n, cols] = w[p, a:a + n]
    else:
        wgs[mine] = w[...]
    for copy in loads[1:]:
        copy.wait()
    if share:
        pairs = [
            (wo.at[0:128], wo_o.at[0:128, cols]), (wo.at[128:192], wo_o.at[192:256, cols]),
            (wu, wu_f.at[here]), (wd, wd_f.at[:, cols]),
        ]
        for d, device in enumerate(dp_peers):
            for i, (s, t) in enumerate(pairs):
                weights.append(remote(s, t, s_w.at[d, i], r_w.at[d, i], device))
        for copy in weights:
            copy.start()
        local += fetch(pairs, osem)
    if share:
        wo_o[128:192] = jnp.zeros((64, width), bf16)
    w_full[192:256] = jnp.zeros((64, width), bf16)
    gbs[mine] = gb[...]
    cnts[mine] = cnt[...]

    def table(count, base, start):
        def body(i):
            shape = (CH, 128)
            lane = lax.broadcasted_iota(jnp.int32, shape, 1)
            row = lax.broadcasted_iota(jnp.int32, shape, 0)
            turns = lax.rem(lane, 32).astype(f32) * (-2.0 * math.log(10000.0) / HEAD_DIM)
            angle = (row + (start + i * CH)).astype(f32) * jnp.exp(turns)
            sin = jnp.sin(angle)
            left = lax.rem(lane, 64) < 32
            at = rows(base + i * CH, CH)
            tab[at, 0:128] = jnp.cos(angle)
            tab[at, 128:256] = jnp.where(left, -sin, 0.0)
            tab[at, 256:384] = jnp.where(left, 0.0, sin)

        loop(count // CH, body)

    table(plen, 0, me * plen)
    table(clen, plen, n_ctx * plen)

    def save(src, dst, i):
        copy = pltpu.make_async_copy(src, dst, osem.at[i])
        copy.start()
        local.append(copy)

    save(tab, tab_o, 4)
    for group in copies:
        group[0].wait_recv()
        group[1].wait_recv()

    def one_hot(d):
        row = lax.broadcasted_iota(jnp.int32, (depth, width), 0) + d * depth
        col = lax.broadcasted_iota(jnp.int32, (depth, width), 1)
        return (row == col).astype(f32).astype(bf16)

    total = jnp.zeros(gains.shape, f32)
    count = jnp.zeros(cnt.shape, f32)
    for d in range(n_dp):
        total += dot(gbs[d].astype(bf16), one_hot(d))
        count += cnts[d]
    gains[...] = total
    note = notes.at[me]
    notes[me] = count
    for i in range(conts):
        notes[me, 1 + i:2 + i] = jnp.zeros((1, 128), f32) + sel[i].astype(f32)
    counts = [remote(note, note, s_c.at[d], r_c.at[d], device) for d, device in enumerate(peers)]
    for copy in counts:
        copy.start()

    def norm_part(x, base):
        def body(i):
            whitened, _ = norm_rows(x[rows(i * CH, CH)].astype(f32))
            xn[rows(base + i * CH, CH)] = (whitened * gains[0:1] + gains[1:2]).astype(bf16)

        loop(x.shape[0] // CH, body)

    norm_part(px, 0)
    norm_part(cx, n_prompt)
    save(xn, xn_o, 5)

    def arrive(i):
        if share:
            for group in copies:
                group[2 + i].wait_recv()
        elif i == 0:
            for group in copies:
                group[2].wait_recv()
            for p, a, n, t in W_PARTS:
                part = jnp.zeros((n, width), f32)
                for d in range(n_dp):
                    part += dot(wgs[d, p, a:a + n], one_hot(d))
                w_full[t:t + n] = part.astype(bf16)

    def hop(slot, g, step, side):
        there = kvs.at[slot, rows(g * plen, plen)]
        return remote(there, there, s_kv.at[side, slot, g], r_kv.at[slot, g], {"ctx": me + step})

    def kv_rows(count, base, tab_base, period, dst, first):
        def body(i):
            at = rows(first + i * BIG, BIG)
            t = tab[rows(tab_base + lax.rem(i * BIG, period), BIG)]
            x = xn[rows(base + i * BIG, BIG)]
            y = dot_nt(x, w_full[256:512])
            dst[at, 0:128] = turn(y[:, 0:128], t, 1.0, False).astype(bf16)
            dst[at, 128:256] = y[:, 128:256].astype(bf16)
            dst[at, 256:384] = turn(dot_nt(x, w_full[512:640]), t, 1.0, True).astype(bf16)

        loop(count // BIG, body)

    def q_rows_of(count, base, tab_base, period):
        def body(i):
            at = rows(base + i * BIG, BIG)
            t = tab[rows(tab_base + lax.rem(i * BIG, period), BIG)]
            y = dot_nt(xn[at], w_full[0:256])
            q[at, 0:128] = (turn(y[:, 0:128], t, 1.0, False) * 0.125).astype(bf16)
            q[at, 128:256] = (turn(y[:, 128:256], t, 1.0, True) * 0.125).astype(bf16)

        loop(count // BIG, body)

    for i in range(4):
        arrive(i)

    def send_own(g):
        kv_rows(plen, g * plen, 0, plen, kvs.at[me], g * plen)

        @pl.when(me < last)
        def _():
            hop(me, g, 1, 0).start()

        @pl.when(me > 0)
        def _():
            hop(me, g, -1, 1).start()

    loop(groups, send_own)
    save(kvs.at[me], kv_o.at[0:n_prompt], 6)
    kv_rows(n_cont, n_prompt, plen, clen, kvc, 0)
    save(kvc, kv_o.at[n_prompt:n_prompt + n_cont], 7)
    arrive(4)
    save(w_full, w_o, 8)
    q_rows_of(n_cont, n_prompt, plen, clen)
    q_rows_of(n_prompt, 0, 0, plen)

    def update(at, q_rows, k, v, mask, first):
        s = dot_nt(q_rows, k)
        if mask is not None:
            s = mask(s)
        top = jnp.max(s, -1, keepdims=True)
        if first:
            m_new = jnp.broadcast_to(top, (s.shape[0], 128))
        else:
            m_old = m_s[at]
            m_new = jnp.maximum(m_old, top)
        total = None
        parts = []
        for j in range(s.shape[1] // 128):
            p = jnp.exp(s[:, 128 * j:128 * j + 128] - m_new)
            total = p if total is None else total + p
            parts.append(p.astype(bf16))
        pv = dot(jnp.concatenate(parts, 1), v)
        m_s[at] = m_new
        if first:
            l_s[at] = total
            acc_s[at] = pv
        else:
            fade = jnp.exp(m_old - m_new)
            l_s[at] = l_s[at] * fade + total
            acc_s[at] = acc_s[at] * fade + pv

    low = lanes_below((tile, 128), 64)

    def heads(q_at, state, k_b, k_c, k_d, mask, first):
        a = q[q_at, 0:128]
        zero = jnp.zeros_like(a)
        update(state, jnp.where(low, a, zero), k_b, k_c, mask, first)
        update(state + 1, jnp.where(low, zero, a), k_b, k_c, mask, first)
        update(state + 2, q[q_at, 128:256], k_d, k_d, mask, first)

    tiles = plen // tile

    def prompt_part(slot, group, diagonal):
        def body(t):
            i = group * tiles + t
            at = rows(group * plen, plen)
            mask = None
            if diagonal:
                def mask(s):
                    row = lax.broadcasted_iota(jnp.int32, s.shape, 0) + t * tile
                    col = lax.broadcasted_iota(jnp.int32, s.shape, 1)
                    return jnp.where(col <= row, s, NEG)
            heads(
                rows(i * tile, tile), 3 * i,
                kvs[slot, at, 0:128], kvs[slot, at, 128:256], kvs[slot, at, 256:384],
                mask, diagonal,
            )

        loop(tiles, body)

    def cont_part(slot, first):
        def body(i):
            k = kvs[slot, 0:plen]
            for g in range(1, groups):
                k = jnp.where(sel[i] == g, kvs[slot, g * plen:(g + 1) * plen], k)
            heads(
                rows(n_prompt + i * tile, tile), 3 * (groups * tiles + i),
                k[:, 0:128], k[:, 128:256], k[:, 256:384], None, first,
            )

        loop(conts, body)

    def self_part():
        def body(i):
            at = rows(i * tile, tile)

            def mask(s):
                row = lax.broadcasted_iota(jnp.int32, s.shape, 0)
                col = lax.broadcasted_iota(jnp.int32, s.shape, 1)
                bias = (valid[pl.ds(i, 1)].astype(f32) - 1.0) * (-NEG)
                return jnp.where(col <= row, s + bias, NEG)

            heads(
                rows(n_prompt + i * tile, tile), 3 * (groups * tiles + i),
                kvc[at, 0:128], kvc[at, 128:256], kvc[at, 256:384], mask, False,
            )

        loop(conts, body)

    cont_part(me, True)
    loop(groups, lambda g: prompt_part(me, g, True))
    self_part()
    e0 = q[n_prompt:n_prompt + clen, 128:256].astype(f32)
    e1 = q[n_prompt + clen:n_prompt + n_cont, 128:256].astype(f32)
    qpack[0:n_cont] = q[n_prompt:n_prompt + n_cont, 0:128]
    qpack[n_cont:n_cont + clen] = jnp.where(low, e0, pltpu.roll(e1, 64, 1)).astype(bf16)

    def ring(e):
        d = e + 1

        def group(g):
            @pl.when(me - d >= 0)
            def _():
                hop(me - d, g, 1, 0).wait_recv()

                @pl.when(me < last)
                def _():
                    hop(me - d, g, 1, 0).start()

            @pl.when(me + d <= last)
            def _():
                hop(me + d, g, -1, 1).wait_recv()

                @pl.when(me > 0)
                def _():
                    hop(me + d, g, -1, 1).start()

            @pl.when((me - d > 0) | ((me == d) & (g < groups - 1)))
            def _():
                prompt_part(me - d, g, False)

        loop(groups, group)

        @pl.when(me - d >= 0)
        def _():
            cont_part(me - d, False)

        @pl.when(me + d <= last)
        def _():
            cont_part(me + d, False)

    loop(last, ring)

    for copy in counts:
        copy.wait()
    for d in range(n_ctx):
        msgs[8 * d:8 * d + 8] = notes[d]

    def finish(at, state):
        l0 = jnp.sum(l_s[state], -1, keepdims=True)
        l1 = jnp.sum(l_s[state + 1], -1, keepdims=True)
        l2 = jnp.sum(l_s[state + 2], -1, keepdims=True)
        o[at, 0:128] = jnp.where(low, acc_s[state] / l0, acc_s[state + 1] / l1).astype(bf16)
        o[at, 128:256] = jnp.where(low, 0.0, acc_s[state + 2] / l2).astype(bf16)
        return (l0, l1, l2)

    def rest_of_prompts():
        @pl.when(me > 0)
        def _():
            prompt_part(0, groups - 1, False)

        loop(groups * tiles, lambda i: finish(rows(i * tile, tile), 3 * i))

    for i in range(conts):
        state = 3 * (groups * tiles + i)
        sums = finish(rows(n_prompt + i * tile, tile), state)
        lse[8 * i:8 * i + 8] = jnp.zeros((8, tile), f32)
        for h in range(3):
            value = m_s[state + h] + jnp.log(sums[h])
            lse[8 * i + h:8 * i + h + 1] = jnp.transpose(value)[0:1]

    for copy in weights:
        copy.wait()
    for copy in local:
        copy.wait()
    if share:
        local = fetch(((wu_f, wu_o), (wd_f, wd_o)), osem)
    else:
        local = []
    middle_part(
        n_ctx, n_dp, share, n_prompt, clen, depth, rest_of_prompts,
        ids, dwa, o, qpack, msgs, wo_o, wu_f, wd_f, cx, gains, valid, hist, teach,
        gdn, middle_outs, refs, leave,
    )
    for copy in leave:
        copy.wait()
    for slot in range(n_ctx):
        for g in range(groups):
            @pl.when((slot <= me) & (me < last))
            def _():
                hop(slot, g, 1, 0).wait_send()

            @pl.when((slot >= me) & (me > 0))
            def _():
                hop(slot, g, -1, 1).wait_send()

    for group in copies:
        for copy in group:
            copy.wait_send()
    for copy in local:
        copy.wait()


def full_at(a, core, split, c_split):
    b = a // split
    return a + core * split * (1 - b) + b * (split + core * c_split)


class TpSum:
    @staticmethod
    def scratch(half, width):
        n = half // CH
        return [
            pltpu.VMEM((half, width), bf16), pltpu.VMEM((half, width), bf16),
            pltpu.VMEM((half, width), bf16), pltpu.VMEM((half, width), bf16),
            pltpu.VMEM((half, width), f32), DMA((2, n)), DMA((2, n)),
        ]

    def __init__(self, half, start, place, scratch, compute):
        self.half, self.start, self.place, self.compute = half, start, place, compute
        self.snd1, self.rcv1, self.snd2, self.rcv2, self.own, self.send, self.recv = scratch
        self.core, self.mate, self.across = tp_place()
        self.n = half // CH

    def row(self, i):
        return lax.rem(self.start + i * CH, self.half)

    def pair(self, i):
        at = rows(self.row(i), CH)
        return remote(
            self.snd1.at[at], self.rcv1.at[at], self.send.at[0, i], self.recv.at[0, i], self.mate
        )

    def link(self, i):
        at = rows(self.row(i), CH)
        return remote(
            self.snd2.at[at], self.rcv2.at[at], self.send.at[1, i], self.recv.at[1, i], self.across
        )

    def second(self, i):
        at = rows(self.row(i), CH)
        self.pair(i).wait()
        self.snd2[at] = (self.own[at] + self.rcv1[at].astype(f32)).astype(bf16)
        self.link(i).start()

    def launch(self, i):
        a = self.row(i)
        at = rows(a, CH)
        self.snd1[at] = self.compute(self.place(a, 1 - self.core), CH).astype(bf16)
        self.pair(i).start()
        self.own[at] = self.compute(self.place(a, self.core), CH)

    def begin(self, held=0, after=None):
        def body(i):
            self.launch(i)

            @pl.when((i > 0) & (i <= self.n - held))
            def _():
                self.second(i - 1)

            if after is not None:
                after(i)

        loop(self.n, body)
        if not held:
            self.second(self.n - 1)

    def resume(self, held):
        for i in range(self.n - held, self.n):
            self.second(i)

    def take(self, i):
        at = rows(self.row(i), CH)
        self.link(i).wait()
        return self.snd2[at].astype(f32) + self.rcv2[at].astype(f32)

class Share:
    def __init__(self, ref, place, sems):
        self.ref, self.place = ref, place
        self.send, self.recv = sems
        _, self.mate, _ = tp_place()

    def copy(self, i, a):
        at = rows(self.place(a), CH)
        return remote(self.ref.at[at], self.ref.at[at], self.send.at[i], self.recv.at[i], self.mate)


def share_scratch(half):
    return [DMA((half // CH,)), DMA((half // CH,))]


GELU = 0.7978845608028654


def gelu_tanh(u):
    return jnp.tanh(GELU * (u + 0.044715 * (u * u * u)))


def mixed_states(ids, dwa, hist, at, y):
    mixed = dwa[4] * y
    for j in range(4):
        mixed += dwa[ids[j]] * hist[j, at].astype(f32)
    return mixed


def column(row):
    return jnp.transpose(jnp.broadcast_to(row, (128, row.shape[1])))


def down_grads(hid, dm, cols, lo, hi, store):
    for j in range(lo, hi, 128):
        store(j, dot_tn(hid[:, j:j + 128], dm[:, cols]))


def other_grads(ff, xn, du, o, da, cols, store):
    size = cols.size
    for j in range(ff // size):
        store(j * size, dot_tn(xn[:, cols], du[:, size * j:size * j + size]))
    g = dot_tn(o[...], da[:, cols])
    store(ff, g[0:128])
    store(ff + 128, g[192:256])


def middle_part(
    n_ctx, n_dp, share, n_prompt, clen, depth, between,
    ids, dwa, o, qpack, msgs, wo, wu, wd, cx, gains, valid, hist, teach, gdn, outs, refs, leave,
):
    out, dm, hid, xn, du, da, do, dh1, stat, qs = outs
    hc, tc, slope, h1, dy, mask, hsem, s_q, r_q = refs[:9]
    scratch = refs[9:]
    core, mate, across = tp_place()
    ctx = lax.axis_index("ctx")
    dp = lax.axis_index("dp")
    half = clen
    n_cont = 2 * half
    mine = rows(core * half, half)
    loads = fetch(((hist.at[:, mine], hc), (teach.at[mine], tc)), hsem)
    qs[ctx] = qpack[...]
    mask[...] = column(valid[pl.ds(core, 1)].astype(f32))
    stat[...] = jnp.zeros(stat.shape, f32)
    others = axis_peers("ctx", n_ctx)
    s1, s2, s3 = scratch[0:7], scratch[7:14], scratch[14:21]
    shares = scratch[21:29]

    def place(a, c):
        return a + c * half

    def home(a):
        return a + core * half

    def each(body):
        loop(half // CH, body)

    def attn(at, size):
        return dot(o[rows(n_prompt + at, size)], wo[...])

    first = TpSum(half, 0, place, s1, attn)
    each(first.launch)
    each(first.second)
    moves = [
        remote(qs.at[ctx], qs.at[ctx], s_q.at[d], r_q.at[d], device)
        for d, device in enumerate(others)
    ]
    between()
    leave[0].start()
    give_xn = Share(xn, home, shares[0:2])

    def normed(i):
        a = first.row(i)
        h = cx[rows(home(a), CH)].astype(f32) + first.take(i)
        h1[rows(a, CH)] = h
        whitened, _ = norm_rows(h)
        xn[rows(home(a), CH)] = (whitened * gains[2:3] + gains[3:4]).astype(bf16)
        give_xn.copy(i, a).start()

    def hidden(at, size):
        here = rows(at, size)
        u = dot(xn[here], wu[...])
        t = gelu_tanh(u)
        g = (0.5 * u * (1.0 + t)).astype(bf16)
        hid[here] = g
        slope[here] = 0.5 * (1.0 + t) + (0.5 * GELU) * u * (1.0 - t * t) * (
            1.0 + (3.0 * 0.044715) * (u * u)
        )
        return dot(g, wd[...])

    second = TpSum(half, 0, place, s2, hidden)

    def onward(before, share, after):
        def body(i):
            before(i)

            @pl.when(i > 0)
            def _():
                after.second(i - 1)

            share.copy(i, after.row(i)).wait()
            after.launch(i)

        each(body)
        after.second(after.n - 1)

    for copy in loads:
        copy.wait()
    onward(normed, give_xn, second)
    leave[2].start()
    leave[3].start()
    for copy in moves:
        copy.start()
    give_dm = Share(dm, home, shares[2:4])
    give_out = Share(out, home, shares[4:6])
    count = msgs[0:1]
    for j in range(1, n_ctx):
        count += msgs[8 * j:8 * j + 1]
    coef = (2.0 * dwa[4]) / (jnp.maximum(count, 1.0) * (1.0 * xn.shape[1]))

    def add(row, value):
        stat[row:row + 1] += jnp.sum(value, 0, keepdims=True)

    def lossy(i):
        a = second.row(i)
        here, there = rows(a, CH), rows(home(a), CH)
        y = h1[here] + second.take(i)
        mixed = mixed_states(ids, dwa, hc, here, y)
        diff = mixed - tc[here].astype(f32)
        weighted = diff * mask[here][:, 0:1]
        grad = weighted * coef[:, 0:1]
        dy[here] = grad
        dm[there] = grad.astype(bf16)
        give_dm.copy(i, a).start()
        out[there] = mixed.astype(bf16)
        give_out.copy(i, a).start()
        add(4, weighted * diff)
        for j in range(4):
            add(5 + j, weighted * hc[j, here].astype(f32))
        add(9, weighted * y)

    def back(at, size):
        here = rows(at, size)
        d = (dot_nt(dm[here], wd[...]) * slope[here]).astype(bf16)
        du[here] = d
        return dot_nt(d, wu[...])

    third = TpSum(half, 0, place, s3, back)
    onward(lossy, give_dm, third)
    leave[1].start()
    leave[4].start()
    if share:
        gsnd, grcv, gown, s_g, r_g = scratch[29:34]
        gives = []
        for d in range(1, n_dp):
            def lay(at, value, d=d):
                gsnd[d - 1, at:at + value.shape[0]] = value.astype(bf16)

            other = lax.rem(dp + d, n_dp)
            down_grads(hid, dm, pl.ds(pl.multiple_of(other * depth, 128), depth), 0, EARLY, lay)
            copy = remote(
                gsnd.at[d - 1], grcv.at[d - 1], s_g.at[d - 1], r_g.at[d - 1], {"dp": other}
            )
            copy.start()
            gives.append(copy)

        def stay(at, value):
            gown[at:at + value.shape[0]] = value

        down_grads(hid, dm, pl.ds(pl.multiple_of(dp * depth, 128), depth), 0, EARLY, stay)
    give_da = Share(da, home, shares[6:8])

    def grads(i):
        a = third.row(i)
        here = rows(a, CH)
        total = third.take(i)
        whitened, inverse = norm_rows(h1[here])
        grad = dy[here] + norm_back(total, whitened, inverse, gains[2:3])
        dh1[here] = grad
        da[rows(home(a), CH)] = grad.astype(bf16)
        give_da.copy(i, a).start()
        add(2, total * whitened)
        add(3, total)

    each(grads)
    each(lambda i: give_da.copy(i, third.row(i)).wait())

    def last(i):
        at = rows(i * BIG, BIG)
        do[at] = dot_nt(da[at], wo[...]).astype(bf16)

    loop(n_cont // BIG, last)
    each(lambda i: give_out.copy(i, second.row(i)).wait())
    for copy in moves:
        copy.wait()
    if share:
        for copy in gives:
            copy.wait()

        def settle(i):
            at = rows(i * 64, 64)
            total = gown[at]
            for d in range(n_dp - 1):
                total += grcv[d, at].astype(f32)
            gdn[at] = total.astype(bf16)

        loop(gdn.shape[0] // 64, settle)


class LineSum:
    @staticmethod
    def scratch(count, width):
        count = count * SUB
        buffer = pltpu.VMEM((count, PIECE, width), bf16)
        return [buffer, buffer, buffer, DMA((2, count)), DMA((2, count))]

    def __init__(self, me, src, dst, scratch):
        self.src, self.dst = src, dst
        self.got, self.pair, self.far, self.send, self.recv = scratch
        side = me // 2
        self.outer = (me == 0) | (me == 3)
        self.inner = (me == 1) | (me == 2)
        self.near = {"ctx": 1 + side}
        self.back = {"ctx": 3 * side}
        self.twin = {"ctx": 2 - side}

    def at(self, k):
        return rows(k * PIECE, PIECE)

    def up(self, k):
        return remote(
            self.src.at[self.at(k)], self.got.at[k], self.send.at[0, k], self.recv.at[0, k], self.near
        )

    def cross(self, k):
        return remote(
            self.pair.at[k], self.far.at[k], self.send.at[1, k], self.recv.at[1, k], self.twin
        )

    def down(self, k):
        return remote(
            self.pair.at[k], self.got.at[k], self.send.at[0, k], self.recv.at[0, k], self.back
        )

    def launch(self, k):
        @pl.when(self.outer)
        def _():
            for s in range(SUB):
                self.up(k * SUB + s).start()

    def meet(self, k):
        @pl.when(self.inner)
        def _():
            for s in range(SUB):
                j = k * SUB + s
                self.up(j).wait_recv()
                self.pair[j] = (
                    self.src[self.at(j)].astype(f32) + self.got[j].astype(f32)
                ).astype(bf16)
                self.cross(j).start()

    def turn(self, k):
        @pl.when(self.inner)
        def _():
            for s in range(SUB):
                j = k * SUB + s
                self.cross(j).wait()
                total = (self.pair[j].astype(f32) + self.far[j].astype(f32)).astype(bf16)
                self.pair[j] = total
                self.down(j).start()
                self.dst[self.at(j)] = total

    def land(self, k):
        @pl.when(self.outer)
        def _():
            for s in range(SUB):
                j = k * SUB + s
                self.up(j).wait_send()
                self.down(j).wait_recv()
                self.dst[self.at(j)] = self.got[j]

        @pl.when(self.inner)
        def _():
            for s in range(SUB):
                self.down(k * SUB + s).wait_send()


def input_grad_tail(
    n_dp, n_ctx, share, split, c_split, depth,
    dcat, w, px, cx, gains, dh1, stat_in, xn1, grad_p, grad_c, fin,
    smalls, sums, shares, prompts_out, *q_state,
):
    grad, stat, stats_m, stats_y, stats_c, stats_d, s_s, r_s, osem = smalls
    core, mate, across = tp_place()
    me = lax.axis_index("ctx")
    dp = lax.axis_index("dp")
    ctx_peers = axis_peers("ctx", n_ctx)
    dp_peers = axis_peers("dp", n_dp)
    half = split + c_split
    n_prompt = 2 * split
    n_cont = 2 * c_split
    if share:
        qsnd, qrcv, s_q, r_q, gall, line, settle_kv, n_late = q_state
        n_line = gall.shape[0] // LINE - 1
    else:
        (g_q,) = q_state

    def q_grads(cols):
        part = dot_tn(dcat[n_prompt:n_prompt + n_cont, 0:256], xn1[n_prompt:n_prompt + n_cont, cols])
        return part[0:3 * HEAD_DIM]

    gives = []
    if share:
        for d in range(1, n_dp):
            other = lax.rem(dp + d, n_dp)
            cols = pl.ds(pl.multiple_of(other * depth, 128), depth)
            qsnd[d - 1] = q_grads(cols).astype(bf16)
            copy = remote(
                qsnd.at[d - 1], qrcv.at[d - 1], s_q.at[d - 1], r_q.at[d - 1], {"dp": other}
            )
            copy.start()
            gives.append(copy)

    stat[...] = 0.5 * stat_in[...]

    def place(a, c):
        return full_at(a, c, split, c_split)

    def home(a):
        return full_at(a, core, split, c_split)

    def compute(at, size):
        part = dot(dcat[rows(at, size)], w[...])
        b = at // n_prompt
        p = px[rows(at * (1 - b), size)].astype(f32)
        c = cx[rows((at - n_prompt) * b, size)].astype(f32)
        whitened, _ = norm_rows(jnp.where(b == 0, p, c))
        stat[0:1] += jnp.sum(part * whitened, 0, keepdims=True)
        stat[1:2] += jnp.sum(part, 0, keepdims=True)
        return part

    total = TpSum(half, split, place, sums, compute)

    def also(i):
        if share:
            @pl.when(lax.rem(i, 2) == 0)
            def _():
                line.meet(2 + i // 2)

    total.begin(2, also)

    def small(src, dst, i, device):
        return remote(src, dst, s_s.at[i], r_s.at[i], device)

    stats_m[0] = stat[...]
    to_mate = small(stats_m.at[0], stats_m.at[1], 0, mate)
    to_mate.start()
    if share:
        settle_kv()
        loop(n_line - n_late, lambda k: line.launch(k + n_late))
    else:
        g_q[...] = q_grads(slice(None)).astype(bf16)
    to_mate.wait()
    stats_y[0] = stats_m[0] + stats_m[1]
    to_far = small(stats_y.at[0], stats_y.at[1], 1, across)
    to_far.start()
    total.resume(2)
    if share:
        line.meet(5)
        for copy in gives:
            copy.wait()
        value = q_grads(pl.ds(pl.multiple_of(dp * depth, 128), depth))
        for d in range(n_dp - 1):
            value += qrcv[d].astype(f32)
        gall[n_line * LINE:n_line * LINE + 3 * HEAD_DIM] = value.astype(bf16)
        line.launch(n_line)
    if share:
        line.turn(0)
        line.meet(6)
    give = Share(grad, home, shares)

    def finish(i):
        a = total.row(i)
        b = a // split
        value = total.take(i)
        p = px[rows((core * split + a) * (1 - b), CH)].astype(f32)
        c = cx[rows((core * c_split + a - split) * b, CH)].astype(f32)
        whitened, inverse = norm_rows(jnp.where(b == 0, p, c))
        back = norm_back(value, whitened, inverse, gains[0:1])
        extra = dh1[rows((a - split) * b, CH)]
        grad[rows(home(a), CH)] = jnp.where(b == 0, back, back + extra).astype(bf16)
        give.copy(i, a).start()
        if share:
            k = 1 + i + i // 3
            line.turn(k)

            @pl.when(i < 5)
            def _():
                line.meet(7 + i)

            @pl.when(lax.rem(i, 3) == 2)
            def _():
                line.turn(k + 1)

    def part(lo, hi):
        loop(hi - lo, lambda i: finish(i + lo))

    part(0, 2)
    prompts_out()
    part(2, 4)
    to_far.wait()
    stats_c[me] = stats_y[0] + stats_y[1]
    to_ctx = [
        small(stats_c.at[me], stats_c.at[me], 2 + d, device) for d, device in enumerate(ctx_peers)
    ]
    for copy in to_ctx:
        copy.start()
    part(4, 6)
    if share:
        line.turn(9)
    for copy in to_ctx:
        copy.wait()
    value = stats_c[0]
    for d in range(1, n_ctx):
        value += stats_c[d]
    stats_d[dp] = value
    to_dp = [
        small(stats_d.at[dp], stats_d.at[dp], 1 + n_ctx + d, device)
        for d, device in enumerate(dp_peers)
    ]
    for copy in to_dp:
        copy.start()
    if share:
        for k in range(10, n_line + 1):
            line.turn(k)
    loop(total.n, lambda i: give.copy(i, total.row(i)).wait())
    saves = fetch(
        ((grad.at[0:n_prompt], grad_p), (grad.at[n_prompt:n_prompt + n_cont], grad_c)), osem
    )
    for copy in to_dp:
        copy.wait()
    value = stats_d[0]
    for d in range(1, n_dp):
        value += stats_d[d]
    fin[...] = value
    if share:
        loop(n_line + 1, line.land)
    for copy in saves:
        copy.wait()


def attend_back_body(
    n_ctx, n_dp, share, plen, clen, groups, conts, depth,
    ids, dwa, msgs, do_h, o_h, lse, valid, gains, kv_h, tab_h, qs_h, hid_h, dm_h, xn2_h, du_h, da_h,
    wo_h, wu_h, wd_h, px_h, hist_h, xn1_h, w_h, cx_h, dh1_h, stat_in, *refs,
):
    if share:
        g_first, out, grad_p, grad_c, fin, g_sum = refs[:6]
        refs = refs[6:]
    else:
        out, grad_p, grad_c, fin, g_down, g_up, g_out, g_kv, g_q = refs[:9]
        refs = refs[9:]
    (
        hid, dm, xn2, du, da, wo, wu, wd, px, hist, lsem,
        dos, sts, dqs, kd, acc_k, acc_v, acc_kd, acc_vd, dq_f, send, recv,
        xp, h1, xn1, flags, do, o, kv, tab, qs, w, cx, dh1, dcat,
    ) = refs[:35]
    snd1, own = refs[35:37]
    s1 = (snd1, refs[37], refs[39], refs[38], own, *refs[40:42])
    s2 = (snd1, refs[42], refs[39], refs[43], own, *refs[44:46])
    s3 = (snd1, refs[46], refs[47], refs[48], own, *refs[49:51])
    shares = refs[51:57]
    smalls = refs[57:66]
    refs = refs[66:]
    if share:
        gsnd, grcv, s_g, r_g, qsnd, qrcv, s_q, r_q, gall = refs[:9]
        line = LineSum(me_of("ctx"), gall, g_sum, refs[9:14])
    core, mate, across = tp_place()
    me = lax.axis_index("ctx")
    dp = lax.axis_index("dp")
    peers = axis_peers("ctx", n_ctx)
    dp_peers = axis_peers("dp", n_dp) if share else []
    n_prompt = groups * plen
    n_cont = conts * clen
    half = plen
    own_rows = rows(core * half, half)
    loads = fetch(
        (
            (do_h, do), (o_h, o), (wo_h, wo), (px_h, px), (kv_h, kv), (qs_h, qs),
            (hid_h, hid), (dm_h, dm), (xn2_h, xn2), (du_h, du), (da_h, da), (wu_h, wu), (wd_h, wd),
            (tab_h, tab), (xn1_h, xn1), (hist_h.at[:, own_rows], hist),
            (w_h, w), (cx_h, cx), (dh1_h, dh1),
        )
        + (((g_first, gall.at[0:EARLY]),) if share else ()),
        lsem,
    )
    low = lanes_below((clen, 128), 64)
    zero = jnp.zeros((clen, 128), bf16)
    for c in range(conts):
        flags[c * clen:(c + 1) * clen] = column(valid[c:c + 1].astype(f32))

    loads[0].wait()
    loads[1].wait()
    g0 = do[0:clen, 128:256].astype(f32)
    g1 = do[clen:2 * clen, 128:256].astype(f32)
    dos[me, 0:n_cont] = do[:, 0:128]
    dos[me, n_cont:n_cont + clen] = jnp.where(low, pltpu.roll(g0, 64, 1), g1).astype(bf16)
    for c in range(conts):
        at = slice(c * clen, (c + 1) * clen)
        full = slice(n_prompt + c * clen, n_prompt + (c + 1) * clen)
        pa = do[at, 0:128].astype(f32) * o[full, 0:128].astype(f32)
        pe = do[at, 128:256].astype(f32) * o[full, 128:256].astype(f32)
        ta = jnp.transpose(pa)
        te = jnp.transpose(pe)
        st = 8 * c
        sts[me, st:st + 8] = lse[8 * c:8 * c + 8]
        sts[me, st + 3:st + 4] = jnp.sum(ta[0:64], 0, keepdims=True)
        sts[me, st + 4:st + 5] = jnp.sum(ta[64:128], 0, keepdims=True)
        sts[me, st + 5:st + 6] = jnp.sum(te[64:128], 0, keepdims=True)
    greet(peers + [mate, across] + dp_peers)
    sends = []
    for d, device in enumerate(peers):
        for i, ref in enumerate((sts, dos)):
            sends.append(remote(ref.at[me], ref.at[me], send.at[d, i], recv.at[d, i], device))
    for copy in sends:
        copy.start()
    if share:
        loads[19].wait()
        loop(EARLY // LINE, line.launch)

    def place(a, c):
        return a + c * half

    def home(a):
        return a + core * half

    loads[2].wait()
    loads[3].wait()

    def attn(at, size):
        return dot(o[rows(at, size)], wo[...])

    first = TpSum(half, 0, place, s1, attn)
    first.begin()

    for copy in loads[4:11]:
        copy.wait()
    ff = hid.shape[1]
    o_c = o.at[n_prompt:n_prompt + n_cont]
    late = ff - EARLY
    bounds = (0, late + ff + 192, late + ff + 576)
    def cols_of(d):
        return pl.ds(pl.multiple_of(lax.rem(dp + d, n_dp) * depth, 128), depth)

    def give(d, i):
        span = slice(bounds[i], bounds[i + 1])
        return remote(
            gsnd.at[d - 1, span], grcv.at[d - 1, span], s_g.at[d - 1, i], r_g.at[d - 1, i],
            {"dp": lax.rem(dp + d, n_dp)},
        )

    def keeper(d):
        def store(at, value):
            here = slice(at, at + value.shape[0])
            if d > 0:
                gsnd[d - 1, here] = value.astype(bf16)
            else:
                for k in range(n_dp - 1):
                    value = value + grcv[k, here].astype(f32)
                gall[EARLY + at:EARLY + at + value.shape[0]] = value.astype(bf16)

        return store

    def late_grads(cols, store):
        down_grads(hid, dm, cols, EARLY, ff, lambda at, value: store(at - EARLY, value))
        other_grads(ff, xn2, du, o_c, da, cols, lambda at, value: store(at + late, value))

    def kv_grads(cols, store):
        for lo, hi in ((256, 384), (384, 512), (512, 640)):
            store(late + ff + 192 + lo - 256, dot_tn(dcat[:, lo:hi], xn1[:, cols]))

    def settle(i):
        for d in range(1, n_dp):
            give(d, i).wait()
        (late_grads, kv_grads)[i](cols_of(0), keeper(0))

    if share:
        for d in range(1, n_dp):
            late_grads(cols_of(d), keeper(d))
            give(d, 0).start()
    else:
        width = dm.shape[1]
        for j in range(width // 256):
            cols = pl.ds(256 * j, 256)
            span = slice(256 * j, 256 * j + 256)

            def lay_down(at, value, span=span):
                g_down[at:at + 128, span] = value.astype(bf16)

            def lay(at, value, span=span):
                if at < ff:
                    g_up[span, at:at + 256] = value.astype(bf16)
                else:
                    g_out[at - ff:at - ff + value.shape[0], span] = value.astype(bf16)

            down_grads(hid, dm, cols, 0, ff, lay_down)
            other_grads(ff, xn2, du, o_c, da, cols, lay)

    kd[...] = pltpu.roll(kv[0:n_prompt, 256:384].astype(f32), 64, 1).astype(bf16)
    for acc in (acc_k, acc_v, acc_kd, acc_vd):
        acc[...] = jnp.zeros(acc.shape, f32)

    def one_head(q_rows, do_rows, k, v, lse_row, delta_row, mask):
        s = dot_nt(k, q_rows)
        p = jnp.exp(s - lse_row)
        if mask is not None:
            p = mask(p)
        dp_ = dot_nt(v, do_rows)
        ds = (p * (dp_ - delta_row)).astype(bf16)
        return p.astype(bf16), ds

    def halves(a):
        return jnp.where(low, a, zero), jnp.where(low, zero, a)

    def beside(a, keeps):
        return a if keeps is None else jnp.concatenate([a * keep for keep in keeps], 1)

    def continuation(src, c, k_b, k_c, k_d, k_s, mask, keeps):
        base = c * clen
        a0, a1 = halves(qs[src, base:base + clen])
        d0, d1 = halves(dos[src, base:base + clen])
        e = halves(qs[src, n_cont:n_cont + clen])[c]
        g = halves(dos[src, n_cont:n_cont + clen])[c]
        st = 8 * c
        row = lambda i: sts[src, st + i:st + i + 1]
        p0, s0 = one_head(a0, d0, k_b, k_c, row(0), row(3), mask)
        p1, s1_ = one_head(a1, d1, k_b, k_c, row(1), row(4), mask)
        dv = dot(jnp.concatenate([p0, p1], 1), beside(jnp.concatenate([d0, d1], 0), keeps))
        dk = dot(jnp.concatenate([s0, s1_], 1), beside(jnp.concatenate([a0, a1], 0), keeps))
        dq = jnp.where(low, dot_tn(s0, k_b), dot_tn(s1_, k_b))
        keys, values = (k_d, k_s) if c == 0 else (k_s, k_d)
        p2, s2_ = one_head(e, g, keys, values, row(2), row(5), mask)
        dvd = dot(p2, beside(g, keeps))
        dkd = dot(s2_, beside(e, keeps))
        return dk, dv, dkd, dvd, dq, dot_tn(s2_, keys)

    def source(src, own):
        pair = []
        for c in range(conts):
            pick = msgs[pl.ds(src * 8 + 1 + c, 1)]
            keeps = [(pick == 1.0 * g).astype(f32).astype(bf16) for g in range(groups)]

            def choose(ref, lo, hi):
                return sum(
                    ref[g * plen:(g + 1) * plen, lo:hi] * keep for g, keep in enumerate(keeps)
                )

            dk, dv, dkd, dvd, dqa, dqd = continuation(
                src, c, choose(kv, 0, 128), choose(kv, 128, 256), choose(kv, 256, 384),
                choose(kd, 0, 128), None, keeps,
            )
            acc_k[...] += dk
            acc_v[...] += dv
            acc_kd[...] += dkd
            acc_vd[...] += dvd
            pair.append(dqd)
            if own:
                dq_f[c * clen:(c + 1) * clen] = dqa
            else:
                dqs[n_ctx + src, c * clen:(c + 1) * clen] = dqa.astype(bf16)
        third = jnp.where(low, pair[0], pair[1])
        if own:
            dq_f[n_cont:n_cont + clen] = third
        else:
            dqs[n_ctx + src, n_cont:n_cont + clen] = third.astype(bf16)

    def other_of(d):
        return lax.rem(me + 2 * n_ctx - (d + 1), n_ctx)

    def back_copy(d):
        other = other_of(d)
        return remote(
            dqs.at[n_ctx + other], dqs.at[me], send.at[d, 2], recv.at[d, 2], {"ctx": other}
        )

    def visit(d):
        other = other_of(d)
        for i, ref in enumerate((sts, dos)):
            remote(ref.at[other], ref.at[other], send.at[d, i], recv.at[d, i], {"ctx": other}).wait_recv()
        source(other, False)
        back_copy(d).start()

    give_xn = Share(xp, home, shares[0:2])

    def normed(i):
        a = first.row(i)
        h = px[rows(home(a), CH)].astype(f32) + first.take(i)
        h1[rows(a, CH)] = h
        whitened, _ = norm_rows(h)
        xp[rows(home(a), CH)] = (whitened * gains[2:3] + gains[3:4]).astype(bf16)
        give_xn.copy(i, a).start()

    def hidden(at, size):
        u = dot(xp[rows(at, size)], wu[...])
        return dot((0.5 * u * (1.0 + gelu_tanh(u))).astype(bf16), wd[...])

    second = TpSum(half, 0, place, s2, hidden)
    source(me, True)
    for copy in loads[11:13]:
        copy.wait()

    def step(i):
        @pl.when(i < first.n)
        def _():
            normed(i)

        @pl.when((i > 0) & (i <= first.n))
        def _():
            second.second(i - 1)

        @pl.when((i > 0) & (i < n_ctx))
        def _():
            visit(i - 1)

        @pl.when(i < first.n)
        def _():
            give_xn.copy(i, first.row(i)).wait()
            second.launch(i)

    loop(max(half // CH + 1, n_ctx), step)
    if share:
        settle(0)
        n_late = (EARLY + bounds[1]) // LINE
        loop(n_late - EARLY // LINE, lambda k: line.launch(k + EARLY // LINE))
        loop(EARLY // LINE, line.meet)
    loads[13].wait()

    for c in range(conts):
        at = slice(n_prompt + c * clen, n_prompt + (c + 1) * clen)
        k_d = kv[at, 256:384]
        k_s = pltpu.roll(k_d.astype(f32), 64, 1).astype(bf16)

        def mask(p):
            key = lax.broadcasted_iota(jnp.int32, p.shape, 0)
            query = lax.broadcasted_iota(jnp.int32, p.shape, 1)
            return jnp.where(
                key <= query, p * flags[c * clen:(c + 1) * clen, 0:1], 0.0
            )

        dk, dv, dkd, dvd, dqa, dqd = continuation(
            me, c, kv[at, 0:128], kv[at, 128:256], k_d, k_s, mask, None
        )
        dq_f[c * clen:(c + 1) * clen] += dqa
        keep = low if c == 0 else jnp.logical_not(low)
        dq_f[n_cont:n_cont + clen] += jnp.where(keep, dqd, 0.0)
        t = tab[plen:plen + clen]
        dcat[at, 256:384] = turn(dk, t, -1.0, False).astype(bf16)
        dcat[at, 384:512] = dv.astype(bf16)
        if c == 0:
            joined = jnp.where(low, dkd, pltpu.roll(dvd, 64, 1))
        else:
            joined = jnp.where(low, pltpu.roll(dkd, 64, 1), dvd)
        dcat[at, 512:640] = turn(joined, t, -1.0, True).astype(bf16)

    zq = jnp.zeros((plen, 256), bf16)
    wide = lanes_below((plen, 128), 64)
    for g in range(groups):
        at = slice(g * plen, (g + 1) * plen)
        t = tab[0:plen]
        dcat[at, 0:256] = zq
        part = slice(128 * g, 128 * g + 128)
        dcat[at, 256:384] = turn(acc_k[:, part], t, -1.0, False).astype(bf16)
        dcat[at, 384:512] = acc_v[:, part].astype(bf16)
        k2 = acc_kd[:, part] + pltpu.roll(acc_kd[:, part], 64, 1)
        v2 = acc_vd[:, part] + pltpu.roll(acc_vd[:, part], 64, 1)
        dcat[at, 512:640] = turn(jnp.where(wide, k2, v2), t, -1.0, True).astype(bf16)

    loads[14].wait()
    if share:
        for d in range(1, n_dp):
            kv_grads(cols_of(d), keeper(d))
            give(d, 1).start()
    else:
        for j in range(xn1.shape[1] // 256):
            span = slice(256 * j, 256 * j + 256)

            def lay_kv(at, value, span=span):
                at = at - late - ff - 192
                g_kv[at:at + 128, span] = value.astype(bf16)

            kv_grads(pl.ds(256 * j, 256), lay_kv)

    for d in range(n_ctx - 1):
        back_copy(d).wait_send()
        other = lax.rem(me + d + 1, n_ctx)
        remote(
            dqs.at[n_ctx + other], dqs.at[other], send.at[d, 2], recv.at[d, 2], {"ctx": other}
        ).wait_recv()
        dq_f[...] += dqs[other].astype(f32)
    for c in range(conts):
        at = slice(n_prompt + c * clen, n_prompt + (c + 1) * clen)
        t = tab[plen:plen + clen]
        pair = dq_f[c * clen:(c + 1) * clen] * 0.125
        dcat[at, 0:128] = turn(pair, t, -1.0, False).astype(bf16)
        third = dq_f[n_cont:n_cont + clen] * 0.125
        if c == 1:
            third = pltpu.roll(third, 64, 1)
        third = jnp.where(low, third, 0.0)
        dcat[at, 128:256] = turn(third, t, -1.0, True).astype(bf16)

    give_out = Share(out, home, shares[2:4])

    def mixed(i):
        a = second.row(i)
        here = rows(a, CH)
        y = h1[here] + second.take(i)
        out[rows(home(a), CH)] = mixed_states(ids, dwa, hist, here, y).astype(bf16)
        give_out.copy(i, a).start()

    def prompts_out():
        loads[15].wait()
        loop(half // CH, mixed)

    for copy in loads[16:19]:
        copy.wait()
    if share:
        q_state = (qsnd, qrcv, s_q, r_q, gall, line, lambda: settle(1), n_late)
    else:
        q_state = (g_q,)
    input_grad_tail(
        n_dp, n_ctx, share, plen, clen, depth,
        dcat, w, px, cx, gains, dh1, stat_in, xn1, grad_p, grad_c, fin,
        smalls, s3, shares[4:6], prompts_out, *q_state,
    )
    loop(half // CH, lambda i: give_out.copy(i, second.row(i)).wait())
    for copy in sends:
        copy.wait_send()


def output_body(
    n_ctx, n_dp, share, ff,
    ids, msgs, fin, p_out, c_out, p_grad, c_grad, *refs,
):
    n = 1 if share else 0
    parts = refs[:n]
    p_out_o, c_out_o, p_grad_o, c_grad_o, loss, dwa_g, g1, b1, g2, b2 = refs[n:n + 10]
    refs = refs[n + 10:]
    if share:
        results = refs[:4]
        refs = refs[4:]
    held, sem = refs[:4], refs[4]
    if share:
        g_all, r_qkv, r_out, r_up, r_down, gsem = refs[5:]
        g_read = pltpu.make_async_copy(parts[0], g_all, gsem.at[4])
        g_read.start()
    moves = (
        (p_out, p_out_o), (c_out, c_out_o), (p_grad, p_grad_o), (c_grad, c_grad_o)
    )
    reads = [
        pltpu.make_async_copy(s, h, sem.at[0, i]) for i, ((s, _), h) in enumerate(zip(moves, held))
    ]
    copies = [
        pltpu.make_async_copy(h, t, sem.at[1, i]) for i, ((_, t), h) in enumerate(zip(moves, held))
    ]
    for copy in reads:
        copy.start()
    depth = g1.shape[0]
    width = fin.shape[1]
    for read, copy in zip(reads, copies):
        read.wait()
        copy.start()
    if share:
        done = [
            pltpu.make_async_copy(s, r, gsem.at[i])
            for i, (s, r) in enumerate(zip((r_qkv, r_out, r_up, r_down), results))
        ]
        g_read.wait()
        rest = g_all.at[ff:]
        r_down[...] = g_all[0:ff].astype(f32)
        done[3].start()
        for j in range(ff // depth):
            r_up[:, j * depth:(j + 1) * depth] = rest[j * depth:(j + 1) * depth].astype(f32)
        done[2].start()
        r_out[...] = rest[ff:ff + 192].astype(f32)
        done[1].start()
        base = ff + 192
        r_qkv[1, 0:128] = rest[base:base + 128].astype(f32)
        r_qkv[2, 0:128] = rest[base + 128:base + 256].astype(f32)
        r_qkv[1, 128:192] = rest[base + 256:base + 320].astype(f32)
        r_qkv[2, 128:192] = rest[base + 320:base + 384].astype(f32)
        r_qkv[0] = rest[base + 384:base + 576].astype(f32)
        done[0].start()
        copies = copies + done
    count = msgs[0:1, 0:1]
    for j in range(1, n_ctx):
        count += msgs[8 * j:8 * j + 1, 0:1]
    factor = 1.0 / (jnp.maximum(count, 1.0) * (1.0 * width))
    sums = jnp.sum(fin[...], -1, keepdims=True) * factor
    row = lax.broadcasted_iota(jnp.int32, sums.shape, 0)

    def entry(i):
        return jnp.sum(jnp.where(row == i, sums, 0.0))

    loss[0] = entry(4)
    for k in range(4):
        value = 0.0
        for j in range(4):
            value += jnp.where(ids[j] == k, 2.0 * entry(5 + j), 0.0)
        dwa_g[k] = value
    dwa_g[4] = 2.0 * entry(9)
    for i, ref in enumerate((g1, b1, g2, b2)):
        if share:
            ref[...] = fin[i, pl.ds(pl.multiple_of(lax.axis_index("dp") * depth, 128), depth)]
        else:
            piece = jnp.zeros((1, depth), f32)
            for d in range(n_dp):
                here = fin[i:i + 1, d * depth:(d + 1) * depth]
                piece += jnp.where(lax.axis_index("dp") == d, here, 0.0)
            ref[...] = piece.reshape(depth)
    for copy in copies:
        copy.wait()


def per_device(
    n_dp, n_ctx,
    prompt_x, cont_x, prompt_hist, cont_hist, teacher, valid_mask, cont_group, layer_ids,
    dwa_weights, qkv_weight, out_weight, up_weight, down_weight,
    ln1_gain, ln1_bias, ln2_gain, ln2_bias,
):
    groups, plen, width = prompt_x.shape
    conts, clen, _ = cont_x.shape
    depth = qkv_weight.shape[0]
    n_prompt, n_cont = groups * plen, conts * clen
    n_rows = n_prompt + n_cont
    split, c_split = n_prompt // 2, n_cont // 2
    half = split + c_split
    ff = up_weight.shape[1]
    share = depth % 128 == 0
    packed = n_cont + clen
    tab_rows = plen + clen
    vmem = pltpu.VMEM

    w_t = qkv_weight.transpose(1, 2, 0)
    px = prompt_x.reshape(n_prompt, width)
    cx = cont_x.reshape(n_cont, width)
    vectors = (ln1_gain, ln1_bias, ln2_gain, ln2_bias)
    states = vmem((3 * (n_prompt // clen + conts), clen, 128), f32)
    if share:
        given = (out_weight, up_weight, down_weight)
    else:
        out_w = lax.all_gather(out_weight, "dp", axis=1, tiled=True)
        given = (
            jnp.concatenate([out_w[:128], jnp.zeros((64, width), bf16), out_w[128:]], 0),
            lax.all_gather(up_weight, "dp", axis=0, tiled=True),
            lax.all_gather(down_weight, "dp", axis=1, tiled=True),
        )
    outs = [
        ((n_rows, width), bf16), ((n_rows, 384), bf16), ((tab_rows, 384), f32),
        ((640, width), bf16),
        ((n_rows, 256), bf16), ((8 * conts, clen), f32), ((8 * n_ctx, 128), f32),
        ((8, width), f32),
        ((n_cont, width), bf16), ((n_cont, width), bf16), ((n_cont, ff), bf16),
        ((n_cont, width), bf16), ((n_cont, ff), bf16), ((n_cont, width), bf16),
        ((n_cont, 256), bf16), ((c_split, width), f32), ((16, width), f32),
        ((n_ctx, packed, 128), bf16),
    ]
    out_specs = (
        [HBM_SPEC] * 5 + [VMEM_SPEC] * 4 + [HBM_SPEC] * 4 + [VMEM_SPEC] * 5
    )
    leaving = [vmem(s, d) for s, d in outs[4:5] + outs[9:13]] + [DMA((5,))]
    whole_out = vmem((256, width), bf16)
    extra = []
    held = [whole_out]
    if share:
        outs += [
            ((EARLY, depth), bf16), ((width, ff), bf16), ((ff, width), bf16), ((256, width), bf16),
        ]
        out_specs += [VMEM_SPEC] + [HBM_SPEC] * 2 + [VMEM_SPEC]
        held = like(*given)
        extra = [
            vmem((n_dp - 1, EARLY, depth), bf16), vmem((n_dp - 1, EARLY, depth), bf16),
            vmem((EARLY, depth), f32), DMA((n_dp - 1,)), DMA((n_dp - 1,)),
        ]
    got = kernel_call(
        functools.partial(front_body, n_ctx, n_dp, share, plen, clen, groups, conts),
        outs,
        [
            vmem((packed, 128), bf16),
            vmem((n_rows, width), bf16), vmem((n_rows, 256), bf16),
            vmem((n_ctx, n_prompt, 384), bf16), vmem((n_cont, 384), bf16),
            vmem((tab_rows, 384), f32), vmem((640, width), bf16),
            vmem((8, depth), f32), vmem((n_dp, 8, depth), f32),
            vmem((8, 128), f32), vmem((n_dp, 8, 128), f32), vmem((n_ctx, 8, 128), f32),
            states, states, states,
            vmem((1, 3, 192, depth) if share else (n_dp, 3, 192, depth), bf16),
            DMA((n_dp - 1, 7)), DMA((n_dp - 1, 7)),
            DMA((2, n_ctx, groups)), DMA((n_ctx, groups)), DMA((n_ctx - 1,)), DMA((n_ctx - 1,)),
            DMA((n_dp - 1, 4)), DMA((n_dp - 1, 4)), DMA((9,)),
        ]
        + like(w_t, px, cx)
        + [DMA((6,)), vmem((width, ff), bf16), vmem((ff, width), bf16)]
        + held
        + [
            vmem((4, c_split, width), bf16), vmem((c_split, width), bf16),
            vmem((n_cont, ff), f32), vmem((c_split, width), f32),
            vmem((c_split, width), f32), vmem((clen, 128), f32),
            DMA((2,)), DMA((n_ctx - 1,)), DMA((n_ctx - 1,)),
        ]
        + TpSum.scratch(c_split, width) * 3
        + share_scratch(c_split) * 4
        + extra
        + leaving,
        0,
        [SMEM_SPEC] * 3 + [HBM_SPEC] * 3 + [VMEM_SPEC] * 5 + [HBM_SPEC] * 5,
        (
            cont_group, layer_ids, dwa_weights, px, cx, w_t, *vectors, valid_mask, *given,
            cont_hist.reshape(4, n_cont, width), teacher.reshape(n_cont, width),
        ),
        "front",
        out_specs,
    )
    xn1, kv, tab, w_full, o, lse, msgs, gains = got[:8]
    cont_out, dm, hid, xn2, du, da, do, dh1, stat, qs = got[8:18]
    if share:
        g_first = [got[18]]
        wu, wd, wo = got[19:22]
    else:
        g_first = []
        wo, wu, wd = given

    grad_rows = 2 * ff + 12 * HEAD_DIM
    outs = [
        ((n_prompt, width), bf16), ((n_prompt, width), bf16), ((n_cont, width), bf16),
        ((16, width), f32),
    ]
    out_specs = [VMEM_SPEC] + [HBM_SPEC] * 2 + [VMEM_SPEC]
    if share:
        outs += [((grad_rows, depth), bf16)]
        out_specs += [VMEM_SPEC]
        late = grad_rows - EARLY - 3 * HEAD_DIM
        third = (n_dp - 1, 3 * HEAD_DIM, depth)
        extra = [
            vmem((n_dp - 1, late, depth), bf16), vmem((n_dp - 1, late, depth), bf16),
            DMA((n_dp - 1, 2)), DMA((n_dp - 1, 2)),
            vmem(third, bf16), vmem(third, bf16),
            DMA((n_dp - 1,)), DMA((n_dp - 1,)), vmem((grad_rows, depth), bf16),
        ] + LineSum.scratch(grad_rows // LINE, depth)
    else:
        outs += [
            ((ff, width), bf16), ((width, ff), bf16), ((3 * HEAD_DIM, width), bf16),
            ((384, width), bf16), ((3 * HEAD_DIM, width), bf16),
        ]
        out_specs += [VMEM_SPEC] * 5
        extra = []
    acc = vmem((plen, 128 * groups), f32)
    wide = vmem((split, width), bf16)
    tall = vmem((half, width), bf16)
    n_p, n_h = split // CH, half // CH
    back = kernel_call(
        functools.partial(
            attend_back_body, n_ctx, n_dp, share, plen, clen, groups, conts, depth
        ),
        outs,
        [
            vmem((n_cont, ff), bf16), vmem((n_cont, width), bf16),
            vmem((n_cont, width), bf16), vmem((n_cont, ff), bf16),
            vmem((n_cont, width), bf16), vmem((256, width), bf16),
            vmem((width, ff), bf16), vmem((ff, width), bf16),
            vmem((n_prompt, width), bf16), vmem((4, split, width), bf16), DMA((20,)),
            vmem((n_ctx, packed, 128), bf16), vmem((n_ctx, 8 * conts, clen), f32),
            vmem((2 * n_ctx, packed, 128), bf16), vmem((n_prompt, 128), bf16),
            acc, acc, acc, acc, vmem((packed, 128), f32),
            DMA((n_ctx - 1, 3)), DMA((n_ctx - 1, 3)),
            vmem((n_prompt, width), bf16), vmem((split, width), f32),
            vmem((n_rows, width), bf16), vmem((n_cont, 128), f32),
        ]
        + like(do, o, kv, tab, qs, w_full, cx, dh1)
        + [
            vmem((n_rows, 640), bf16), tall, vmem((half, width), f32),
            wide, wide, wide, DMA((2, n_p)), DMA((2, n_p)),
            wide, wide, DMA((2, n_p)), DMA((2, n_p)),
            tall, tall, tall, DMA((2, n_h)), DMA((2, n_h)),
        ]
        + share_scratch(split) * 2
        + share_scratch(half)
        + [
            vmem((n_rows, width), bf16), vmem((16, width), f32), vmem((2, 16, width), f32),
            vmem((2, 16, width), f32), vmem((n_ctx, 16, width), f32),
            vmem((n_dp, 16, width), f32),
            DMA((1 + n_ctx + n_dp,)), DMA((1 + n_ctx + n_dp,)), DMA((2,)),
        ]
        + extra,
        2,
        [SMEM_SPEC] * 2
        + [VMEM_SPEC] + [HBM_SPEC] * 2 + [VMEM_SPEC] * 3 + [HBM_SPEC] * 17 + [VMEM_SPEC]
        + [HBM_SPEC] * len(g_first),
        (
            layer_ids, dwa_weights, msgs, do, o, lse, valid_mask, gains, kv, tab, qs,
            hid, dm, xn2, du, da, wo, wu, wd, px, prompt_hist.reshape(4, n_prompt, width), xn1,
            w_full, cx, dh1, stat, *g_first,
        ),
        "back",
        out_specs,
    )
    prompt_out, grad_p, grad_c, fin = back[:4]

    outs = [
        ((n_prompt, width), bf16), ((n_cont, width), bf16), ((n_prompt, width), bf16),
        ((n_cont, width), bf16), ((1,), f32), ((5,), f32),
    ] + [((depth,), f32)] * 4
    out_specs = [HBM_SPEC] * 4 + [SMEM_SPEC] * 2 + [VMEM_SPEC] * 4
    specs = [SMEM_SPEC] + [VMEM_SPEC] * 2 + [HBM_SPEC] * 4
    args = (layer_ids, msgs, fin, prompt_out, cont_out, grad_p, grad_c)
    if share:
        shapes = [(3, 192, depth), (192, depth), (depth, ff), (ff, depth)]
        outs += [(s, f32) for s in shapes]
        out_specs += [HBM_SPEC] * 4
        args += (back[4],)
        specs += [HBM_SPEC]
        held_grads = like(back[4]) + [vmem(s, f32) for s in shapes] + [DMA((5,))]
    else:
        held_grads = []
    done = pl.pallas_call(
        functools.partial(output_body, n_ctx, n_dp, share, ff),
        out_shape=[jax.ShapeDtypeStruct(s, d) for s, d in outs],
        in_specs=specs,
        out_specs=out_specs,
        scratch_shapes=[
            vmem((n_prompt, width), bf16), vmem((n_cont, width), bf16),
            vmem((n_prompt, width), bf16), vmem((n_cont, width), bf16), DMA((2, 4)),
        ]
        + held_grads,
        compiler_params=pltpu.CompilerParams(vmem_limit_bytes=LIMIT),
        name="outputs",
    )(*args)
    if share:
        r_qkv, r_out, r_up, r_down = done[10:]
        r_qkv = r_qkv.transpose(2, 0, 1)
    else:
        def scattered(g, dim):
            part = lax.psum_scatter(g, "dp", scatter_dimension=dim, tiled=True)
            return lax.psum(part, "ctx").astype(f32)

        g_down, g_up, g_out, g_kv, g_q = back[4:]
        r_down = scattered(g_down, 1)
        r_up = scattered(g_up, 0)
        r_out = scattered(g_out, 1)
        g_k = jnp.concatenate([g_kv[0:128], g_kv[256:320]], 0)
        g_v = jnp.concatenate([g_kv[128:256], g_kv[320:384]], 0)
        r_qkv = scattered(jnp.stack([g_q, g_k, g_v]).transpose(2, 0, 1), 0)
    return (
        done[0].reshape(groups, plen, width),
        done[1].reshape(conts, clen, width),
        done[4].reshape(()),
        done[2].reshape(groups, plen, width),
        done[3].reshape(conts, clen, width),
        r_qkv, r_out, r_up, r_down,
        done[6], done[7], done[8], done[9],
        done[5],
    )


def solution(mesh):
    n_dp, n_ctx = mesh.shape["dp"], mesh.shape["ctx"]
    in_specs = (
        P("dp", "ctx", None), P(("dp", "ctx"), None, None), P(None, "dp", "ctx", None),
        P(None, ("dp", "ctx"), None, None), P(("dp", "ctx"), None, None), P(("dp", "ctx"), None),
        P(("dp", "ctx")), P(), P(), P("dp", None, "tp"), P("tp", "dp"), P("dp", "tp"),
        P("tp", "dp"), P("dp"), P("dp"), P("dp"), P("dp"),
    )
    out_specs = (
        P("dp", "ctx", None), P(("dp", "ctx"), None, None), P(), P("dp", "ctx", None),
        P(("dp", "ctx"), None, None), P("dp", None, "tp"), P("tp", "dp"), P("dp", "tp"),
        P("tp", "dp"), P("dp"), P("dp"), P("dp"), P("dp"), P(),
    )
    return jax.shard_map(
        functools.partial(per_device, n_dp, n_ctx),
        mesh=mesh, in_specs=in_specs, out_specs=out_specs, check_vma=False,
    )
```

```python
import functools
import math

import jax
import jax.numpy as jnp
from jax import lax
from jax.experimental import pallas as pl
from jax.experimental.pallas import tpu as pltpu
from jax.sharding import PartitionSpec as P

HEAD_DIM = 64
EPS = 1e-05
NEG = -1e30
MESH = pl.DeviceIdType.MESH
f32 = jnp.float32
bf16 = jnp.bfloat16
VMEM_SPEC = pl.BlockSpec(memory_space=pltpu.VMEM)
SMEM_SPEC = pl.BlockSpec(memory_space=pltpu.SMEM)
HBM_SPEC = pl.BlockSpec(memory_space=pl.ANY)
DMA = pltpu.SemaphoreType.DMA
LIMIT = 62 << 20
NT = (((1,), (1,)), ((), ()))
TN = (((0,), (0,)), ((), ()))
CH = 128
BIG = 256
LINE = 192
SUB = 2
PIECE = LINE // SUB
EARLY = 2 * LINE


def dot(a, b):
    return jnp.dot(a, b, preferred_element_type=f32)


def dot_nt(a, b):
    return lax.dot_general(a, b, NT, preferred_element_type=f32)


def dot_tn(a, b):
    return lax.dot_general(a, b, TN, preferred_element_type=f32)


def rows(start, size):
    return pl.ds(pl.multiple_of(start, size), size)


def loop(count, body):
    def step(i, carry):
        body(i)
        return carry

    lax.fori_loop(0, count, step, 0)


def kernel_call(body, outs, scratch, cid, specs, args, name, out_specs=None):
    return pl.pallas_call(
        body,
        out_shape=[jax.ShapeDtypeStruct(s, d) for s, d in outs],
        in_specs=specs,
        out_specs=out_specs or [VMEM_SPEC] * len(outs),
        scratch_shapes=scratch,
        compiler_params=pltpu.CompilerParams(
            collective_id=cid, has_side_effects=True, vmem_limit_bytes=LIMIT
        ),
        cost_estimate=pl.CostEstimate(flops=0, bytes_accessed=30 << 20, transcendentals=0),
        name=name,
    )(*args)


def greet(partners):
    barrier = pltpu.get_barrier_semaphore()
    for device in partners:
        pl.semaphore_signal(barrier, inc=1, device_id=device, device_id_type=MESH)
    pl.semaphore_wait(barrier, len(partners))


def remote(src, dst, send, recv, device):
    return pltpu.make_async_remote_copy(
        src_ref=src,
        dst_ref=dst,
        send_sem=send,
        recv_sem=recv,
        device_id=device,
        device_id_type=MESH,
    )


def fetch(pairs, sems):
    copies = [pltpu.make_async_copy(s, d, sems.at[i]) for i, (s, d) in enumerate(pairs)]
    for copy in copies:
        copy.start()
    return copies


def like(*arrays):
    return [pltpu.VMEM(a.shape, a.dtype) for a in arrays]


def axis_peers(axis, count):
    me = lax.axis_index(axis)
    return [{axis: lax.rem(me + d, count)} for d in range(1, count)]


def me_of(axis):
    return lax.axis_index(axis)


def tp_place():
    tp = lax.axis_index("tp")
    core = lax.rem(tp, 2)
    mate = {"tp": tp + 1 - 2 * core}
    across = {"tp": lax.rem(tp + 2, 4)}
    return core, mate, across


def norm_rows(x):
    mean = jnp.mean(x, -1, keepdims=True)
    centered = x - mean
    var = jnp.mean(centered * centered, -1, keepdims=True)
    inverse = lax.rsqrt(var + EPS)
    return centered * inverse, inverse


def norm_back(gradient, whitened, inverse, gain):
    e = gradient * gain
    return inverse * (
        e - jnp.mean(e, -1, keepdims=True) - whitened * jnp.mean(e * whitened, -1, keepdims=True)
    )


def lanes_below(shape, bound):
    return lax.broadcasted_iota(jnp.int32, shape, len(shape) - 1) < bound


def turn(y, tab, sign, half):
    cos, low, high = tab[:, :128], tab[:, 128:256], tab[:, 256:384]
    turned = sign * (pltpu.roll(y, 96, 1) * low + pltpu.roll(y, 32, 1) * high)
    if not half:
        return y * cos + turned
    return jnp.where(lanes_below(y.shape, 64), y * cos + turned, y)


W_PARTS = ((1, 0, 128, 256), (2, 0, 128, 384), (1, 128, 64, 512), (2, 128, 64, 576), (0, 0, 192, 0))


def front_body(
    n_ctx, n_dp, share, plen, clen, groups, conts,
    sel, ids, dwa, px_h, cx_h, w_h, g1, b1, g2, b2, valid, wo_h, wu_h, wd_h, hist, teach, *refs,
):
    xn_o, kv_o, tab_o, w_o, o_o, lse, msgs, gains = refs[:8]
    out, *big, da, do, dh1, stat, qs = refs[8:18]
    o, *kept, ksem = refs[-6:]
    middle_outs = (out, *kept, da, do, dh1, stat, qs)
    leave = [
        pltpu.make_async_copy(s, d, ksem.at[i])
        for i, (s, d) in enumerate(zip((o, *kept), (o_o, *big)))
    ]
    refs = refs[18:-6]
    if share:
        gdn, wu_o, wd_o, wo_o = refs[:4]
        refs = refs[4:]
    (
        qpack, xn, q, kvs, kvc, tab, w_full, gb, gbs, cnt, cnts, notes, m_s, l_s, acc_s,
        wgs, s_x, r_x, s_kv, r_kv, s_c, r_c, s_w, r_w, osem, w, px, cx, lsem, wu_f, wd_f,
    ) = refs[:31]
    refs = refs[31:]
    if share:
        wo, wu, wd = refs[:3]
        refs = refs[3:]
        weight_pairs = ((wo_h, wo), (wu_h, wu), (wd_h, wd))
    else:
        wo_o = refs[0]
        gdn = None
        refs = refs[1:]
        weight_pairs = ((wo_h, wo_o), (wu_h, wu_f), (wd_h, wd_f))
    core, mate, across = tp_place()
    loads = fetch(((w_h, w), (px_h, px), (cx_h, cx)) + weight_pairs, lsem)
    me = lax.axis_index("ctx")
    mine = lax.axis_index("dp")
    depth = w.shape[2]
    width = px.shape[1]
    last = n_ctx - 1
    n_prompt = groups * plen
    n_cont = conts * clen
    tile = clen
    dp_peers = axis_peers("dp", n_dp)
    peers = axis_peers("ctx", n_ctx)
    for i, vector in enumerate((g1, b1, g2, b2)):
        gb[i:i + 1] = vector[...].astype(f32).reshape(1, depth)
    gb[4:8] = jnp.zeros((4, depth), f32)
    cnt[...] = jnp.zeros(cnt.shape, f32) + jnp.sum(valid[...].astype(f32))
    greet(dp_peers + peers + [mate, across])
    loads[0].wait()

    copies = []
    weights = []
    if share:
        cols = pl.ds(pl.multiple_of(mine * depth, 128), depth)
        here = rows(mine * depth, depth)
    for d, device in enumerate(dp_peers):
        pairs = [(gb, gbs.at[mine]), (cnt, cnts.at[mine])]
        if share:
            pairs += [
                (w.at[p, a:a + n], w_full.at[t:t + n, cols]) for p, a, n, t in W_PARTS
            ]
        else:
            pairs += [(w, wgs.at[mine])]
        copies.append(
            [remote(s, t, s_x.at[d, i], r_x.at[d, i], device) for i, (s, t) in enumerate(pairs)]
        )
    for i in range(len(copies[0])):
        for group in copies:
            group[i].start()
    local = []
    if share:
        for p, a, n, t in W_PARTS:
            w_full[t:t + n, cols] = w[p, a:a + n]
    else:
        wgs[mine] = w[...]
    for copy in loads[1:]:
        copy.wait()
    if share:
        pairs = [
            (wo.at[0:128], wo_o.at[0:128, cols]), (wo.at[128:192], wo_o.at[192:256, cols]),
            (wu, wu_f.at[here]), (wd, wd_f.at[:, cols]),
        ]
        for d, device in enumerate(dp_peers):
            for i, (s, t) in enumerate(pairs):
                weights.append(remote(s, t, s_w.at[d, i], r_w.at[d, i], device))
        for copy in weights:
            copy.start()
        local += fetch(pairs, osem)
    if share:
        wo_o[128:192] = jnp.zeros((64, width), bf16)
    w_full[192:256] = jnp.zeros((64, width), bf16)
    gbs[mine] = gb[...]
    cnts[mine] = cnt[...]

    def table(count, base, start):
        def body(i):
            shape = (CH, 128)
            lane = lax.broadcasted_iota(jnp.int32, shape, 1)
            row = lax.broadcasted_iota(jnp.int32, shape, 0)
            turns = lax.rem(lane, 32).astype(f32) * (-2.0 * math.log(10000.0) / HEAD_DIM)
            angle = (row + (start + i * CH)).astype(f32) * jnp.exp(turns)
            sin = jnp.sin(angle)
            left = lax.rem(lane, 64) < 32
            at = rows(base + i * CH, CH)
            tab[at, 0:128] = jnp.cos(angle)
            tab[at, 128:256] = jnp.where(left, -sin, 0.0)
            tab[at, 256:384] = jnp.where(left, 0.0, sin)

        loop(count // CH, body)

    table(plen, 0, me * plen)
    table(clen, plen, n_ctx * plen)

    def save(src, dst, i):
        copy = pltpu.make_async_copy(src, dst, osem.at[i])
        copy.start()
        local.append(copy)

    save(tab, tab_o, 4)
    for group in copies:
        group[0].wait_recv()
        group[1].wait_recv()

    def one_hot(d):
        row = lax.broadcasted_iota(jnp.int32, (depth, width), 0) + d * depth
        col = lax.broadcasted_iota(jnp.int32, (depth, width), 1)
        return (row == col).astype(f32).astype(bf16)

    total = jnp.zeros(gains.shape, f32)
    count = jnp.zeros(cnt.shape, f32)
    for d in range(n_dp):
        total += dot(gbs[d].astype(bf16), one_hot(d))
        count += cnts[d]
    gains[...] = total
    note = notes.at[me]
    notes[me] = count
    for i in range(conts):
        notes[me, 1 + i:2 + i] = jnp.zeros((1, 128), f32) + sel[i].astype(f32)
    counts = [remote(note, note, s_c.at[d], r_c.at[d], device) for d, device in enumerate(peers)]
    for copy in counts:
        copy.start()

    def norm_part(x, base):
        def body(i):
            whitened, _ = norm_rows(x[rows(i * CH, CH)].astype(f32))
            xn[rows(base + i * CH, CH)] = (whitened * gains[0:1] + gains[1:2]).astype(bf16)

        loop(x.shape[0] // CH, body)

    norm_part(px, 0)
    norm_part(cx, n_prompt)
    save(xn, xn_o, 5)

    def arrive(i):
        if share:
            for group in copies:
                group[2 + i].wait_recv()
        elif i == 0:
            for group in copies:
                group[2].wait_recv()
            for p, a, n, t in W_PARTS:
                part = jnp.zeros((n, width), f32)
                for d in range(n_dp):
                    part += dot(wgs[d, p, a:a + n], one_hot(d))
                w_full[t:t + n] = part.astype(bf16)

    def hop(slot, g, step, side):
        there = kvs.at[slot, rows(g * plen, plen)]
        return remote(there, there, s_kv.at[side, slot, g], r_kv.at[slot, g], {"ctx": me + step})

    def kv_rows(count, base, tab_base, period, dst, first):
        def body(i):
            at = rows(first + i * BIG, BIG)
            t = tab[rows(tab_base + lax.rem(i * BIG, period), BIG)]
            x = xn[rows(base + i * BIG, BIG)]
            y = dot_nt(x, w_full[256:512])
            dst[at, 0:128] = turn(y[:, 0:128], t, 1.0, False).astype(bf16)
            dst[at, 128:256] = y[:, 128:256].astype(bf16)
            dst[at, 256:384] = turn(dot_nt(x, w_full[512:640]), t, 1.0, True).astype(bf16)

        loop(count // BIG, body)

    def q_rows_of(count, base, tab_base, period):
        def body(i):
            at = rows(base + i * BIG, BIG)
            t = tab[rows(tab_base + lax.rem(i * BIG, period), BIG)]
            y = dot_nt(xn[at], w_full[0:256])
            q[at, 0:128] = (turn(y[:, 0:128], t, 1.0, False) * 0.125).astype(bf16)
            q[at, 128:256] = (turn(y[:, 128:256], t, 1.0, True) * 0.125).astype(bf16)

        loop(count // BIG, body)

    for i in range(4):
        arrive(i)

    def send_own(g):
        kv_rows(plen, g * plen, 0, plen, kvs.at[me], g * plen)

        @pl.when(me < last)
        def _():
            hop(me, g, 1, 0).start()

        @pl.when(me > 0)
        def _():
            hop(me, g, -1, 1).start()

    loop(groups, send_own)
    save(kvs.at[me], kv_o.at[0:n_prompt], 6)
    kv_rows(n_cont, n_prompt, plen, clen, kvc, 0)
    save(kvc, kv_o.at[n_prompt:n_prompt + n_cont], 7)
    arrive(4)
    save(w_full, w_o, 8)
    q_rows_of(n_cont, n_prompt, plen, clen)
    q_rows_of(n_prompt, 0, 0, plen)

    def update(at, q_rows, k, v, mask, first):
        s = dot_nt(q_rows, k)
        if mask is not None:
            s = mask(s)
        top = jnp.max(s, -1, keepdims=True)
        if first:
            m_new = jnp.broadcast_to(top, (s.shape[0], 128))
        else:
            m_old = m_s[at]
            m_new = jnp.maximum(m_old, top)
        total = None
        parts = []
        for j in range(s.shape[1] // 128):
            p = jnp.exp(s[:, 128 * j:128 * j + 128] - m_new)
            total = p if total is None else total + p
            parts.append(p.astype(bf16))
        pv = dot(jnp.concatenate(parts, 1), v)
        m_s[at] = m_new
        if first:
            l_s[at] = total
            acc_s[at] = pv
        else:
            fade = jnp.exp(m_old - m_new)
            l_s[at] = l_s[at] * fade + total
            acc_s[at] = acc_s[at] * fade + pv

    low = lanes_below((tile, 128), 64)

    def heads(q_at, state, k_b, k_c, k_d, mask, first):
        a = q[q_at, 0:128]
        zero = jnp.zeros_like(a)
        update(state, jnp.where(low, a, zero), k_b, k_c, mask, first)
        update(state + 1, jnp.where(low, zero, a), k_b, k_c, mask, first)
        update(state + 2, q[q_at, 128:256], k_d, k_d, mask, first)

    tiles = plen // tile

    def prompt_part(slot, group, diagonal):
        def body(t):
            i = group * tiles + t
            at = rows(group * plen, plen)
            mask = None
            if diagonal:
                def mask(s):
                    row = lax.broadcasted_iota(jnp.int32, s.shape, 0) + t * tile
                    col = lax.broadcasted_iota(jnp.int32, s.shape, 1)
                    return jnp.where(col <= row, s, NEG)
            heads(
                rows(i * tile, tile), 3 * i,
                kvs[slot, at, 0:128], kvs[slot, at, 128:256], kvs[slot, at, 256:384],
                mask, diagonal,
            )

        loop(tiles, body)

    def cont_part(slot, first):
        def body(i):
            k = kvs[slot, 0:plen]
            for g in range(1, groups):
                k = jnp.where(sel[i] == g, kvs[slot, g * plen:(g + 1) * plen], k)
            heads(
                rows(n_prompt + i * tile, tile), 3 * (groups * tiles + i),
                k[:, 0:128], k[:, 128:256], k[:, 256:384], None, first,
            )

        loop(conts, body)

    def self_part():
        def body(i):
            at = rows(i * tile, tile)

            def mask(s):
                row = lax.broadcasted_iota(jnp.int32, s.shape, 0)
                col = lax.broadcasted_iota(jnp.int32, s.shape, 1)
                bias = (valid[pl.ds(i, 1)].astype(f32) - 1.0) * (-NEG)
                return jnp.where(col <= row, s + bias, NEG)

            heads(
                rows(n_prompt + i * tile, tile), 3 * (groups * tiles + i),
                kvc[at, 0:128], kvc[at, 128:256], kvc[at, 256:384], mask, False,
            )

        loop(conts, body)

    cont_part(me, True)
    loop(groups, lambda g: prompt_part(me, g, True))
    self_part()
    e0 = q[n_prompt:n_prompt + clen, 128:256].astype(f32)
    e1 = q[n_prompt + clen:n_prompt + n_cont, 128:256].astype(f32)
    qpack[0:n_cont] = q[n_prompt:n_prompt + n_cont, 0:128]
    qpack[n_cont:n_cont + clen] = jnp.where(low, e0, pltpu.roll(e1, 64, 1)).astype(bf16)

    def ring(e):
        d = e + 1

        def group(g):
            @pl.when(me - d >= 0)
            def _():
                hop(me - d, g, 1, 0).wait_recv()

                @pl.when(me < last)
                def _():
                    hop(me - d, g, 1, 0).start()

            @pl.when(me + d <= last)
            def _():
                hop(me + d, g, -1, 1).wait_recv()

                @pl.when(me > 0)
                def _():
                    hop(me + d, g, -1, 1).start()

            @pl.when((me - d > 0) | ((me == d) & (g < groups - 1)))
            def _():
                prompt_part(me - d, g, False)

        loop(groups, group)

        @pl.when(me - d >= 0)
        def _():
            cont_part(me - d, False)

        @pl.when(me + d <= last)
        def _():
            cont_part(me + d, False)

    loop(last, ring)

    for copy in counts:
        copy.wait()
    for d in range(n_ctx):
        msgs[8 * d:8 * d + 8] = notes[d]

    def finish(at, state):
        l0 = jnp.sum(l_s[state], -1, keepdims=True)
        l1 = jnp.sum(l_s[state + 1], -1, keepdims=True)
        l2 = jnp.sum(l_s[state + 2], -1, keepdims=True)
        o[at, 0:128] = jnp.where(low, acc_s[state] / l0, acc_s[state + 1] / l1).astype(bf16)
        o[at, 128:256] = jnp.where(low, 0.0, acc_s[state + 2] / l2).astype(bf16)
        return (l0, l1, l2)

    def rest_of_prompts():
        @pl.when(me > 0)
        def _():
            prompt_part(0, groups - 1, False)

        loop(groups * tiles, lambda i: finish(rows(i * tile, tile), 3 * i))

    for i in range(conts):
        state = 3 * (groups * tiles + i)
        sums = finish(rows(n_prompt + i * tile, tile), state)
        lse[8 * i:8 * i + 8] = jnp.zeros((8, tile), f32)
        for h in range(3):
            value = m_s[state + h] + jnp.log(sums[h])
            lse[8 * i + h:8 * i + h + 1] = jnp.transpose(value)[0:1]

    for copy in weights:
        copy.wait()
    for copy in local:
        copy.wait()
    if share:
        local = fetch(((wu_f, wu_o), (wd_f, wd_o)), osem)
    else:
        local = []
    middle_part(
        n_ctx, n_dp, share, n_prompt, clen, depth, rest_of_prompts,
        ids, dwa, o, qpack, msgs, wo_o, wu_f, wd_f, cx, gains, valid, hist, teach,
        gdn, middle_outs, refs, leave,
    )
    for copy in leave:
        copy.wait()
    for slot in range(n_ctx):
        for g in range(groups):
            @pl.when((slot <= me) & (me < last))
            def _():
                hop(slot, g, 1, 0).wait_send()

            @pl.when((slot >= me) & (me > 0))
            def _():
                hop(slot, g, -1, 1).wait_send()

    for group in copies:
        for copy in group:
            copy.wait_send()
    for copy in local:
        copy.wait()


def full_at(a, core, split, c_split):
    b = a // split
    return a + core * split * (1 - b) + b * (split + core * c_split)


class TpSum:
    @staticmethod
    def scratch(half, width):
        n = half // CH
        return [
            pltpu.VMEM((half, width), bf16), pltpu.VMEM((half, width), bf16),
            pltpu.VMEM((half, width), bf16), pltpu.VMEM((half, width), bf16),
            pltpu.VMEM((half, width), f32), DMA((2, n)), DMA((2, n)),
        ]

    def __init__(self, half, start, place, scratch, compute):
        self.half, self.start, self.place, self.compute = half, start, place, compute
        self.snd1, self.rcv1, self.snd2, self.rcv2, self.own, self.send, self.recv = scratch
        self.core, self.mate, self.across = tp_place()
        self.n = half // CH

    def row(self, i):
        return lax.rem(self.start + i * CH, self.half)

    def pair(self, i):
        at = rows(self.row(i), CH)
        return remote(
            self.snd1.at[at], self.rcv1.at[at], self.send.at[0, i], self.recv.at[0, i], self.mate
        )

    def link(self, i):
        at = rows(self.row(i), CH)
        return remote(
            self.snd2.at[at], self.rcv2.at[at], self.send.at[1, i], self.recv.at[1, i], self.across
        )

    def second(self, i):
        at = rows(self.row(i), CH)
        self.pair(i).wait()
        self.snd2[at] = (self.own[at] + self.rcv1[at].astype(f32)).astype(bf16)
        self.link(i).start()

    def launch(self, i):
        a = self.row(i)
        at = rows(a, CH)
        self.snd1[at] = self.compute(self.place(a, 1 - self.core), CH).astype(bf16)
        self.pair(i).start()
        self.own[at] = self.compute(self.place(a, self.core), CH)

    def begin(self, held=0, after=None):
        def body(i):
            self.launch(i)

            @pl.when((i > 0) & (i <= self.n - held))
            def _():
                self.second(i - 1)

            if after is not None:
                after(i)

        loop(self.n, body)
        if not held:
            self.second(self.n - 1)

    def resume(self, held):
        for i in range(self.n - held, self.n):
            self.second(i)

    def take(self, i):
        at = rows(self.row(i), CH)
        self.link(i).wait()
        return self.snd2[at].astype(f32) + self.rcv2[at].astype(f32)

class Share:
    def __init__(self, ref, place, sems):
        self.ref, self.place = ref, place
        self.send, self.recv = sems
        _, self.mate, _ = tp_place()

    def copy(self, i, a):
        at = rows(self.place(a), CH)
        return remote(self.ref.at[at], self.ref.at[at], self.send.at[i], self.recv.at[i], self.mate)


def share_scratch(half):
    return [DMA((half // CH,)), DMA((half // CH,))]


GELU = 0.7978845608028654


def gelu_tanh(u):
    return jnp.tanh(GELU * (u + 0.044715 * (u * u * u)))


def mixed_states(ids, dwa, hist, at, y):
    mixed = dwa[4] * y
    for j in range(4):
        mixed += dwa[ids[j]] * hist[j, at].astype(f32)
    return mixed


def column(row):
    return jnp.transpose(jnp.broadcast_to(row, (128, row.shape[1])))


def down_grads(hid, dm, cols, lo, hi, store):
    for j in range(lo, hi, 128):
        store(j, dot_tn(hid[:, j:j + 128], dm[:, cols]))


def other_grads(ff, xn, du, o, da, cols, store):
    size = cols.size
    for j in range(ff // size):
        store(j * size, dot_tn(xn[:, cols], du[:, size * j:size * j + size]))
    g = dot_tn(o[...], da[:, cols])
    store(ff, g[0:128])
    store(ff + 128, g[192:256])


def middle_part(
    n_ctx, n_dp, share, n_prompt, clen, depth, between,
    ids, dwa, o, qpack, msgs, wo, wu, wd, cx, gains, valid, hist, teach, gdn, outs, refs, leave,
):
    out, dm, hid, xn, du, da, do, dh1, stat, qs = outs
    hc, tc, slope, h1, dy, mask, hsem, s_q, r_q = refs[:9]
    scratch = refs[9:]
    core, mate, across = tp_place()
    ctx = lax.axis_index("ctx")
    dp = lax.axis_index("dp")
    half = clen
    n_cont = 2 * half
    mine = rows(core * half, half)
    loads = fetch(((hist.at[:, mine], hc), (teach.at[mine], tc)), hsem)
    qs[ctx] = qpack[...]
    mask[...] = column(valid[pl.ds(core, 1)].astype(f32))
    stat[...] = jnp.zeros(stat.shape, f32)
    others = axis_peers("ctx", n_ctx)
    s1, s2, s3 = scratch[0:7], scratch[7:14], scratch[14:21]
    shares = scratch[21:29]

    def place(a, c):
        return a + c * half

    def home(a):
        return a + core * half

    def each(body):
        loop(half // CH, body)

    def attn(at, size):
        return dot(o[rows(n_prompt + at, size)], wo[...])

    first = TpSum(half, 0, place, s1, attn)
    each(first.launch)
    each(first.second)
    moves = [
        remote(qs.at[ctx], qs.at[ctx], s_q.at[d], r_q.at[d], device)
        for d, device in enumerate(others)
    ]
    between()
    leave[0].start()
    give_xn = Share(xn, home, shares[0:2])

    def normed(i):
        a = first.row(i)
        h = cx[rows(home(a), CH)].astype(f32) + first.take(i)
        h1[rows(a, CH)] = h
        whitened, _ = norm_rows(h)
        xn[rows(home(a), CH)] = (whitened * gains[2:3] + gains[3:4]).astype(bf16)
        give_xn.copy(i, a).start()

    def hidden(at, size):
        here = rows(at, size)
        u = dot(xn[here], wu[...])
        t = gelu_tanh(u)
        g = (0.5 * u * (1.0 + t)).astype(bf16)
        hid[here] = g
        slope[here] = 0.5 * (1.0 + t) + (0.5 * GELU) * u * (1.0 - t * t) * (
            1.0 + (3.0 * 0.044715) * (u * u)
        )
        return dot(g, wd[...])

    second = TpSum(half, 0, place, s2, hidden)

    def onward(before, share, after):
        def body(i):
            before(i)

            @pl.when(i > 0)
            def _():
                after.second(i - 1)

            share.copy(i, after.row(i)).wait()
            after.launch(i)

        each(body)
        after.second(after.n - 1)

    for copy in loads:
        copy.wait()
    onward(normed, give_xn, second)
    leave[2].start()
    leave[3].start()
    for copy in moves:
        copy.start()
    give_dm = Share(dm, home, shares[2:4])
    give_out = Share(out, home, shares[4:6])
    count = msgs[0:1]
    for j in range(1, n_ctx):
        count += msgs[8 * j:8 * j + 1]
    coef = (2.0 * dwa[4]) / (jnp.maximum(count, 1.0) * (1.0 * xn.shape[1]))

    def add(row, value):
        stat[row:row + 1] += jnp.sum(value, 0, keepdims=True)

    def lossy(i):
        a = second.row(i)
        here, there = rows(a, CH), rows(home(a), CH)
        y = h1[here] + second.take(i)
        mixed = mixed_states(ids, dwa, hc, here, y)
        diff = mixed - tc[here].astype(f32)
        weighted = diff * mask[here][:, 0:1]
        grad = weighted * coef[:, 0:1]
        dy[here] = grad
        dm[there] = grad.astype(bf16)
        give_dm.copy(i, a).start()
        out[there] = mixed.astype(bf16)
        give_out.copy(i, a).start()
        add(4, weighted * diff)
        for j in range(4):
            add(5 + j, weighted * hc[j, here].astype(f32))
        add(9, weighted * y)

    def back(at, size):
        here = rows(at, size)
        d = (dot_nt(dm[here], wd[...]) * slope[here]).astype(bf16)
        du[here] = d
        return dot_nt(d, wu[...])

    third = TpSum(half, 0, place, s3, back)
    onward(lossy, give_dm, third)
    leave[1].start()
    leave[4].start()
    if share:
        gsnd, grcv, gown, s_g, r_g = scratch[29:34]
        gives = []
        for d in range(1, n_dp):
            def lay(at, value, d=d):
                gsnd[d - 1, at:at + value.shape[0]] = value.astype(bf16)

            other = lax.rem(dp + d, n_dp)
            down_grads(hid, dm, pl.ds(pl.multiple_of(other * depth, 128), depth), 0, EARLY, lay)
            copy = remote(
                gsnd.at[d - 1], grcv.at[d - 1], s_g.at[d - 1], r_g.at[d - 1], {"dp": other}
            )
            copy.start()
            gives.append(copy)

        def stay(at, value):
            gown[at:at + value.shape[0]] = value

        down_grads(hid, dm, pl.ds(pl.multiple_of(dp * depth, 128), depth), 0, EARLY, stay)
    give_da = Share(da, home, shares[6:8])

    def grads(i):
        a = third.row(i)
        here = rows(a, CH)
        total = third.take(i)
        whitened, inverse = norm_rows(h1[here])
        grad = dy[here] + norm_back(total, whitened, inverse, gains[2:3])
        dh1[here] = grad
        da[rows(home(a), CH)] = grad.astype(bf16)
        give_da.copy(i, a).start()
        add(2, total * whitened)
        add(3, total)

    each(grads)
    each(lambda i: give_da.copy(i, third.row(i)).wait())

    def last(i):
        at = rows(i * BIG, BIG)
        do[at] = dot_nt(da[at], wo[...]).astype(bf16)

    loop(n_cont // BIG, last)
    each(lambda i: give_out.copy(i, second.row(i)).wait())
    for copy in moves:
        copy.wait()
    if share:
        for copy in gives:
            copy.wait()

        def settle(i):
            at = rows(i * 64, 64)
            total = gown[at]
            for d in range(n_dp - 1):
                total += grcv[d, at].astype(f32)
            gdn[at] = total.astype(bf16)

        loop(gdn.shape[0] // 64, settle)


class LineSum:
    @staticmethod
    def scratch(count, width):
        count = count * SUB
        buffer = pltpu.VMEM((count, PIECE, width), bf16)
        return [buffer, buffer, buffer, DMA((2, count)), DMA((2, count))]

    def __init__(self, me, src, dst, scratch):
        self.src, self.dst = src, dst
        self.got, self.pair, self.far, self.send, self.recv = scratch
        side = me // 2
        self.outer = (me == 0) | (me == 3)
        self.inner = (me == 1) | (me == 2)
        self.near = {"ctx": 1 + side}
        self.back = {"ctx": 3 * side}
        self.twin = {"ctx": 2 - side}

    def at(self, k):
        return rows(k * PIECE, PIECE)

    def up(self, k):
        return remote(
            self.src.at[self.at(k)], self.got.at[k], self.send.at[0, k], self.recv.at[0, k], self.near
        )

    def cross(self, k):
        return remote(
            self.pair.at[k], self.far.at[k], self.send.at[1, k], self.recv.at[1, k], self.twin
        )

    def down(self, k):
        return remote(
            self.pair.at[k], self.got.at[k], self.send.at[0, k], self.recv.at[0, k], self.back
        )

    def launch(self, k):
        @pl.when(self.outer)
        def _():
            for s in range(SUB):
                self.up(k * SUB + s).start()

    def meet(self, k):
        @pl.when(self.inner)
        def _():
            for s in range(SUB):
                j = k * SUB + s
                self.up(j).wait_recv()
                self.pair[j] = (
                    self.src[self.at(j)].astype(f32) + self.got[j].astype(f32)
                ).astype(bf16)
                self.cross(j).start()

    def turn(self, k):
        @pl.when(self.inner)
        def _():
            for s in range(SUB):
                j = k * SUB + s
                self.cross(j).wait()
                total = (self.pair[j].astype(f32) + self.far[j].astype(f32)).astype(bf16)
                self.pair[j] = total
                self.down(j).start()
                self.dst[self.at(j)] = total

    def land(self, k):
        @pl.when(self.outer)
        def _():
            for s in range(SUB):
                j = k * SUB + s
                self.up(j).wait_send()
                self.down(j).wait_recv()
                self.dst[self.at(j)] = self.got[j]

        @pl.when(self.inner)
        def _():
            for s in range(SUB):
                self.down(k * SUB + s).wait_send()


def input_grad_tail(
    n_dp, n_ctx, share, split, c_split, depth,
    dcat, w, px, cx, gains, dh1, stat_in, xn1, grad_p, grad_c, fin,
    smalls, sums, shares, prompts_out, prompts_done, *q_state,
):
    grad, stat, stats_m, stats_y, stats_c, stats_d, s_s, r_s, osem = smalls
    core, mate, across = tp_place()
    me = lax.axis_index("ctx")
    dp = lax.axis_index("dp")
    ctx_peers = axis_peers("ctx", n_ctx)
    dp_peers = axis_peers("dp", n_dp)
    half = split + c_split
    n_prompt = 2 * split
    n_cont = 2 * c_split
    if share:
        qsnd, qrcv, s_q, r_q, gall, line, settle_kv, n_late = q_state
        n_line = gall.shape[0] // LINE - 1
    else:
        (g_q,) = q_state

    def q_grads(cols):
        part = dot_tn(dcat[n_prompt:n_prompt + n_cont, 0:256], xn1[n_prompt:n_prompt + n_cont, cols])
        return part[0:3 * HEAD_DIM]

    gives = []
    if share:
        for d in range(1, n_dp):
            other = lax.rem(dp + d, n_dp)
            cols = pl.ds(pl.multiple_of(other * depth, 128), depth)
            qsnd[d - 1] = q_grads(cols).astype(bf16)
            copy = remote(
                qsnd.at[d - 1], qrcv.at[d - 1], s_q.at[d - 1], r_q.at[d - 1], {"dp": other}
            )
            copy.start()
            gives.append(copy)

    stat[...] = 0.5 * stat_in[...]

    def place(a, c):
        return full_at(a, c, split, c_split)

    def home(a):
        return full_at(a, core, split, c_split)

    def compute(at, size):
        part = dot(dcat[rows(at, size)], w[...])
        b = at // n_prompt
        p = px[rows(at * (1 - b), size)].astype(f32)
        c = cx[rows((at - n_prompt) * b, size)].astype(f32)
        whitened, _ = norm_rows(jnp.where(b == 0, p, c))
        stat[0:1] += jnp.sum(part * whitened, 0, keepdims=True)
        stat[1:2] += jnp.sum(part, 0, keepdims=True)
        return part

    total = TpSum(half, split, place, sums, compute)

    def also(i):
        if share:
            @pl.when(lax.rem(i, 2) == 0)
            def _():
                line.meet(2 + i // 2)

    total.begin(2, also)

    def small(src, dst, i, device):
        return remote(src, dst, s_s.at[i], r_s.at[i], device)

    stats_m[0] = stat[...]
    to_mate = small(stats_m.at[0], stats_m.at[1], 0, mate)
    to_mate.start()
    if share:
        settle_kv()
        loop(n_line - n_late, lambda k: line.launch(k + n_late))
    else:
        g_q[...] = q_grads(slice(None)).astype(bf16)
    to_mate.wait()
    stats_y[0] = stats_m[0] + stats_m[1]
    to_far = small(stats_y.at[0], stats_y.at[1], 1, across)
    to_far.start()
    total.resume(2)
    if share:
        line.meet(5)
        for copy in gives:
            copy.wait()
        value = q_grads(pl.ds(pl.multiple_of(dp * depth, 128), depth))
        for d in range(n_dp - 1):
            value += qrcv[d].astype(f32)
        gall[n_line * LINE:n_line * LINE + 3 * HEAD_DIM] = value.astype(bf16)
        line.launch(n_line)
    if share:
        line.turn(0)
        line.meet(6)
    give = Share(grad, home, shares)

    def finish(i):
        a = total.row(i)
        b = a // split
        value = total.take(i)
        p = px[rows((core * split + a) * (1 - b), CH)].astype(f32)
        c = cx[rows((core * c_split + a - split) * b, CH)].astype(f32)
        whitened, inverse = norm_rows(jnp.where(b == 0, p, c))
        back = norm_back(value, whitened, inverse, gains[0:1])
        extra = dh1[rows((a - split) * b, CH)]
        grad[rows(home(a), CH)] = jnp.where(b == 0, back, back + extra).astype(bf16)
        give.copy(i, a).start()
        if share:
            k = 1 + i + i // 3
            line.turn(k)

            @pl.when(i < 5)
            def _():
                line.meet(7 + i)

            @pl.when(lax.rem(i, 3) == 2)
            def _():
                line.turn(k + 1)

    def part(lo, hi):
        loop(hi - lo, lambda i: finish(i + lo))

    part(0, 2)
    prompts_out()
    part(2, 4)
    to_far.wait()
    stats_c[me] = stats_y[0] + stats_y[1]
    to_ctx = [
        small(stats_c.at[me], stats_c.at[me], 2 + d, device) for d, device in enumerate(ctx_peers)
    ]
    for copy in to_ctx:
        copy.start()
    part(4, 6)
    if share:
        line.turn(9)
    for copy in to_ctx:
        copy.wait()
    value = stats_c[0]
    for d in range(1, n_ctx):
        value += stats_c[d]
    stats_d[dp] = value
    to_dp = [
        small(stats_d.at[dp], stats_d.at[dp], 1 + n_ctx + d, device)
        for d, device in enumerate(dp_peers)
    ]
    for copy in to_dp:
        copy.start()
    if share:
        for k in range(10, n_line + 1):
            line.turn(k)
    prompts_done()
    loop(total.n, lambda i: give.copy(i, total.row(i)).wait())
    saves = fetch(
        ((grad.at[0:n_prompt], grad_p), (grad.at[n_prompt:n_prompt + n_cont], grad_c)), osem
    )
    for copy in to_dp:
        copy.wait()
    value = stats_d[0]
    for d in range(1, n_dp):
        value += stats_d[d]
    fin[...] = value
    if share:
        loop(n_line + 1, line.land)
    for copy in saves:
        copy.wait()


def attend_back_body(
    n_ctx, n_dp, share, plen, clen, groups, conts, depth,
    ids, dwa, msgs, do_h, o_h, lse, valid, gains, kv_h, tab_h, qs_h, hid_h, dm_h, xn2_h, du_h, da_h,
    wo_h, wu_h, wd_h, px_h, hist_h, xn1_h, w_h, cx_h, dh1_h, stat_in, *refs,
):
    if share:
        g_first, out_o, grad_p, grad_c, fin, g_sum = refs[:6]
        refs = refs[6:]
    else:
        out_o, grad_p, grad_c, fin, g_down, g_up, g_out, g_kv, g_q = refs[:9]
        refs = refs[9:]
    (
        hid, dm, xn2, du, da, wo, wu, wd, px, hist, lsem,
        dos, sts, dqs, kd, acc_k, acc_v, acc_kd, acc_vd, dq_f, send, recv,
        xp, h1, xn1, flags, do, o, kv, tab, qs, w, cx, dh1, dcat,
    ) = refs[:35]
    out, refs = refs[-1], refs[:-1]
    snd1, own = refs[35:37]
    s1 = (snd1, refs[37], refs[39], refs[38], own, *refs[40:42])
    s2 = (snd1, refs[42], refs[39], refs[43], own, *refs[44:46])
    s3 = (snd1, refs[46], refs[47], refs[48], own, *refs[49:51])
    shares = refs[51:57]
    smalls = refs[57:66]
    refs = refs[66:]
    if share:
        gsnd, grcv, s_g, r_g, qsnd, qrcv, s_q, r_q, gall = refs[:9]
        line = LineSum(me_of("ctx"), gall, g_sum, refs[9:14])
    core, mate, across = tp_place()
    me = lax.axis_index("ctx")
    dp = lax.axis_index("dp")
    peers = axis_peers("ctx", n_ctx)
    dp_peers = axis_peers("dp", n_dp) if share else []
    n_prompt = groups * plen
    n_cont = conts * clen
    half = plen
    own_rows = rows(core * half, half)
    loads = fetch(
        (
            (do_h, do), (o_h, o), (wo_h, wo), (px_h, px), (kv_h, kv), (qs_h, qs),
            (hid_h, hid), (dm_h, dm), (xn2_h, xn2), (du_h, du), (da_h, da), (wu_h, wu), (wd_h, wd),
            (tab_h, tab), (xn1_h, xn1), (hist_h.at[:, own_rows], hist),
            (w_h, w), (cx_h, cx), (dh1_h, dh1),
        )
        + (((g_first, gall.at[0:EARLY]),) if share else ()),
        lsem,
    )
    low = lanes_below((clen, 128), 64)
    zero = jnp.zeros((clen, 128), bf16)
    for c in range(conts):
        flags[c * clen:(c + 1) * clen] = column(valid[c:c + 1].astype(f32))

    loads[0].wait()
    loads[1].wait()
    g0 = do[0:clen, 128:256].astype(f32)
    g1 = do[clen:2 * clen, 128:256].astype(f32)
    dos[me, 0:n_cont] = do[:, 0:128]
    dos[me, n_cont:n_cont + clen] = jnp.where(low, pltpu.roll(g0, 64, 1), g1).astype(bf16)
    for c in range(conts):
        at = slice(c * clen, (c + 1) * clen)
        full = slice(n_prompt + c * clen, n_prompt + (c + 1) * clen)
        pa = do[at, 0:128].astype(f32) * o[full, 0:128].astype(f32)
        pe = do[at, 128:256].astype(f32) * o[full, 128:256].astype(f32)
        ta = jnp.transpose(pa)
        te = jnp.transpose(pe)
        st = 8 * c
        sts[me, st:st + 8] = lse[8 * c:8 * c + 8]
        sts[me, st + 3:st + 4] = jnp.sum(ta[0:64], 0, keepdims=True)
        sts[me, st + 4:st + 5] = jnp.sum(ta[64:128], 0, keepdims=True)
        sts[me, st + 5:st + 6] = jnp.sum(te[64:128], 0, keepdims=True)
    greet(peers + [mate, across] + dp_peers)
    sends = []
    for d, device in enumerate(peers):
        for i, ref in enumerate((sts, dos)):
            sends.append(remote(ref.at[me], ref.at[me], send.at[d, i], recv.at[d, i], device))
    for copy in sends:
        copy.start()
    if share:
        loads[19].wait()
        loop(EARLY // LINE, line.launch)

    def place(a, c):
        return a + c * half

    def home(a):
        return a + core * half

    loads[2].wait()
    loads[3].wait()

    def attn(at, size):
        return dot(o[rows(at, size)], wo[...])

    first = TpSum(half, 0, place, s1, attn)
    first.begin()

    for copy in loads[4:11]:
        copy.wait()
    ff = hid.shape[1]
    o_c = o.at[n_prompt:n_prompt + n_cont]
    late = ff - EARLY
    bounds = (0, late + ff + 192, late + ff + 576)
    def cols_of(d):
        return pl.ds(pl.multiple_of(lax.rem(dp + d, n_dp) * depth, 128), depth)

    def give(d, i):
        span = slice(bounds[i], bounds[i + 1])
        return remote(
            gsnd.at[d - 1, span], grcv.at[d - 1, span], s_g.at[d - 1, i], r_g.at[d - 1, i],
            {"dp": lax.rem(dp + d, n_dp)},
        )

    def keeper(d):
        def store(at, value):
            here = slice(at, at + value.shape[0])
            if d > 0:
                gsnd[d - 1, here] = value.astype(bf16)
            else:
                for k in range(n_dp - 1):
                    value = value + grcv[k, here].astype(f32)
                gall[EARLY + at:EARLY + at + value.shape[0]] = value.astype(bf16)

        return store

    def late_grads(cols, store):
        down_grads(hid, dm, cols, EARLY, ff, lambda at, value: store(at - EARLY, value))
        other_grads(ff, xn2, du, o_c, da, cols, lambda at, value: store(at + late, value))

    def kv_grads(cols, store):
        for lo, hi in ((256, 384), (384, 512), (512, 640)):
            store(late + ff + 192 + lo - 256, dot_tn(dcat[:, lo:hi], xn1[:, cols]))

    def settle(i):
        for d in range(1, n_dp):
            give(d, i).wait()
        (late_grads, kv_grads)[i](cols_of(0), keeper(0))

    if share:
        for d in range(1, n_dp):
            late_grads(cols_of(d), keeper(d))
            give(d, 0).start()
    else:
        width = dm.shape[1]
        for j in range(width // 256):
            cols = pl.ds(256 * j, 256)
            span = slice(256 * j, 256 * j + 256)

            def lay_down(at, value, span=span):
                g_down[at:at + 128, span] = value.astype(bf16)

            def lay(at, value, span=span):
                if at < ff:
                    g_up[span, at:at + 256] = value.astype(bf16)
                else:
                    g_out[at - ff:at - ff + value.shape[0], span] = value.astype(bf16)

            down_grads(hid, dm, cols, 0, ff, lay_down)
            other_grads(ff, xn2, du, o_c, da, cols, lay)

    kd[...] = pltpu.roll(kv[0:n_prompt, 256:384].astype(f32), 64, 1).astype(bf16)
    for acc in (acc_k, acc_v, acc_kd, acc_vd):
        acc[...] = jnp.zeros(acc.shape, f32)

    def one_head(q_rows, do_rows, k, v, lse_row, delta_row, mask):
        s = dot_nt(k, q_rows)
        p = jnp.exp(s - lse_row)
        if mask is not None:
            p = mask(p)
        dp_ = dot_nt(v, do_rows)
        ds = (p * (dp_ - delta_row)).astype(bf16)
        return p.astype(bf16), ds

    def halves(a):
        return jnp.where(low, a, zero), jnp.where(low, zero, a)

    def beside(a, keeps):
        return a if keeps is None else jnp.concatenate([a * keep for keep in keeps], 1)

    def continuation(src, c, k_b, k_c, k_d, k_s, mask, keeps):
        base = c * clen
        a0, a1 = halves(qs[src, base:base + clen])
        d0, d1 = halves(dos[src, base:base + clen])
        e = halves(qs[src, n_cont:n_cont + clen])[c]
        g = halves(dos[src, n_cont:n_cont + clen])[c]
        st = 8 * c
        row = lambda i: sts[src, st + i:st + i + 1]
        p0, s0 = one_head(a0, d0, k_b, k_c, row(0), row(3), mask)
        p1, s1_ = one_head(a1, d1, k_b, k_c, row(1), row(4), mask)
        dv = dot(jnp.concatenate([p0, p1], 1), beside(jnp.concatenate([d0, d1], 0), keeps))
        dk = dot(jnp.concatenate([s0, s1_], 1), beside(jnp.concatenate([a0, a1], 0), keeps))
        dq = jnp.where(low, dot_tn(s0, k_b), dot_tn(s1_, k_b))
        keys, values = (k_d, k_s) if c == 0 else (k_s, k_d)
        p2, s2_ = one_head(e, g, keys, values, row(2), row(5), mask)
        dvd = dot(p2, beside(g, keeps))
        dkd = dot(s2_, beside(e, keeps))
        return dk, dv, dkd, dvd, dq, dot_tn(s2_, keys)

    def source(src, own):
        pair = []
        for c in range(conts):
            pick = msgs[pl.ds(src * 8 + 1 + c, 1)]
            keeps = [(pick == 1.0 * g).astype(f32).astype(bf16) for g in range(groups)]

            def choose(ref, lo, hi):
                return sum(
                    ref[g * plen:(g + 1) * plen, lo:hi] * keep for g, keep in enumerate(keeps)
                )

            dk, dv, dkd, dvd, dqa, dqd = continuation(
                src, c, choose(kv, 0, 128), choose(kv, 128, 256), choose(kv, 256, 384),
                choose(kd, 0, 128), None, keeps,
            )
            acc_k[...] += dk
            acc_v[...] += dv
            acc_kd[...] += dkd
            acc_vd[...] += dvd
            pair.append(dqd)
            if own:
                dq_f[c * clen:(c + 1) * clen] = dqa
            else:
                dqs[n_ctx + src, c * clen:(c + 1) * clen] = dqa.astype(bf16)
        third = jnp.where(low, pair[0], pair[1])
        if own:
            dq_f[n_cont:n_cont + clen] = third
        else:
            dqs[n_ctx + src, n_cont:n_cont + clen] = third.astype(bf16)

    def other_of(d):
        return lax.rem(me + 2 * n_ctx - (d + 1), n_ctx)

    def back_copy(d):
        other = other_of(d)
        return remote(
            dqs.at[n_ctx + other], dqs.at[me], send.at[d, 2], recv.at[d, 2], {"ctx": other}
        )

    def visit(d):
        other = other_of(d)
        for i, ref in enumerate((sts, dos)):
            remote(ref.at[other], ref.at[other], send.at[d, i], recv.at[d, i], {"ctx": other}).wait_recv()
        source(other, False)
        back_copy(d).start()

    give_xn = Share(xp, home, shares[0:2])

    def normed(i):
        a = first.row(i)
        h = px[rows(home(a), CH)].astype(f32) + first.take(i)
        h1[rows(a, CH)] = h
        whitened, _ = norm_rows(h)
        xp[rows(home(a), CH)] = (whitened * gains[2:3] + gains[3:4]).astype(bf16)
        give_xn.copy(i, a).start()

    def hidden(at, size):
        u = dot(xp[rows(at, size)], wu[...])
        return dot((0.5 * u * (1.0 + gelu_tanh(u))).astype(bf16), wd[...])

    second = TpSum(half, 0, place, s2, hidden)
    source(me, True)
    for copy in loads[11:13]:
        copy.wait()

    def step(i):
        @pl.when(i < first.n)
        def _():
            normed(i)

        @pl.when((i > 0) & (i <= first.n))
        def _():
            second.second(i - 1)

        @pl.when((i > 0) & (i < n_ctx))
        def _():
            visit(i - 1)

        @pl.when(i < first.n)
        def _():
            give_xn.copy(i, first.row(i)).wait()
            second.launch(i)

    loop(max(half // CH + 1, n_ctx), step)
    if share:
        settle(0)
        n_late = (EARLY + bounds[1]) // LINE
        loop(n_late - EARLY // LINE, lambda k: line.launch(k + EARLY // LINE))
        loop(EARLY // LINE, line.meet)
    loads[13].wait()

    for c in range(conts):
        at = slice(n_prompt + c * clen, n_prompt + (c + 1) * clen)
        k_d = kv[at, 256:384]
        k_s = pltpu.roll(k_d.astype(f32), 64, 1).astype(bf16)

        def mask(p):
            key = lax.broadcasted_iota(jnp.int32, p.shape, 0)
            query = lax.broadcasted_iota(jnp.int32, p.shape, 1)
            return jnp.where(
                key <= query, p * flags[c * clen:(c + 1) * clen, 0:1], 0.0
            )

        dk, dv, dkd, dvd, dqa, dqd = continuation(
            me, c, kv[at, 0:128], kv[at, 128:256], k_d, k_s, mask, None
        )
        dq_f[c * clen:(c + 1) * clen] += dqa
        keep = low if c == 0 else jnp.logical_not(low)
        dq_f[n_cont:n_cont + clen] += jnp.where(keep, dqd, 0.0)
        t = tab[plen:plen + clen]
        dcat[at, 256:384] = turn(dk, t, -1.0, False).astype(bf16)
        dcat[at, 384:512] = dv.astype(bf16)
        if c == 0:
            joined = jnp.where(low, dkd, pltpu.roll(dvd, 64, 1))
        else:
            joined = jnp.where(low, pltpu.roll(dkd, 64, 1), dvd)
        dcat[at, 512:640] = turn(joined, t, -1.0, True).astype(bf16)

    zq = jnp.zeros((plen, 256), bf16)
    wide = lanes_below((plen, 128), 64)
    for g in range(groups):
        at = slice(g * plen, (g + 1) * plen)
        t = tab[0:plen]
        dcat[at, 0:256] = zq
        part = slice(128 * g, 128 * g + 128)
        dcat[at, 256:384] = turn(acc_k[:, part], t, -1.0, False).astype(bf16)
        dcat[at, 384:512] = acc_v[:, part].astype(bf16)
        k2 = acc_kd[:, part] + pltpu.roll(acc_kd[:, part], 64, 1)
        v2 = acc_vd[:, part] + pltpu.roll(acc_vd[:, part], 64, 1)
        dcat[at, 512:640] = turn(jnp.where(wide, k2, v2), t, -1.0, True).astype(bf16)

    loads[14].wait()
    if share:
        for d in range(1, n_dp):
            kv_grads(cols_of(d), keeper(d))
            give(d, 1).start()
    else:
        for j in range(xn1.shape[1] // 256):
            span = slice(256 * j, 256 * j + 256)

            def lay_kv(at, value, span=span):
                at = at - late - ff - 192
                g_kv[at:at + 128, span] = value.astype(bf16)

            kv_grads(pl.ds(256 * j, 256), lay_kv)

    for d in range(n_ctx - 1):
        back_copy(d).wait_send()
        other = lax.rem(me + d + 1, n_ctx)
        remote(
            dqs.at[n_ctx + other], dqs.at[other], send.at[d, 2], recv.at[d, 2], {"ctx": other}
        ).wait_recv()
        dq_f[...] += dqs[other].astype(f32)
    for c in range(conts):
        at = slice(n_prompt + c * clen, n_prompt + (c + 1) * clen)
        t = tab[plen:plen + clen]
        pair = dq_f[c * clen:(c + 1) * clen] * 0.125
        dcat[at, 0:128] = turn(pair, t, -1.0, False).astype(bf16)
        third = dq_f[n_cont:n_cont + clen] * 0.125
        if c == 1:
            third = pltpu.roll(third, 64, 1)
        third = jnp.where(low, third, 0.0)
        dcat[at, 128:256] = turn(third, t, -1.0, True).astype(bf16)

    give_out = Share(out, home, shares[2:4])

    def mixed(i):
        a = second.row(i)
        here = rows(a, CH)
        y = h1[here] + second.take(i)
        out[rows(home(a), CH)] = mixed_states(ids, dwa, hist, here, y).astype(bf16)
        give_out.copy(i, a).start()

    def prompts_out():
        loads[15].wait()
        loop(half // CH, mixed)

    leave_out = pltpu.make_async_copy(out, out_o, lsem.at[20])

    def prompts_done():
        loop(half // CH, lambda i: give_out.copy(i, second.row(i)).wait())
        leave_out.start()

    for copy in loads[16:19]:
        copy.wait()
    if share:
        q_state = (qsnd, qrcv, s_q, r_q, gall, line, lambda: settle(1), n_late)
    else:
        q_state = (g_q,)
    input_grad_tail(
        n_dp, n_ctx, share, plen, clen, depth,
        dcat, w, px, cx, gains, dh1, stat_in, xn1, grad_p, grad_c, fin,
        smalls, s3, shares[4:6], prompts_out, prompts_done, *q_state,
    )
    leave_out.wait()
    for copy in sends:
        copy.wait_send()


def output_body(
    n_ctx, n_dp, share, ff,
    ids, msgs, fin, p_out, c_out, p_grad, c_grad, *refs,
):
    n = 1 if share else 0
    parts = refs[:n]
    p_out_o, c_out_o, p_grad_o, c_grad_o, loss, dwa_g, g1, b1, g2, b2 = refs[n:n + 10]
    refs = refs[n + 10:]
    if share:
        results = refs[:4]
        refs = refs[4:]
    held, sem = refs[:4], refs[4]
    if share:
        g_all, r_qkv, r_out, r_up, r_down, gsem = refs[5:]
        g_read = pltpu.make_async_copy(parts[0], g_all, gsem.at[4])
        g_read.start()
    moves = (
        (p_out, p_out_o), (c_out, c_out_o), (p_grad, p_grad_o), (c_grad, c_grad_o)
    )
    reads = [
        pltpu.make_async_copy(s, h, sem.at[0, i]) for i, ((s, _), h) in enumerate(zip(moves, held))
    ]
    copies = [
        pltpu.make_async_copy(h, t, sem.at[1, i]) for i, ((_, t), h) in enumerate(zip(moves, held))
    ]
    for copy in reads:
        copy.start()
    depth = g1.shape[0]
    width = fin.shape[1]
    for read, copy in zip(reads, copies):
        read.wait()
        copy.start()
    if share:
        done = [
            pltpu.make_async_copy(s, r, gsem.at[i])
            for i, (s, r) in enumerate(zip((r_qkv, r_out, r_up, r_down), results))
        ]
        g_read.wait()
        rest = g_all.at[ff:]
        r_down[...] = g_all[0:ff].astype(f32)
        done[3].start()
        for j in range(ff // depth):
            r_up[:, j * depth:(j + 1) * depth] = rest[j * depth:(j + 1) * depth].astype(f32)
        done[2].start()
        r_out[...] = rest[ff:ff + 192].astype(f32)
        done[1].start()
        base = ff + 192
        r_qkv[1, 0:128] = rest[base:base + 128].astype(f32)
        r_qkv[2, 0:128] = rest[base + 128:base + 256].astype(f32)
        r_qkv[1, 128:192] = rest[base + 256:base + 320].astype(f32)
        r_qkv[2, 128:192] = rest[base + 320:base + 384].astype(f32)
        r_qkv[0] = rest[base + 384:base + 576].astype(f32)
        done[0].start()
        copies = copies + done
    count = msgs[0:1, 0:1]
    for j in range(1, n_ctx):
        count += msgs[8 * j:8 * j + 1, 0:1]
    factor = 1.0 / (jnp.maximum(count, 1.0) * (1.0 * width))
    sums = jnp.sum(fin[...], -1, keepdims=True) * factor
    row = lax.broadcasted_iota(jnp.int32, sums.shape, 0)

    def entry(i):
        return jnp.sum(jnp.where(row == i, sums, 0.0))

    loss[0] = entry(4)
    for k in range(4):
        value = 0.0
        for j in range(4):
            value += jnp.where(ids[j] == k, 2.0 * entry(5 + j), 0.0)
        dwa_g[k] = value
    dwa_g[4] = 2.0 * entry(9)
    for i, ref in enumerate((g1, b1, g2, b2)):
        if share:
            ref[...] = fin[i, pl.ds(pl.multiple_of(lax.axis_index("dp") * depth, 128), depth)]
        else:
            piece = jnp.zeros((1, depth), f32)
            for d in range(n_dp):
                here = fin[i:i + 1, d * depth:(d + 1) * depth]
                piece += jnp.where(lax.axis_index("dp") == d, here, 0.0)
            ref[...] = piece.reshape(depth)
    for copy in copies:
        copy.wait()


def per_device(
    n_dp, n_ctx,
    prompt_x, cont_x, prompt_hist, cont_hist, teacher, valid_mask, cont_group, layer_ids,
    dwa_weights, qkv_weight, out_weight, up_weight, down_weight,
    ln1_gain, ln1_bias, ln2_gain, ln2_bias,
):
    groups, plen, width = prompt_x.shape
    conts, clen, _ = cont_x.shape
    depth = qkv_weight.shape[0]
    n_prompt, n_cont = groups * plen, conts * clen
    n_rows = n_prompt + n_cont
    split, c_split = n_prompt // 2, n_cont // 2
    half = split + c_split
    ff = up_weight.shape[1]
    share = depth % 128 == 0
    packed = n_cont + clen
    tab_rows = plen + clen
    vmem = pltpu.VMEM

    w_t = qkv_weight.transpose(1, 2, 0)
    px = prompt_x.reshape(n_prompt, width)
    cx = cont_x.reshape(n_cont, width)
    vectors = (ln1_gain, ln1_bias, ln2_gain, ln2_bias)
    states = vmem((3 * (n_prompt // clen + conts), clen, 128), f32)
    if share:
        given = (out_weight, up_weight, down_weight)
    else:
        out_w = lax.all_gather(out_weight, "dp", axis=1, tiled=True)
        given = (
            jnp.concatenate([out_w[:128], jnp.zeros((64, width), bf16), out_w[128:]], 0),
            lax.all_gather(up_weight, "dp", axis=0, tiled=True),
            lax.all_gather(down_weight, "dp", axis=1, tiled=True),
        )
    outs = [
        ((n_rows, width), bf16), ((n_rows, 384), bf16), ((tab_rows, 384), f32),
        ((640, width), bf16),
        ((n_rows, 256), bf16), ((8 * conts, clen), f32), ((8 * n_ctx, 128), f32),
        ((8, width), f32),
        ((n_cont, width), bf16), ((n_cont, width), bf16), ((n_cont, ff), bf16),
        ((n_cont, width), bf16), ((n_cont, ff), bf16), ((n_cont, width), bf16),
        ((n_cont, 256), bf16), ((c_split, width), f32), ((16, width), f32),
        ((n_ctx, packed, 128), bf16),
    ]
    out_specs = (
        [HBM_SPEC] * 5 + [VMEM_SPEC] * 4 + [HBM_SPEC] * 4 + [VMEM_SPEC] * 5
    )
    leaving = [vmem(s, d) for s, d in outs[4:5] + outs[9:13]] + [DMA((5,))]
    whole_out = vmem((256, width), bf16)
    extra = []
    held = [whole_out]
    if share:
        outs += [
            ((EARLY, depth), bf16), ((width, ff), bf16), ((ff, width), bf16), ((256, width), bf16),
        ]
        out_specs += [VMEM_SPEC] + [HBM_SPEC] * 2 + [VMEM_SPEC]
        held = like(*given)
        extra = [
            vmem((n_dp - 1, EARLY, depth), bf16), vmem((n_dp - 1, EARLY, depth), bf16),
            vmem((EARLY, depth), f32), DMA((n_dp - 1,)), DMA((n_dp - 1,)),
        ]
    got = kernel_call(
        functools.partial(front_body, n_ctx, n_dp, share, plen, clen, groups, conts),
        outs,
        [
            vmem((packed, 128), bf16),
            vmem((n_rows, width), bf16), vmem((n_rows, 256), bf16),
            vmem((n_ctx, n_prompt, 384), bf16), vmem((n_cont, 384), bf16),
            vmem((tab_rows, 384), f32), vmem((640, width), bf16),
            vmem((8, depth), f32), vmem((n_dp, 8, depth), f32),
            vmem((8, 128), f32), vmem((n_dp, 8, 128), f32), vmem((n_ctx, 8, 128), f32),
            states, states, states,
            vmem((1, 3, 192, depth) if share else (n_dp, 3, 192, depth), bf16),
            DMA((n_dp - 1, 7)), DMA((n_dp - 1, 7)),
            DMA((2, n_ctx, groups)), DMA((n_ctx, groups)), DMA((n_ctx - 1,)), DMA((n_ctx - 1,)),
            DMA((n_dp - 1, 4)), DMA((n_dp - 1, 4)), DMA((9,)),
        ]
        + like(w_t, px, cx)
        + [DMA((6,)), vmem((width, ff), bf16), vmem((ff, width), bf16)]
        + held
        + [
            vmem((4, c_split, width), bf16), vmem((c_split, width), bf16),
            vmem((n_cont, ff), f32), vmem((c_split, width), f32),
            vmem((c_split, width), f32), vmem((clen, 128), f32),
            DMA((2,)), DMA((n_ctx - 1,)), DMA((n_ctx - 1,)),
        ]
        + TpSum.scratch(c_split, width) * 3
        + share_scratch(c_split) * 4
        + extra
        + leaving,
        0,
        [SMEM_SPEC] * 3 + [HBM_SPEC] * 3 + [VMEM_SPEC] * 5 + [HBM_SPEC] * 5,
        (
            cont_group, layer_ids, dwa_weights, px, cx, w_t, *vectors, valid_mask, *given,
            cont_hist.reshape(4, n_cont, width), teacher.reshape(n_cont, width),
        ),
        "front",
        out_specs,
    )
    xn1, kv, tab, w_full, o, lse, msgs, gains = got[:8]
    cont_out, dm, hid, xn2, du, da, do, dh1, stat, qs = got[8:18]
    if share:
        g_first = [got[18]]
        wu, wd, wo = got[19:22]
    else:
        g_first = []
        wo, wu, wd = given

    grad_rows = 2 * ff + 12 * HEAD_DIM
    outs = [
        ((n_prompt, width), bf16), ((n_prompt, width), bf16), ((n_cont, width), bf16),
        ((16, width), f32),
    ]
    out_specs = [HBM_SPEC] * 3 + [VMEM_SPEC]
    if share:
        outs += [((grad_rows, depth), bf16)]
        out_specs += [VMEM_SPEC]
        late = grad_rows - EARLY - 3 * HEAD_DIM
        third = (n_dp - 1, 3 * HEAD_DIM, depth)
        extra = [
            vmem((n_dp - 1, late, depth), bf16), vmem((n_dp - 1, late, depth), bf16),
            DMA((n_dp - 1, 2)), DMA((n_dp - 1, 2)),
            vmem(third, bf16), vmem(third, bf16),
            DMA((n_dp - 1,)), DMA((n_dp - 1,)), vmem((grad_rows, depth), bf16),
        ] + LineSum.scratch(grad_rows // LINE, depth)
    else:
        outs += [
            ((ff, width), bf16), ((width, ff), bf16), ((3 * HEAD_DIM, width), bf16),
            ((384, width), bf16), ((3 * HEAD_DIM, width), bf16),
        ]
        out_specs += [VMEM_SPEC] * 5
        extra = []
    acc = vmem((plen, 128 * groups), f32)
    wide = vmem((split, width), bf16)
    tall = vmem((half, width), bf16)
    n_p, n_h = split // CH, half // CH
    back = kernel_call(
        functools.partial(
            attend_back_body, n_ctx, n_dp, share, plen, clen, groups, conts, depth
        ),
        outs,
        [
            vmem((n_cont, ff), bf16), vmem((n_cont, width), bf16),
            vmem((n_cont, width), bf16), vmem((n_cont, ff), bf16),
            vmem((n_cont, width), bf16), vmem((256, width), bf16),
            vmem((width, ff), bf16), vmem((ff, width), bf16),
            vmem((n_prompt, width), bf16), vmem((4, split, width), bf16), DMA((21,)),
            vmem((n_ctx, packed, 128), bf16), vmem((n_ctx, 8 * conts, clen), f32),
            vmem((2 * n_ctx, packed, 128), bf16), vmem((n_prompt, 128), bf16),
            acc, acc, acc, acc, vmem((packed, 128), f32),
            DMA((n_ctx - 1, 3)), DMA((n_ctx - 1, 3)),
            vmem((n_prompt, width), bf16), vmem((split, width), f32),
            vmem((n_rows, width), bf16), vmem((n_cont, 128), f32),
        ]
        + like(do, o, kv, tab, qs, w_full, cx, dh1)
        + [
            vmem((n_rows, 640), bf16), tall, vmem((half, width), f32),
            wide, wide, wide, DMA((2, n_p)), DMA((2, n_p)),
            wide, wide, DMA((2, n_p)), DMA((2, n_p)),
            tall, tall, tall, DMA((2, n_h)), DMA((2, n_h)),
        ]
        + share_scratch(split) * 2
        + share_scratch(half)
        + [
            vmem((n_rows, width), bf16), vmem((16, width), f32), vmem((2, 16, width), f32),
            vmem((2, 16, width), f32), vmem((n_ctx, 16, width), f32),
            vmem((n_dp, 16, width), f32),
            DMA((1 + n_ctx + n_dp,)), DMA((1 + n_ctx + n_dp,)), DMA((2,)),
        ]
        + extra
        + [vmem((n_prompt, width), bf16)],
        2,
        [SMEM_SPEC] * 2
        + [VMEM_SPEC] + [HBM_SPEC] * 2 + [VMEM_SPEC] * 3 + [HBM_SPEC] * 17 + [VMEM_SPEC]
        + [HBM_SPEC] * len(g_first),
        (
            layer_ids, dwa_weights, msgs, do, o, lse, valid_mask, gains, kv, tab, qs,
            hid, dm, xn2, du, da, wo, wu, wd, px, prompt_hist.reshape(4, n_prompt, width), xn1,
            w_full, cx, dh1, stat, *g_first,
        ),
        "back",
        out_specs,
    )
    prompt_out, grad_p, grad_c, fin = back[:4]

    outs = [
        ((n_prompt, width), bf16), ((n_cont, width), bf16), ((n_prompt, width), bf16),
        ((n_cont, width), bf16), ((1,), f32), ((5,), f32),
    ] + [((depth,), f32)] * 4
    out_specs = [HBM_SPEC] * 4 + [SMEM_SPEC] * 2 + [VMEM_SPEC] * 4
    specs = [SMEM_SPEC] + [VMEM_SPEC] * 2 + [HBM_SPEC] * 4
    args = (layer_ids, msgs, fin, prompt_out, cont_out, grad_p, grad_c)
    if share:
        shapes = [(3, 192, depth), (192, depth), (depth, ff), (ff, depth)]
        outs += [(s, f32) for s in shapes]
        out_specs += [HBM_SPEC] * 4
        args += (back[4],)
        specs += [HBM_SPEC]
        held_grads = like(back[4]) + [vmem(s, f32) for s in shapes] + [DMA((5,))]
    else:
        held_grads = []
    done = pl.pallas_call(
        functools.partial(output_body, n_ctx, n_dp, share, ff),
        out_shape=[jax.ShapeDtypeStruct(s, d) for s, d in outs],
        in_specs=specs,
        out_specs=out_specs,
        scratch_shapes=[
            vmem((n_prompt, width), bf16), vmem((n_cont, width), bf16),
            vmem((n_prompt, width), bf16), vmem((n_cont, width), bf16), DMA((2, 4)),
        ]
        + held_grads,
        compiler_params=pltpu.CompilerParams(vmem_limit_bytes=LIMIT),
        name="outputs",
    )(*args)
    if share:
        r_qkv, r_out, r_up, r_down = done[10:]
        r_qkv = r_qkv.transpose(2, 0, 1)
    else:
        def scattered(g, dim):
            part = lax.psum_scatter(g, "dp", scatter_dimension=dim, tiled=True)
            return lax.psum(part, "ctx").astype(f32)

        g_down, g_up, g_out, g_kv, g_q = back[4:]
        r_down = scattered(g_down, 1)
        r_up = scattered(g_up, 0)
        r_out = scattered(g_out, 1)
        g_k = jnp.concatenate([g_kv[0:128], g_kv[256:320]], 0)
        g_v = jnp.concatenate([g_kv[128:256], g_kv[320:384]], 0)
        r_qkv = scattered(jnp.stack([g_q, g_k, g_v]).transpose(2, 0, 1), 0)
    return (
        done[0].reshape(groups, plen, width),
        done[1].reshape(conts, clen, width),
        done[4].reshape(()),
        done[2].reshape(groups, plen, width),
        done[3].reshape(conts, clen, width),
        r_qkv, r_out, r_up, r_down,
        done[6], done[7], done[8], done[9],
        done[5],
    )


def solution(mesh):
    n_dp, n_ctx = mesh.shape["dp"], mesh.shape["ctx"]
    in_specs = (
        P("dp", "ctx", None), P(("dp", "ctx"), None, None), P(None, "dp", "ctx", None),
        P(None, ("dp", "ctx"), None, None), P(("dp", "ctx"), None, None), P(("dp", "ctx"), None),
        P(("dp", "ctx")), P(), P(), P("dp", None, "tp"), P("tp", "dp"), P("dp", "tp"),
        P("tp", "dp"), P("dp"), P("dp"), P("dp"), P("dp"),
    )
    out_specs = (
        P("dp", "ctx", None), P(("dp", "ctx"), None, None), P(), P("dp", "ctx", None),
        P(("dp", "ctx"), None, None), P("dp", None, "tp"), P("tp", "dp"), P("dp", "tp"),
        P("tp", "dp"), P("dp"), P("dp"), P("dp"), P("dp"), P(),
    )
    return jax.shard_map(
        functools.partial(per_device, n_dp, n_ctx),
        mesh=mesh, in_specs=in_specs, out_specs=out_specs, check_vma=False,
    )
```
